32 devices in a mesh: wide: 16 (over z, x, core), narrow: 2 (over y).
Axes of the slice: x: 2, y: 2, z: 4, core: 2. Of those that a mesh axis runs over, the one named last changes fastest.
Arguments:
- tokens: bfloat16 [8192, 1024], P(('wide', 'narrow')), may hold values from -6 to 6
- skip: bfloat16 [8192, 1024], P(('wide', 'narrow')), may hold values from -6 to 6
- seg_ids: int32 [32, 256], P(('wide', 'narrow')), may hold values from 0 to 7, never falling along the last dimension, each value on 1 to 128 neighbouring positions
- valid: int32 [32, 256], P(('wide', 'narrow')), may hold values 0 or 1
- w_skip: bfloat16 [2048, 1024], P(('wide', 'narrow')), may hold values from -0.125 to 0.125
- b_skip: bfloat16 [1024], P(('wide', 'narrow')), may hold values from -4 to 4
- g_one: bfloat16 [1024], P(('wide', 'narrow')), may hold values from 0.5 to 1.5
- beta_one: bfloat16 [1024], P(('wide', 'narrow')), may hold values from -4 to 4
- w_qkv: bfloat16 [1024, 3072], P(('wide', 'narrow')), may hold values from -0.1875 to 0.1875
- w_out: bfloat16 [1024, 1024], P(('wide', 'narrow')), may hold values from -0.75 to 0.75
- g_two: bfloat16 [1024], P(('wide', 'narrow')), may hold values from 0.5 to 1.5
- beta_two: bfloat16 [1024], P(('wide', 'narrow')), may hold values from -4 to 4
- w_up: bfloat16 [1024, 4096], P(('wide', 'narrow')), may hold values from -0.1875 to 0.1875
- b_up: bfloat16 [4096], P(('wide', 'narrow')), may hold values from -4 to 4
- w_down: bfloat16 [4096, 1024], P(('wide', 'narrow')), may hold values from -0.09375 to 0.09375
- b_down: bfloat16 [1024], P(('wide', 'narrow')), may hold values from -4 to 4
- cotangent: bfloat16 [8192, 1024], P(('wide', 'narrow')), may hold values from -6 to 6
Outputs:
- result: bfloat16 [8192, 1024], P(('wide', 'narrow'))
- grad_tokens: bfloat16 [8192, 1024], P(('wide', 'narrow'))
- grad_skip: bfloat16 [8192, 1024], P(('wide', 'narrow'))
- grad_w_skip: float32 [2048, 1024], P(('wide', 'narrow'))
- grad_b_skip: float32 [1024], P(('wide', 'narrow'))
- grad_g_one: float32 [1024], P(('wide', 'narrow'))
- grad_beta_one: float32 [1024], P(('wide', 'narrow'))
- grad_w_qkv: float32 [1024, 3072], P(('wide', 'narrow'))
- grad_w_out: float32 [1024, 1024], P(('wide', 'narrow'))
- grad_g_two: float32 [1024], P(('wide', 'narrow'))
- grad_beta_two: float32 [1024], P(('wide', 'narrow'))
- grad_w_up: float32 [1024, 4096], P(('wide', 'narrow'))
- grad_b_up: float32 [4096], P(('wide', 'narrow'))
- grad_w_down: float32 [4096, 1024], P(('wide', 'narrow'))
- grad_b_down: float32 [1024], P(('wide', 'narrow'))
The draws below stay inside these ranges and needn't reach their ends.
Inputs may be any that keep to these rules, and one draw needn't show every extreme that they name: `seg_ids`: ids never fall along a pack; an utterance has at most 128 frames.
All inputs are finite; a program needn't handle non-finite values. No bound on the sum of `valid` on one device may be relied on, other than what follows from the above.
Results may differ from the reference program's by a relative error of at most 0.015.
Values may be sent and summed in bfloat16 or wider, within the bound.
A program may use at most 256 MiB of HBM per device.

```python
import math
import jax
import jax.numpy as jnp
import numpy as np
from jax import lax

D = 1024
HEADS = 16
HEAD = 64
FF = 4096
TOK_DEV = 256
UTTS = 8
BLOCKS = 32
TOKENS = 8192


def place_ends(result, key, least, top_value):
    longest = result.shape.index(max(result.shape))
    spots = []
    for shift in (0, 1):
        where = [jax.random.randint(jax.random.fold_in(key, axis), (), 0, length) for axis, length in enumerate(result.shape)]
        where[longest] = (where[longest] + shift) % result.shape[longest]
        spots.append(tuple(where))
    return result.at[spots[0]].set(least).at[spots[1]].set(top_value)


def raised(result, key, source, target, blocks, factor):
    def block_of(position):
        return (jnp.arange(result.shape[position]) // (result.shape[position] // blocks)).reshape((-1,) + (1,) * (result.ndim - 1 - position))

    one_side = jax.random.permutation(key, blocks)[block_of(target)]
    other_side = (block_of(target) + blocks // 2) % blocks
    return jnp.where((block_of(source) == one_side) | (block_of(source) == other_side), factor * result, result)


def block_levels(stream_key, dims, split, least, largest):
    level = 1.0
    for axis_at, shards_of in split:
        heights = jax.random.uniform(jax.random.fold_in(jax.random.fold_in(stream_key, 6), axis_at), (shards_of,), jnp.float32, least / len(split), largest / len(split))
        level = level * jnp.repeat(jnp.exp(heights), dims[axis_at] // shards_of).reshape((-1,) + (1,) * (len(dims) - 1 - axis_at))
    return level


def length_profile(count, total, limit, skew):
    portions = [(1 << 20) // math.isqrt(grade ** skew) + 1 for grade in range(2, count + 1)]
    spare, given = total - limit - (count - 1), [1] * (count - 1)
    while spare > 0:
        movable = [i for i in range(count - 1) if given[i] < limit]
        mass, remaining = sum([portions[i] for i in movable]), spare
        for i in movable:
            extra = min(limit - given[i], max(1, remaining * portions[i] // mass), spare)
            given[i] = given[i] + extra
            spare = spare - extra
    return np.array([limit] + given)


def uneven_parts(stream_key, number_of, total, reach, skew):
    if number_of == 2:
        one = jax.random.randint(stream_key, (), max(1, total - reach), min(reach, total - 1) + 1)
        return jnp.stack([one, total - one])
    lengths = jnp.asarray(length_profile(number_of, total, reach, skew), jnp.int32)
    pairs = (number_of - 1) // 2
    giver, receiver = lengths[1:1 + 2 * pairs:2], lengths[2:2 + 2 * pairs:2]
    slack = jnp.minimum(giver - 1, reach - receiver)
    shifted = jax.random.randint(jax.random.fold_in(stream_key, 1), (pairs,), 0, 1 << 20) % (slack + 1)
    lengths = lengths.at[1:1 + 2 * pairs:2].set(giver - shifted).at[2:2 + 2 * pairs:2].set(receiver + shifted)
    return lengths[jax.random.permutation(jax.random.fold_in(stream_key, 2), number_of)]


def normal_values(key, shape, scale, reach, shards=(), held_as=jnp.bfloat16):
    array = scale * jax.random.normal(key, shape, jnp.float32)
    if shards:
        array = array * block_levels(key, shape, shards, -0.22, 0.18)
    return jnp.clip(array, -reach, reach).astype(held_as)


def bell_draw_with(stream_key, shape, scale, limit, cuts, heavy, kind=jnp.bfloat16):
    values = scale * jax.random.normal(stream_key, shape, jnp.float32)
    if cuts:
        values = values * block_levels(stream_key, shape, cuts, -0.22, 0.18)
    return jnp.clip(raised(values, jax.random.fold_in(stream_key, 3), *heavy), -limit, limit).astype(kind)


def setup_inputs(seed: int = 0) -> dict:
    streams_of = jax.random.split(jax.random.key(seed), 18)
    return {
        "tokens": bell_draw_with(streams_of[0], (TOKENS, D), 1.0, 6.0, ((0, 32),), (0, 1, 32, 2.75)),
        "skip": bell_draw_with(streams_of[1], (TOKENS, D), 1.0, 6.0, ((0, 32),), (0, 1, 32, 2.75)),
        "seg_ids": jax.vmap(lambda own: jnp.searchsorted(jnp.cumsum(uneven_parts(own, UTTS, TOK_DEV, TOK_DEV // 2, 2)), jnp.arange(TOK_DEV), side="right"))(jax.random.split(streams_of[2], BLOCKS)).reshape((BLOCKS, TOK_DEV)).astype(jnp.int32),
        "valid": place_ends((jax.random.randint(streams_of[3], (BLOCKS, TOK_DEV), 0, 8) < 7).astype(jnp.int32), jax.random.fold_in(streams_of[3], 1), 0, 1),
        "w_skip": normal_values(streams_of[4], (2 * D, D), (2 * D) ** -0.5, 0.125, ((0, 32),)),
        "b_skip": normal_values(streams_of[5], (D,), 0.3, 4.0, ((0, 32),)),
        "g_one": jnp.clip(1.0 + 0.1 * jax.random.normal(streams_of[6], (D,), jnp.float32), 0.5, 1.5).astype(jnp.bfloat16),
        "beta_one": normal_values(streams_of[7], (D,), 0.3, 4.0, ((0, 32),)),
        "w_qkv": normal_values(streams_of[8], (D, 3 * D), D ** -0.5, 0.1875, ((0, 32),)),
        "w_out": normal_values(streams_of[9], (D, D), (D // 16) ** -0.5, 0.75, ((0, 32),)),
        "g_two": jnp.clip(1.0 + 0.1 * jax.random.normal(streams_of[10], (D,), jnp.float32), 0.5, 1.5).astype(jnp.bfloat16),
        "beta_two": normal_values(streams_of[11], (D,), 0.3, 4.0, ((0, 32),)),
        "w_up": normal_values(streams_of[12], (D, FF), D ** -0.5, 0.1875, ((0, 32),)),
        "b_up": normal_values(streams_of[13], (FF,), 0.3, 4.0, ((0, 32),)),
        "w_down": normal_values(streams_of[14], (FF, D), FF ** -0.5, 0.09375, ((0, 32),)),
        "b_down": normal_values(streams_of[15], (D,), 0.3, 4.0, ((0, 32),)),
        "cotangent": bell_draw_with(streams_of[16], (TOKENS, D), 1.0, 6.0, ((0, 32),), (0, 1, 32, 2.75)),
    }


epsilon = 1e-05

@jax.custom_vjp
def low(v):
    return lax.optimization_barrier(v.astype(jnp.bfloat16)).astype(jnp.float32)

@jax.custom_vjp
def low_back(v):
    return v

def low_keep(v):
    return (low(v), None)

def low_pass(kept, grad):
    return (grad,)

def back_keep(v):
    return (v, None)

def back_low(kept, grad):
    return (low(grad),)
low.defvjp(low_keep, low_pass)
low_back.defvjp(back_keep, back_low)

def product(left, right):
    return jnp.dot(left, right, precision=lax.Precision.HIGHEST)

def norm_rows(values, gain, shift):
    center = values - lax.optimization_barrier(jnp.mean(values, axis=-1, keepdims=True))
    spread = lax.optimization_barrier(jnp.mean(center * center, axis=-1, keepdims=True))
    return center * lax.rsqrt(spread + epsilon) * gain + shift

def gelu_exact(values):
    return 0.5 * values * (1.0 + lax.erf(values * 0.7071067811865476))

def attend_mask(seg_row, valid_row, head_count):
    count_rows = seg_row.shape[0]
    places = jnp.arange(count_rows, dtype=jnp.int32)
    same_utt = seg_row[:, None] == seg_row[None, :]
    diagonal = places[:, None] == places[None, :]
    allowed = same_utt & ((valid_row[None, :] == 1) | diagonal)
    slopes = 2.0 ** (-8.0 * (jnp.arange(head_count, dtype=jnp.float32) + 1.0) / head_count)
    distance = jnp.abs(places[:, None] - places[None, :]).astype(jnp.float32)
    return (allowed, -slopes[:, None, None] * distance[None, :, :])

def layer_block(block_in, parameters):
    tokens_blk, skip_blk, seg_row, valid_row = block_in
    w_skip, b_skip, g_one, beta_one, w_qkv, w_out, g_two, beta_two, w_up, b_up, w_down, b_down = parameters
    row_count = tokens_blk.shape[0]
    joined = jnp.concatenate([tokens_blk, skip_blk], axis=1)
    hidden = low_back(product(joined, w_skip) + b_skip)
    normed = low(norm_rows(hidden, g_one, beta_one))
    projected = low(low_back(product(normed, w_qkv)))
    queries = projected[:, :D].reshape(row_count, HEADS, HEAD)
    keys_all = projected[:, D:2 * D].reshape(row_count, HEADS, HEAD)
    values_all = projected[:, 2 * D:].reshape(row_count, HEADS, HEAD)
    allowed, linear_bias = attend_mask(seg_row, valid_row, HEADS)
    raw = jnp.einsum('qhd,khd->hqk', queries, keys_all, precision=lax.Precision.HIGHEST) * HEAD ** (-0.5) + linear_bias
    scores = low_back(raw)
    masked = jnp.where(allowed[None, :, :], scores, -1e+30)
    row_top = lax.optimization_barrier(jnp.max(masked, axis=-1, keepdims=True))
    exponent = jnp.exp(masked - row_top)
    soft_weights = exponent / lax.optimization_barrier(jnp.sum(exponent, axis=-1, keepdims=True))
    weighted = jnp.einsum('hqk,khd->qhd', low(soft_weights), values_all, precision=lax.Precision.HIGHEST)
    attended = low(low_back(weighted.reshape(row_count, D)))
    branch = low_back(product(attended, w_out))
    middle = hidden + branch
    normed_two = low(norm_rows(middle, g_two, beta_two))
    hidden_up = low_back(product(normed_two, w_up) + b_up)
    activated = low(gelu_exact(hidden_up))
    feed_out = low_back(product(activated, w_down) + b_down)
    return middle + feed_out

def reference(tokens, skip, seg_ids, valid, w_skip, b_skip, g_one, beta_one, w_qkv, w_out, g_two, beta_two, w_up, b_up, w_down, b_down, cotangent):
    block_count = tokens.shape[0] // TOK_DEV
    parameters = tuple((argument.astype(jnp.float32) for argument in (w_skip, b_skip, g_one, beta_one, w_qkv, w_out, g_two, beta_two, w_up, b_up, w_down, b_down)))
    tokens_in = tokens.astype(jnp.float32).reshape(block_count, TOK_DEV, D)
    skip_in = skip.astype(jnp.float32).reshape(block_count, TOK_DEV, D)

    def forward(tokens_all, skip_all, params_all):

        def one_block(block_in):
            return jax.checkpoint(layer_block)(block_in, params_all)
        return lax.map(one_block, (tokens_all, skip_all, seg_ids, valid))
    outcome, pull_back = jax.vjp(forward, tokens_in, skip_in, parameters)
    grad_in, grad_side, grad_params = pull_back(cotangent.astype(jnp.float32).reshape(block_count, TOK_DEV, D))
    return (outcome.reshape(block_count * TOK_DEV, D).astype(jnp.bfloat16), grad_in.reshape(block_count * TOK_DEV, D).astype(jnp.bfloat16), grad_side.reshape(block_count * TOK_DEV, D).astype(jnp.bfloat16), grad_params[0], grad_params[1], grad_params[2], grad_params[3], grad_params[4], grad_params[5], grad_params[6], grad_params[7], grad_params[8], grad_params[9], grad_params[10], grad_params[11])
```

```python
import functools

import jax
import jax.numpy as jnp
from jax import lax
from jax.experimental import pallas as pl
from jax.experimental.pallas import tpu as pltpu
from jax.sharding import PartitionSpec as P

f32 = jnp.float32
bf16 = jnp.bfloat16

MESH = pl.DeviceIdType.MESH
ZN = 4
SLOTS = 38
ZM, ZX, ZY, XM, XY, YM, YX, CP = 0, 6, 12, 18, 22, 26, 30, 34
OFFSET = 4


def stage_list(count, offset):
    one = [("own",), ("near",)]
    for s in range(3):
        one += [("chain", s), ("side", s)]
    one += [("cross", s) for s in range(3)] + [("last",)]
    merged = []
    for k in range(count):
        for i, e in enumerate(one):
            merged.append((k * offset + i, k, e))
    merged.sort(key=lambda a: (a[0], a[1]))
    return [(k, e) for _, k, e in merged]


def here():
    w = lax.axis_index("wide")
    y = lax.axis_index("narrow")
    c = lax.rem(w, 2)
    x = lax.rem(lax.div(w, 2), 2)
    z = lax.div(w, 4)
    return z, x, c, y


def place(z, x, c, y):
    return ((z * 2 + x) * 2 + c, y)


def greet_all(total_w, total_n):
    barrier = pltpu.get_barrier_semaphore()
    w = lax.axis_index("wide")
    y = lax.axis_index("narrow")
    me = w * total_n + y
    count = total_w * total_n

    @pl.loop(1, count)
    def _(o):
        to = lax.rem(me + o, count)
        pl.semaphore_signal(
            barrier, inc=1, device_id=(lax.div(to, total_n), lax.rem(to, total_n)), device_id_type=MESH
        )

    pl.semaphore_wait(barrier, count - 1)


def gather_kernel(small_ref, *refs):
    n = 5
    own = refs[:n]
    small_out = refs[n]
    full = refs[n + 1 : 2 * n + 1]
    send_sem, recv_sem, local_sem, small_send, small_recv = refs[2 * n + 1 :]
    z, x, c, y = here()
    me = lax.axis_index("wide") * 2 + lax.axis_index("narrow")
    greet_all(16, 2)

    def part(k, zo, xo, yo, first=0, quarters=4):
        width = own[k].shape[1] // 4
        return full[k].at[zo, xo, c, yo, :, pl.ds(first * width, quarters * width)]

    def link(k, slot, src, dst, to):
        return pltpu.make_async_remote_copy(
            src_ref=src, dst_ref=dst, send_sem=send_sem.at[k, slot], recv_sem=recv_sem.at[k, slot],
            device_id=to, device_id_type=MESH)

    xp = place(z, 1 - x, c, y)
    yp = place(z, x, c, 1 - y)
    cpart = place(z, x, 1 - c, y)

    def zto(d):
        return place(z + 1 - 2 * d, x, c, y)

    def z_has(d, s):
        return (z - s >= 0) if d == 0 else (z + s <= ZN - 1)

    def z_next(d):
        return (z < ZN - 1) if d == 0 else (z > 0)

    def zo_of(d, s):
        return z - s if d == 0 else z + s

    sends = []

    def z_send(k, base, d, s, xo, yo, first, quarters, src=None):
        cond = jnp.logical_and(z_has(d, s), z_next(d))
        zo = zo_of(d, s)
        dst = part(k, zo, xo, yo, first, quarters)
        cp = link(k, base + d * 3 + s, dst if src is None else src, dst, zto(d))
        sends.append((cond, cp))

        @pl.when(cond)
        def _():
            cp.start()

    def z_wait(k, base, d, s, xo, yo, first, quarters):
        zo = zo_of(d, s + 1)
        dst = part(k, zo, xo, yo, first, quarters)
        link(k, base + d * 3 + s, dst, dst, zto(d)).wait_recv()

    def go(k, slot, ref, to, src=None, cond=None):
        cp = link(k, slot, ref if src is None else src, ref, to)
        sends.append((cond, cp))
        cp.start()

    def wait(k, slot, ref):
        link(k, slot, ref, ref, xp).wait_recv()

    small_copies = []
    for k in range(n):
        pltpu.make_async_copy(own[k], part(k, z, x, y), local_sem.at[k]).start()

    def do(k, e):
        kind = e[0]
        if kind == "own":
            for d in (0, 1):
                z_send(k, ZM, d, 0, x, y, 0, 4, src=own[k])
            go(k, XM + z, part(k, z, x, y), xp, src=own[k])
            go(k, YM + z, part(k, z, x, y), yp, src=own[k])
        elif kind == "near":
            wait(k, XM + z, part(k, z, 1 - x, y))
            for d in (0, 1):
                z_send(k, ZX, d, 0, 1 - x, y, 0, 1)
            go(k, YX + z, part(k, z, 1 - x, y, 0, 2), yp)
            wait(k, YM + z, part(k, z, x, 1 - y))
            for d in (0, 1):
                z_send(k, ZY, d, 0, x, 1 - y, 3, 1)
            go(k, XY + z, part(k, z, x, 1 - y, 2, 2), xp)
        elif kind == "chain":
            s = e[1]
            for d in (0, 1):
                @pl.when(z_has(d, s + 1))
                def _():
                    z_wait(k, ZM, d, s, x, y, 0, 4)
                    zo = zo_of(d, s + 1)
                    if s < 2:
                        @pl.when(z_next(d))
                        def _():
                            ref = part(k, zo, x, y)
                            link(k, ZM + d * 3 + s + 1, ref, ref, zto(d)).start()
                    ref = part(k, zo, x, y, 1, 3)
                    link(k, XM + zo, ref, ref, xp).start()
                    ref = part(k, zo, x, y, 0, 3)
                    link(k, YM + zo, ref, ref, yp).start()
        elif kind == "side":
            s = e[1]
            for d in (0, 1):
                @pl.when(z_has(d, s + 1))
                def _():
                    zo = zo_of(d, s + 1)
                    for base, xo, yo, first in ((ZX, 1 - x, y, 0), (ZY, x, 1 - y, 3)):
                        z_wait(k, base, d, s, xo, yo, first, 1)
                        if s < 2:
                            @pl.when(z_next(d))
                            def _():
                                ref = part(k, zo, xo, yo, first, 1)
                                link(k, base + d * 3 + s + 1, ref, ref, zto(d)).start()
        elif kind == "cross":
            s = e[1]
            for d in (0, 1):
                @pl.when(z_has(d, s + 1))
                def _():
                    zo = zo_of(d, s + 1)
                    wait(k, XM + zo, part(k, zo, 1 - x, y, 1, 3))
                    ref = part(k, zo, 1 - x, y, 0, 2)
                    link(k, YX + zo, ref, ref, yp).start()
                    wait(k, YM + zo, part(k, zo, x, 1 - y, 0, 3))
                    ref = part(k, zo, x, 1 - y, 2, 2)
                    link(k, XY + zo, ref, ref, xp).start()
            if s == 0:
                pltpu.make_async_copy(own[k], part(k, z, x, y), local_sem.at[k]).wait()
                ref = full[k].at[:, x, c, y]
                link(k, CP, ref, ref, cpart).start()
            if s == 2:
                ref = full[k].at[:, 1 - x, c, y]
                link(k, CP + 1, ref, ref, cpart).start()
                ref = full[k].at[:, x, c, 1 - y]
                link(k, CP + 2, ref, ref, cpart).start()
        elif kind == "last":
            for zo in range(ZN):
                wait(k, XY + zo, part(k, zo, 1 - x, 1 - y, 2, 2))
                wait(k, YX + zo, part(k, zo, 1 - x, 1 - y, 0, 2))
            ref = full[k].at[:, 1 - x, c, 1 - y]
            link(k, CP + 3, ref, ref, cpart).start()

    def small_copy(o, to):
        return pltpu.make_async_remote_copy(
            src_ref=small_ref, dst_ref=small_out.at[me], send_sem=small_send.at[o], recv_sem=small_recv.at[o],
            device_id=(lax.div(to, 2), lax.rem(to, 2)), device_id_type=MESH)

    for i, (k, e) in enumerate(stage_list(n, OFFSET)):
        if i == 1:
            small_out[me] = small_ref[...]

            @pl.loop(1, 32)
            def _(o):
                small_copy(o, lax.rem(me + o, 32)).start()
        do(k, e)

    for k in range(n):
        for j, (xo, yo) in enumerate(((x, y), (1 - x, y), (x, 1 - y), (1 - x, 1 - y))):
            ref = full[k].at[:, xo, 1 - c, yo]
            link(k, CP + j, ref, ref, cpart).wait_recv()
            ref = full[k].at[:, xo, c, yo]
            link(k, CP + j, ref, ref, cpart).wait_send()
        for d in (0, 1):
            for s in range(3):
                @pl.when(jnp.logical_and(z_has(d, s), z_next(d)))
                def _():
                    zo = zo_of(d, s)
                    for base, xo, yo, first, q in ((ZM, x, y, 0, 4), (ZX, 1 - x, y, 0, 1), (ZY, x, 1 - y, 3, 1)):
                        ref = part(k, zo, xo, yo, first, q)
                        link(k, base + d * 3 + s, ref, ref, zto(d)).wait_send()
        ref = part(k, z, x, y)
        link(k, XM + z, ref, ref, xp).wait_send()
        link(k, YM + z, ref, ref, yp).wait_send()
        for t in range(1, ZN):
            zo = lax.rem(z + t, ZN)
            ref = part(k, zo, x, y, 1, 3)
            link(k, XM + zo, ref, ref, xp).wait_send()
            ref = part(k, zo, x, y, 0, 3)
            link(k, YM + zo, ref, ref, yp).wait_send()
        for zo in range(ZN):
            ref = part(k, zo, 1 - x, y, 0, 2)
            link(k, YX + zo, ref, ref, yp).wait_send()
            ref = part(k, zo, x, 1 - y, 2, 2)
            link(k, XY + zo, ref, ref, xp).wait_send()

    @pl.loop(1, 32)
    def _(o):
        small_copy(o, 0).wait_send()
        small_copy(o, 0).wait_recv()


def gather_all(small, shards):
    n = len(shards)
    outs = [jax.ShapeDtypeStruct((32,) + small.shape, small.dtype)] + [
        jax.ShapeDtypeStruct((4, 2, 2, 2) + s.shape, s.dtype) for s in shards]
    sem = pltpu.SemaphoreType.DMA
    return pl.pallas_call(
        gather_kernel, out_shape=outs,
        in_specs=[pl.BlockSpec(memory_space=pltpu.VMEM)] * (n + 1),
        out_specs=[pl.BlockSpec(memory_space=pltpu.VMEM)] + [pl.BlockSpec(memory_space=pl.ANY)] * n,
        scratch_shapes=[sem((n, SLOTS)), sem((n, SLOTS)), sem((n,)), sem((32,)), sem((32,))],
        compiler_params=pltpu.CompilerParams(collective_id=0, has_side_effects=True),
        name="gather_weights",
    )(small, *shards)


def scatter_kernel(n, *refs):
    small_in = refs[0]
    lts = refs[1 : n + 1]
    gs = refs[n + 1 : 2 * n + 1]
    small_out = refs[2 * n + 1]
    outs = refs[2 * n + 2 : 3 * n + 2]
    r = refs[3 * n + 2 :]
    lcat, gcat, part_sums = r[:n], r[n : 2 * n], r[2 * n : 3 * n]
    lxm, lym, lxy, lyx, lzm, lzx, lzy = (r[(3 + i) * n : (4 + i) * n] for i in range(7))
    small_land, send_sem, recv_sem, pair_send, pair_recv, local_sem, small_send, small_recv = r[10 * n :]
    z, x, c, y = here()
    me = lax.axis_index("wide") * 2 + lax.axis_index("narrow")
    greet_all(16, 2)
    xp = place(z, 1 - x, c, y)
    yp = place(z, x, c, 1 - y)
    cpart = place(z, x, 1 - c, y)
    T = lts[0].shape[2]

    def pair(k, j):
        src, dst = (
            (lts[k].at[1 - c], lcat[k].at[:, pl.ds(T, T)]),
            (gs[k], gcat[k].at[pl.ds(T, T), :]),
        )[j]
        return pltpu.make_async_remote_copy(
            src_ref=src, dst_ref=dst, send_sem=pair_send.at[k, j], recv_sem=pair_recv.at[k, j],
            device_id=cpart, device_id_type=MESH)

    def local(k, j):
        src, dst = (
            (lts[k].at[c], lcat[k].at[:, pl.ds(0, T)]),
            (gs[k], gcat[k].at[pl.ds(0, T), :]),
        )[j]
        return pltpu.make_async_copy(src, dst, local_sem.at[k, j])

    order = list(range(n))[::-1]
    for k in order:
        for j in (0, 1):
            pair(k, j).start()
            local(k, j).start()

    def small_copy(o, to):
        return pltpu.make_async_remote_copy(
            src_ref=small_in.at[to], dst_ref=small_land.at[o], send_sem=small_send.at[o], recv_sem=small_recv.at[o],
            device_id=(lax.div(to, 2), lax.rem(to, 2)), device_id_type=MESH)

    @pl.loop(1, 32)
    def _(o):
        small_copy(o, lax.rem(me + o, 32)).start()

    def rows_of(k):
        return outs[k].shape[0]

    def width(k):
        return outs[k].shape[1]

    def mine(k, zo, xo, yo, first=0, quarters=4):
        h, w = rows_of(k), width(k) // 4
        row = pl.multiple_of(((zo * 2 + xo) * 2 + yo) * h, h)
        return part_sums[k].at[pl.ds(row, h), pl.ds(first * w, quarters * w)]

    def link(k, slot, src, dst, to):
        return pltpu.make_async_remote_copy(
            src_ref=src, dst_ref=dst, send_sem=send_sem.at[k, slot], recv_sem=recv_sem.at[k, slot],
            device_id=to, device_id_type=MESH)

    def quarter_slice(k, first, quarters):
        w = width(k) // 4
        return pl.ds(first * w, quarters * w)

    def land_x(k, zo, first, quarters):
        return lxm[k].at[zo, :, quarter_slice(k, first, quarters)]

    def land_y(k, zo, first, quarters):
        return lym[k].at[zo, :, quarter_slice(k, first, quarters)]

    def z_has(d, s):
        return (z - s >= 0) if d == 0 else (z + s <= ZN - 1)

    def z_next(d):
        return (z < ZN - 1) if d == 0 else (z > 0)

    def zo_of(d, s):
        return z - s if d == 0 else z + s

    def z_slot(d, s, zo):
        return ZN if (d == 1 and s == 0) else zo

    def toward(d):
        return place(z - 1 + 2 * d, x, c, y)

    def add_in(k, zo, xo, yo, first, quarters, others):
        ref = mine(k, zo, xo, yo, first, quarters)
        h = rows_of(k)

        @pl.loop(0, h // 16)
        def _(i):
            rows = pl.ds(pl.multiple_of(i * 16, 16), 16)
            total = ref[rows, :].astype(f32)
            for o in others:
                total = total + o[rows, :].astype(f32)
            ref[rows, :] = total.astype(bf16)

    def wait(k, slot, dst):
        link(k, slot, dst, dst, xp).wait_recv()

    def product(k):
        for j in (0, 1):
            local(k, j).wait()
            pair(k, j).wait_recv()
        half, wide = part_sums[k].shape
        tile, cols = 256, min(wide, 1024)

        @pl.loop(0, half // tile)
        def _(i):
            rows = pl.ds(pl.multiple_of(i * tile, tile), tile)
            for j in range(wide // cols):
                part_sums[k][rows, pl.ds(j * cols, cols)] = jnp.dot(
                    lcat[k][rows, :], gcat[k][:, pl.ds(j * cols, cols)], preferred_element_type=f32
                ).astype(bf16)

    def do(k, e):
        kind = e[0]
        if kind == "last":
            product(k)
            for zo in range(ZN):
                link(k, XY + zo, mine(k, zo, 1 - x, 1 - y, 2, 2), lxy[k].at[zo], xp).start()
                link(k, YX + zo, mine(k, zo, 1 - x, 1 - y, 0, 2), lyx[k].at[zo], yp).start()
        elif kind == "cross":
            s = e[1]
            for d in (0, 1):
                @pl.when(z_has(d, s + 1))
                def _():
                    zo = zo_of(d, s + 1)
                    wait(k, YX + zo, lyx[k].at[zo])
                    add_in(k, zo, 1 - x, y, 0, 2, [lyx[k].at[zo]])
                    link(k, XM + zo, mine(k, zo, 1 - x, y, 1, 3), land_x(k, zo, 1, 3), xp).start()
                    wait(k, XY + zo, lxy[k].at[zo])
                    add_in(k, zo, x, 1 - y, 2, 2, [lxy[k].at[zo]])
                    link(k, YM + zo, mine(k, zo, x, 1 - y, 0, 3), land_y(k, zo, 0, 3), yp).start()
        elif kind == "side":
            s = e[1]
            for d in (0, 1):
                @pl.when(z_has(d, s + 1))
                def _():
                    zo = zo_of(d, s + 1)
                    for base, landing, xo, yo, first in ((ZX, lzx, 1 - x, y, 0), (ZY, lzy, x, 1 - y, 3)):
                        if s < 2:
                            @pl.when(z_next(d))
                            def _():
                                got = landing[k].at[z_slot(d, s + 1, zo)]
                                wait(k, base + d * 3 + s + 1, got)
                                add_in(k, zo, xo, yo, first, 1, [got])
                        link(k, base + d * 3 + s, mine(k, zo, xo, yo, first, 1),
                             landing[k].at[z_slot(d, s, zo)], toward(d)).start()
        elif kind == "chain":
            s = e[1]
            for d in (0, 1):
                @pl.when(z_has(d, s + 1))
                def _():
                    zo = zo_of(d, s + 1)
                    wait(k, XM + zo, land_x(k, zo, 1, 3))
                    wait(k, YM + zo, land_y(k, zo, 0, 3))
                    add_in(k, zo, x, y, 0, 1, [land_y(k, zo, 0, 1)])
                    add_in(k, zo, x, y, 1, 2, [land_y(k, zo, 1, 2), land_x(k, zo, 1, 2)])
                    add_in(k, zo, x, y, 3, 1, [land_x(k, zo, 3, 1)])
                    if s < 2:
                        @pl.when(z_next(d))
                        def _():
                            got = lzm[k].at[z_slot(d, s + 1, zo)]
                            wait(k, ZM + d * 3 + s + 1, got)
                            add_in(k, zo, x, y, 0, 4, [got])
                    link(k, ZM + d * 3 + s, mine(k, zo, x, y), lzm[k].at[z_slot(d, s, zo)], toward(d)).start()
        elif kind == "near":
            for slot, own_slot, xo, yo, first, cross_land, side_base, side_land, side_first, to, land in (
                (YX, XM, 1 - x, y, 0, lyx, ZX, lzx, 0, xp, land_x),
                (XY, YM, x, 1 - y, 2, lxy, ZY, lzy, 3, yp, land_y),
            ):
                wait(k, slot + z, cross_land[k].at[z])
                add_in(k, z, xo, yo, first, 2, [cross_land[k].at[z]])
                for d in (0, 1):
                    @pl.when(z_next(d))
                    def _():
                        got = side_land[k].at[z_slot(d, 0, z)]
                        wait(k, side_base + d * 3, got)
                        add_in(k, z, xo, yo, side_first, 1, [got])
                link(k, own_slot + z, mine(k, z, xo, yo), land(k, z, 0, 4), to).start()
        elif kind == "own":
            wait(k, XM + z, land_x(k, z, 0, 4))
            wait(k, YM + z, land_y(k, z, 0, 4))
            h = rows_of(k)
            own = mine(k, z, x, y)
            from_x, from_y = land_x(k, z, 0, 4), land_y(k, z, 0, 4)

            @pl.loop(0, h // 16)
            def _(i):
                rows = pl.ds(pl.multiple_of(i * 16, 16), 16)
                outs[k][rows, :] = own[rows, :].astype(f32) + from_x[rows, :].astype(f32) + from_y[rows, :].astype(f32)

            for d in (0, 1):
                @pl.when(z_next(d))
                def _():
                    got = lzm[k].at[z_slot(d, 0, z)]
                    wait(k, ZM + d * 3, got)

                    @pl.loop(0, h // 16)
                    def _(i):
                        rows = pl.ds(pl.multiple_of(i * 16, 16), 16)
                        outs[k][rows, :] += got[rows, :].astype(f32)

    for k, e in stage_list(n, OFFSET)[::-1]:
        do(k, e)

    small_land[0] = small_in[me]

    @pl.loop(1, 32)
    def _(o):
        small_copy(o, 0).wait_send()
        small_copy(o, 0).wait_recv()

    small_out[...] = jnp.sum(small_land[...], axis=0)

    for k in range(n):
        for j in (0, 1):
            pair(k, j).wait_send()
        for zo in range(ZN):
            link(k, XY + zo, mine(k, zo, 1 - x, 1 - y, 2, 2), lxy[k].at[zo], xp).wait_send()
            link(k, YX + zo, mine(k, zo, 1 - x, 1 - y, 0, 2), lyx[k].at[zo], yp).wait_send()
        for t in range(1, ZN):
            zo = lax.rem(z + t, ZN)
            link(k, XM + zo, mine(k, zo, 1 - x, y, 1, 3), land_x(k, zo, 1, 3), xp).wait_send()
            link(k, YM + zo, mine(k, zo, x, 1 - y, 0, 3), land_y(k, zo, 0, 3), yp).wait_send()
        link(k, XM + z, mine(k, z, 1 - x, y), land_x(k, z, 0, 4), xp).wait_send()
        link(k, YM + z, mine(k, z, x, 1 - y), land_y(k, z, 0, 4), yp).wait_send()
        for d in (0, 1):
            for s in range(3):
                @pl.when(z_has(d, s + 1))
                def _():
                    zo = zo_of(d, s + 1)
                    to = z_slot(d, s, zo)
                    link(k, ZX + d * 3 + s, mine(k, zo, 1 - x, y, 0, 1), lzx[k].at[to], toward(d)).wait_send()
                    link(k, ZY + d * 3 + s, mine(k, zo, x, 1 - y, 3, 1), lzy[k].at[to], toward(d)).wait_send()
                    link(k, ZM + d * 3 + s, mine(k, zo, x, y), lzm[k].at[to], toward(d)).wait_send()


def scatter_all(small, lts, gs):
    n = len(lts)
    halves = [lt.shape[1] for lt in lts]
    wides = [g.shape[1] for g in gs]
    hs = [h // 16 for h in halves]
    T = lts[0].shape[2]
    sem = pltpu.SemaphoreType.DMA
    V = pltpu.VMEM
    outs = [jax.ShapeDtypeStruct(small.shape[1:], f32)] + [jax.ShapeDtypeStruct((h, w), f32) for h, w in zip(hs, wides)]
    hw = list(zip(hs, wides))
    scratch = (
        [V((h, 2 * T), bf16) for h in halves]
        + [V((2 * T, w), bf16) for w in wides]
        + [V((h, w), bf16) for h, w in zip(halves, wides)]
        + [V((4, h, w), bf16) for h, w in hw]
        + [V((4, h, w), bf16) for h, w in hw]
        + [V((4, h, w // 2), bf16) for h, w in hw]
        + [V((4, h, w // 2), bf16) for h, w in hw]
        + [V((5, h, w), bf16) for h, w in hw]
        + [V((5, h, w // 4), bf16) for h, w in hw]
        + [V((5, h, w // 4), bf16) for h, w in hw]
        + [V(small.shape, f32), sem((n, SLOTS)), sem((n, SLOTS)), sem((n, 2)), sem((n, 2)), sem((n, 2)), sem((32,)), sem((32,))]
    )
    return pl.pallas_call(
        functools.partial(scatter_kernel, n), out_shape=outs,
        in_specs=[pl.BlockSpec(memory_space=pltpu.VMEM)] + [pl.BlockSpec(memory_space=pl.ANY)] * (2 * n),
        out_specs=[pl.BlockSpec(memory_space=pltpu.VMEM)] * (n + 1),
        scratch_shapes=scratch,
        compiler_params=pltpu.CompilerParams(collective_id=1, has_side_effects=True, vmem_limit_bytes=63 << 20),
        name="scatter_grads",
    )(small, *lts, *gs)


HEADS = 16


epsilon = 1e-05


def product(left, right):
    return jnp.dot(left, right, preferred_element_type=jnp.float32)


def outer_product(left, right):
    return lax.dot_general(
        left, right, (((0,), (0,)), ((), ())), preferred_element_type=jnp.float32
    )


def product_back(left, right):
    return lax.dot_general(
        left, right, (((1,), (1,)), ((), ())), preferred_element_type=jnp.float32
    )


def norm_rows(values, gain, shift):
    center = values - jnp.mean(values, axis=-1, keepdims=True)
    spread = jnp.mean(center * center, axis=-1, keepdims=True)
    return center * lax.rsqrt(spread + epsilon) * gain + shift


def gelu_exact(values):
    return 0.5 * values * (1.0 + lax.erf(values * 0.7071067811865476))


def attend_mask(seg_row, valid_row, head_count):
    count_rows = seg_row.shape[0]
    places = jnp.arange(count_rows, dtype=jnp.int32)
    same_utt = seg_row[:, None] == seg_row[None, :]
    diagonal = places[:, None] == places[None, :]
    allowed = same_utt & ((valid_row[None, :] == 1) | diagonal)
    slopes = 2.0 ** (-8.0 * (jnp.arange(head_count, dtype=jnp.float32) + 1.0) / head_count)
    distance = jnp.abs(places[:, None] - places[None, :]).astype(jnp.float32)
    return (allowed, -slopes[:, None, None] * distance[None, :, :])


def split_heads(projected, head_count):
    row_count = projected.shape[0]
    feature_width = projected.shape[1] // 3
    head_size = feature_width // head_count
    queries = projected[:, :feature_width].reshape(row_count, head_count, head_size)
    keys_all = projected[:, feature_width : 2 * feature_width].reshape(
        row_count, head_count, head_size
    )
    values_all = projected[:, 2 * feature_width :].reshape(row_count, head_count, head_size)
    return (queries, keys_all, values_all)


def masked_scores(queries, keys_all, allowed, linear_bias):
    score_scale = queries.shape[2] ** (-0.5)
    raw = (
        jnp.einsum("qhd,khd->hqk", queries, keys_all, preferred_element_type=jnp.float32)
        * score_scale
        + linear_bias
    )
    return jnp.where(allowed[None, :, :], raw, -1e30)


def forward_pass(tokens, skip, weights, allowed, linear_bias, head_count):
    w_skip, b_skip, g_one, beta_one, w_qkv, w_out, g_two, beta_two, w_up, b_up, w_down, b_down = (
        weights
    )
    row_count, feature_width = tokens.shape
    joined = jnp.concatenate([tokens, skip], axis=1)
    hidden = product(joined, w_skip) + b_skip.astype(jnp.float32)
    normed = norm_rows(hidden, g_one.astype(jnp.float32), beta_one.astype(jnp.float32)).astype(
        jnp.bfloat16
    )
    projected = product(normed, w_qkv).astype(jnp.bfloat16)
    queries, keys_all, values_all = split_heads(projected, head_count)
    masked = masked_scores(queries, keys_all, allowed, linear_bias)
    row_top = jnp.max(masked, axis=-1, keepdims=True)
    exponent = jnp.exp(masked - row_top)
    row_total = jnp.sum(exponent, axis=-1, keepdims=True)
    soft_weights = (exponent / row_total).astype(jnp.bfloat16)
    log_total = row_top + jnp.log(row_total)
    weighted = jnp.einsum(
        "hqk,khd->qhd", soft_weights, values_all, preferred_element_type=jnp.float32
    )
    attended = weighted.reshape(row_count, feature_width).astype(jnp.bfloat16)
    middle = hidden + product(attended, w_out)
    normed_two = norm_rows(middle, g_two.astype(jnp.float32), beta_two.astype(jnp.float32)).astype(
        jnp.bfloat16
    )
    hidden_up = product(normed_two, w_up) + b_up.astype(jnp.float32)
    activated = gelu_exact(hidden_up).astype(jnp.bfloat16)
    result = middle + (product(activated, w_down) + b_down.astype(jnp.float32))
    stored = (
        joined,
        hidden,
        normed,
        projected,
        log_total,
        attended,
        middle,
        normed_two,
        hidden_up,
        activated,
    )
    return (stored, result)


def backward_feed(stored, weights, cotangent):
    (
        joined,
        hidden,
        normed,
        projected,
        log_total,
        attended,
        middle,
        normed_two,
        hidden_up,
        activated,
    ) = stored
    w_skip, b_skip, g_one, beta_one, w_qkv, w_out, g_two, beta_two, w_up, b_up, w_down, b_down = (
        weights
    )
    grad_result = cotangent.astype(jnp.float32)
    grad_activated = product_back(cotangent, w_down)
    grad_b_down = jnp.sum(grad_result, axis=0)
    gelu_value, gelu_pull = jax.vjp(gelu_exact, hidden_up)
    grad_up = gelu_pull(grad_activated)[0].astype(jnp.bfloat16)
    grad_b_up = jnp.sum(grad_up.astype(jnp.float32), axis=0)
    grad_normed_two = product_back(grad_up, w_up)
    norm_value, norm_pull = jax.vjp(
        norm_rows, middle, g_two.astype(jnp.float32), beta_two.astype(jnp.float32)
    )
    grad_middle_norm, grad_g_two, grad_beta_two = norm_pull(grad_normed_two)
    grad_middle = grad_result + grad_middle_norm
    feed_terms = (grad_up, grad_b_up, cotangent, grad_b_down, grad_g_two, grad_beta_two)
    return (feed_terms, grad_middle)


def backward_front(stored, weights, grad_middle, allowed, linear_bias, head_count):
    (
        joined,
        hidden,
        normed,
        projected,
        log_total,
        attended,
        middle,
        normed_two,
        hidden_up,
        activated,
    ) = stored
    w_skip, b_skip, g_one, beta_one, w_qkv, w_out, g_two, beta_two, w_up, b_up, w_down, b_down = (
        weights
    )
    row_count, feature_width = hidden.shape
    branch_grad = grad_middle.astype(jnp.bfloat16)
    grad_attended = product_back(branch_grad, w_out).astype(jnp.bfloat16)
    queries, keys_all, values_all = split_heads(projected, head_count)
    score_scale = queries.shape[2] ** (-0.5)
    masked = masked_scores(queries, keys_all, allowed, linear_bias)
    probable = jnp.exp(masked - log_total)
    soft_weights = probable.astype(jnp.bfloat16)
    grad_heads = grad_attended.reshape(row_count, head_count, feature_width // head_count)
    grad_probable = jnp.einsum(
        "qhd,khd->hqk", grad_heads, values_all, preferred_element_type=jnp.float32
    )
    grad_values = jnp.einsum(
        "hqk,qhd->khd", soft_weights, grad_heads, preferred_element_type=jnp.float32
    )
    inner_sum = jnp.sum(grad_probable * probable, axis=-1, keepdims=True)
    grad_scores = (probable * (grad_probable - inner_sum)).astype(jnp.bfloat16)
    grad_queries = (
        jnp.einsum("hqk,khd->qhd", grad_scores, keys_all, preferred_element_type=jnp.float32)
        * score_scale
    )
    grad_keys = (
        jnp.einsum("hqk,qhd->khd", grad_scores, queries, preferred_element_type=jnp.float32)
        * score_scale
    )
    grad_projected = jnp.concatenate(
        [
            grad_queries.reshape(row_count, feature_width),
            grad_keys.reshape(row_count, feature_width),
            grad_values.reshape(row_count, feature_width),
        ],
        axis=1,
    ).astype(jnp.bfloat16)
    grad_normed = product_back(grad_projected, w_qkv)
    norm_value, norm_pull = jax.vjp(
        norm_rows, hidden, g_one.astype(jnp.float32), beta_one.astype(jnp.float32)
    )
    grad_hidden_norm, grad_g_one, grad_beta_one = norm_pull(grad_normed)
    grad_hidden = (grad_middle + grad_hidden_norm).astype(jnp.bfloat16)
    grad_b_skip = jnp.sum(grad_hidden.astype(jnp.float32), axis=0)
    grad_joined = product_back(grad_hidden, w_skip)
    grad_tokens = grad_joined[:, :feature_width].astype(jnp.bfloat16)
    grad_skip = grad_joined[:, feature_width:].astype(jnp.bfloat16)
    front_terms = (grad_hidden, grad_b_skip, grad_g_one, grad_beta_one, grad_projected, branch_grad)
    return (grad_tokens, grad_skip, front_terms)


AXES = ("wide", "narrow")


def pack_small(b_skip, g_one, beta_one, g_two, beta_two, b_up, b_down):
    row = jnp.concatenate(
        [b_skip, g_one, beta_one, g_two, beta_two, b_down, jnp.zeros((64,), b_skip.dtype), b_up]
    ).reshape(3, 128)
    return jnp.pad(row, ((0, 13), (0, 0)))


def unpack_small(table):
    def column(row, at):
        return table[:, row, at : at + 32].reshape(-1)

    return (
        column(0, 0), column(0, 32), column(0, 64), column(0, 96),
        column(1, 0), table[:, 2, :].reshape(-1), column(1, 32),
    )


def pack_small_grads(b_skip, g_one, beta_one, g_two, beta_two, b_up, b_down):
    def cut(v):
        return v.reshape(32, -1)

    rows = jnp.concatenate(
        [cut(b_skip), cut(g_one), cut(beta_one), cut(g_two), cut(beta_two), cut(b_down),
         jnp.zeros((32, 64), f32), cut(b_up)], axis=1
    ).reshape(32, 3, 128)
    return jnp.pad(rows, ((0, 0), (0, 5), (0, 0)))


def halves_by_core(left):
    tokens, rows = left.shape
    return left.reshape(tokens, 8, 2, rows // 16).transpose(2, 1, 3, 0).reshape(2, rows // 2, tokens)


def gather_plain(values):
    return [lax.all_gather(v, AXES, axis=0, tiled=True) for v in values]


def shards(tokens, skip, seg_ids, valid, w_skip, b_skip, g_one, beta_one, w_qkv, w_out, g_two, beta_two,
           w_up, b_up, w_down, b_down, cotangent, own_kernels):
    head_count = HEADS
    if own_kernels:
        gathered = gather_all(
            pack_small(b_skip, g_one, beta_one, g_two, beta_two, b_up, b_down),
            (w_skip, w_qkv, w_out, w_up, w_down),
        )
        b_skip, g_one, beta_one, g_two, beta_two, b_up, b_down = unpack_small(gathered[0])
        w_skip, w_qkv, w_out, w_up, w_down = [w.reshape(-1, w.shape[-1]) for w in gathered[1:]]
    else:
        (w_skip, b_skip, g_one, beta_one, w_qkv, w_out, g_two, beta_two, w_up, b_up, w_down, b_down) = gather_plain(
            (w_skip, b_skip, g_one, beta_one, w_qkv, w_out, g_two, beta_two, w_up, b_up, w_down, b_down))
    weights = (w_skip, b_skip, g_one, beta_one, w_qkv, w_out, g_two, beta_two, w_up, b_up, w_down, b_down)
    allowed, linear_bias = attend_mask(seg_ids[0], valid[0], head_count)
    stored, result = forward_pass(tokens, skip, weights, allowed, linear_bias, head_count)
    (joined, hidden, normed, projected, log_total, attended, middle, normed_two, hidden_up, activated) = stored
    feed_terms, grad_middle = backward_feed(stored, weights, cotangent)
    grad_tokens, grad_skip, front_terms = backward_front(
        stored, weights, grad_middle, allowed, linear_bias, head_count)
    grad_up, grad_b_up, grad_result, grad_b_down, grad_g_two, grad_beta_two = feed_terms
    grad_hidden, grad_b_skip, grad_g_one, grad_beta_one, grad_projected, branch_grad = front_terms
    lefts = (joined, normed, attended, normed_two, activated)
    rights = (grad_hidden, grad_projected, branch_grad, grad_up, grad_result)
    if own_kernels:
        small, *big = scatter_all(
            pack_small_grads(grad_b_skip, grad_g_one, grad_beta_one, grad_g_two, grad_beta_two, grad_b_up, grad_b_down),
            [halves_by_core(left) for left in lefts],
            list(rights),
        )
        small = small[:3].reshape(-1)
        grad_b_skip, grad_g_one, grad_beta_one, grad_g_two, grad_beta_two, grad_b_down = [
            small[i * 32 : (i + 1) * 32] for i in range(6)]
        grad_b_up = small[256:]
    else:
        def scatter(v):
            return lax.psum_scatter(v, AXES, scatter_dimension=0, tiled=True)

        big = [scatter(outer_product(a, b)) for a, b in zip(lefts, rights)]
        grad_b_skip, grad_g_one, grad_beta_one, grad_g_two, grad_beta_two, grad_b_up, grad_b_down = [
            scatter(v) for v in
            (grad_b_skip, grad_g_one, grad_beta_one, grad_g_two, grad_beta_two, grad_b_up, grad_b_down)]
    return (
        result.astype(jnp.bfloat16), grad_tokens, grad_skip,
        big[0], grad_b_skip, grad_g_one, grad_beta_one, big[1], big[2],
        grad_g_two, grad_beta_two, big[3], grad_b_up, big[4], grad_b_down,
    )


def solution(mesh):
    return jax.shard_map(
        functools.partial(shards, own_kernels=dict(mesh.shape) == {"wide": 16, "narrow": 2}),
        mesh=mesh,
        in_specs=(
            P(("wide", "narrow"), None),
            P(("wide", "narrow"), None),
            P(("wide", "narrow"), None),
            P(("wide", "narrow"), None),
            P(("wide", "narrow"), None),
            P(("wide", "narrow")),
            P(("wide", "narrow")),
            P(("wide", "narrow")),
            P(("wide", "narrow"), None),
            P(("wide", "narrow"), None),
            P(("wide", "narrow")),
            P(("wide", "narrow")),
            P(("wide", "narrow"), None),
            P(("wide", "narrow")),
            P(("wide", "narrow"), None),
            P(("wide", "narrow")),
            P(("wide", "narrow"), None),
        ),
        out_specs=(
            P(("wide", "narrow"), None),
            P(("wide", "narrow"), None),
            P(("wide", "narrow"), None),
            P(("wide", "narrow"), None),
            P(("wide", "narrow")),
            P(("wide", "narrow")),
            P(("wide", "narrow")),
            P(("wide", "narrow"), None),
            P(("wide", "narrow"), None),
            P(("wide", "narrow")),
            P(("wide", "narrow")),
            P(("wide", "narrow"), None),
            P(("wide", "narrow")),
            P(("wide", "narrow"), None),
            P(("wide", "narrow")),
        ),
        check_vma=False,
    )
```

```python
import jax
import jax.numpy as jnp
from jax import lax
from jax.experimental import pallas as pl
from jax.experimental.pallas import tpu as pltpu
from jax.sharding import PartitionSpec as P

f32 = jnp.float32
bf16 = jnp.bfloat16

MESH = pl.DeviceIdType.MESH
ZN = 4
SLOTS = 38
ZM, ZX, ZY, XM, XY, YM, YX, CP = 0, 6, 12, 18, 22, 26, 30, 34
OFFSET = 4


def stage_list(count, offset):
    one = [("own",), ("near",)]
    for s in range(3):
        one += [("chain", s), ("side", s)]
    one += [("cross", s) for s in range(3)] + [("last",)]
    merged = []
    for k in range(count):
        for i, e in enumerate(one):
            merged.append((k * offset + i, k, e))
    merged.sort(key=lambda a: (a[0], a[1]))
    return [(k, e) for _, k, e in merged]


def here():
    w = lax.axis_index("wide")
    y = lax.axis_index("narrow")
    c = lax.rem(w, 2)
    x = lax.rem(lax.div(w, 2), 2)
    z = lax.div(w, 4)
    return z, x, c, y


def place(z, x, c, y):
    return ((z * 2 + x) * 2 + c, y)


def greet_all(total_w, total_n):
    barrier = pltpu.get_barrier_semaphore()
    w = lax.axis_index("wide")
    y = lax.axis_index("narrow")
    me = w * total_n + y
    count = total_w * total_n

    @pl.loop(1, count)
    def _(o):
        to = lax.rem(me + o, count)
        pl.semaphore_signal(
            barrier, inc=1, device_id=(lax.div(to, total_n), lax.rem(to, total_n)), device_id_type=MESH
        )

    pl.semaphore_wait(barrier, count - 1)


def gather_kernel(small_ref, *refs):
    n = 5
    own = refs[:n]
    small_out = refs[n]
    full = refs[n + 1 : 2 * n + 1]
    send_sem, recv_sem, local_sem, small_send, small_recv = refs[2 * n + 1 :]
    z, x, c, y = here()
    me = lax.axis_index("wide") * 2 + lax.axis_index("narrow")
    greet_all(16, 2)

    def part(k, zo, xo, yo, first=0, quarters=4):
        width = own[k].shape[1] // 4
        return full[k].at[zo, xo, c, yo, :, pl.ds(first * width, quarters * width)]

    def link(k, slot, src, dst, to):
        return pltpu.make_async_remote_copy(
            src_ref=src, dst_ref=dst, send_sem=send_sem.at[k, slot], recv_sem=recv_sem.at[k, slot],
            device_id=to, device_id_type=MESH)

    xp = place(z, 1 - x, c, y)
    yp = place(z, x, c, 1 - y)
    cpart = place(z, x, 1 - c, y)

    def zto(d):
        return place(z + 1 - 2 * d, x, c, y)

    def z_has(d, s):
        return (z - s >= 0) if d == 0 else (z + s <= ZN - 1)

    def z_next(d):
        return (z < ZN - 1) if d == 0 else (z > 0)

    def zo_of(d, s):
        return z - s if d == 0 else z + s

    sends = []

    def z_send(k, base, d, s, xo, yo, first, quarters, src=None):
        cond = jnp.logical_and(z_has(d, s), z_next(d))
        zo = zo_of(d, s)
        dst = part(k, zo, xo, yo, first, quarters)
        cp = link(k, base + d * 3 + s, dst if src is None else src, dst, zto(d))
        sends.append((cond, cp))

        @pl.when(cond)
        def _():
            cp.start()

    def z_wait(k, base, d, s, xo, yo, first, quarters):
        zo = zo_of(d, s + 1)
        dst = part(k, zo, xo, yo, first, quarters)
        link(k, base + d * 3 + s, dst, dst, zto(d)).wait_recv()

    def go(k, slot, ref, to, src=None, cond=None):
        cp = link(k, slot, ref if src is None else src, ref, to)
        sends.append((cond, cp))
        cp.start()

    def wait(k, slot, ref):
        link(k, slot, ref, ref, xp).wait_recv()

    small_copies = []
    for k in range(n):
        pltpu.make_async_copy(own[k], part(k, z, x, y), local_sem.at[k]).start()

    def do(k, e):
        kind = e[0]
        if kind == "own":
            for d in (0, 1):
                z_send(k, ZM, d, 0, x, y, 0, 4, src=own[k])
            go(k, XM + z, part(k, z, x, y), xp, src=own[k])
            go(k, YM + z, part(k, z, x, y), yp, src=own[k])
        elif kind == "near":
            wait(k, XM + z, part(k, z, 1 - x, y))
            for d in (0, 1):
                z_send(k, ZX, d, 0, 1 - x, y, 0, 1)
            go(k, YX + z, part(k, z, 1 - x, y, 0, 2), yp)
            wait(k, YM + z, part(k, z, x, 1 - y))
            for d in (0, 1):
                z_send(k, ZY, d, 0, x, 1 - y, 3, 1)
            go(k, XY + z, part(k, z, x, 1 - y, 2, 2), xp)
        elif kind == "chain":
            s = e[1]
            for d in (0, 1):
                @pl.when(z_has(d, s + 1))
                def _():
                    z_wait(k, ZM, d, s, x, y, 0, 4)
                    zo = zo_of(d, s + 1)
                    if s < 2:
                        @pl.when(z_next(d))
                        def _():
                            ref = part(k, zo, x, y)
                            link(k, ZM + d * 3 + s + 1, ref, ref, zto(d)).start()
                    ref = part(k, zo, x, y, 1, 3)
                    link(k, XM + zo, ref, ref, xp).start()
                    ref = part(k, zo, x, y, 0, 3)
                    link(k, YM + zo, ref, ref, yp).start()
        elif kind == "side":
            s = e[1]
            for d in (0, 1):
                @pl.when(z_has(d, s + 1))
                def _():
                    zo = zo_of(d, s + 1)
                    for base, xo, yo, first in ((ZX, 1 - x, y, 0), (ZY, x, 1 - y, 3)):
                        z_wait(k, base, d, s, xo, yo, first, 1)
                        if s < 2:
                            @pl.when(z_next(d))
                            def _():
                                ref = part(k, zo, xo, yo, first, 1)
                                link(k, base + d * 3 + s + 1, ref, ref, zto(d)).start()
        elif kind == "cross":
            s = e[1]
            for d in (0, 1):
                @pl.when(z_has(d, s + 1))
                def _():
                    zo = zo_of(d, s + 1)
                    wait(k, XM + zo, part(k, zo, 1 - x, y, 1, 3))
                    ref = part(k, zo, 1 - x, y, 0, 2)
                    link(k, YX + zo, ref, ref, yp).start()
                    wait(k, YM + zo, part(k, zo, x, 1 - y, 0, 3))
                    ref = part(k, zo, x, 1 - y, 2, 2)
                    link(k, XY + zo, ref, ref, xp).start()
            if s == 0:
                pltpu.make_async_copy(own[k], part(k, z, x, y), local_sem.at[k]).wait()
                ref = full[k].at[:, x, c, y]
                link(k, CP, ref, ref, cpart).start()
            if s == 2:
                ref = full[k].at[:, 1 - x, c, y]
                link(k, CP + 1, ref, ref, cpart).start()
                ref = full[k].at[:, x, c, 1 - y]
                link(k, CP + 2, ref, ref, cpart).start()
        elif kind == "last":
            for zo in range(ZN):
                wait(k, XY + zo, part(k, zo, 1 - x, 1 - y, 2, 2))
                wait(k, YX + zo, part(k, zo, 1 - x, 1 - y, 0, 2))
            ref = full[k].at[:, 1 - x, c, 1 - y]
            link(k, CP + 3, ref, ref, cpart).start()

    def small_copy(o, to):
        return pltpu.make_async_remote_copy(
            src_ref=small_ref, dst_ref=small_out.at[me], send_sem=small_send.at[o], recv_sem=small_recv.at[o],
            device_id=(lax.div(to, 2), lax.rem(to, 2)), device_id_type=MESH)

    for i, (k, e) in enumerate(stage_list(n, OFFSET)):
        if i == 1:
            small_out[me] = small_ref[...]

            @pl.loop(1, 32)
            def _(o):
                small_copy(o, lax.rem(me + o, 32)).start()
        do(k, e)

    for k in range(n):
        for j, (xo, yo) in enumerate(((x, y), (1 - x, y), (x, 1 - y), (1 - x, 1 - y))):
            ref = full[k].at[:, xo, 1 - c, yo]
            link(k, CP + j, ref, ref, cpart).wait_recv()
            ref = full[k].at[:, xo, c, yo]
            link(k, CP + j, ref, ref, cpart).wait_send()
        for d in (0, 1):
            for s in range(3):
                @pl.when(jnp.logical_and(z_has(d, s), z_next(d)))
                def _():
                    zo = zo_of(d, s)
                    for base, xo, yo, first, q in ((ZM, x, y, 0, 4), (ZX, 1 - x, y, 0, 1), (ZY, x, 1 - y, 3, 1)):
                        ref = part(k, zo, xo, yo, first, q)
                        link(k, base + d * 3 + s, ref, ref, zto(d)).wait_send()
        ref = part(k, z, x, y)
        link(k, XM + z, ref, ref, xp).wait_send()
        link(k, YM + z, ref, ref, yp).wait_send()
        for t in range(1, ZN):
            zo = lax.rem(z + t, ZN)
            ref = part(k, zo, x, y, 1, 3)
            link(k, XM + zo, ref, ref, xp).wait_send()
            ref = part(k, zo, x, y, 0, 3)
            link(k, YM + zo, ref, ref, yp).wait_send()
        for zo in range(ZN):
            ref = part(k, zo, 1 - x, y, 0, 2)
            link(k, YX + zo, ref, ref, yp).wait_send()
            ref = part(k, zo, x, 1 - y, 2, 2)
            link(k, XY + zo, ref, ref, xp).wait_send()

    @pl.loop(1, 32)
    def _(o):
        small_copy(o, 0).wait_send()
        small_copy(o, 0).wait_recv()


def gather_all(small, shards):
    n = len(shards)
    outs = [jax.ShapeDtypeStruct((32,) + small.shape, small.dtype)] + [
        jax.ShapeDtypeStruct((4, 2, 2, 2) + s.shape, s.dtype) for s in shards]
    sem = pltpu.SemaphoreType.DMA
    return pl.pallas_call(
        gather_kernel, out_shape=outs,
        in_specs=[pl.BlockSpec(memory_space=pltpu.VMEM)] * (n + 1),
        out_specs=[pl.BlockSpec(memory_space=pltpu.VMEM)] + [pl.BlockSpec(memory_space=pl.ANY)] * n,
        scratch_shapes=[sem((n, SLOTS)), sem((n, SLOTS)), sem((n,)), sem((32,)), sem((32,))],
        compiler_params=pltpu.CompilerParams(collective_id=0, has_side_effects=True),
        name="gather_weights",
    )(small, *shards)


HEADS = 16


epsilon = 1e-05


def nt(a, b):
    return lax.dot_general(a, b, (((1,), (1,)), ((), ())), preferred_element_type=f32)


def tn(a, b):
    return lax.dot_general(a, b, (((0,), (0,)), ((), ())), preferred_element_type=f32)


CH = 1024
BACK_CHUNKS = [("d", i) for i in range(4)] + [("u", i) for i in range(4)] + [("o", 0)] + [
    ("q", i) for i in range(3)] + [("s", i) for i in range(2)]
LEFT_CHUNKS = [(4, i) for i in range(4)] + [(3, 0), (2, 0), (1, 0), (0, 0), (0, 1)]
BACK_PLAN = [
    "T.0 T.1 T.2 T.3",
    "B1.0 B1.1 W4.0 W4.1",
    "e4.11 B1.2 B1.3 T.4",
    "B2.0 B2.1 B2.2 B2.3",
    "W3.0 W3.1 e4.10 e4.9",
    "e4.8 e4.7 e3.11 L2.0",
    "L2.1 L2.2 e4.6 e4.5",
    "L2.3 B3.0 T.5 A.0",
    "W2.0 e4.4 e2.11 A.1",
    "e4.3 A.2 A.3 e4.2",
    "e4.1 e3.10 e3.9 e3.8",
    "e3.7 e2.10 e2.9 e2.8",
    "e2.7 T.6 B5.0 B5.1",
    "B5.2 e4.0 e3.6 e3.5",
    "W1.0 W1.1 e1.11 L1.0",
    "L1.1 e3.4 e2.6 e2.5",
    "L1.2 e3.3 L1.3 T.7",
    "T.8 R.0 e3.2 e2.4",
    "e2.3 e1.10 W0.0 e3.1",
    "e1.9 e1.8 e1.7 e0.11",
    "e1.6 R.1 B6.0 e2.2",
    "e2.1 e3.0 e1.5 e1.4",
    "e1.3 e0.10 e1.2 e1.1",
    "e0.9 e0.8 e0.7 R.2",
    "B6.1 e2.0 e0.6 e0.5",
    "e1.0 e0.4 e0.3 R.3",
    "e0.2 e0.1 R.4 e0.0",
    "R.5",
]
SKIP, QKV, OUT, UP, DOWN = range(5)


def backward_kernel(*refs):
    n = 5
    (cot, tokens, skip, normed, attended, normed_two, activated,
     w_skip, w_qkv, w_out, w_up, w_down, slope, middle, hidden, projected,
     log_total, steep, distance, gains) = refs[:20]
    small_out = refs[20]
    outs = refs[21:26]
    grad_tokens, grad_skip = refs[26:28]
    r = refs[28:]
    turned, theirs, gcat, part_sums = r[:n], r[n : 2 * n], r[2 * n : 3 * n], r[3 * n : 4 * n]
    lxm, lym, lxy, lyx, lzm, lzx, lzy = (r[(4 + i) * n : (5 + i) * n] for i in range(7))
    (wbuf, lbuf, slopebuf, vbuf, gnorm, gmid, pbuf, gatt, acc, small, small_land,
     send_sem, recv_sem, pair_send, pair_recv, wsem, lsem, psem, misc_sem, small_send, small_recv) = r[11 * n :]
    z, x, c, y = here()
    xp = place(z, 1 - x, c, y)
    yp = place(z, x, c, 1 - y)
    cpart = place(z, x, 1 - c, y)
    T = cot.shape[0]

    def w_copy(i):
        kind, j = BACK_CHUNKS[i]
        at = pl.ds(j * CH, CH)
        src = {"d": lambda: w_down.at[at, :], "u": lambda: w_up.at[:, at], "o": lambda: w_out,
               "q": lambda: w_qkv.at[:, at], "s": lambda: w_skip.at[at, :]}[kind]()
        return pltpu.make_async_copy(src, wbuf.at[i % 2], wsem.at[i % 2])

    def l_copy(i):
        k, j = LEFT_CHUNKS[i]
        src = {DOWN: lambda: activated.at[:, pl.ds(j * CH, CH)], UP: lambda: normed_two, OUT: lambda: attended,
               QKV: lambda: normed, SKIP: lambda: (tokens, skip)[j]}[k]()
        return pltpu.make_async_copy(src, lbuf.at[i % 2], lsem.at[i % 2])

    def p_copy(i):
        return pltpu.make_async_copy(slope.at[:, pl.ds(i * CH, CH)], slopebuf.at[i % 2], psem.at[i % 2])

    cot_copy = pltpu.make_async_copy(cot, gcat[DOWN].at[pl.ds(0, T), :], misc_sem.at[0])
    mid_copy = pltpu.make_async_copy(middle, vbuf, misc_sem.at[1])
    proj_copy = pltpu.make_async_copy(projected, pbuf, misc_sem.at[2])
    hid_copy = pltpu.make_async_copy(hidden, vbuf, misc_sem.at[3])
    out_copies = [pltpu.make_async_copy(lbuf.at[i], o, misc_sem.at[4 + i]) for i, o in enumerate((grad_tokens, grad_skip))]
    for i in (0, 1):
        l_copy(i).start()
        w_copy(i).start()
        p_copy(i).start()
    cot_copy.start()
    mid_copy.start()
    proj_copy.start()
    greet_all(16, 2)

    def pair(k, j):
        if j == 0:
            src, dst = turned[k].at[1 - c], theirs[k]
        elif k == DOWN:
            src, dst = cot, gcat[k].at[pl.ds(T, T), :]
        elif k == UP:
            cols = pl.ds((j - 1) * CH, CH)
            src, dst = gcat[k].at[pl.ds(0, T), cols], gcat[k].at[pl.ds(T, T), cols]
        else:
            src, dst = gcat[k].at[pl.ds(0, T), :], gcat[k].at[pl.ds(T, T), :]
        return pltpu.make_async_remote_copy(
            src_ref=src, dst_ref=dst, send_sem=pair_send.at[k, j], recv_sem=pair_recv.at[k, j],
            device_id=cpart, device_id_type=MESH)

    def pieces(k):
        return range(5) if k == UP else range(2)

    pair(DOWN, 1).start()
    acc[...] = jnp.zeros_like(acc)
    small[...] = jnp.zeros_like(small)

    def rows_of(k):
        return outs[k].shape[0]

    def width(k):
        return outs[k].shape[1]

    def mine(k, zo, xo, yo, first=0, quarters=4):
        h, w = rows_of(k), width(k) // 4
        row = pl.multiple_of(((zo * 2 + xo) * 2 + yo) * h, h)
        return part_sums[k].at[pl.ds(row, h), pl.ds(first * w, quarters * w)]

    def link(k, slot, src, dst, to):
        return pltpu.make_async_remote_copy(
            src_ref=src, dst_ref=dst, send_sem=send_sem.at[k, slot], recv_sem=recv_sem.at[k, slot],
            device_id=to, device_id_type=MESH)

    def quarter_slice(k, first, quarters):
        w = width(k) // 4
        return pl.ds(first * w, quarters * w)

    def land_x(k, zo, first, quarters):
        return lxm[k].at[zo, :, quarter_slice(k, first, quarters)]

    def land_y(k, zo, first, quarters):
        return lym[k].at[zo, :, quarter_slice(k, first, quarters)]

    def z_has(d, s):
        return (z - s >= 0) if d == 0 else (z + s <= ZN - 1)

    def z_next(d):
        return (z < ZN - 1) if d == 0 else (z > 0)

    def zo_of(d, s):
        return z - s if d == 0 else z + s

    def z_slot(d, s, zo):
        return ZN if (d == 1 and s == 0) else zo

    def toward(d):
        return place(z - 1 + 2 * d, x, c, y)

    def add_in(k, zo, xo, yo, first, quarters, others):
        ref = mine(k, zo, xo, yo, first, quarters)
        h = rows_of(k)

        @pl.loop(0, h // 16)
        def _(i):
            rows = pl.ds(pl.multiple_of(i * 16, 16), 16)
            total = ref[rows, :].astype(f32)
            for o in others:
                total = total + o[rows, :].astype(f32)
            ref[rows, :] = total.astype(bf16)

    def wait(k, slot, dst):
        link(k, slot, dst, dst, xp).wait_recv()

    def do(k, e):
        kind = e[0]
        if kind == "last":
            for zo in range(ZN):
                link(k, XY + zo, mine(k, zo, 1 - x, 1 - y, 2, 2), lxy[k].at[zo], xp).start()
                link(k, YX + zo, mine(k, zo, 1 - x, 1 - y, 0, 2), lyx[k].at[zo], yp).start()
        elif kind == "cross":
            s = e[1]
            for d in (0, 1):
                @pl.when(z_has(d, s + 1))
                def _():
                    zo = zo_of(d, s + 1)
                    wait(k, YX + zo, lyx[k].at[zo])
                    add_in(k, zo, 1 - x, y, 0, 2, [lyx[k].at[zo]])
                    link(k, XM + zo, mine(k, zo, 1 - x, y, 1, 3), land_x(k, zo, 1, 3), xp).start()
                    wait(k, XY + zo, lxy[k].at[zo])
                    add_in(k, zo, x, 1 - y, 2, 2, [lxy[k].at[zo]])
                    link(k, YM + zo, mine(k, zo, x, 1 - y, 0, 3), land_y(k, zo, 0, 3), yp).start()
        elif kind == "side":
            s = e[1]
            for d in (0, 1):
                @pl.when(z_has(d, s + 1))
                def _():
                    zo = zo_of(d, s + 1)
                    for base, landing, xo, yo, first in ((ZX, lzx, 1 - x, y, 0), (ZY, lzy, x, 1 - y, 3)):
                        if s < 2:
                            @pl.when(z_next(d))
                            def _():
                                got = landing[k].at[z_slot(d, s + 1, zo)]
                                wait(k, base + d * 3 + s + 1, got)
                                add_in(k, zo, xo, yo, first, 1, [got])
                        link(k, base + d * 3 + s, mine(k, zo, xo, yo, first, 1),
                             landing[k].at[z_slot(d, s, zo)], toward(d)).start()
        elif kind == "chain":
            s = e[1]
            for d in (0, 1):
                @pl.when(z_has(d, s + 1))
                def _():
                    zo = zo_of(d, s + 1)
                    wait(k, XM + zo, land_x(k, zo, 1, 3))
                    wait(k, YM + zo, land_y(k, zo, 0, 3))
                    add_in(k, zo, x, y, 0, 1, [land_y(k, zo, 0, 1)])
                    add_in(k, zo, x, y, 1, 2, [land_y(k, zo, 1, 2), land_x(k, zo, 1, 2)])
                    add_in(k, zo, x, y, 3, 1, [land_x(k, zo, 3, 1)])
                    if s < 2:
                        @pl.when(z_next(d))
                        def _():
                            got = lzm[k].at[z_slot(d, s + 1, zo)]
                            wait(k, ZM + d * 3 + s + 1, got)
                            add_in(k, zo, x, y, 0, 4, [got])
                    link(k, ZM + d * 3 + s, mine(k, zo, x, y), lzm[k].at[z_slot(d, s, zo)], toward(d)).start()
        elif kind == "near":
            for slot, own_slot, xo, yo, first, cross_land, side_base, side_land, side_first, to, land in (
                (YX, XM, 1 - x, y, 0, lyx, ZX, lzx, 0, xp, land_x),
                (XY, YM, x, 1 - y, 2, lxy, ZY, lzy, 3, yp, land_y),
            ):
                wait(k, slot + z, cross_land[k].at[z])
                add_in(k, z, xo, yo, first, 2, [cross_land[k].at[z]])
                for d in (0, 1):
                    @pl.when(z_next(d))
                    def _():
                        got = side_land[k].at[z_slot(d, 0, z)]
                        wait(k, side_base + d * 3, got)
                        add_in(k, z, xo, yo, side_first, 1, [got])
                link(k, own_slot + z, mine(k, z, xo, yo), land(k, z, 0, 4), to).start()
        elif kind == "own":
            wait(k, XM + z, land_x(k, z, 0, 4))
            wait(k, YM + z, land_y(k, z, 0, 4))
            h = rows_of(k)
            own = mine(k, z, x, y)
            from_x, from_y = land_x(k, z, 0, 4), land_y(k, z, 0, 4)

            @pl.loop(0, h // 16)
            def _(i):
                rows = pl.ds(pl.multiple_of(i * 16, 16), 16)
                outs[k][rows, :] = own[rows, :].astype(f32) + from_x[rows, :].astype(f32) + from_y[rows, :].astype(f32)

            for d in (0, 1):
                @pl.when(z_next(d))
                def _():
                    got = lzm[k].at[z_slot(d, 0, z)]
                    wait(k, ZM + d * 3, got)

                    @pl.loop(0, h // 16)
                    def _(i):
                        rows = pl.ds(pl.multiple_of(i * 16, 16), 16)
                        outs[k][rows, :] += got[rows, :].astype(f32)

    def turn(i):
        k, j = LEFT_CHUNKS[i]
        l_copy(i).wait()
        group = 2 * outs[k].shape[0]
        seg = min(group, 128)
        for t in range(CH // 128):
            block = lbuf[i % 2, :, t * 128 : (t + 1) * 128].T
            for s in range(0, 128, seg):
                row = j * CH + t * 128 + s
                core, at = (row // group) % 2, row // (2 * group) * group + row % group
                turned[k][core, at : at + seg, :] = block[s : s + seg, :]
        if i + 2 < len(LEFT_CHUNKS):
            l_copy(i + 2).start()
        if i == len(LEFT_CHUNKS) - 1 or LEFT_CHUNKS[i + 1][0] != k:
            pair(k, 0).start()

    def weight_product(k, lo, hi):
        half, wide = part_sums[k].shape
        tiles = wide // CH
        if lo == 0:
            pair(k, 0).wait_recv()
            for j in pieces(k):
                if j:
                    pair(k, j).wait_recv()

        @pl.loop(lo, hi)
        def _(i):
            rows = pl.ds(pl.multiple_of(lax.div(i, tiles) * 256, 256), 256)
            for s in (0, 512):
                cols = pl.ds(pl.multiple_of(lax.rem(i, tiles) * CH + s, 512), 512)
                both = jnp.dot(turned[k][c, rows, :], gcat[k][pl.ds(0, T), cols], preferred_element_type=f32)
                both += jnp.dot(theirs[k][rows, :], gcat[k][pl.ds(T, T), cols], preferred_element_type=f32)
                part_sums[k][rows, cols] = both.astype(bf16)

    def back_product(i, left, finish):
        w_copy(i).wait()

        @pl.loop(0, 2)
        def _(j):
            at = pl.multiple_of(j * 512, 512)
            finish(at, nt(left(), wbuf[i % 2, pl.ds(at, 512), :]))

        if i + 2 < len(BACK_CHUNKS):
            w_copy(i + 2).start()

    def through_gelu(i):
        if i == 0:
            cot_copy.wait()
            small[5:6, :] = jnp.sum(gcat[DOWN][0:T, :].astype(f32), axis=0, keepdims=True)
        p_copy(i).wait()

        def finish(at, value):
            got = (value * slopebuf[i % 2, :, pl.ds(at, 512)].astype(f32)).astype(bf16)
            gcat[UP][0:T, pl.ds(pl.multiple_of(i * CH + at, 512), 512)] = got
            small[6 + i : 7 + i, pl.ds(at, 512)] = jnp.sum(got.astype(f32), axis=0, keepdims=True)

        back_product(i, lambda: gcat[DOWN][0:T, :], finish)
        if i < 2:
            p_copy(i + 2).start()
        pair(UP, 1 + i).start()

    def into_norm(first, i, base, k):
        def finish(at, value):
            cols = pl.ds(at, 512)
            if i == 0:
                gnorm[:, cols] = value
            else:
                gnorm[:, cols] += value

        back_product(base + i, lambda: gcat[k][0:T, i * CH : (i + 1) * CH], finish)

    def norm_back(i, gain, base, emit):
        @pl.loop(0, 4)
        def _(j):
            rows = pl.ds(pl.multiple_of(i * 64 + j * 16, 16), 16)
            v = vbuf[rows, :]
            center = v - jnp.mean(v, axis=-1, keepdims=True)
            rate = lax.rsqrt(jnp.mean(center * center, axis=-1, keepdims=True) + epsilon)
            xhat = center * rate
            g = gnorm[rows, :]
            gx = g * xhat
            acc[base] += gx[0:8] + gx[8:16]
            acc[base + 1] += g[0:8] + g[8:16]
            e = g * gains[gain : gain + 1, :]
            emit(rows, rate * (e - jnp.mean(e, axis=-1, keepdims=True) - xhat * jnp.mean(e * xhat, axis=-1, keepdims=True)))

    def second_norm(i):
        if i == 0:
            mid_copy.wait()

        def emit(rows, value):
            total = gcat[DOWN][rows, :].astype(f32) + value
            gmid[rows, :] = total
            gcat[OUT][rows, :] = total.astype(bf16)

        norm_back(i, 1, 0, emit)
        if i == 3:
            pair(OUT, 1).start()
            hid_copy.start()

    def to_attended():
        def finish(at, value):
            gatt[:, pl.ds(at, 512)] = value.astype(bf16)

        back_product(8, lambda: gcat[OUT][0:T, :], finish)

    def attention(i):
        if i == 0:
            proj_copy.wait()
        low = lax.broadcasted_iota(jnp.int32, (T, 128), 1) < 64

        @pl.loop(2 * i, 2 * i + 2)
        def _(p):
            at = pl.multiple_of(p * 128, 128)
            q = pbuf[:, pl.ds(at, 128)]
            k = pbuf[:, pl.ds(pl.multiple_of(at + CH, 128), 128)]
            v = pbuf[:, pl.ds(pl.multiple_of(at + 2 * CH, 128), 128)]
            g = gatt[:, pl.ds(at, 128)]
            res = []
            for e in (0, 1):
                mask = low if e == 0 else jnp.logical_not(low)
                head = pl.ds(2 * p + e, 1)
                scores = nt(k, jnp.where(mask, q, jnp.zeros_like(q))) * 0.125 - distance[...] * steep[head, :]
                probable = jnp.exp(scores - log_total[head, :])
                gp = nt(v, jnp.where(mask, g, jnp.zeros_like(g)))
                gv = jnp.dot(probable.astype(bf16), g, preferred_element_type=f32)
                inner = jnp.sum(gp * probable, axis=0, keepdims=True)
                gs = (probable * (gp - inner)).astype(bf16)
                res.append((tn(gs, k) * 0.125, jnp.dot(gs, q, preferred_element_type=f32) * 0.125, gv))
            for j in range(3):
                gcat[QKV][0:T, pl.ds(pl.multiple_of(at + CH * j, 128), 128)] = jnp.where(low, res[0][j], res[1][j]).astype(bf16)

        if i == 3:
            pair(QKV, 1).start()

    def first_norm(i):
        if i == 0:
            hid_copy.wait()

        def emit(rows, value):
            total = (gmid[rows, :] + value).astype(bf16)
            gcat[SKIP][rows, :] = total
            wide = total.astype(f32)
            acc[4] += wide[0:8] + wide[8:16]

        norm_back(i, 0, 2, emit)
        if i == 3:
            pair(SKIP, 1).start()
            for row, a in ((0, 4), (1, 2), (2, 3), (3, 0), (4, 1)):
                small[row : row + 1, :] = jnp.sum(acc[a], axis=0, keepdims=True)

    def to_inputs(i):
        def finish(at, value):
            lbuf[i, :, pl.ds(at, 512)] = value.astype(bf16)

        back_product(12 + i, lambda: gcat[SKIP][0:T, :], finish)
        out_copies[i].start()

    meet = [cpart, xp, yp, place(z + 1 - 2 * lax.rem(z, 2), x, c, y), place(lax.rem(z + 2, 4), x, c, y)]

    def small_copy(t):
        return pltpu.make_async_remote_copy(
            src_ref=small, dst_ref=small_land.at[t], send_sem=small_send.at[t], recv_sem=small_recv.at[t],
            device_id=meet[t], device_id_type=MESH)

    def small_step(t):
        if t:
            small_copy(t - 1).wait_send()
            small_copy(t - 1).wait_recv()
            small[...] += small_land[t - 1]
        if t < 5:
            small_copy(t).start()
        else:
            small_out[...] = small[...]

    steps = {
        "T": turn, "B1": through_gelu, "B2": lambda i: into_norm(None, i, 4, UP), "L2": second_norm,
        "B3": lambda i: to_attended(), "A": attention, "B5": lambda i: into_norm(None, i, 9, QKV),
        "L1": first_norm, "B6": to_inputs, "R": small_step,
        "W4": lambda i: weight_product(DOWN, 4 * i, 4 * i + 4), "W3": lambda i: weight_product(UP, 4 * i, 4 * i + 4),
        "W2": lambda i: weight_product(OUT, 0, 2), "W1": lambda i: weight_product(QKV, 3 * i, 3 * i + 3),
        "W0": lambda i: weight_product(SKIP, 0, 4),
    }
    for item in " ".join(BACK_PLAN).split():
        name, at = item.split(".")
        if name[0] == "e":
            do(int(name[1]), STAGES[int(at)])
        else:
            steps[name](int(at))

    for o in out_copies:
        o.wait()
    for k in range(n):
        for j in pieces(k):
            pair(k, j).wait_send()
        for zo in range(ZN):
            link(k, XY + zo, mine(k, zo, 1 - x, 1 - y, 2, 2), lxy[k].at[zo], xp).wait_send()
            link(k, YX + zo, mine(k, zo, 1 - x, 1 - y, 0, 2), lyx[k].at[zo], yp).wait_send()
        for t in range(1, ZN):
            zo = lax.rem(z + t, ZN)
            link(k, XM + zo, mine(k, zo, 1 - x, y, 1, 3), land_x(k, zo, 1, 3), xp).wait_send()
            link(k, YM + zo, mine(k, zo, x, 1 - y, 0, 3), land_y(k, zo, 0, 3), yp).wait_send()
        link(k, XM + z, mine(k, z, 1 - x, y), land_x(k, z, 0, 4), xp).wait_send()
        link(k, YM + z, mine(k, z, x, 1 - y), land_y(k, z, 0, 4), yp).wait_send()
        for d in (0, 1):
            for s in range(3):
                @pl.when(z_has(d, s + 1))
                def _():
                    zo = zo_of(d, s + 1)
                    to = z_slot(d, s, zo)
                    link(k, ZX + d * 3 + s, mine(k, zo, 1 - x, y, 0, 1), lzx[k].at[to], toward(d)).wait_send()
                    link(k, ZY + d * 3 + s, mine(k, zo, x, 1 - y, 3, 1), lzy[k].at[to], toward(d)).wait_send()
                    link(k, ZM + d * 3 + s, mine(k, zo, x, y), lzm[k].at[to], toward(d)).wait_send()


STAGES = [("own",), ("near",)] + [(e, s) for s in range(3) for e in ("chain", "side")] + [
    ("cross", s) for s in range(3)] + [("last",)]


def backward_all(cot, tokens, skip, normed, attended, normed_two, activated, weights, slope, middle, hidden,
                 projected, log_total, steep, distance, gains):
    T, d = cot.shape
    dims = [(w.shape[0] // 2, w.shape[1]) for w in weights]
    hw = [(h // 16, w) for h, w in dims]
    sem = pltpu.SemaphoreType.DMA
    V = pltpu.VMEM
    n = len(weights)
    scratch = (
        [V((2, h, T), bf16) for h, _ in dims]
        + [V((h, T), bf16) for h, _ in dims]
        + [V((2 * T, w), bf16) for _, w in dims]
        + [V((h, w), bf16) for h, w in dims]
        + [V((4, h, w), bf16) for h, w in hw]
        + [V((4, h, w), bf16) for h, w in hw]
        + [V((4, h, w // 2), bf16) for h, w in hw]
        + [V((4, h, w // 2), bf16) for h, w in hw]
        + [V((5, h, w), bf16) for h, w in hw]
        + [V((5, h, w // 4), bf16) for h, w in hw]
        + [V((5, h, w // 4), bf16) for h, w in hw]
        + [V((2, CH, CH), bf16), V((2, T, CH), bf16), V((2, T, CH), bf16), V((T, d), f32), V((T, d), f32), V((T, d), f32),
           V((T, 3 * d), bf16), V((T, d), bf16), V((5, 8, d), f32), V((16, d), f32), V((5, 16, d), f32),
           sem((n, SLOTS)), sem((n, SLOTS)), sem((n, 5)), sem((n, 5)), sem((2,)), sem((2,)), sem((2,)), sem((6,)),
           sem((5,)), sem((5,))]
    )
    vm, anywhere = pl.BlockSpec(memory_space=V), pl.BlockSpec(memory_space=pl.ANY)
    outs = [jax.ShapeDtypeStruct((16, d), f32)] + [jax.ShapeDtypeStruct(s, f32) for s in hw] + [
        jax.ShapeDtypeStruct((T, d), bf16)] * 2
    return pl.pallas_call(
        backward_kernel, out_shape=outs,
        in_specs=[anywhere] * 16 + [vm] * 4,
        out_specs=[vm] * 6 + [anywhere] * 2,
        scratch_shapes=scratch,
        compiler_params=pltpu.CompilerParams(collective_id=1, has_side_effects=True, vmem_limit_bytes=67043328),
        name="backward_and_scatter",
    )(cot, tokens, skip, normed, attended, normed_two, activated, *weights, slope, middle, hidden, projected,
      log_total, steep, distance, gains)


def product(left, right):
    return jnp.dot(left, right, preferred_element_type=jnp.float32)


def outer_product(left, right):
    return lax.dot_general(
        left, right, (((0,), (0,)), ((), ())), preferred_element_type=jnp.float32
    )


def product_back(left, right):
    return lax.dot_general(
        left, right, (((1,), (1,)), ((), ())), preferred_element_type=jnp.float32
    )


def norm_rows(values, gain, shift):
    center = values - jnp.mean(values, axis=-1, keepdims=True)
    spread = jnp.mean(center * center, axis=-1, keepdims=True)
    return center * lax.rsqrt(spread + epsilon) * gain + shift


def gelu_exact(values):
    return 0.5 * values * (1.0 + lax.erf(values * 0.7071067811865476))


def attend_mask(seg_row, valid_row, head_count):
    count_rows = seg_row.shape[0]
    places = jnp.arange(count_rows, dtype=jnp.int32)
    same_utt = seg_row[:, None] == seg_row[None, :]
    diagonal = places[:, None] == places[None, :]
    allowed = same_utt & ((valid_row[None, :] == 1) | diagonal)
    slopes = 2.0 ** (-8.0 * (jnp.arange(head_count, dtype=jnp.float32) + 1.0) / head_count)
    distance = jnp.abs(places[:, None] - places[None, :]).astype(jnp.float32)
    return (allowed, -slopes[:, None, None] * distance[None, :, :])


def split_heads(projected, head_count):
    row_count = projected.shape[0]
    feature_width = projected.shape[1] // 3
    head_size = feature_width // head_count
    queries = projected[:, :feature_width].reshape(row_count, head_count, head_size)
    keys_all = projected[:, feature_width : 2 * feature_width].reshape(
        row_count, head_count, head_size
    )
    values_all = projected[:, 2 * feature_width :].reshape(row_count, head_count, head_size)
    return (queries, keys_all, values_all)


def masked_scores(queries, keys_all, allowed, linear_bias):
    score_scale = queries.shape[2] ** (-0.5)
    raw = (
        jnp.einsum("qhd,khd->hqk", queries, keys_all, preferred_element_type=jnp.float32)
        * score_scale
        + linear_bias
    )
    return jnp.where(allowed[None, :, :], raw, -1e30)


def forward_pass(tokens, skip, weights, allowed, linear_bias, head_count):
    w_skip, b_skip, g_one, beta_one, w_qkv, w_out, g_two, beta_two, w_up, b_up, w_down, b_down = (
        weights
    )
    row_count, feature_width = tokens.shape
    joined = jnp.concatenate([tokens, skip], axis=1)
    hidden = product(joined, w_skip) + b_skip.astype(jnp.float32)
    normed = norm_rows(hidden, g_one.astype(jnp.float32), beta_one.astype(jnp.float32)).astype(
        jnp.bfloat16
    )
    projected = product(normed, w_qkv).astype(jnp.bfloat16)
    queries, keys_all, values_all = split_heads(projected, head_count)
    masked = masked_scores(queries, keys_all, allowed, linear_bias)
    row_top = jnp.max(masked, axis=-1, keepdims=True)
    exponent = jnp.exp(masked - row_top)
    row_total = jnp.sum(exponent, axis=-1, keepdims=True)
    soft_weights = (exponent / row_total).astype(jnp.bfloat16)
    log_total = row_top + jnp.log(row_total)
    weighted = jnp.einsum(
        "hqk,khd->qhd", soft_weights, values_all, preferred_element_type=jnp.float32
    )
    attended = weighted.reshape(row_count, feature_width).astype(jnp.bfloat16)
    middle = hidden + product(attended, w_out)
    normed_two = norm_rows(middle, g_two.astype(jnp.float32), beta_two.astype(jnp.float32)).astype(
        jnp.bfloat16
    )
    hidden_up = product(normed_two, w_up) + b_up.astype(jnp.float32)
    activated = gelu_exact(hidden_up).astype(jnp.bfloat16)
    result = middle + (product(activated, w_down) + b_down.astype(jnp.float32))
    stored = (
        joined,
        hidden,
        normed,
        projected,
        log_total,
        attended,
        middle,
        normed_two,
        hidden_up,
        activated,
    )
    return (stored, result)


def backward_feed(stored, weights, cotangent):
    (
        joined,
        hidden,
        normed,
        projected,
        log_total,
        attended,
        middle,
        normed_two,
        hidden_up,
        activated,
    ) = stored
    w_skip, b_skip, g_one, beta_one, w_qkv, w_out, g_two, beta_two, w_up, b_up, w_down, b_down = (
        weights
    )
    grad_result = cotangent.astype(jnp.float32)
    grad_activated = product_back(cotangent, w_down)
    grad_b_down = jnp.sum(grad_result, axis=0)
    gelu_value, gelu_pull = jax.vjp(gelu_exact, hidden_up)
    grad_up = gelu_pull(grad_activated)[0].astype(jnp.bfloat16)
    grad_b_up = jnp.sum(grad_up.astype(jnp.float32), axis=0)
    grad_normed_two = product_back(grad_up, w_up)
    norm_value, norm_pull = jax.vjp(
        norm_rows, middle, g_two.astype(jnp.float32), beta_two.astype(jnp.float32)
    )
    grad_middle_norm, grad_g_two, grad_beta_two = norm_pull(grad_normed_two)
    grad_middle = grad_result + grad_middle_norm
    feed_terms = (grad_up, grad_b_up, cotangent, grad_b_down, grad_g_two, grad_beta_two)
    return (feed_terms, grad_middle)


def backward_front(stored, weights, grad_middle, allowed, linear_bias, head_count):
    (
        joined,
        hidden,
        normed,
        projected,
        log_total,
        attended,
        middle,
        normed_two,
        hidden_up,
        activated,
    ) = stored
    w_skip, b_skip, g_one, beta_one, w_qkv, w_out, g_two, beta_two, w_up, b_up, w_down, b_down = (
        weights
    )
    row_count, feature_width = hidden.shape
    branch_grad = grad_middle.astype(jnp.bfloat16)
    grad_attended = product_back(branch_grad, w_out).astype(jnp.bfloat16)
    queries, keys_all, values_all = split_heads(projected, head_count)
    score_scale = queries.shape[2] ** (-0.5)
    masked = masked_scores(queries, keys_all, allowed, linear_bias)
    probable = jnp.exp(masked - log_total)
    soft_weights = probable.astype(jnp.bfloat16)
    grad_heads = grad_attended.reshape(row_count, head_count, feature_width // head_count)
    grad_probable = jnp.einsum(
        "qhd,khd->hqk", grad_heads, values_all, preferred_element_type=jnp.float32
    )
    grad_values = jnp.einsum(
        "hqk,qhd->khd", soft_weights, grad_heads, preferred_element_type=jnp.float32
    )
    inner_sum = jnp.sum(grad_probable * probable, axis=-1, keepdims=True)
    grad_scores = (probable * (grad_probable - inner_sum)).astype(jnp.bfloat16)
    grad_queries = (
        jnp.einsum("hqk,khd->qhd", grad_scores, keys_all, preferred_element_type=jnp.float32)
        * score_scale
    )
    grad_keys = (
        jnp.einsum("hqk,qhd->khd", grad_scores, queries, preferred_element_type=jnp.float32)
        * score_scale
    )
    grad_projected = jnp.concatenate(
        [
            grad_queries.reshape(row_count, feature_width),
            grad_keys.reshape(row_count, feature_width),
            grad_values.reshape(row_count, feature_width),
        ],
        axis=1,
    ).astype(jnp.bfloat16)
    grad_normed = product_back(grad_projected, w_qkv)
    norm_value, norm_pull = jax.vjp(
        norm_rows, hidden, g_one.astype(jnp.float32), beta_one.astype(jnp.float32)
    )
    grad_hidden_norm, grad_g_one, grad_beta_one = norm_pull(grad_normed)
    grad_hidden = (grad_middle + grad_hidden_norm).astype(jnp.bfloat16)
    grad_b_skip = jnp.sum(grad_hidden.astype(jnp.float32), axis=0)
    grad_joined = product_back(grad_hidden, w_skip)
    grad_tokens = grad_joined[:, :feature_width].astype(jnp.bfloat16)
    grad_skip = grad_joined[:, feature_width:].astype(jnp.bfloat16)
    front_terms = (grad_hidden, grad_b_skip, grad_g_one, grad_beta_one, grad_projected, branch_grad)
    return (grad_tokens, grad_skip, front_terms)


AXES = ("wide", "narrow")


def pack_small(b_skip, g_one, beta_one, g_two, beta_two, b_up, b_down):
    row = jnp.concatenate(
        [b_skip, g_one, beta_one, g_two, beta_two, b_down, jnp.zeros((64,), b_skip.dtype), b_up]
    ).reshape(3, 128)
    return jnp.pad(row, ((0, 13), (0, 0)))


def unpack_small(table):
    def column(row, at):
        return table[:, row, at : at + 32].reshape(-1)

    return (
        column(0, 0), column(0, 32), column(0, 64), column(0, 96),
        column(1, 0), table[:, 2, :].reshape(-1), column(1, 32),
    )


def gather_plain(values):
    return [lax.all_gather(v, AXES, axis=0, tiled=True) for v in values]


def own_layer(tokens, skip, seg_ids, valid, w_skip, b_skip, g_one, beta_one, w_qkv, w_out, g_two, beta_two,
              w_up, b_up, w_down, b_down, cotangent):
    gathered = gather_all(
        pack_small(b_skip, g_one, beta_one, g_two, beta_two, b_up, b_down),
        (w_skip, w_qkv, w_out, w_up, w_down),
    )
    b_skip, g_one, beta_one, g_two, beta_two, b_up, b_down = unpack_small(gathered[0])
    big = [w.reshape(-1, w.shape[-1]) for w in gathered[1:]]
    w_skip, w_qkv, w_out, w_up, w_down = big
    weights = (w_skip, b_skip, g_one, beta_one, w_qkv, w_out, g_two, beta_two, w_up, b_up, w_down, b_down)
    allowed, linear_bias = attend_mask(seg_ids[0], valid[0], HEADS)
    stored, result = forward_pass(tokens, skip, weights, allowed, linear_bias, HEADS)
    (joined, hidden, normed, projected, log_total, attended, middle, normed_two, hidden_up, activated) = stored
    count = tokens.shape[0]
    places = jnp.arange(count, dtype=jnp.int32)
    apart = jnp.abs(places[:, None] - places[None, :]).astype(f32)
    distance = jnp.where(allowed.T, apart, 1e33)
    steep = jnp.broadcast_to((2.0 ** (-8.0 * (jnp.arange(HEADS, dtype=f32) + 1.0) / HEADS))[:, None], (HEADS, count))
    half = 0.5 * (1.0 + lax.erf(hidden_up * 0.7071067811865476))
    slope = (half + hidden_up * jnp.exp(-0.5 * hidden_up * hidden_up) * 0.3989422804014327).astype(bf16)
    gains = jnp.stack([g_one, g_two]).astype(f32)
    small, *rest = backward_all(
        cotangent, tokens, skip, normed, attended, normed_two, activated, big, slope, middle, hidden,
        projected, log_total[:, :, 0], steep, distance, gains)
    me = lax.axis_index("wide") * 2 + lax.axis_index("narrow")
    rows = [lax.dynamic_slice(small[i], (me * 32,), (32,)) for i in range(6)]
    grad_b_up = lax.dynamic_slice(small[6:10].reshape(-1), (me * 128,), (128,))
    big, grad_tokens, grad_skip = rest[:5], rest[5], rest[6]
    return (
        result.astype(bf16), grad_tokens, grad_skip,
        big[0], rows[0], rows[1], rows[2], big[1], big[2],
        rows[3], rows[4], big[3], grad_b_up, big[4], rows[5],
    )


def plain_layer(tokens, skip, seg_ids, valid, w_skip, b_skip, g_one, beta_one, w_qkv, w_out, g_two, beta_two,
                w_up, b_up, w_down, b_down, cotangent):
    weights = gather_plain(
        (w_skip, b_skip, g_one, beta_one, w_qkv, w_out, g_two, beta_two, w_up, b_up, w_down, b_down))
    allowed, linear_bias = attend_mask(seg_ids[0], valid[0], HEADS)
    stored, result = forward_pass(tokens, skip, weights, allowed, linear_bias, HEADS)
    (joined, hidden, normed, projected, log_total, attended, middle, normed_two, hidden_up, activated) = stored
    feed_terms, grad_middle = backward_feed(stored, weights, cotangent)
    grad_tokens, grad_skip, front_terms = backward_front(
        stored, weights, grad_middle, allowed, linear_bias, HEADS)
    grad_up, grad_b_up, grad_result, grad_b_down, grad_g_two, grad_beta_two = feed_terms
    grad_hidden, grad_b_skip, grad_g_one, grad_beta_one, grad_projected, branch_grad = front_terms
    lefts = (joined, normed, attended, normed_two, activated)
    rights = (grad_hidden, grad_projected, branch_grad, grad_up, grad_result)

    def scatter(v):
        return lax.psum_scatter(v, AXES, scatter_dimension=0, tiled=True)

    big = [scatter(outer_product(a, b)) for a, b in zip(lefts, rights)]
    grad_b_skip, grad_g_one, grad_beta_one, grad_g_two, grad_beta_two, grad_b_up, grad_b_down = [
        scatter(v) for v in
        (grad_b_skip, grad_g_one, grad_beta_one, grad_g_two, grad_beta_two, grad_b_up, grad_b_down)]
    return (
        result.astype(bf16), grad_tokens, grad_skip,
        big[0], grad_b_skip, grad_g_one, grad_beta_one, big[1], big[2],
        grad_g_two, grad_beta_two, big[3], grad_b_up, big[4], grad_b_down,
    )


def solution(mesh):
    return jax.shard_map(
        own_layer if dict(mesh.shape) == {"wide": 16, "narrow": 2} else plain_layer,
        mesh=mesh,
        in_specs=(
            P(("wide", "narrow"), None),
            P(("wide", "narrow"), None),
            P(("wide", "narrow"), None),
            P(("wide", "narrow"), None),
            P(("wide", "narrow"), None),
            P(("wide", "narrow")),
            P(("wide", "narrow")),
            P(("wide", "narrow")),
            P(("wide", "narrow"), None),
            P(("wide", "narrow"), None),
            P(("wide", "narrow")),
            P(("wide", "narrow")),
            P(("wide", "narrow"), None),
            P(("wide", "narrow")),
            P(("wide", "narrow"), None),
            P(("wide", "narrow")),
            P(("wide", "narrow"), None),
        ),
        out_specs=(
            P(("wide", "narrow"), None),
            P(("wide", "narrow"), None),
            P(("wide", "narrow"), None),
            P(("wide", "narrow"), None),
            P(("wide", "narrow")),
            P(("wide", "narrow")),
            P(("wide", "narrow")),
            P(("wide", "narrow"), None),
            P(("wide", "narrow"), None),
            P(("wide", "narrow")),
            P(("wide", "narrow")),
            P(("wide", "narrow"), None),
            P(("wide", "narrow")),
            P(("wide", "narrow"), None),
            P(("wide", "narrow")),
        ),
        check_vma=False,
    )
```

```python
import jax
import jax.numpy as jnp
from jax import lax
from jax.experimental import pallas as pl
from jax.experimental.pallas import tpu as pltpu
from jax.sharding import PartitionSpec as P

f32 = jnp.float32
bf16 = jnp.bfloat16

MESH = pl.DeviceIdType.MESH
ZN = 4
SLOTS = 38
ZM, ZX, ZY, XM, XY, YM, YX, CP = 0, 6, 12, 18, 22, 26, 30, 34


def here():
    w = lax.axis_index("wide")
    y = lax.axis_index("narrow")
    c = lax.rem(w, 2)
    x = lax.rem(lax.div(w, 2), 2)
    z = lax.div(w, 4)
    return z, x, c, y


def place(z, x, c, y):
    return ((z * 2 + x) * 2 + c, y)


def greet_all(total_w, total_n):
    barrier = pltpu.get_barrier_semaphore()
    w = lax.axis_index("wide")
    y = lax.axis_index("narrow")
    me = w * total_n + y
    count = total_w * total_n

    @pl.loop(1, count)
    def _(o):
        to = lax.rem(me + o, count)
        pl.semaphore_signal(
            barrier, inc=1, device_id=(lax.div(to, total_n), lax.rem(to, total_n)), device_id_type=MESH
        )

    pl.semaphore_wait(barrier, count - 1)


def gather_events(own, full, send_sem, recv_sem, local_sem):
    n = len(own)
    z, x, c, y = here()

    def block(k, xo, co, yo):
        h = own[k].shape[0]
        return pl.ds(pl.multiple_of(((xo * 2 + co) * 2 + yo) * h, h), h)

    def part(k, zo, xo, yo, first=0, quarters=4):
        width = own[k].shape[1] // 4
        return full[k].at[zo, block(k, xo, c, yo), pl.ds(first * width, quarters * width)]

    def link(k, slot, src, dst, to):
        return pltpu.make_async_remote_copy(
            src_ref=src, dst_ref=dst, send_sem=send_sem.at[k, slot], recv_sem=recv_sem.at[k, slot],
            device_id=to, device_id_type=MESH)

    xp = place(z, 1 - x, c, y)
    yp = place(z, x, c, 1 - y)
    cpart = place(z, x, 1 - c, y)

    def zto(d):
        return place(z + 1 - 2 * d, x, c, y)

    def z_has(d, s):
        return (z - s >= 0) if d == 0 else (z + s <= ZN - 1)

    def z_next(d):
        return (z < ZN - 1) if d == 0 else (z > 0)

    def zo_of(d, s):
        return z - s if d == 0 else z + s

    def z_send(k, base, d, s, xo, yo, first, quarters, src=None):
        cond = jnp.logical_and(z_has(d, s), z_next(d))
        zo = zo_of(d, s)
        dst = part(k, zo, xo, yo, first, quarters)
        cp = link(k, base + d * 3 + s, dst if src is None else src, dst, zto(d))

        @pl.when(cond)
        def _():
            cp.start()

    def z_wait(k, base, d, s, xo, yo, first, quarters):
        zo = zo_of(d, s + 1)
        dst = part(k, zo, xo, yo, first, quarters)
        link(k, base + d * 3 + s, dst, dst, zto(d)).wait_recv()

    def go(k, slot, ref, to, src=None, cond=None):
        cp = link(k, slot, ref if src is None else src, ref, to)
        cp.start()

    def wait(k, slot, ref):
        link(k, slot, ref, ref, xp).wait_recv()

    def begin():
        for k in range(n):
            pltpu.make_async_copy(own[k], part(k, z, x, y), local_sem.at[k]).start()

    def do(k, e):
        kind = e[0]
        if kind == "own":
            for d in (0, 1):
                z_send(k, ZM, d, 0, x, y, 0, 4, src=own[k])
            go(k, XM + z, part(k, z, x, y), xp, src=own[k])
            go(k, YM + z, part(k, z, x, y), yp, src=own[k])
        elif kind == "near":
            wait(k, XM + z, part(k, z, 1 - x, y))
            for d in (0, 1):
                z_send(k, ZX, d, 0, 1 - x, y, 0, 1)
            go(k, YX + z, part(k, z, 1 - x, y, 0, 2), yp)
            wait(k, YM + z, part(k, z, x, 1 - y))
            for d in (0, 1):
                z_send(k, ZY, d, 0, x, 1 - y, 3, 1)
            go(k, XY + z, part(k, z, x, 1 - y, 2, 2), xp)
        elif kind == "chain":
            s = e[1]
            for d in (0, 1):
                @pl.when(z_has(d, s + 1))
                def _():
                    z_wait(k, ZM, d, s, x, y, 0, 4)
                    zo = zo_of(d, s + 1)
                    if s < 2:
                        @pl.when(z_next(d))
                        def _():
                            ref = part(k, zo, x, y)
                            link(k, ZM + d * 3 + s + 1, ref, ref, zto(d)).start()
                    ref = part(k, zo, x, y, 1, 3)
                    link(k, XM + zo, ref, ref, xp).start()
                    ref = part(k, zo, x, y, 0, 3)
                    link(k, YM + zo, ref, ref, yp).start()
        elif kind == "side":
            s = e[1]
            for d in (0, 1):
                @pl.when(z_has(d, s + 1))
                def _():
                    zo = zo_of(d, s + 1)
                    for base, xo, yo, first in ((ZX, 1 - x, y, 0), (ZY, x, 1 - y, 3)):
                        z_wait(k, base, d, s, xo, yo, first, 1)
                        if s < 2:
                            @pl.when(z_next(d))
                            def _():
                                ref = part(k, zo, xo, yo, first, 1)
                                link(k, base + d * 3 + s + 1, ref, ref, zto(d)).start()
        elif kind == "cross":
            s = e[1]
            for d in (0, 1):
                @pl.when(z_has(d, s + 1))
                def _():
                    zo = zo_of(d, s + 1)
                    wait(k, XM + zo, part(k, zo, 1 - x, y, 1, 3))
                    ref = part(k, zo, 1 - x, y, 0, 2)
                    link(k, YX + zo, ref, ref, yp).start()
                    wait(k, YM + zo, part(k, zo, x, 1 - y, 0, 3))
                    ref = part(k, zo, x, 1 - y, 2, 2)
                    link(k, XY + zo, ref, ref, xp).start()
            if s == 0:
                pltpu.make_async_copy(own[k], part(k, z, x, y), local_sem.at[k]).wait()
                ref = full[k].at[:, block(k, x, c, y), :]
                link(k, CP, ref, ref, cpart).start()
            if s == 2:
                ref = full[k].at[:, block(k, 1 - x, c, y), :]
                link(k, CP + 1, ref, ref, cpart).start()
                ref = full[k].at[:, block(k, x, c, 1 - y), :]
                link(k, CP + 2, ref, ref, cpart).start()
        elif kind == "last":
            for zo in range(ZN):
                wait(k, XY + zo, part(k, zo, 1 - x, 1 - y, 2, 2))
                wait(k, YX + zo, part(k, zo, 1 - x, 1 - y, 0, 2))
            ref = full[k].at[:, block(k, 1 - x, c, 1 - y), :]
            link(k, CP + 3, ref, ref, cpart).start()
        elif kind == "ready":
            for j, (xo, yo) in enumerate(((x, y), (1 - x, y), (x, 1 - y), (1 - x, 1 - y))):
                ref = full[k].at[:, block(k, xo, 1 - c, yo), :]
                link(k, CP + j, ref, ref, cpart).wait_recv()

    def finish():
        for k in range(n):
            for j, (xo, yo) in enumerate(((x, y), (1 - x, y), (x, 1 - y), (1 - x, 1 - y))):
                ref = full[k].at[:, block(k, xo, c, yo), :]
                link(k, CP + j, ref, ref, cpart).wait_send()
            for d in (0, 1):
                for s in range(3):
                    @pl.when(jnp.logical_and(z_has(d, s), z_next(d)))
                    def _():
                        zo = zo_of(d, s)
                        for base, xo, yo, first, q in ((ZM, x, y, 0, 4), (ZX, 1 - x, y, 0, 1), (ZY, x, 1 - y, 3, 1)):
                            ref = part(k, zo, xo, yo, first, q)
                            link(k, base + d * 3 + s, ref, ref, zto(d)).wait_send()
            ref = part(k, z, x, y)
            link(k, XM + z, ref, ref, xp).wait_send()
            link(k, YM + z, ref, ref, yp).wait_send()
            for t in range(1, ZN):
                zo = lax.rem(z + t, ZN)
                ref = part(k, zo, x, y, 1, 3)
                link(k, XM + zo, ref, ref, xp).wait_send()
                ref = part(k, zo, x, y, 0, 3)
                link(k, YM + zo, ref, ref, yp).wait_send()
            for zo in range(ZN):
                ref = part(k, zo, 1 - x, y, 0, 2)
                link(k, YX + zo, ref, ref, yp).wait_send()
                ref = part(k, zo, x, 1 - y, 2, 2)
                link(k, XY + zo, ref, ref, xp).wait_send()

    return begin, do, finish


def scatter_events(outs, part_sums, landings, send_sem, recv_sem):
    n = len(outs)
    lxm, lym, lxy, lyx, lzm, lzx, lzy = landings
    z, x, c, y = here()
    xp = place(z, 1 - x, c, y)
    yp = place(z, x, c, 1 - y)

    def rows_of(k):
        return outs[k].shape[0]

    def width(k):
        return outs[k].shape[1]

    def mine(k, zo, xo, yo, first=0, quarters=4):
        h, w = rows_of(k), width(k) // 4
        row = pl.multiple_of(((zo * 2 + xo) * 2 + yo) * h, h)
        return part_sums[k].at[pl.ds(row, h), pl.ds(first * w, quarters * w)]

    def link(k, slot, src, dst, to):
        return pltpu.make_async_remote_copy(
            src_ref=src, dst_ref=dst, send_sem=send_sem.at[k, slot], recv_sem=recv_sem.at[k, slot],
            device_id=to, device_id_type=MESH)

    def quarter_slice(k, first, quarters):
        w = width(k) // 4
        return pl.ds(first * w, quarters * w)

    def land_x(k, zo, first, quarters):
        return lxm[k].at[zo, :, quarter_slice(k, first, quarters)]

    def land_y(k, zo, first, quarters):
        return lym[k].at[zo, :, quarter_slice(k, first, quarters)]

    def z_has(d, s):
        return (z - s >= 0) if d == 0 else (z + s <= ZN - 1)

    def z_next(d):
        return (z < ZN - 1) if d == 0 else (z > 0)

    def zo_of(d, s):
        return z - s if d == 0 else z + s

    def z_slot(d, s, zo):
        return ZN if (d == 1 and s == 0) else zo

    def toward(d):
        return place(z - 1 + 2 * d, x, c, y)

    def add_in(k, zo, xo, yo, first, quarters, others):
        ref = mine(k, zo, xo, yo, first, quarters)
        h = rows_of(k)

        @pl.loop(0, h // 16)
        def _(i):
            rows = pl.ds(pl.multiple_of(i * 16, 16), 16)
            total = ref[rows, :].astype(f32)
            for o in others:
                total = total + o[rows, :].astype(f32)
            ref[rows, :] = total.astype(bf16)

    def wait(k, slot, dst):
        link(k, slot, dst, dst, xp).wait_recv()

    def do(k, e):
        kind = e[0]
        if kind == "last":
            for zo in range(ZN):
                link(k, XY + zo, mine(k, zo, 1 - x, 1 - y, 2, 2), lxy[k].at[zo], xp).start()
                link(k, YX + zo, mine(k, zo, 1 - x, 1 - y, 0, 2), lyx[k].at[zo], yp).start()
        elif kind == "cross":
            s = e[1]
            for d in (0, 1):
                @pl.when(z_has(d, s + 1))
                def _():
                    zo = zo_of(d, s + 1)
                    wait(k, YX + zo, lyx[k].at[zo])
                    add_in(k, zo, 1 - x, y, 0, 2, [lyx[k].at[zo]])
                    link(k, XM + zo, mine(k, zo, 1 - x, y, 1, 3), land_x(k, zo, 1, 3), xp).start()
                    wait(k, XY + zo, lxy[k].at[zo])
                    add_in(k, zo, x, 1 - y, 2, 2, [lxy[k].at[zo]])
                    link(k, YM + zo, mine(k, zo, x, 1 - y, 0, 3), land_y(k, zo, 0, 3), yp).start()
        elif kind == "side":
            s = e[1]
            for d in (0, 1):
                @pl.when(z_has(d, s + 1))
                def _():
                    zo = zo_of(d, s + 1)
                    for base, landing, xo, yo, first in ((ZX, lzx, 1 - x, y, 0), (ZY, lzy, x, 1 - y, 3)):
                        if s < 2:
                            @pl.when(z_next(d))
                            def _():
                                got = landing[k].at[z_slot(d, s + 1, zo)]
                                wait(k, base + d * 3 + s + 1, got)
                                add_in(k, zo, xo, yo, first, 1, [got])
                        link(k, base + d * 3 + s, mine(k, zo, xo, yo, first, 1),
                             landing[k].at[z_slot(d, s, zo)], toward(d)).start()
        elif kind == "chain":
            s = e[1]
            for d in (0, 1):
                @pl.when(z_has(d, s + 1))
                def _():
                    zo = zo_of(d, s + 1)
                    wait(k, XM + zo, land_x(k, zo, 1, 3))
                    wait(k, YM + zo, land_y(k, zo, 0, 3))
                    add_in(k, zo, x, y, 0, 1, [land_y(k, zo, 0, 1)])
                    add_in(k, zo, x, y, 1, 2, [land_y(k, zo, 1, 2), land_x(k, zo, 1, 2)])
                    add_in(k, zo, x, y, 3, 1, [land_x(k, zo, 3, 1)])
                    if s < 2:
                        @pl.when(z_next(d))
                        def _():
                            got = lzm[k].at[z_slot(d, s + 1, zo)]
                            wait(k, ZM + d * 3 + s + 1, got)
                            add_in(k, zo, x, y, 0, 4, [got])
                    link(k, ZM + d * 3 + s, mine(k, zo, x, y), lzm[k].at[z_slot(d, s, zo)], toward(d)).start()
        elif kind == "near":
            for slot, own_slot, xo, yo, first, cross_land, side_base, side_land, side_first, to, land in (
                (YX, XM, 1 - x, y, 0, lyx, ZX, lzx, 0, xp, land_x),
                (XY, YM, x, 1 - y, 2, lxy, ZY, lzy, 3, yp, land_y),
            ):
                wait(k, slot + z, cross_land[k].at[z])
                add_in(k, z, xo, yo, first, 2, [cross_land[k].at[z]])
                for d in (0, 1):
                    @pl.when(z_next(d))
                    def _():
                        got = side_land[k].at[z_slot(d, 0, z)]
                        wait(k, side_base + d * 3, got)
                        add_in(k, z, xo, yo, side_first, 1, [got])
                link(k, own_slot + z, mine(k, z, xo, yo), land(k, z, 0, 4), to).start()
        elif kind == "own":
            wait(k, XM + z, land_x(k, z, 0, 4))
            wait(k, YM + z, land_y(k, z, 0, 4))
            h = rows_of(k)
            own = mine(k, z, x, y)
            from_x, from_y = land_x(k, z, 0, 4), land_y(k, z, 0, 4)

            @pl.loop(0, h // 16)
            def _(i):
                rows = pl.ds(pl.multiple_of(i * 16, 16), 16)
                outs[k][rows, :] = own[rows, :].astype(f32) + from_x[rows, :].astype(f32) + from_y[rows, :].astype(f32)

            for d in (0, 1):
                @pl.when(z_next(d))
                def _():
                    got = lzm[k].at[z_slot(d, 0, z)]
                    wait(k, ZM + d * 3, got)

                    @pl.loop(0, h // 16)
                    def _(i):
                        rows = pl.ds(pl.multiple_of(i * 16, 16), 16)
                        outs[k][rows, :] += got[rows, :].astype(f32)

    def finish():
        for k in range(n):
            for zo in range(ZN):
                link(k, XY + zo, mine(k, zo, 1 - x, 1 - y, 2, 2), lxy[k].at[zo], xp).wait_send()
                link(k, YX + zo, mine(k, zo, 1 - x, 1 - y, 0, 2), lyx[k].at[zo], yp).wait_send()
            for t in range(1, ZN):
                zo = lax.rem(z + t, ZN)
                link(k, XM + zo, mine(k, zo, 1 - x, y, 1, 3), land_x(k, zo, 1, 3), xp).wait_send()
                link(k, YM + zo, mine(k, zo, x, 1 - y, 0, 3), land_y(k, zo, 0, 3), yp).wait_send()
            link(k, XM + z, mine(k, z, 1 - x, y), land_x(k, z, 0, 4), xp).wait_send()
            link(k, YM + z, mine(k, z, x, 1 - y), land_y(k, z, 0, 4), yp).wait_send()
            for d in (0, 1):
                for s in range(3):
                    @pl.when(z_has(d, s + 1))
                    def _():
                        zo = zo_of(d, s + 1)
                        to = z_slot(d, s, zo)
                        link(k, ZX + d * 3 + s, mine(k, zo, 1 - x, y, 0, 1), lzx[k].at[to], toward(d)).wait_send()
                        link(k, ZY + d * 3 + s, mine(k, zo, x, 1 - y, 3, 1), lzy[k].at[to], toward(d)).wait_send()
                        link(k, ZM + d * 3 + s, mine(k, zo, x, y), lzm[k].at[to], toward(d)).wait_send()

    return do, finish


HEADS = 16


epsilon = 1e-05


def nn(a, b):
    return jnp.dot(a, b, preferred_element_type=f32)


def nt(a, b):
    return lax.dot_general(a, b, (((1,), (1,)), ((), ())), preferred_element_type=f32)


def tn(a, b):
    return lax.dot_general(a, b, (((0,), (0,)), ((), ())), preferred_element_type=f32)


CH = 1024
SKIP, QKV, OUT, UP, DOWN = range(5)
CHUNKS = (
    [(SKIP, 0), (SKIP, 1), (QKV, 0), (QKV, 1), (QKV, 2), (OUT, 0)] + [(UP, i) for i in range(4)]
    + [(DOWN, i) for i in range(4)] + [(UP, i) for i in range(4)] + [(OUT, 0)] + [(QKV, i) for i in range(3)]
    + [(SKIP, 0), (SKIP, 1)]
)
LEFTS = [(DOWN, 0), (DOWN, 1), (DOWN, 2), (DOWN, 3), (UP, 0), (OUT, 0), (QKV, 0), (SKIP, 0), (SKIP, 1)]
STAGES = [("own",), ("near",)] + [(e, s) for s in range(3) for e in ("chain", "side")] + [
    ("cross", s) for s in range(3)] + [("last",), ("ready",)]
(PR, MK, TR, F1, F2, F3, AF, F5, F6, F7, F8, FR, B2, B3, B5, B6, A, L1, L2, R, W0, W1, W2, W3, W4,
 G0, G1, G2, G3, G4, E0, E1, E2, E3, E4) = range(35)
GATHER = [G0, G1, G2, G3, G4]
SCATTER = [E0, E1, E2, E3, E4]
PLAN = [
    (G0, 0), (PR, 0), (MK, 0), (TR, 7), (PR, 1), (TR, 8), (G0, 1), (G0, 2),
    (PR, 2), (G0, 3), (G1, 0), (G0, 4), (G0, 5), (PR, 3), (G1, 1), (G1, 2),
    (G0, 6), (G0, 7), (G0, 8), (G0, 9), (PR, 4), (G1, 3), (G2, 0), (G0, 10),
    (G1, 4), (PR, 5), (G1, 5), (G0, 11), (G2, 1), (G2, 2), (G0, 12), (F1, 0),
    (G1, 6), (F1, 1), (F2, 0), (G1, 7), (G1, 8), (G1, 9), (G2, 3), (G3, 0),
    (F2, 1), (G2, 4), (F2, 2), (G1, 10), (F2, 3), (G2, 5), (TR, 6), (G2, 6),
    (G2, 7), (G2, 8), (G3, 1), (G3, 2), (G2, 9), (G1, 11), (G2, 10), (G1, 12),
    (G3, 3), (G4, 0), (F3, 0), (F3, 1), (F3, 2), (G3, 4), (AF, 0), (G3, 5),
    (AF, 1), (G2, 11), (AF, 2), (G2, 12), (AF, 3), (G4, 1), (G4, 2), (TR, 5),
    (F5, 0), (F6, 0), (G3, 6), (F6, 1), (F6, 2), (F6, 3), (TR, 4), (G3, 7),
    (G3, 8), (G3, 9), (G4, 3), (G3, 10), (G4, 4), (G4, 5), (G3, 11), (G4, 6),
    (G4, 7), (G4, 8), (G3, 12), (F7, 0), (G4, 9), (G4, 10), (TR, 0), (F7, 1),
    (TR, 1), (F7, 2), (TR, 2), (F7, 3), (G4, 11), (TR, 3), (G4, 12), (W4, 0),
    (W4, 1), (E4, 11), (F8, 0), (F8, 1), (F8, 2), (F8, 3), (FR, 0), (E4, 10),
    (E4, 9), (E4, 8), (E4, 7), (B2, 0), (B2, 1), (B2, 2), (E4, 6), (E4, 5),
    (B2, 3), (W3, 0), (W3, 1), (E3, 11), (L2, 0), (E4, 4), (L2, 1), (E4, 3),
    (L2, 2), (L2, 3), (B3, 0), (E4, 2), (A, 0), (E4, 1), (E3, 10), (E3, 9),
    (E3, 8), (E3, 7), (W2, 0), (E2, 11), (A, 1), (A, 2), (E4, 0), (E3, 6),
    (E3, 5), (A, 3), (B5, 0), (B5, 1), (B5, 2), (E3, 4), (W1, 0), (E3, 3),
    (E2, 10), (W1, 1), (E2, 9), (E2, 8), (E2, 7), (E2, 6), (E1, 11), (L1, 0),
    (E3, 2), (E2, 5), (E3, 1), (E2, 4), (L1, 1), (L1, 2), (L1, 3), (E1, 10),
    (R, 0), (E2, 3), (E1, 9), (E1, 8), (E2, 2), (E1, 7), (E2, 1), (W0, 0),
    (E0, 11), (E3, 0), (E1, 6), (E1, 5), (R, 1), (B6, 0), (E1, 4), (E1, 3),
    (E2, 0), (E0, 10), (E1, 2), (E0, 9), (E1, 1), (E0, 8), (E0, 7), (E0, 6),
    (R, 2), (B6, 1), (E0, 5), (E0, 4), (E1, 0), (E0, 3), (E0, 2), (R, 3),
    (E0, 1), (E0, 0), (R, 4), (R, 5),
]


def layer_kernel(*refs):
    n = 5
    tokens, skip, cot, seg, valid, mine_small = refs[:6]
    own = refs[6 : 6 + n]
    small_out = refs[11]
    outs = refs[12:17]
    result, grad_tokens, grad_skip = refs[17:20]
    full = refs[20:25]
    r = refs[25:]
    turned, theirs, gcat, part_sums = r[:n], r[n : 2 * n], r[2 * n : 3 * n], r[3 * n : 4 * n]
    landings = [r[(4 + i) * n : (5 + i) * n] for i in range(7)]
    (wbuf, lbuf, hid, gnorm, mid, pbuf, abuf, acc, small, small_land, params, params_wide, params_land,
     log_total, steep, distance,
     ag_send, ag_recv, ag_local, rs_send, rs_recv, pair_send, pair_recv, wsem, lsem, misc_sem,
     small_send, small_recv, params_send, params_recv) = r[11 * n :]
    z, x, c, y = here()
    cpart = place(z, x, 1 - c, y)
    T = cot.shape[0]

    ag_begin, ag_do, ag_finish = gather_events(own, full, ag_send, ag_recv, ag_local)
    rs_do, rs_finish = scatter_events(outs, part_sums, landings, rs_send, rs_recv)

    def chunk_copies(i):
        k, j = CHUNKS[i]
        slot, depth = i % 2, full[k].shape[1]
        if k in (SKIP, DOWN):
            blocks = CH // depth
            return [pltpu.make_async_copy(full[k].at[j * blocks + b], wbuf.at[slot, pl.ds(b * depth, depth), :], wsem.at[slot, b])
                    for b in range(blocks)]
        return [pltpu.make_async_copy(full[k].at[b, :, pl.ds(j * CH, CH)], wbuf.at[slot, pl.ds(b * depth, depth), :], wsem.at[slot, b])
                for b in range(ZN)]

    state = {"next": 0, "done": 0, "ready": set()}

    def pump():
        while state["next"] < min(len(CHUNKS), state["done"] + 2) and CHUNKS[state["next"]][0] in state["ready"]:
            for cp in chunk_copies(state["next"]):
                cp.start()
            state["next"] += 1

    def ready(k):
        state["ready"].add(k)
        pump()

    def take(i):
        assert state["done"] == i and state["next"] > i
        for cp in chunk_copies(i):
            cp.wait()

    def release(i):
        state["done"] = i + 1
        pump()

    in_copies = [pltpu.make_async_copy(a, lbuf.at[i], lsem.at[i]) for i, a in enumerate((tokens, skip))]
    cot_copy = pltpu.make_async_copy(cot, gcat[DOWN].at[pl.ds(0, T), :], misc_sem.at[0])
    result_copy = pltpu.make_async_copy(lbuf.at[0], result, misc_sem.at[1])
    out_copies = [pltpu.make_async_copy(lbuf.at[i], o, misc_sem.at[2 + i]) for i, o in enumerate((grad_tokens, grad_skip))]
    ag_begin()
    for cp in in_copies:
        cp.start()
    cot_copy.start()
    greet_all(16, 2)

    def pair(k, j):
        if j == 0:
            src, dst = turned[k].at[1 - c], theirs[k]
        elif k == DOWN:
            src, dst = cot, gcat[k].at[pl.ds(T, T), :]
        elif k == UP:
            cols = pl.ds((j - 1) * CH, CH)
            src, dst = gcat[k].at[pl.ds(0, T), cols], gcat[k].at[pl.ds(T, T), cols]
        else:
            src, dst = gcat[k].at[pl.ds(0, T), :], gcat[k].at[pl.ds(T, T), :]
        return pltpu.make_async_remote_copy(
            src_ref=src, dst_ref=dst, send_sem=pair_send.at[k, j], recv_sem=pair_recv.at[k, j],
            device_id=cpart, device_id_type=MESH)

    def pieces(k):
        return range(5) if k == UP else range(2)

    meet = [cpart, place(z, 1 - x, c, y), place(z, x, c, 1 - y),
            place(z + 1 - 2 * lax.rem(z, 2), x, c, y), place(lax.rem(z + 2, 4), x, c, y)]

    def meeting(ref, land, send, recv, t):
        return pltpu.make_async_remote_copy(
            src_ref=ref, dst_ref=land.at[t], send_sem=send.at[t], recv_sem=recv.at[t],
            device_id=meet[t], device_id_type=MESH)

    def params_step(t):
        if t == 0:
            params[...] = mine_small[...]
        else:
            cp = meeting(params, params_land, params_send, params_recv, t - 1)
            cp.wait_send()
            cp.wait_recv()
            params[...] = (params[...].astype(f32) + params_land[t - 1].astype(f32)).astype(bf16)
        if t < 5:
            meeting(params, params_land, params_send, params_recv, t).start()
        else:
            params_wide[...] = params[...].astype(f32)

    def small_step(t):
        if t:
            cp = meeting(small, small_land, small_send, small_recv, t - 1)
            cp.wait_send()
            cp.wait_recv()
            small[...] += small_land[t - 1]
        if t < 5:
            meeting(small, small_land, small_send, small_recv, t).start()
        else:
            small_out[...] = small[...]

    def make_masks():
        acc[...] = jnp.zeros_like(acc)
        small[...] = jnp.zeros_like(small)
        heads = lax.broadcasted_iota(jnp.int32, steep.shape, 0).astype(f32)
        steep[...] = jnp.exp((heads + 1.0) * -0.34657359027997264)
        seg_row = jnp.broadcast_to(seg[...].astype(f32), (T, T))
        live = jnp.broadcast_to(valid[...].astype(f32), (T, T)).T
        key_at = lax.broadcasted_iota(jnp.int32, (T, T), 0)
        query_at = lax.broadcasted_iota(jnp.int32, (T, T), 1)
        allowed = jnp.logical_and(seg_row.T == seg_row, jnp.logical_or(live == 1.0, key_at == query_at))
        distance[...] = jnp.where(allowed, jnp.abs(key_at - query_at).astype(f32), 1e33)
        pair(DOWN, 1).start()

    def turn(i):
        k, j = LEFTS[i]
        group = 2 * outs[k].shape[0]
        seg = min(group, 128)
        if k == SKIP:
            in_copies[j].wait()
        for t in range(CH // 128):
            cols = slice(t * 128, (t + 1) * 128)
            if k == SKIP:
                block = lbuf[j, :, cols].T
            elif k == DOWN:
                block = part_sums[UP][0:T, j * CH + t * 128 : j * CH + (t + 1) * 128].T
            else:
                block = abuf[:, cols].T
            for s in range(0, 128, seg):
                row = j * CH + t * 128 + s
                core, at = (row // group) % 2, row // (2 * group) * group + row % group
                turned[k][core, at : at + seg, :] = block[s : s + seg, :]
        if i + 1 == len(LEFTS) or LEFTS[i + 1][0] != k:
            pair(k, 0).start()

    def forward_product(left, slot, finish):
        @pl.loop(0, 2)
        def _(j):
            at = pl.multiple_of(j * 512, 512)
            finish(at, nn(left(), wbuf[slot, :, pl.ds(at, 512)]))

    def back_product(left, slot, finish):
        @pl.loop(0, 2)
        def _(j):
            at = pl.multiple_of(j * 512, 512)
            finish(at, nt(left(), wbuf[slot, pl.ds(at, 512), :]))

    def store_in(ref, offset=0):
        def finish(at, value):
            ref[:, pl.ds(pl.multiple_of(at + offset, 512), 512)] = value.astype(ref.dtype)

        return finish

    def add_to(ref):
        def finish(at, value):
            ref[:, pl.ds(at, 512)] += value

        return finish

    def to_hidden(i):
        take(i)

        def first(at, value):
            hid[:, pl.ds(at, 512)] = value + params_wide[0:1, pl.ds(at, 512)]

        forward_product(lambda: lbuf[i], i % 2, add_to(hid) if i else first)
        release(i)

    def norm_forward(source, gain, i):
        @pl.loop(0, 4)
        def _(j):
            rows = pl.ds(pl.multiple_of(i * 64 + j * 16, 16), 16)
            v = source[rows, :]
            center = v - jnp.mean(v, axis=-1, keepdims=True)
            rate = lax.rsqrt(jnp.mean(center * center, axis=-1, keepdims=True) + epsilon)
            abuf[rows, :] = (
                center * rate * params_wide[gain : gain + 1, :] + params_wide[gain + 1 : gain + 2, :]).astype(bf16)

    def to_projected(i):
        take(2 + i)
        forward_product(lambda: abuf[...], i % 2, store_in(pbuf, i * CH))
        release(2 + i)

    def heads_of(p):
        at = pl.multiple_of(p * 128, 128)
        return [pbuf[:, pl.ds(pl.multiple_of(at + j * CH, 128), 128)] for j in range(3)]

    def half_masks():
        low = lax.broadcasted_iota(jnp.int32, (T, 128), 1) < 64
        return low, jnp.logical_not(low)

    def attend(i):
        masks = half_masks()

        @pl.loop(2 * i, 2 * i + 2)
        def _(p):
            q, k, v = heads_of(p)
            res = []
            for e in (0, 1):
                head = pl.ds(2 * p + e, 1)
                scores = nt(k, jnp.where(masks[e], q, jnp.zeros_like(q))) * 0.125 - distance[...] * steep[head, :]
                top = jnp.max(scores, axis=0, keepdims=True)
                raised = jnp.exp(scores - top)
                total = jnp.sum(raised, axis=0, keepdims=True)
                log_total[head, :] = top + jnp.log(total)
                res.append(tn((raised / total).astype(bf16), v))
            abuf[:, pl.ds(pl.multiple_of(p * 128, 128), 128)] = jnp.where(masks[0], res[0], res[1]).astype(bf16)

    def to_middle():
        take(5)

        def finish(at, value):
            mid[:, pl.ds(at, 512)] = hid[:, pl.ds(at, 512)] + value

        forward_product(lambda: abuf[...], 1, finish)
        release(5)

    def to_activated(i):
        take(6 + i)

        def finish(at, value):
            cols = pl.ds(pl.multiple_of(i * CH + at, 512), 512)
            u = value + params_wide[6 + i : 7 + i, pl.ds(at, 512)]
            cdf = 0.5 * (1.0 + lax.erf(u * 0.7071067811865476))
            part_sums[UP][0:T, cols] = (u * cdf).astype(bf16)
            gcat[UP][0:T, cols] = (cdf + u * jnp.exp(-0.5 * u * u) * 0.3989422804014327).astype(bf16)

        forward_product(lambda: abuf[...], i % 2, finish)
        release(6 + i)

    def through_down(i):
        take(10 + i)
        forward_product(
            lambda: part_sums[UP][0:T, i * CH : (i + 1) * CH], i % 2, add_to(gnorm) if i else store_in(gnorm))

        def finish(at, value):
            cols = pl.ds(pl.multiple_of(i * CH + at, 512), 512)
            got = (value * gcat[UP][0:T, cols].astype(f32)).astype(bf16)
            gcat[UP][0:T, cols] = got
            small[6 + i : 7 + i, pl.ds(at, 512)] = jnp.sum(got.astype(f32), axis=0, keepdims=True)

        back_product(lambda: gcat[DOWN][0:T, :], i % 2, finish)
        release(10 + i)
        pair(UP, 1 + i).start()

    def to_result():
        @pl.loop(0, T // 16)
        def _(i):
            rows = pl.ds(pl.multiple_of(i * 16, 16), 16)
            lbuf[0, rows, :] = (mid[rows, :] + (gnorm[rows, :] + params_wide[5:6, :])).astype(bf16)

        result_copy.start()

    def weight_product(k, lo, hi):
        tiles = part_sums[k].shape[1] // CH
        if lo == 0:
            if k == DOWN:
                cot_copy.wait()
                small[5:6, :] = jnp.sum(gcat[DOWN][0:T, :].astype(f32), axis=0, keepdims=True)
            for j in pieces(k):
                pair(k, j).wait_recv()

        @pl.loop(lo, hi)
        def _(i):
            rows = pl.ds(pl.multiple_of(lax.div(i, tiles) * 256, 256), 256)
            for s in (0, 512):
                cols = pl.ds(pl.multiple_of(lax.rem(i, tiles) * CH + s, 512), 512)
                both = nn(turned[k][c, rows, :], gcat[k][pl.ds(0, T), cols])
                both += nn(theirs[k][rows, :], gcat[k][pl.ds(T, T), cols])
                part_sums[k][rows, cols] = both.astype(bf16)

    def into_norm(i, base, k):
        take(base + i)
        back_product(lambda: gcat[k][0:T, i * CH : (i + 1) * CH], (base + i) % 2, add_to(gnorm) if i else store_in(gnorm))
        release(base + i)

    def norm_back(source, i, gain, base, emit):
        @pl.loop(0, 4)
        def _(j):
            rows = pl.ds(pl.multiple_of(i * 64 + j * 16, 16), 16)
            v = source[rows, :]
            center = v - jnp.mean(v, axis=-1, keepdims=True)
            rate = lax.rsqrt(jnp.mean(center * center, axis=-1, keepdims=True) + epsilon)
            xhat = center * rate
            g = gnorm[rows, :]
            gx = g * xhat
            acc[base] += gx[0:8] + gx[8:16]
            acc[base + 1] += g[0:8] + g[8:16]
            e = g * params_wide[gain : gain + 1, :]
            emit(rows, rate * (e - jnp.mean(e, axis=-1, keepdims=True) - xhat * jnp.mean(e * xhat, axis=-1, keepdims=True)))

    def second_norm(i):
        def emit(rows, value):
            total = gcat[DOWN][rows, :].astype(f32) + value
            mid[rows, :] = total
            gcat[OUT][rows, :] = total.astype(bf16)

        norm_back(mid, i, 3, 0, emit)
        if i == 3:
            pair(OUT, 1).start()

    def to_attended():
        take(18)
        back_product(lambda: gcat[OUT][0:T, :], 0, store_in(abuf))
        release(18)

    def attend_back(i):
        masks = half_masks()

        @pl.loop(2 * i, 2 * i + 2)
        def _(p):
            at = pl.multiple_of(p * 128, 128)
            q, k, v = heads_of(p)
            g = abuf[:, pl.ds(at, 128)]
            res = []
            for e in (0, 1):
                head = pl.ds(2 * p + e, 1)
                scores = nt(k, jnp.where(masks[e], q, jnp.zeros_like(q))) * 0.125 - distance[...] * steep[head, :]
                probable = jnp.exp(scores - log_total[head, :])
                gp = nt(v, jnp.where(masks[e], g, jnp.zeros_like(g)))
                gv = nn(probable.astype(bf16), g)
                inner = jnp.sum(gp * probable, axis=0, keepdims=True)
                gs = (probable * (gp - inner)).astype(bf16)
                res.append((tn(gs, k) * 0.125, nn(gs, q) * 0.125, gv))
            for j in range(3):
                gcat[QKV][0:T, pl.ds(pl.multiple_of(at + CH * j, 128), 128)] = jnp.where(
                    masks[0], res[0][j], res[1][j]).astype(bf16)

        if i == 3:
            pair(QKV, 1).start()

    def first_norm(i):
        def emit(rows, value):
            total = (mid[rows, :] + value).astype(bf16)
            gcat[SKIP][rows, :] = total
            wide = total.astype(f32)
            acc[4] += wide[0:8] + wide[8:16]

        norm_back(hid, i, 1, 2, emit)
        if i == 3:
            pair(SKIP, 1).start()
            for row, a in ((0, 4), (1, 2), (2, 3), (3, 0), (4, 1)):
                small[row : row + 1, :] = jnp.sum(acc[a], axis=0, keepdims=True)

    def to_inputs(i):
        take(22 + i)
        if i == 0:
            result_copy.wait()
        back_product(lambda: gcat[SKIP][0:T, :], i % 2, store_in(lbuf.at[i]))
        release(22 + i)
        out_copies[i].start()

    steps = {
        PR: params_step, MK: lambda i: make_masks(), TR: turn, F1: to_hidden, F2: lambda i: norm_forward(hid, 1, i),
        F3: to_projected, AF: attend, F5: lambda i: to_middle(), F6: lambda i: norm_forward(mid, 3, i),
        F7: to_activated, F8: through_down, FR: lambda i: to_result(),
        B2: lambda i: into_norm(i, 14, UP), L2: second_norm, B3: lambda i: to_attended(), A: attend_back,
        B5: lambda i: into_norm(i, 19, QKV), L1: first_norm, B6: to_inputs, R: small_step,
        W4: lambda i: weight_product(DOWN, 4 * i, 4 * i + 4), W3: lambda i: weight_product(UP, 4 * i, 4 * i + 4),
        W2: lambda i: weight_product(OUT, 0, 2), W1: lambda i: weight_product(QKV, 3 * i, 3 * i + 3),
        W0: lambda i: weight_product(SKIP, 0, 4),
    }
    for name, at in PLAN:
        if name in GATHER:
            k = GATHER.index(name)
            ag_do(k, STAGES[at])
            if STAGES[at] == ("ready",):
                ready(k)
        elif name in SCATTER:
            rs_do(SCATTER.index(name), STAGES[at])
        else:
            steps[name](at)

    for cp in out_copies:
        cp.wait()
    for k in range(n):
        for j in pieces(k):
            pair(k, j).wait_send()
    ag_finish()
    rs_finish()


def whole_layer(tokens, skip, cot, seg_ids, valid, small, shards):
    T, d = cot.shape
    n = len(shards)
    hw = [s.shape for s in shards]
    dims = [(16 * h, w) for h, w in hw]
    sem = pltpu.SemaphoreType.DMA
    V = pltpu.VMEM
    scratch = (
        [V((2, h, T), bf16) for h, _ in dims]
        + [V((h, T), bf16) for h, _ in dims]
        + [V((2 * T, w), bf16) for _, w in dims]
        + [V((h, w), bf16) for h, w in dims]
        + [V((4, h, w), bf16) for h, w in hw]
        + [V((4, h, w), bf16) for h, w in hw]
        + [V((4, h, w // 2), bf16) for h, w in hw]
        + [V((4, h, w // 2), bf16) for h, w in hw]
        + [V((5, h, w), bf16) for h, w in hw]
        + [V((5, h, w // 4), bf16) for h, w in hw]
        + [V((5, h, w // 4), bf16) for h, w in hw]
        + [V((2, CH, CH), bf16), V((2, T, CH), bf16), V((T, d), f32), V((T, d), f32), V((T, d), f32),
           V((T, 3 * d), bf16), V((T, d), bf16), V((5, 8, d), f32), V((16, d), f32), V((5, 16, d), f32),
           V((16, d), bf16), V((16, d), f32), V((5, 16, d), bf16), V((HEADS, T), f32), V((HEADS, T), f32), V((T, T), f32),
           sem((n, SLOTS)), sem((n, SLOTS)), sem((n,)), sem((n, SLOTS)), sem((n, SLOTS)), sem((n, 5)), sem((n, 5)),
           sem((2, 4)), sem((2,)), sem((4,)), sem((5,)), sem((5,)), sem((5,)), sem((5,))]
    )
    vm, anywhere = pl.BlockSpec(memory_space=V), pl.BlockSpec(memory_space=pl.ANY)
    outs = ([jax.ShapeDtypeStruct((16, d), f32)] + [jax.ShapeDtypeStruct(s, f32) for s in hw]
            + [jax.ShapeDtypeStruct((T, d), bf16)] * 3 + [jax.ShapeDtypeStruct((4, 8 * h, w), bf16) for h, w in hw])
    return pl.pallas_call(
        layer_kernel, out_shape=outs,
        in_specs=[anywhere] * 3 + [vm] * 8,
        out_specs=[vm] * 6 + [anywhere] * 8,
        scratch_shapes=scratch,
        compiler_params=pltpu.CompilerParams(collective_id=0, has_side_effects=True, vmem_limit_bytes=67043328),
        name="whole_layer",
    )(tokens, skip, cot, seg_ids, valid, small, *shards)


def product(left, right):
    return jnp.dot(left, right, preferred_element_type=jnp.float32)


def outer_product(left, right):
    return lax.dot_general(
        left, right, (((0,), (0,)), ((), ())), preferred_element_type=jnp.float32
    )


def product_back(left, right):
    return lax.dot_general(
        left, right, (((1,), (1,)), ((), ())), preferred_element_type=jnp.float32
    )


def norm_rows(values, gain, shift):
    center = values - jnp.mean(values, axis=-1, keepdims=True)
    spread = jnp.mean(center * center, axis=-1, keepdims=True)
    return center * lax.rsqrt(spread + epsilon) * gain + shift


def gelu_exact(values):
    return 0.5 * values * (1.0 + lax.erf(values * 0.7071067811865476))


def attend_mask(seg_row, valid_row, head_count):
    count_rows = seg_row.shape[0]
    places = jnp.arange(count_rows, dtype=jnp.int32)
    same_utt = seg_row[:, None] == seg_row[None, :]
    diagonal = places[:, None] == places[None, :]
    allowed = same_utt & ((valid_row[None, :] == 1) | diagonal)
    slopes = 2.0 ** (-8.0 * (jnp.arange(head_count, dtype=jnp.float32) + 1.0) / head_count)
    distance = jnp.abs(places[:, None] - places[None, :]).astype(jnp.float32)
    return (allowed, -slopes[:, None, None] * distance[None, :, :])


def split_heads(projected, head_count):
    row_count = projected.shape[0]
    feature_width = projected.shape[1] // 3
    head_size = feature_width // head_count
    queries = projected[:, :feature_width].reshape(row_count, head_count, head_size)
    keys_all = projected[:, feature_width : 2 * feature_width].reshape(
        row_count, head_count, head_size
    )
    values_all = projected[:, 2 * feature_width :].reshape(row_count, head_count, head_size)
    return (queries, keys_all, values_all)


def masked_scores(queries, keys_all, allowed, linear_bias):
    score_scale = queries.shape[2] ** (-0.5)
    raw = (
        jnp.einsum("qhd,khd->hqk", queries, keys_all, preferred_element_type=jnp.float32)
        * score_scale
        + linear_bias
    )
    return jnp.where(allowed[None, :, :], raw, -1e30)


def forward_pass(tokens, skip, weights, allowed, linear_bias, head_count):
    w_skip, b_skip, g_one, beta_one, w_qkv, w_out, g_two, beta_two, w_up, b_up, w_down, b_down = (
        weights
    )
    row_count, feature_width = tokens.shape
    joined = jnp.concatenate([tokens, skip], axis=1)
    hidden = product(joined, w_skip) + b_skip.astype(jnp.float32)
    normed = norm_rows(hidden, g_one.astype(jnp.float32), beta_one.astype(jnp.float32)).astype(
        jnp.bfloat16
    )
    projected = product(normed, w_qkv).astype(jnp.bfloat16)
    queries, keys_all, values_all = split_heads(projected, head_count)
    masked = masked_scores(queries, keys_all, allowed, linear_bias)
    row_top = jnp.max(masked, axis=-1, keepdims=True)
    exponent = jnp.exp(masked - row_top)
    row_total = jnp.sum(exponent, axis=-1, keepdims=True)
    soft_weights = (exponent / row_total).astype(jnp.bfloat16)
    log_total = row_top + jnp.log(row_total)
    weighted = jnp.einsum(
        "hqk,khd->qhd", soft_weights, values_all, preferred_element_type=jnp.float32
    )
    attended = weighted.reshape(row_count, feature_width).astype(jnp.bfloat16)
    middle = hidden + product(attended, w_out)
    normed_two = norm_rows(middle, g_two.astype(jnp.float32), beta_two.astype(jnp.float32)).astype(
        jnp.bfloat16
    )
    hidden_up = product(normed_two, w_up) + b_up.astype(jnp.float32)
    activated = gelu_exact(hidden_up).astype(jnp.bfloat16)
    result = middle + (product(activated, w_down) + b_down.astype(jnp.float32))
    stored = (
        joined,
        hidden,
        normed,
        projected,
        log_total,
        attended,
        middle,
        normed_two,
        hidden_up,
        activated,
    )
    return (stored, result)


def backward_feed(stored, weights, cotangent):
    (
        joined,
        hidden,
        normed,
        projected,
        log_total,
        attended,
        middle,
        normed_two,
        hidden_up,
        activated,
    ) = stored
    w_skip, b_skip, g_one, beta_one, w_qkv, w_out, g_two, beta_two, w_up, b_up, w_down, b_down = (
        weights
    )
    grad_result = cotangent.astype(jnp.float32)
    grad_activated = product_back(cotangent, w_down)
    grad_b_down = jnp.sum(grad_result, axis=0)
    gelu_value, gelu_pull = jax.vjp(gelu_exact, hidden_up)
    grad_up = gelu_pull(grad_activated)[0].astype(jnp.bfloat16)
    grad_b_up = jnp.sum(grad_up.astype(jnp.float32), axis=0)
    grad_normed_two = product_back(grad_up, w_up)
    norm_value, norm_pull = jax.vjp(
        norm_rows, middle, g_two.astype(jnp.float32), beta_two.astype(jnp.float32)
    )
    grad_middle_norm, grad_g_two, grad_beta_two = norm_pull(grad_normed_two)
    grad_middle = grad_result + grad_middle_norm
    feed_terms = (grad_up, grad_b_up, cotangent, grad_b_down, grad_g_two, grad_beta_two)
    return (feed_terms, grad_middle)


def backward_front(stored, weights, grad_middle, allowed, linear_bias, head_count):
    (
        joined,
        hidden,
        normed,
        projected,
        log_total,
        attended,
        middle,
        normed_two,
        hidden_up,
        activated,
    ) = stored
    w_skip, b_skip, g_one, beta_one, w_qkv, w_out, g_two, beta_two, w_up, b_up, w_down, b_down = (
        weights
    )
    row_count, feature_width = hidden.shape
    branch_grad = grad_middle.astype(jnp.bfloat16)
    grad_attended = product_back(branch_grad, w_out).astype(jnp.bfloat16)
    queries, keys_all, values_all = split_heads(projected, head_count)
    score_scale = queries.shape[2] ** (-0.5)
    masked = masked_scores(queries, keys_all, allowed, linear_bias)
    probable = jnp.exp(masked - log_total)
    soft_weights = probable.astype(jnp.bfloat16)
    grad_heads = grad_attended.reshape(row_count, head_count, feature_width // head_count)
    grad_probable = jnp.einsum(
        "qhd,khd->hqk", grad_heads, values_all, preferred_element_type=jnp.float32
    )
    grad_values = jnp.einsum(
        "hqk,qhd->khd", soft_weights, grad_heads, preferred_element_type=jnp.float32
    )
    inner_sum = jnp.sum(grad_probable * probable, axis=-1, keepdims=True)
    grad_scores = (probable * (grad_probable - inner_sum)).astype(jnp.bfloat16)
    grad_queries = (
        jnp.einsum("hqk,khd->qhd", grad_scores, keys_all, preferred_element_type=jnp.float32)
        * score_scale
    )
    grad_keys = (
        jnp.einsum("hqk,qhd->khd", grad_scores, queries, preferred_element_type=jnp.float32)
        * score_scale
    )
    grad_projected = jnp.concatenate(
        [
            grad_queries.reshape(row_count, feature_width),
            grad_keys.reshape(row_count, feature_width),
            grad_values.reshape(row_count, feature_width),
        ],
        axis=1,
    ).astype(jnp.bfloat16)
    grad_normed = product_back(grad_projected, w_qkv)
    norm_value, norm_pull = jax.vjp(
        norm_rows, hidden, g_one.astype(jnp.float32), beta_one.astype(jnp.float32)
    )
    grad_hidden_norm, grad_g_one, grad_beta_one = norm_pull(grad_normed)
    grad_hidden = (grad_middle + grad_hidden_norm).astype(jnp.bfloat16)
    grad_b_skip = jnp.sum(grad_hidden.astype(jnp.float32), axis=0)
    grad_joined = product_back(grad_hidden, w_skip)
    grad_tokens = grad_joined[:, :feature_width].astype(jnp.bfloat16)
    grad_skip = grad_joined[:, feature_width:].astype(jnp.bfloat16)
    front_terms = (grad_hidden, grad_b_skip, grad_g_one, grad_beta_one, grad_projected, branch_grad)
    return (grad_tokens, grad_skip, front_terms)


AXES = ("wide", "narrow")


def gather_plain(values):
    return [lax.all_gather(v, AXES, axis=0, tiled=True) for v in values]


def own_layer(tokens, skip, seg_ids, valid, w_skip, b_skip, g_one, beta_one, w_qkv, w_out, g_two, beta_two,
              w_up, b_up, w_down, b_down, cotangent):
    me = lax.axis_index("wide") * 2 + lax.axis_index("narrow")
    narrow = jnp.stack([b_skip, g_one, beta_one, g_two, beta_two, b_down])
    place_of = jnp.arange(1024, dtype=jnp.int32)
    narrow = jnp.where(place_of // 32 == me, jnp.tile(narrow, (1, 32)), jnp.zeros((), bf16))
    wide_at = (jnp.arange(4, dtype=jnp.int32)[:, None] * 8 + place_of[None, :] // 128)
    wide = jnp.where(wide_at == me, jnp.tile(b_up[None, :], (4, 8)), jnp.zeros((), bf16))
    small = jnp.concatenate([narrow, wide, jnp.zeros((6, 1024), bf16)])
    small, *rest = whole_layer(
        tokens, skip, cotangent, seg_ids, valid, small, (w_skip, w_qkv, w_out, w_up, w_down))
    rows = [lax.dynamic_slice(small[i], (me * 32,), (32,)) for i in range(6)]
    grad_b_up = lax.dynamic_slice(small[6:10].reshape(-1), (me * 128,), (128,))
    big, result, grad_tokens, grad_skip = rest[:5], rest[5], rest[6], rest[7]
    return (
        result, grad_tokens, grad_skip,
        big[0], rows[0], rows[1], rows[2], big[1], big[2],
        rows[3], rows[4], big[3], grad_b_up, big[4], rows[5],
    )


def plain_layer(tokens, skip, seg_ids, valid, w_skip, b_skip, g_one, beta_one, w_qkv, w_out, g_two, beta_two,
                w_up, b_up, w_down, b_down, cotangent):
    weights = gather_plain(
        (w_skip, b_skip, g_one, beta_one, w_qkv, w_out, g_two, beta_two, w_up, b_up, w_down, b_down))
    allowed, linear_bias = attend_mask(seg_ids[0], valid[0], HEADS)
    stored, result = forward_pass(tokens, skip, weights, allowed, linear_bias, HEADS)
    (joined, hidden, normed, projected, log_total, attended, middle, normed_two, hidden_up, activated) = stored
    feed_terms, grad_middle = backward_feed(stored, weights, cotangent)
    grad_tokens, grad_skip, front_terms = backward_front(
        stored, weights, grad_middle, allowed, linear_bias, HEADS)
    grad_up, grad_b_up, grad_result, grad_b_down, grad_g_two, grad_beta_two = feed_terms
    grad_hidden, grad_b_skip, grad_g_one, grad_beta_one, grad_projected, branch_grad = front_terms
    lefts = (joined, normed, attended, normed_two, activated)
    rights = (grad_hidden, grad_projected, branch_grad, grad_up, grad_result)

    def scatter(v):
        return lax.psum_scatter(v, AXES, scatter_dimension=0, tiled=True)

    big = [scatter(outer_product(a, b)) for a, b in zip(lefts, rights)]
    grad_b_skip, grad_g_one, grad_beta_one, grad_g_two, grad_beta_two, grad_b_up, grad_b_down = [
        scatter(v) for v in
        (grad_b_skip, grad_g_one, grad_beta_one, grad_g_two, grad_beta_two, grad_b_up, grad_b_down)]
    return (
        result.astype(bf16), grad_tokens, grad_skip,
        big[0], grad_b_skip, grad_g_one, grad_beta_one, big[1], big[2],
        grad_g_two, grad_beta_two, big[3], grad_b_up, big[4], grad_b_down,
    )


def solution(mesh):
    return jax.shard_map(
        own_layer if dict(mesh.shape) == {"wide": 16, "narrow": 2} else plain_layer,
        mesh=mesh,
        in_specs=(
            P(("wide", "narrow"), None),
            P(("wide", "narrow"), None),
            P(("wide", "narrow"), None),
            P(("wide", "narrow"), None),
            P(("wide", "narrow"), None),
            P(("wide", "narrow")),
            P(("wide", "narrow")),
            P(("wide", "narrow")),
            P(("wide", "narrow"), None),
            P(("wide", "narrow"), None),
            P(("wide", "narrow")),
            P(("wide", "narrow")),
            P(("wide", "narrow"), None),
            P(("wide", "narrow")),
            P(("wide", "narrow"), None),
            P(("wide", "narrow")),
            P(("wide", "narrow"), None),
        ),
        out_specs=(
            P(("wide", "narrow"), None),
            P(("wide", "narrow"), None),
            P(("wide", "narrow"), None),
            P(("wide", "narrow"), None),
            P(("wide", "narrow")),
            P(("wide", "narrow")),
            P(("wide", "narrow")),
            P(("wide", "narrow"), None),
            P(("wide", "narrow"), None),
            P(("wide", "narrow")),
            P(("wide", "narrow")),
            P(("wide", "narrow"), None),
            P(("wide", "narrow")),
            P(("wide", "narrow"), None),
            P(("wide", "narrow")),
        ),
        check_vma=False,
    )
```

```python
import jax
import jax.numpy as jnp
from jax import lax
from jax.experimental import pallas as pl
from jax.experimental.pallas import tpu as pltpu
from jax.sharding import PartitionSpec as P

f32 = jnp.float32
bf16 = jnp.bfloat16

MESH = pl.DeviceIdType.MESH
ZN = 4
SLOTS = 38
ZM, ZX, ZY, XM, XY, YM, YX, CP = 0, 6, 12, 18, 22, 26, 30, 34


def here():
    w = lax.axis_index("wide")
    y = lax.axis_index("narrow")
    c = lax.rem(w, 2)
    x = lax.rem(lax.div(w, 2), 2)
    z = lax.div(w, 4)
    return z, x, c, y


def place(z, x, c, y):
    return ((z * 2 + x) * 2 + c, y)


def greet_all(total_w, total_n):
    barrier = pltpu.get_barrier_semaphore()
    w = lax.axis_index("wide")
    y = lax.axis_index("narrow")
    me = w * total_n + y
    count = total_w * total_n

    @pl.loop(1, count)
    def _(o):
        to = lax.rem(me + o, count)
        pl.semaphore_signal(
            barrier, inc=1, device_id=(lax.div(to, total_n), lax.rem(to, total_n)), device_id_type=MESH
        )

    pl.semaphore_wait(barrier, count - 1)


SIDES = (256, 768, 256, 1024, 256)


def span(k, width, first, quarters):
    cuts = (0, SIDES[k], width // 2, width - SIDES[k], width)
    return pl.ds(cuts[first], cuts[first + quarters] - cuts[first])


def gather_events(own, full, send_sem, recv_sem, local_sem):
    n = len(own)
    z, x, c, y = here()

    def block(k, xo, co, yo):
        h = own[k].shape[0]
        return pl.ds(pl.multiple_of(((xo * 2 + co) * 2 + yo) * h, h), h)

    def part(k, zo, xo, yo, first=0, quarters=4):
        return full[k].at[zo, block(k, xo, c, yo), span(k, own[k].shape[1], first, quarters)]

    def link(k, slot, src, dst, to):
        return pltpu.make_async_remote_copy(
            src_ref=src, dst_ref=dst, send_sem=send_sem.at[k, slot], recv_sem=recv_sem.at[k, slot],
            device_id=to, device_id_type=MESH)

    xp = place(z, 1 - x, c, y)
    yp = place(z, x, c, 1 - y)
    cpart = place(z, x, 1 - c, y)

    def zto(d):
        return place(z + 1 - 2 * d, x, c, y)

    def z_has(d, s):
        return (z - s >= 0) if d == 0 else (z + s <= ZN - 1)

    def z_next(d):
        return (z < ZN - 1) if d == 0 else (z > 0)

    def zo_of(d, s):
        return z - s if d == 0 else z + s

    def z_send(k, base, d, s, xo, yo, first, quarters, src=None):
        cond = jnp.logical_and(z_has(d, s), z_next(d))
        zo = zo_of(d, s)
        dst = part(k, zo, xo, yo, first, quarters)
        cp = link(k, base + d * 3 + s, dst if src is None else src, dst, zto(d))

        @pl.when(cond)
        def _():
            cp.start()

    def z_wait(k, base, d, s, xo, yo, first, quarters):
        zo = zo_of(d, s + 1)
        dst = part(k, zo, xo, yo, first, quarters)
        link(k, base + d * 3 + s, dst, dst, zto(d)).wait_recv()

    def go(k, slot, ref, to, src=None, cond=None):
        cp = link(k, slot, ref if src is None else src, ref, to)
        cp.start()

    def wait(k, slot, ref):
        link(k, slot, ref, ref, xp).wait_recv()

    def begin():
        for k in range(n):
            pltpu.make_async_copy(own[k], part(k, z, x, y), local_sem.at[k]).start()

    def do(k, e):
        kind = e[0]
        if kind == "own":
            for d in (0, 1):
                z_send(k, ZM, d, 0, x, y, 0, 4, src=own[k])
            go(k, XM + z, part(k, z, x, y), xp, src=own[k])
            go(k, YM + z, part(k, z, x, y), yp, src=own[k])
        elif kind == "near":
            wait(k, XM + z, part(k, z, 1 - x, y))
            for d in (0, 1):
                z_send(k, ZX, d, 0, 1 - x, y, 0, 1)
            go(k, YX + z, part(k, z, 1 - x, y, 0, 2), yp)
            wait(k, YM + z, part(k, z, x, 1 - y))
            for d in (0, 1):
                z_send(k, ZY, d, 0, x, 1 - y, 3, 1)
            go(k, XY + z, part(k, z, x, 1 - y, 2, 2), xp)
        elif kind == "chain":
            s = e[1]
            for d in (0, 1):
                @pl.when(z_has(d, s + 1))
                def _():
                    z_wait(k, ZM, d, s, x, y, 0, 4)
                    zo = zo_of(d, s + 1)
                    if s < 2:
                        @pl.when(z_next(d))
                        def _():
                            ref = part(k, zo, x, y)
                            link(k, ZM + d * 3 + s + 1, ref, ref, zto(d)).start()
                    ref = part(k, zo, x, y, 1, 3)
                    link(k, XM + zo, ref, ref, xp).start()
                    ref = part(k, zo, x, y, 0, 3)
                    link(k, YM + zo, ref, ref, yp).start()
        elif kind == "side":
            s = e[1]
            for d in (0, 1):
                @pl.when(z_has(d, s + 1))
                def _():
                    zo = zo_of(d, s + 1)
                    for base, xo, yo, first in ((ZX, 1 - x, y, 0), (ZY, x, 1 - y, 3)):
                        z_wait(k, base, d, s, xo, yo, first, 1)
                        if s < 2:
                            @pl.when(z_next(d))
                            def _():
                                ref = part(k, zo, xo, yo, first, 1)
                                link(k, base + d * 3 + s + 1, ref, ref, zto(d)).start()
        elif kind == "cross":
            s = e[1]
            for d in (0, 1):
                @pl.when(z_has(d, s + 1))
                def _():
                    zo = zo_of(d, s + 1)
                    wait(k, XM + zo, part(k, zo, 1 - x, y, 1, 3))
                    ref = part(k, zo, 1 - x, y, 0, 2)
                    link(k, YX + zo, ref, ref, yp).start()
                    wait(k, YM + zo, part(k, zo, x, 1 - y, 0, 3))
                    ref = part(k, zo, x, 1 - y, 2, 2)
                    link(k, XY + zo, ref, ref, xp).start()
            if s == 0:
                pltpu.make_async_copy(own[k], part(k, z, x, y), local_sem.at[k]).wait()
                ref = full[k].at[:, block(k, x, c, y), :]
                link(k, CP, ref, ref, cpart).start()
            if s == 2:
                ref = full[k].at[:, block(k, 1 - x, c, y), :]
                link(k, CP + 1, ref, ref, cpart).start()
                ref = full[k].at[:, block(k, x, c, 1 - y), :]
                link(k, CP + 2, ref, ref, cpart).start()
        elif kind == "last":
            for zo in range(ZN):
                wait(k, XY + zo, part(k, zo, 1 - x, 1 - y, 2, 2))
                wait(k, YX + zo, part(k, zo, 1 - x, 1 - y, 0, 2))
            ref = full[k].at[:, block(k, 1 - x, c, 1 - y), :]
            link(k, CP + 3, ref, ref, cpart).start()
        elif kind == "ready":
            for j, (xo, yo) in enumerate(((x, y), (1 - x, y), (x, 1 - y), (1 - x, 1 - y))):
                ref = full[k].at[:, block(k, xo, 1 - c, yo), :]
                link(k, CP + j, ref, ref, cpart).wait_recv()

    def finish():
        for k in range(n):
            for j, (xo, yo) in enumerate(((x, y), (1 - x, y), (x, 1 - y), (1 - x, 1 - y))):
                ref = full[k].at[:, block(k, xo, c, yo), :]
                link(k, CP + j, ref, ref, cpart).wait_send()
            for d in (0, 1):
                for s in range(3):
                    @pl.when(jnp.logical_and(z_has(d, s), z_next(d)))
                    def _():
                        zo = zo_of(d, s)
                        for base, xo, yo, first, q in ((ZM, x, y, 0, 4), (ZX, 1 - x, y, 0, 1), (ZY, x, 1 - y, 3, 1)):
                            ref = part(k, zo, xo, yo, first, q)
                            link(k, base + d * 3 + s, ref, ref, zto(d)).wait_send()
            ref = part(k, z, x, y)
            link(k, XM + z, ref, ref, xp).wait_send()
            link(k, YM + z, ref, ref, yp).wait_send()
            for t in range(1, ZN):
                zo = lax.rem(z + t, ZN)
                ref = part(k, zo, x, y, 1, 3)
                link(k, XM + zo, ref, ref, xp).wait_send()
                ref = part(k, zo, x, y, 0, 3)
                link(k, YM + zo, ref, ref, yp).wait_send()
            for zo in range(ZN):
                ref = part(k, zo, 1 - x, y, 0, 2)
                link(k, YX + zo, ref, ref, yp).wait_send()
                ref = part(k, zo, x, 1 - y, 2, 2)
                link(k, XY + zo, ref, ref, xp).wait_send()

    return begin, do, finish


def scatter_events(outs, part_sums, landings, send_sem, recv_sem):
    n = len(outs)
    lxm, lym, lxy, lyx, lzm, lzx, lzy = landings
    z, x, c, y = here()
    xp = place(z, 1 - x, c, y)
    yp = place(z, x, c, 1 - y)

    def rows_of(k):
        return outs[k].shape[0]

    def width(k):
        return outs[k].shape[1]

    def mine(k, zo, xo, yo, first=0, quarters=4):
        h = rows_of(k)
        row = pl.multiple_of(((zo * 2 + xo) * 2 + yo) * h, h)
        return part_sums[k].at[pl.ds(row, h), span(k, width(k), first, quarters)]

    def link(k, slot, src, dst, to):
        return pltpu.make_async_remote_copy(
            src_ref=src, dst_ref=dst, send_sem=send_sem.at[k, slot], recv_sem=recv_sem.at[k, slot],
            device_id=to, device_id_type=MESH)

    def quarter_slice(k, first, quarters):
        return span(k, width(k), first, quarters)

    def land_x(k, zo, first, quarters):
        return lxm[k].at[zo, :, quarter_slice(k, first, quarters)]

    def land_y(k, zo, first, quarters):
        return lym[k].at[zo, :, quarter_slice(k, first, quarters)]

    def z_has(d, s):
        return (z - s >= 0) if d == 0 else (z + s <= ZN - 1)

    def z_next(d):
        return (z < ZN - 1) if d == 0 else (z > 0)

    def zo_of(d, s):
        return z - s if d == 0 else z + s

    def z_slot(d, s, zo):
        return ZN if (d == 1 and s == 0) else zo

    def toward(d):
        return place(z - 1 + 2 * d, x, c, y)

    def add_in(k, zo, xo, yo, first, quarters, others):
        ref = mine(k, zo, xo, yo, first, quarters)
        h = rows_of(k)

        @pl.loop(0, h // 16)
        def _(i):
            rows = pl.ds(pl.multiple_of(i * 16, 16), 16)
            total = ref[rows, :].astype(f32)
            for o in others:
                total = total + o[rows, :].astype(f32)
            ref[rows, :] = total.astype(bf16)

    def wait(k, slot, dst):
        link(k, slot, dst, dst, xp).wait_recv()

    def do(k, e):
        kind = e[0]
        if kind == "last":
            for zo in range(ZN):
                link(k, XY + zo, mine(k, zo, 1 - x, 1 - y, 2, 2), lxy[k].at[zo], xp).start()
                link(k, YX + zo, mine(k, zo, 1 - x, 1 - y, 0, 2), lyx[k].at[zo], yp).start()
        elif kind == "cross":
            s = e[1]
            for d in (0, 1):
                @pl.when(z_has(d, s + 1))
                def _():
                    zo = zo_of(d, s + 1)
                    wait(k, YX + zo, lyx[k].at[zo])
                    add_in(k, zo, 1 - x, y, 0, 2, [lyx[k].at[zo]])
                    link(k, XM + zo, mine(k, zo, 1 - x, y, 1, 3), land_x(k, zo, 1, 3), xp).start()
                    wait(k, XY + zo, lxy[k].at[zo])
                    add_in(k, zo, x, 1 - y, 2, 2, [lxy[k].at[zo]])
                    link(k, YM + zo, mine(k, zo, x, 1 - y, 0, 3), land_y(k, zo, 0, 3), yp).start()
        elif kind == "side":
            s = e[1]
            for d in (0, 1):
                @pl.when(z_has(d, s + 1))
                def _():
                    zo = zo_of(d, s + 1)
                    for base, landing, xo, yo, first in ((ZX, lzx, 1 - x, y, 0), (ZY, lzy, x, 1 - y, 3)):
                        if s < 2:
                            @pl.when(z_next(d))
                            def _():
                                got = landing[k].at[z_slot(d, s + 1, zo)]
                                wait(k, base + d * 3 + s + 1, got)
                                add_in(k, zo, xo, yo, first, 1, [got])
                        link(k, base + d * 3 + s, mine(k, zo, xo, yo, first, 1),
                             landing[k].at[z_slot(d, s, zo)], toward(d)).start()
        elif kind == "chain":
            s = e[1]
            for d in (0, 1):
                @pl.when(z_has(d, s + 1))
                def _():
                    zo = zo_of(d, s + 1)
                    wait(k, XM + zo, land_x(k, zo, 1, 3))
                    wait(k, YM + zo, land_y(k, zo, 0, 3))
                    add_in(k, zo, x, y, 0, 1, [land_y(k, zo, 0, 1)])
                    add_in(k, zo, x, y, 1, 2, [land_y(k, zo, 1, 2), land_x(k, zo, 1, 2)])
                    add_in(k, zo, x, y, 3, 1, [land_x(k, zo, 3, 1)])
                    if s < 2:
                        @pl.when(z_next(d))
                        def _():
                            got = lzm[k].at[z_slot(d, s + 1, zo)]
                            wait(k, ZM + d * 3 + s + 1, got)
                            add_in(k, zo, x, y, 0, 4, [got])
                    link(k, ZM + d * 3 + s, mine(k, zo, x, y), lzm[k].at[z_slot(d, s, zo)], toward(d)).start()
        elif kind == "near":
            for slot, own_slot, xo, yo, first, cross_land, side_base, side_land, side_first, to, land in (
                (YX, XM, 1 - x, y, 0, lyx, ZX, lzx, 0, xp, land_x),
                (XY, YM, x, 1 - y, 2, lxy, ZY, lzy, 3, yp, land_y),
            ):
                wait(k, slot + z, cross_land[k].at[z])
                add_in(k, z, xo, yo, first, 2, [cross_land[k].at[z]])
                for d in (0, 1):
                    @pl.when(z_next(d))
                    def _():
                        got = side_land[k].at[z_slot(d, 0, z)]
                        wait(k, side_base + d * 3, got)
                        add_in(k, z, xo, yo, side_first, 1, [got])
                link(k, own_slot + z, mine(k, z, xo, yo), land(k, z, 0, 4), to).start()
        elif kind == "own":
            wait(k, XM + z, land_x(k, z, 0, 4))
            wait(k, YM + z, land_y(k, z, 0, 4))
            h = rows_of(k)
            own = mine(k, z, x, y)
            from_x, from_y = land_x(k, z, 0, 4), land_y(k, z, 0, 4)

            @pl.loop(0, h // 16)
            def _(i):
                rows = pl.ds(pl.multiple_of(i * 16, 16), 16)
                outs[k][rows, :] = own[rows, :].astype(f32) + from_x[rows, :].astype(f32) + from_y[rows, :].astype(f32)

            for d in (0, 1):
                @pl.when(z_next(d))
                def _():
                    got = lzm[k].at[z_slot(d, 0, z)]
                    wait(k, ZM + d * 3, got)

                    @pl.loop(0, h // 16)
                    def _(i):
                        rows = pl.ds(pl.multiple_of(i * 16, 16), 16)
                        outs[k][rows, :] += got[rows, :].astype(f32)

    def finish():
        for k in range(n):
            for zo in range(ZN):
                link(k, XY + zo, mine(k, zo, 1 - x, 1 - y, 2, 2), lxy[k].at[zo], xp).wait_send()
                link(k, YX + zo, mine(k, zo, 1 - x, 1 - y, 0, 2), lyx[k].at[zo], yp).wait_send()
            for t in range(1, ZN):
                zo = lax.rem(z + t, ZN)
                link(k, XM + zo, mine(k, zo, 1 - x, y, 1, 3), land_x(k, zo, 1, 3), xp).wait_send()
                link(k, YM + zo, mine(k, zo, x, 1 - y, 0, 3), land_y(k, zo, 0, 3), yp).wait_send()
            link(k, XM + z, mine(k, z, 1 - x, y), land_x(k, z, 0, 4), xp).wait_send()
            link(k, YM + z, mine(k, z, x, 1 - y), land_y(k, z, 0, 4), yp).wait_send()
            for d in (0, 1):
                for s in range(3):
                    @pl.when(z_has(d, s + 1))
                    def _():
                        zo = zo_of(d, s + 1)
                        to = z_slot(d, s, zo)
                        link(k, ZX + d * 3 + s, mine(k, zo, 1 - x, y, 0, 1), lzx[k].at[to], toward(d)).wait_send()
                        link(k, ZY + d * 3 + s, mine(k, zo, x, 1 - y, 3, 1), lzy[k].at[to], toward(d)).wait_send()
                        link(k, ZM + d * 3 + s, mine(k, zo, x, y), lzm[k].at[to], toward(d)).wait_send()

    return do, finish


HEADS = 16


epsilon = 1e-05


def nn(a, b):
    return jnp.dot(a, b, preferred_element_type=f32)


def nt(a, b):
    return lax.dot_general(a, b, (((1,), (1,)), ((), ())), preferred_element_type=f32)


def tn(a, b):
    return lax.dot_general(a, b, (((0,), (0,)), ((), ())), preferred_element_type=f32)


CH = 1024
SKIP, QKV, OUT, UP, DOWN = range(5)
CHUNKS = (
    [(SKIP, 0), (SKIP, 1), (QKV, 0), (QKV, 1), (QKV, 2), (OUT, 0)] + [(UP, i) for i in range(4)]
    + [(DOWN, i) for i in range(4)] + [(UP, i) for i in range(4)] + [(OUT, 0)] + [(QKV, i) for i in range(3)]
    + [(SKIP, 0), (SKIP, 1)]
)
LEFTS = [(DOWN, 0), (DOWN, 1), (DOWN, 2), (DOWN, 3), (UP, 0), (OUT, 0), (QKV, 0), (SKIP, 0), (SKIP, 1)]
STAGES = [("own",), ("near",)] + [(e, s) for s in range(3) for e in ("chain", "side")] + [
    ("cross", s) for s in range(3)] + [("last",), ("ready",)]
(PR, MK, TR, F1, F2, F3, AF, F5, F6, F7, F8, FR, B2, B3, B5, B6, A, L1, L2, R, W0, W1, W2, W3, W4,
 G0, G1, G2, G3, G4, E0, E1, E2, E3, E4) = range(35)
GATHER = [G0, G1, G2, G3, G4]
SCATTER = [E0, E1, E2, E3, E4]
PLAN = [
    (G0, 0), (PR, 0), (MK, 0), (TR, 7), (PR, 1), (TR, 8), (G0, 1), (G0, 2),
    (PR, 2), (G0, 3), (G1, 0), (G0, 4), (G0, 5), (PR, 3), (G1, 1), (G1, 2),
    (G0, 6), (G0, 7), (G0, 8), (G0, 9), (PR, 4), (G1, 3), (G2, 0), (G0, 10),
    (G1, 4), (PR, 5), (G1, 5), (G0, 11), (G2, 1), (G2, 2), (G0, 12), (F1, 0),
    (G1, 6), (F1, 1), (F2, 0), (G1, 7), (G1, 8), (G1, 9), (G2, 3), (G3, 0),
    (F2, 1), (G2, 4), (F2, 2), (G1, 10), (F2, 3), (G2, 5), (TR, 6), (G2, 6),
    (G2, 7), (G2, 8), (G3, 1), (G3, 2), (G2, 9), (G1, 11), (G2, 10), (G1, 12),
    (G3, 3), (G4, 0), (F3, 0), (F3, 1), (F3, 2), (G3, 4), (AF, 0), (G3, 5),
    (AF, 1), (G2, 11), (AF, 2), (G2, 12), (AF, 3), (G4, 1), (G4, 2), (TR, 5),
    (F5, 0), (F6, 0), (G3, 6), (F6, 1), (F6, 2), (F6, 3), (TR, 4), (G3, 7),
    (G3, 8), (G3, 9), (G4, 3), (G3, 10), (G4, 4), (G4, 5), (G3, 11), (G4, 6),
    (G4, 7), (G4, 8), (G3, 12), (F7, 0), (G4, 9), (G4, 10), (TR, 0), (F7, 1),
    (TR, 1), (F7, 2), (TR, 2), (F7, 3), (G4, 11), (TR, 3), (G4, 12), (W4, 0),
    (W4, 1), (E4, 11), (F8, 0), (F8, 1), (F8, 2), (F8, 3), (FR, 0), (E4, 10),
    (E4, 9), (E4, 8), (E4, 7), (B2, 0), (B2, 1), (B2, 2), (E4, 6), (E4, 5),
    (B2, 3), (W3, 0), (W3, 1), (E3, 11), (L2, 0), (E4, 4), (L2, 1), (E4, 3),
    (L2, 2), (L2, 3), (B3, 0), (E4, 2), (A, 0), (E4, 1), (E3, 10), (E3, 9),
    (E3, 8), (E3, 7), (W2, 0), (E2, 11), (A, 1), (A, 2), (E4, 0), (E3, 6),
    (E3, 5), (A, 3), (B5, 0), (B5, 1), (B5, 2), (E3, 4), (W1, 0), (E3, 3),
    (E2, 10), (W1, 1), (E2, 9), (E2, 8), (E2, 7), (E2, 6), (E1, 11), (L1, 0),
    (E3, 2), (E2, 5), (E3, 1), (E2, 4), (L1, 1), (L1, 2), (L1, 3), (E1, 10),
    (R, 0), (E2, 3), (E1, 9), (E1, 8), (E2, 2), (E1, 7), (E2, 1), (W0, 0),
    (E0, 11), (E3, 0), (E1, 6), (E1, 5), (R, 1), (B6, 0), (E1, 4), (E1, 3),
    (E2, 0), (E0, 10), (E1, 2), (E0, 9), (E1, 1), (E0, 8), (E0, 7), (E0, 6),
    (R, 2), (B6, 1), (E0, 5), (E0, 4), (E1, 0), (E0, 3), (E0, 2), (R, 3),
    (E0, 1), (E0, 0), (R, 4), (R, 5),
]


def layer_kernel(*refs):
    n = 5
    tokens, skip, cot, seg, valid, mine_small = refs[:6]
    own = refs[6 : 6 + n]
    small_out = refs[11]
    outs = refs[12:17]
    result, grad_tokens, grad_skip = refs[17:20]
    full = refs[20:25]
    r = refs[25:]
    turned, theirs, gcat, part_sums = r[:n], r[n : 2 * n], r[2 * n : 3 * n], r[3 * n : 4 * n]
    landings = [r[(4 + i) * n : (5 + i) * n] for i in range(7)]
    (wbuf, lbuf, hid, gnorm, mid, pbuf, abuf, acc, small, small_land, params, params_wide, params_land,
     log_total, steep, distance,
     ag_send, ag_recv, ag_local, rs_send, rs_recv, pair_send, pair_recv, wsem, lsem, misc_sem,
     small_send, small_recv, params_send, params_recv) = r[11 * n :]
    z, x, c, y = here()
    cpart = place(z, x, 1 - c, y)
    T = cot.shape[0]

    ag_begin, ag_do, ag_finish = gather_events(own, full, ag_send, ag_recv, ag_local)
    rs_do, rs_finish = scatter_events(outs, part_sums, landings, rs_send, rs_recv)

    def chunk_copies(i):
        k, j = CHUNKS[i]
        slot, depth = i % 2, full[k].shape[1]
        if k in (SKIP, DOWN):
            blocks = CH // depth
            return [pltpu.make_async_copy(full[k].at[j * blocks + b], wbuf.at[slot, pl.ds(b * depth, depth), :], wsem.at[slot, b])
                    for b in range(blocks)]
        return [pltpu.make_async_copy(full[k].at[b, :, pl.ds(j * CH, CH)], wbuf.at[slot, pl.ds(b * depth, depth), :], wsem.at[slot, b])
                for b in range(ZN)]

    state = {"next": 0, "done": 0, "ready": set()}

    def pump():
        while state["next"] < min(len(CHUNKS), state["done"] + 2) and CHUNKS[state["next"]][0] in state["ready"]:
            for cp in chunk_copies(state["next"]):
                cp.start()
            state["next"] += 1

    def ready(k):
        state["ready"].add(k)
        pump()

    def take(i):
        assert state["done"] == i and state["next"] > i
        for cp in chunk_copies(i):
            cp.wait()

    def release(i):
        state["done"] = i + 1
        pump()

    in_copies = [pltpu.make_async_copy(a, lbuf.at[i], lsem.at[i]) for i, a in enumerate((tokens, skip))]
    cot_copy = pltpu.make_async_copy(cot, gcat[DOWN].at[pl.ds(0, T), :], misc_sem.at[0])
    result_copy = pltpu.make_async_copy(lbuf.at[0], result, misc_sem.at[1])
    out_copies = [pltpu.make_async_copy(lbuf.at[i], o, misc_sem.at[2 + i]) for i, o in enumerate((grad_tokens, grad_skip))]
    ag_begin()
    for cp in in_copies:
        cp.start()
    cot_copy.start()
    greet_all(16, 2)

    def pair(k, j):
        if j == 0:
            src, dst = turned[k].at[1 - c], theirs[k]
        elif k == DOWN:
            src, dst = cot, gcat[k].at[pl.ds(T, T), :]
        elif k == UP:
            cols = pl.ds((j - 1) * CH, CH)
            src, dst = gcat[k].at[pl.ds(0, T), cols], gcat[k].at[pl.ds(T, T), cols]
        else:
            src, dst = gcat[k].at[pl.ds(0, T), :], gcat[k].at[pl.ds(T, T), :]
        return pltpu.make_async_remote_copy(
            src_ref=src, dst_ref=dst, send_sem=pair_send.at[k, j], recv_sem=pair_recv.at[k, j],
            device_id=cpart, device_id_type=MESH)

    def pieces(k):
        return range(5) if k == UP else range(2)

    meet = [cpart, place(z, 1 - x, c, y), place(z, x, c, 1 - y),
            place(z + 1 - 2 * lax.rem(z, 2), x, c, y), place(lax.rem(z + 2, 4), x, c, y)]

    def meeting(ref, land, send, recv, t):
        return pltpu.make_async_remote_copy(
            src_ref=ref, dst_ref=land.at[t], send_sem=send.at[t], recv_sem=recv.at[t],
            device_id=meet[t], device_id_type=MESH)

    def params_step(t):
        if t == 0:
            params[...] = mine_small[...]
        else:
            cp = meeting(params, params_land, params_send, params_recv, t - 1)
            cp.wait_send()
            cp.wait_recv()
            params[...] = (params[...].astype(f32) + params_land[t - 1].astype(f32)).astype(bf16)
        if t < 5:
            meeting(params, params_land, params_send, params_recv, t).start()
        else:
            params_wide[...] = params[...].astype(f32)

    def small_step(t):
        if t:
            cp = meeting(small, small_land, small_send, small_recv, t - 1)
            cp.wait_send()
            cp.wait_recv()
            small[...] += small_land[t - 1]
        if t < 5:
            meeting(small, small_land, small_send, small_recv, t).start()
        else:
            small_out[...] = small[...]

    def make_masks():
        acc[...] = jnp.zeros_like(acc)
        small[...] = jnp.zeros_like(small)
        heads = lax.broadcasted_iota(jnp.int32, steep.shape, 0).astype(f32)
        steep[...] = jnp.exp((heads + 1.0) * -0.34657359027997264)
        seg_row = jnp.broadcast_to(seg[...].astype(f32), (T, T))
        live = jnp.broadcast_to(valid[...].astype(f32), (T, T)).T
        key_at = lax.broadcasted_iota(jnp.int32, (T, T), 0)
        query_at = lax.broadcasted_iota(jnp.int32, (T, T), 1)
        allowed = jnp.logical_and(seg_row.T == seg_row, jnp.logical_or(live == 1.0, key_at == query_at))
        distance[...] = jnp.where(allowed, jnp.abs(key_at - query_at).astype(f32), 1e33)
        pair(DOWN, 1).start()

    def turn(i):
        k, j = LEFTS[i]
        group = 2 * outs[k].shape[0]
        seg = min(group, 128)
        if k == SKIP:
            in_copies[j].wait()
        for t in range(CH // 128):
            cols = slice(t * 128, (t + 1) * 128)
            if k == SKIP:
                block = lbuf[j, :, cols].T
            elif k == DOWN:
                block = part_sums[UP][0:T, j * CH + t * 128 : j * CH + (t + 1) * 128].T
            else:
                block = abuf[:, cols].T
            for s in range(0, 128, seg):
                row = j * CH + t * 128 + s
                core, at = (row // group) % 2, row // (2 * group) * group + row % group
                turned[k][core, at : at + seg, :] = block[s : s + seg, :]
        if i + 1 == len(LEFTS) or LEFTS[i + 1][0] != k:
            pair(k, 0).start()

    def forward_product(left, slot, finish):
        @pl.loop(0, 2)
        def _(j):
            at = pl.multiple_of(j * 512, 512)
            finish(at, nn(left(), wbuf[slot, :, pl.ds(at, 512)]))

    def back_product(left, slot, finish):
        @pl.loop(0, 2)
        def _(j):
            at = pl.multiple_of(j * 512, 512)
            finish(at, nt(left(), wbuf[slot, pl.ds(at, 512), :]))

    def store_in(ref, offset=0):
        def finish(at, value):
            ref[:, pl.ds(pl.multiple_of(at + offset, 512), 512)] = value.astype(ref.dtype)

        return finish

    def add_to(ref):
        def finish(at, value):
            ref[:, pl.ds(at, 512)] += value

        return finish

    def to_hidden(i):
        take(i)

        def first(at, value):
            hid[:, pl.ds(at, 512)] = value + params_wide[0:1, pl.ds(at, 512)]

        forward_product(lambda: lbuf[i], i % 2, add_to(hid) if i else first)
        release(i)

    def norm_forward(source, gain, i):
        @pl.loop(0, 4)
        def _(j):
            rows = pl.ds(pl.multiple_of(i * 64 + j * 16, 16), 16)
            v = source[rows, :]
            center = v - jnp.mean(v, axis=-1, keepdims=True)
            rate = lax.rsqrt(jnp.mean(center * center, axis=-1, keepdims=True) + epsilon)
            abuf[rows, :] = (
                center * rate * params_wide[gain : gain + 1, :] + params_wide[gain + 1 : gain + 2, :]).astype(bf16)

    def to_projected(i):
        take(2 + i)
        forward_product(lambda: abuf[...], i % 2, store_in(pbuf, i * CH))
        release(2 + i)

    def heads_of(p):
        at = pl.multiple_of(p * 128, 128)
        return [pbuf[:, pl.ds(pl.multiple_of(at + j * CH, 128), 128)] for j in range(3)]

    def half_masks():
        low = lax.broadcasted_iota(jnp.int32, (T, 128), 1) < 64
        return low, jnp.logical_not(low)

    def attend(i):
        masks = half_masks()

        @pl.loop(2 * i, 2 * i + 2)
        def _(p):
            q, k, v = heads_of(p)
            res = []
            for e in (0, 1):
                head = pl.ds(2 * p + e, 1)
                scores = nt(k, jnp.where(masks[e], q, jnp.zeros_like(q))) * 0.125 - distance[...] * steep[head, :]
                top = jnp.max(scores, axis=0, keepdims=True)
                raised = jnp.exp(scores - top)
                total = jnp.sum(raised, axis=0, keepdims=True)
                log_total[head, :] = top + jnp.log(total)
                res.append(tn((raised / total).astype(bf16), v))
            abuf[:, pl.ds(pl.multiple_of(p * 128, 128), 128)] = jnp.where(masks[0], res[0], res[1]).astype(bf16)

    def to_middle():
        take(5)

        def finish(at, value):
            mid[:, pl.ds(at, 512)] = hid[:, pl.ds(at, 512)] + value

        forward_product(lambda: abuf[...], 1, finish)
        release(5)

    def to_activated(i):
        take(6 + i)

        def finish(at, value):
            cols = pl.ds(pl.multiple_of(i * CH + at, 512), 512)
            u = value + params_wide[6 + i : 7 + i, pl.ds(at, 512)]
            cdf = 0.5 * (1.0 + lax.erf(u * 0.7071067811865476))
            part_sums[UP][0:T, cols] = (u * cdf).astype(bf16)
            gcat[UP][0:T, cols] = (cdf + u * jnp.exp(-0.5 * u * u) * 0.3989422804014327).astype(bf16)

        forward_product(lambda: abuf[...], i % 2, finish)
        release(6 + i)

    def through_down(i):
        take(10 + i)
        forward_product(
            lambda: part_sums[UP][0:T, i * CH : (i + 1) * CH], i % 2, add_to(gnorm) if i else store_in(gnorm))

        def finish(at, value):
            cols = pl.ds(pl.multiple_of(i * CH + at, 512), 512)
            got = (value * gcat[UP][0:T, cols].astype(f32)).astype(bf16)
            gcat[UP][0:T, cols] = got
            small[6 + i : 7 + i, pl.ds(at, 512)] = jnp.sum(got.astype(f32), axis=0, keepdims=True)

        back_product(lambda: gcat[DOWN][0:T, :], i % 2, finish)
        release(10 + i)
        pair(UP, 1 + i).start()

    def to_result():
        @pl.loop(0, T // 16)
        def _(i):
            rows = pl.ds(pl.multiple_of(i * 16, 16), 16)
            lbuf[0, rows, :] = (mid[rows, :] + (gnorm[rows, :] + params_wide[5:6, :])).astype(bf16)

        result_copy.start()

    def weight_product(k, lo, hi):
        tiles = part_sums[k].shape[1] // CH
        if lo == 0:
            if k == DOWN:
                cot_copy.wait()
                small[5:6, :] = jnp.sum(gcat[DOWN][0:T, :].astype(f32), axis=0, keepdims=True)
            for j in pieces(k):
                pair(k, j).wait_recv()

        @pl.loop(lo, hi)
        def _(i):
            rows = pl.ds(pl.multiple_of(lax.div(i, tiles) * 256, 256), 256)
            for s in (0, 512):
                cols = pl.ds(pl.multiple_of(lax.rem(i, tiles) * CH + s, 512), 512)
                both = nn(turned[k][c, rows, :], gcat[k][pl.ds(0, T), cols])
                both += nn(theirs[k][rows, :], gcat[k][pl.ds(T, T), cols])
                part_sums[k][rows, cols] = both.astype(bf16)

    def into_norm(i, base, k):
        take(base + i)
        back_product(lambda: gcat[k][0:T, i * CH : (i + 1) * CH], (base + i) % 2, add_to(gnorm) if i else store_in(gnorm))
        release(base + i)

    def norm_back(source, i, gain, base, emit):
        @pl.loop(0, 4)
        def _(j):
            rows = pl.ds(pl.multiple_of(i * 64 + j * 16, 16), 16)
            v = source[rows, :]
            center = v - jnp.mean(v, axis=-1, keepdims=True)
            rate = lax.rsqrt(jnp.mean(center * center, axis=-1, keepdims=True) + epsilon)
            xhat = center * rate
            g = gnorm[rows, :]
            gx = g * xhat
            acc[base] += gx[0:8] + gx[8:16]
            acc[base + 1] += g[0:8] + g[8:16]
            e = g * params_wide[gain : gain + 1, :]
            emit(rows, rate * (e - jnp.mean(e, axis=-1, keepdims=True) - xhat * jnp.mean(e * xhat, axis=-1, keepdims=True)))

    def second_norm(i):
        def emit(rows, value):
            total = gcat[DOWN][rows, :].astype(f32) + value
            mid[rows, :] = total
            gcat[OUT][rows, :] = total.astype(bf16)

        norm_back(mid, i, 3, 0, emit)
        if i == 3:
            pair(OUT, 1).start()

    def to_attended():
        take(18)
        back_product(lambda: gcat[OUT][0:T, :], 0, store_in(abuf))
        release(18)

    def attend_back(i):
        masks = half_masks()

        @pl.loop(2 * i, 2 * i + 2)
        def _(p):
            at = pl.multiple_of(p * 128, 128)
            q, k, v = heads_of(p)
            g = abuf[:, pl.ds(at, 128)]
            res = []
            for e in (0, 1):
                head = pl.ds(2 * p + e, 1)
                scores = nt(k, jnp.where(masks[e], q, jnp.zeros_like(q))) * 0.125 - distance[...] * steep[head, :]
                probable = jnp.exp(scores - log_total[head, :])
                gp = nt(v, jnp.where(masks[e], g, jnp.zeros_like(g)))
                gv = nn(probable.astype(bf16), g)
                inner = jnp.sum(gp * probable, axis=0, keepdims=True)
                gs = (probable * (gp - inner)).astype(bf16)
                res.append((tn(gs, k) * 0.125, nn(gs, q) * 0.125, gv))
            for j in range(3):
                gcat[QKV][0:T, pl.ds(pl.multiple_of(at + CH * j, 128), 128)] = jnp.where(
                    masks[0], res[0][j], res[1][j]).astype(bf16)

        if i == 3:
            pair(QKV, 1).start()

    def first_norm(i):
        def emit(rows, value):
            total = (mid[rows, :] + value).astype(bf16)
            gcat[SKIP][rows, :] = total
            wide = total.astype(f32)
            acc[4] += wide[0:8] + wide[8:16]

        norm_back(hid, i, 1, 2, emit)
        if i == 3:
            pair(SKIP, 1).start()
            for row, a in ((0, 4), (1, 2), (2, 3), (3, 0), (4, 1)):
                small[row : row + 1, :] = jnp.sum(acc[a], axis=0, keepdims=True)

    def to_inputs(i):
        take(22 + i)
        if i == 0:
            result_copy.wait()
        back_product(lambda: gcat[SKIP][0:T, :], i % 2, store_in(lbuf.at[i]))
        release(22 + i)
        out_copies[i].start()

    steps = {
        PR: params_step, MK: lambda i: make_masks(), TR: turn, F1: to_hidden, F2: lambda i: norm_forward(hid, 1, i),
        F3: to_projected, AF: attend, F5: lambda i: to_middle(), F6: lambda i: norm_forward(mid, 3, i),
        F7: to_activated, F8: through_down, FR: lambda i: to_result(),
        B2: lambda i: into_norm(i, 14, UP), L2: second_norm, B3: lambda i: to_attended(), A: attend_back,
        B5: lambda i: into_norm(i, 19, QKV), L1: first_norm, B6: to_inputs, R: small_step,
        W4: lambda i: weight_product(DOWN, 4 * i, 4 * i + 4), W3: lambda i: weight_product(UP, 4 * i, 4 * i + 4),
        W2: lambda i: weight_product(OUT, 0, 2), W1: lambda i: weight_product(QKV, 3 * i, 3 * i + 3),
        W0: lambda i: weight_product(SKIP, 0, 4),
    }
    for name, at in PLAN:
        if name in GATHER:
            k = GATHER.index(name)
            ag_do(k, STAGES[at])
            if STAGES[at] == ("ready",):
                ready(k)
        elif name in SCATTER:
            rs_do(SCATTER.index(name), STAGES[at])
        else:
            steps[name](at)

    for cp in out_copies:
        cp.wait()
    for k in range(n):
        for j in pieces(k):
            pair(k, j).wait_send()
    ag_finish()
    rs_finish()


def whole_layer(tokens, skip, cot, seg_ids, valid, small, shards):
    T, d = cot.shape
    n = len(shards)
    hw = [s.shape for s in shards]
    dims = [(16 * h, w) for h, w in hw]
    sem = pltpu.SemaphoreType.DMA
    V = pltpu.VMEM
    scratch = (
        [V((2, h, T), bf16) for h, _ in dims]
        + [V((h, T), bf16) for h, _ in dims]
        + [V((2 * T, w), bf16) for _, w in dims]
        + [V((h, w), bf16) for h, w in dims]
        + [V((4, h, w), bf16) for h, w in hw]
        + [V((4, h, w), bf16) for h, w in hw]
        + [V((4, h, w // 2), bf16) for h, w in hw]
        + [V((4, h, w // 2), bf16) for h, w in hw]
        + [V((5, h, w), bf16) for h, w in hw]
        + [V((5, h, a), bf16) for (h, _), a in zip(hw, SIDES)]
        + [V((5, h, a), bf16) for (h, _), a in zip(hw, SIDES)]
        + [V((2, CH, CH), bf16), V((2, T, CH), bf16), V((T, d), f32), V((T, d), f32), V((T, d), f32),
           V((T, 3 * d), bf16), V((T, d), bf16), V((5, 8, d), f32), V((16, d), f32), V((5, 16, d), f32),
           V((16, d), bf16), V((16, d), f32), V((5, 16, d), bf16), V((HEADS, T), f32), V((HEADS, T), f32), V((T, T), f32),
           sem((n, SLOTS)), sem((n, SLOTS)), sem((n,)), sem((n, SLOTS)), sem((n, SLOTS)), sem((n, 5)), sem((n, 5)),
           sem((2, 4)), sem((2,)), sem((4,)), sem((5,)), sem((5,)), sem((5,)), sem((5,))]
    )
    vm, anywhere = pl.BlockSpec(memory_space=V), pl.BlockSpec(memory_space=pl.ANY)
    outs = ([jax.ShapeDtypeStruct((16, d), f32)] + [jax.ShapeDtypeStruct(s, f32) for s in hw]
            + [jax.ShapeDtypeStruct((T, d), bf16)] * 3 + [jax.ShapeDtypeStruct((4, 8 * h, w), bf16) for h, w in hw])
    return pl.pallas_call(
        layer_kernel, out_shape=outs,
        in_specs=[anywhere] * 3 + [vm] * 8,
        out_specs=[vm] * 6 + [anywhere] * 8,
        scratch_shapes=scratch,
        compiler_params=pltpu.CompilerParams(collective_id=0, has_side_effects=True, vmem_limit_bytes=67043328),
        name="whole_layer",
    )(tokens, skip, cot, seg_ids, valid, small, *shards)


def product(left, right):
    return jnp.dot(left, right, preferred_element_type=jnp.float32)


def outer_product(left, right):
    return lax.dot_general(
        left, right, (((0,), (0,)), ((), ())), preferred_element_type=jnp.float32
    )


def product_back(left, right):
    return lax.dot_general(
        left, right, (((1,), (1,)), ((), ())), preferred_element_type=jnp.float32
    )


def norm_rows(values, gain, shift):
    center = values - jnp.mean(values, axis=-1, keepdims=True)
    spread = jnp.mean(center * center, axis=-1, keepdims=True)
    return center * lax.rsqrt(spread + epsilon) * gain + shift


def gelu_exact(values):
    return 0.5 * values * (1.0 + lax.erf(values * 0.7071067811865476))


def attend_mask(seg_row, valid_row, head_count):
    count_rows = seg_row.shape[0]
    places = jnp.arange(count_rows, dtype=jnp.int32)
    same_utt = seg_row[:, None] == seg_row[None, :]
    diagonal = places[:, None] == places[None, :]
    allowed = same_utt & ((valid_row[None, :] == 1) | diagonal)
    slopes = 2.0 ** (-8.0 * (jnp.arange(head_count, dtype=jnp.float32) + 1.0) / head_count)
    distance = jnp.abs(places[:, None] - places[None, :]).astype(jnp.float32)
    return (allowed, -slopes[:, None, None] * distance[None, :, :])


def split_heads(projected, head_count):
    row_count = projected.shape[0]
    feature_width = projected.shape[1] // 3
    head_size = feature_width // head_count
    queries = projected[:, :feature_width].reshape(row_count, head_count, head_size)
    keys_all = projected[:, feature_width : 2 * feature_width].reshape(
        row_count, head_count, head_size
    )
    values_all = projected[:, 2 * feature_width :].reshape(row_count, head_count, head_size)
    return (queries, keys_all, values_all)


def masked_scores(queries, keys_all, allowed, linear_bias):
    score_scale = queries.shape[2] ** (-0.5)
    raw = (
        jnp.einsum("qhd,khd->hqk", queries, keys_all, preferred_element_type=jnp.float32)
        * score_scale
        + linear_bias
    )
    return jnp.where(allowed[None, :, :], raw, -1e30)


def forward_pass(tokens, skip, weights, allowed, linear_bias, head_count):
    w_skip, b_skip, g_one, beta_one, w_qkv, w_out, g_two, beta_two, w_up, b_up, w_down, b_down = (
        weights
    )
    row_count, feature_width = tokens.shape
    joined = jnp.concatenate([tokens, skip], axis=1)
    hidden = product(joined, w_skip) + b_skip.astype(jnp.float32)
    normed = norm_rows(hidden, g_one.astype(jnp.float32), beta_one.astype(jnp.float32)).astype(
        jnp.bfloat16
    )
    projected = product(normed, w_qkv).astype(jnp.bfloat16)
    queries, keys_all, values_all = split_heads(projected, head_count)
    masked = masked_scores(queries, keys_all, allowed, linear_bias)
    row_top = jnp.max(masked, axis=-1, keepdims=True)
    exponent = jnp.exp(masked - row_top)
    row_total = jnp.sum(exponent, axis=-1, keepdims=True)
    soft_weights = (exponent / row_total).astype(jnp.bfloat16)
    log_total = row_top + jnp.log(row_total)
    weighted = jnp.einsum(
        "hqk,khd->qhd", soft_weights, values_all, preferred_element_type=jnp.float32
    )
    attended = weighted.reshape(row_count, feature_width).astype(jnp.bfloat16)
    middle = hidden + product(attended, w_out)
    normed_two = norm_rows(middle, g_two.astype(jnp.float32), beta_two.astype(jnp.float32)).astype(
        jnp.bfloat16
    )
    hidden_up = product(normed_two, w_up) + b_up.astype(jnp.float32)
    activated = gelu_exact(hidden_up).astype(jnp.bfloat16)
    result = middle + (product(activated, w_down) + b_down.astype(jnp.float32))
    stored = (
        joined,
        hidden,
        normed,
        projected,
        log_total,
        attended,
        middle,
        normed_two,
        hidden_up,
        activated,
    )
    return (stored, result)


def backward_feed(stored, weights, cotangent):
    (
        joined,
        hidden,
        normed,
        projected,
        log_total,
        attended,
        middle,
        normed_two,
        hidden_up,
        activated,
    ) = stored
    w_skip, b_skip, g_one, beta_one, w_qkv, w_out, g_two, beta_two, w_up, b_up, w_down, b_down = (
        weights
    )
    grad_result = cotangent.astype(jnp.float32)
    grad_activated = product_back(cotangent, w_down)
    grad_b_down = jnp.sum(grad_result, axis=0)
    gelu_value, gelu_pull = jax.vjp(gelu_exact, hidden_up)
    grad_up = gelu_pull(grad_activated)[0].astype(jnp.bfloat16)
    grad_b_up = jnp.sum(grad_up.astype(jnp.float32), axis=0)
    grad_normed_two = product_back(grad_up, w_up)
    norm_value, norm_pull = jax.vjp(
        norm_rows, middle, g_two.astype(jnp.float32), beta_two.astype(jnp.float32)
    )
    grad_middle_norm, grad_g_two, grad_beta_two = norm_pull(grad_normed_two)
    grad_middle = grad_result + grad_middle_norm
    feed_terms = (grad_up, grad_b_up, cotangent, grad_b_down, grad_g_two, grad_beta_two)
    return (feed_terms, grad_middle)


def backward_front(stored, weights, grad_middle, allowed, linear_bias, head_count):
    (
        joined,
        hidden,
        normed,
        projected,
        log_total,
        attended,
        middle,
        normed_two,
        hidden_up,
        activated,
    ) = stored
    w_skip, b_skip, g_one, beta_one, w_qkv, w_out, g_two, beta_two, w_up, b_up, w_down, b_down = (
        weights
    )
    row_count, feature_width = hidden.shape
    branch_grad = grad_middle.astype(jnp.bfloat16)
    grad_attended = product_back(branch_grad, w_out).astype(jnp.bfloat16)
    queries, keys_all, values_all = split_heads(projected, head_count)
    score_scale = queries.shape[2] ** (-0.5)
    masked = masked_scores(queries, keys_all, allowed, linear_bias)
    probable = jnp.exp(masked - log_total)
    soft_weights = probable.astype(jnp.bfloat16)
    grad_heads = grad_attended.reshape(row_count, head_count, feature_width // head_count)
    grad_probable = jnp.einsum(
        "qhd,khd->hqk", grad_heads, values_all, preferred_element_type=jnp.float32
    )
    grad_values = jnp.einsum(
        "hqk,qhd->khd", soft_weights, grad_heads, preferred_element_type=jnp.float32
    )
    inner_sum = jnp.sum(grad_probable * probable, axis=-1, keepdims=True)
    grad_scores = (probable * (grad_probable - inner_sum)).astype(jnp.bfloat16)
    grad_queries = (
        jnp.einsum("hqk,khd->qhd", grad_scores, keys_all, preferred_element_type=jnp.float32)
        * score_scale
    )
    grad_keys = (
        jnp.einsum("hqk,qhd->khd", grad_scores, queries, preferred_element_type=jnp.float32)
        * score_scale
    )
    grad_projected = jnp.concatenate(
        [
            grad_queries.reshape(row_count, feature_width),
            grad_keys.reshape(row_count, feature_width),
            grad_values.reshape(row_count, feature_width),
        ],
        axis=1,
    ).astype(jnp.bfloat16)
    grad_normed = product_back(grad_projected, w_qkv)
    norm_value, norm_pull = jax.vjp(
        norm_rows, hidden, g_one.astype(jnp.float32), beta_one.astype(jnp.float32)
    )
    grad_hidden_norm, grad_g_one, grad_beta_one = norm_pull(grad_normed)
    grad_hidden = (grad_middle + grad_hidden_norm).astype(jnp.bfloat16)
    grad_b_skip = jnp.sum(grad_hidden.astype(jnp.float32), axis=0)
    grad_joined = product_back(grad_hidden, w_skip)
    grad_tokens = grad_joined[:, :feature_width].astype(jnp.bfloat16)
    grad_skip = grad_joined[:, feature_width:].astype(jnp.bfloat16)
    front_terms = (grad_hidden, grad_b_skip, grad_g_one, grad_beta_one, grad_projected, branch_grad)
    return (grad_tokens, grad_skip, front_terms)


AXES = ("wide", "narrow")


def gather_plain(values):
    return [lax.all_gather(v, AXES, axis=0, tiled=True) for v in values]


def hand_over_kernel(*refs):
    small = refs[0]
    sources = refs[1:9]
    vectors = refs[9:16]
    targets = refs[16:24]
    buffers = refs[24:32]
    in_sem, out_sem = refs[32:]
    me = lax.axis_index("wide") * 2 + lax.axis_index("narrow")
    arrive = [pltpu.make_async_copy(s, b, in_sem.at[i]) for i, (s, b) in enumerate(zip(sources, buffers))]
    leave = [pltpu.make_async_copy(b, t, out_sem.at[i]) for i, (b, t) in enumerate(zip(buffers, targets))]
    for cp in arrive:
        cp.start()
    rolled = pltpu.roll(small[...], lax.rem(32 - me, 32) * 32, 1)
    for i in range(6):
        vectors[i][...] = rolled[i, 0:32]
    row = 6 + lax.div(me, 8)
    wide = pltpu.roll(jnp.where(lax.broadcasted_iota(jnp.int32, small.shape, 0) == row, small[...], 0.0),
                      lax.rem(8 - lax.rem(me, 8), 8) * 128, 1)
    vectors[6][...] = jnp.sum(wide[:, 0:128], axis=0)
    for a, l in zip(arrive, leave):
        a.wait()
        l.start()
    for l in leave:
        l.wait()


def hand_over(small, arrays):
    vm, anywhere = pl.BlockSpec(memory_space=pltpu.VMEM), pl.BlockSpec(memory_space=pl.ANY)
    sem = pltpu.SemaphoreType.DMA
    n = len(arrays)
    outs = [jax.ShapeDtypeStruct((32,), f32)] * 6 + [jax.ShapeDtypeStruct((128,), f32)] + [
        jax.ShapeDtypeStruct(a.shape, a.dtype) for a in arrays]
    return pl.pallas_call(
        hand_over_kernel, out_shape=outs,
        in_specs=[vm] + [anywhere] * n, out_specs=[vm] * 7 + [anywhere] * n,
        scratch_shapes=[pltpu.VMEM(a.shape, a.dtype) for a in arrays] + [sem((n,)), sem((n,))],
        name="hand_over",
    )(small, *arrays)


def own_layer(tokens, skip, seg_ids, valid, w_skip, b_skip, g_one, beta_one, w_qkv, w_out, g_two, beta_two,
              w_up, b_up, w_down, b_down, cotangent):
    me = lax.axis_index("wide") * 2 + lax.axis_index("narrow")
    narrow = jnp.stack([b_skip, g_one, beta_one, g_two, beta_two, b_down])
    place_of = jnp.arange(1024, dtype=jnp.int32)
    narrow = jnp.where(place_of // 32 == me, jnp.tile(narrow, (1, 32)), jnp.zeros((), bf16))
    wide_at = (jnp.arange(4, dtype=jnp.int32)[:, None] * 8 + place_of[None, :] // 128)
    wide = jnp.where(wide_at == me, jnp.tile(b_up[None, :], (4, 8)), jnp.zeros((), bf16))
    small = jnp.concatenate([narrow, wide, jnp.zeros((6, 1024), bf16)])
    small, *rest = whole_layer(
        tokens, skip, cotangent, seg_ids, valid, small, (w_skip, w_qkv, w_out, w_up, w_down))
    (grad_b_skip, grad_g_one, grad_beta_one, grad_g_two, grad_beta_two, grad_b_down, grad_b_up,
     grad_w_skip, grad_w_qkv, grad_w_out, grad_w_up, grad_w_down, result, grad_tokens, grad_skip) = hand_over(small, rest[:8])
    return (
        result, grad_tokens, grad_skip,
        grad_w_skip, grad_b_skip, grad_g_one, grad_beta_one, grad_w_qkv, grad_w_out,
        grad_g_two, grad_beta_two, grad_w_up, grad_b_up, grad_w_down, grad_b_down,
    )


def plain_layer(tokens, skip, seg_ids, valid, w_skip, b_skip, g_one, beta_one, w_qkv, w_out, g_two, beta_two,
                w_up, b_up, w_down, b_down, cotangent):
    weights = gather_plain(
        (w_skip, b_skip, g_one, beta_one, w_qkv, w_out, g_two, beta_two, w_up, b_up, w_down, b_down))
    allowed, linear_bias = attend_mask(seg_ids[0], valid[0], HEADS)
    stored, result = forward_pass(tokens, skip, weights, allowed, linear_bias, HEADS)
    (joined, hidden, normed, projected, log_total, attended, middle, normed_two, hidden_up, activated) = stored
    feed_terms, grad_middle = backward_feed(stored, weights, cotangent)
    grad_tokens, grad_skip, front_terms = backward_front(
        stored, weights, grad_middle, allowed, linear_bias, HEADS)
    grad_up, grad_b_up, grad_result, grad_b_down, grad_g_two, grad_beta_two = feed_terms
    grad_hidden, grad_b_skip, grad_g_one, grad_beta_one, grad_projected, branch_grad = front_terms
    lefts = (joined, normed, attended, normed_two, activated)
    rights = (grad_hidden, grad_projected, branch_grad, grad_up, grad_result)

    def scatter(v):
        return lax.psum_scatter(v, AXES, scatter_dimension=0, tiled=True)

    big = [scatter(outer_product(a, b)) for a, b in zip(lefts, rights)]
    grad_b_skip, grad_g_one, grad_beta_one, grad_g_two, grad_beta_two, grad_b_up, grad_b_down = [
        scatter(v) for v in
        (grad_b_skip, grad_g_one, grad_beta_one, grad_g_two, grad_beta_two, grad_b_up, grad_b_down)]
    return (
        result.astype(bf16), grad_tokens, grad_skip,
        big[0], grad_b_skip, grad_g_one, grad_beta_one, big[1], big[2],
        grad_g_two, grad_beta_two, big[3], grad_b_up, big[4], grad_b_down,
    )


def solution(mesh):
    return jax.shard_map(
        own_layer if dict(mesh.shape) == {"wide": 16, "narrow": 2} else plain_layer,
        mesh=mesh,
        in_specs=(
            P(("wide", "narrow"), None),
            P(("wide", "narrow"), None),
            P(("wide", "narrow"), None),
            P(("wide", "narrow"), None),
            P(("wide", "narrow"), None),
            P(("wide", "narrow")),
            P(("wide", "narrow")),
            P(("wide", "narrow")),
            P(("wide", "narrow"), None),
            P(("wide", "narrow"), None),
            P(("wide", "narrow")),
            P(("wide", "narrow")),
            P(("wide", "narrow"), None),
            P(("wide", "narrow")),
            P(("wide", "narrow"), None),
            P(("wide", "narrow")),
            P(("wide", "narrow"), None),
        ),
        out_specs=(
            P(("wide", "narrow"), None),
            P(("wide", "narrow"), None),
            P(("wide", "narrow"), None),
            P(("wide", "narrow"), None),
            P(("wide", "narrow")),
            P(("wide", "narrow")),
            P(("wide", "narrow")),
            P(("wide", "narrow"), None),
            P(("wide", "narrow"), None),
            P(("wide", "narrow")),
            P(("wide", "narrow")),
            P(("wide", "narrow"), None),
            P(("wide", "narrow")),
            P(("wide", "narrow"), None),
            P(("wide", "narrow")),
        ),
        check_vma=False,
    )
```

```python
import jax
import jax.numpy as jnp
from jax import lax
from jax.experimental import pallas as pl
from jax.experimental.pallas import tpu as pltpu
from jax.sharding import PartitionSpec as P

f32 = jnp.float32
bf16 = jnp.bfloat16

MESH = pl.DeviceIdType.MESH
ZN = 4
SLOTS = 38
ZM, ZX, ZY, XM, XY, YM, YX, CP = 0, 6, 12, 18, 22, 26, 30, 34


def here():
    w = lax.axis_index("wide")
    y = lax.axis_index("narrow")
    c = lax.rem(w, 2)
    x = lax.rem(lax.div(w, 2), 2)
    z = lax.div(w, 4)
    return z, x, c, y


def place(z, x, c, y):
    return ((z * 2 + x) * 2 + c, y)


def greet_all(total_w, total_n):
    barrier = pltpu.get_barrier_semaphore()
    w = lax.axis_index("wide")
    y = lax.axis_index("narrow")
    me = w * total_n + y
    count = total_w * total_n

    @pl.loop(1, count)
    def _(o):
        to = lax.rem(me + o, count)
        pl.semaphore_signal(
            barrier, inc=1, device_id=(lax.div(to, total_n), lax.rem(to, total_n)), device_id_type=MESH
        )

    pl.semaphore_wait(barrier, count - 1)


def span(width, first, quarters):
    return pl.ds(first * width // 4, quarters * width // 4)


def gather_events(own, full, send_sem, recv_sem, local_sem):
    n = len(own)
    z, x, c, y = here()

    def block(k, xo, co, yo):
        h = own[k].shape[0]
        return pl.ds(pl.multiple_of(((xo * 2 + co) * 2 + yo) * h, h), h)

    def part(k, zo, xo, yo, first=0, quarters=4):
        return full[k].at[zo, block(k, xo, c, yo), span(own[k].shape[1], first, quarters)]

    def link(k, slot, src, dst, to):
        return pltpu.make_async_remote_copy(
            src_ref=src, dst_ref=dst, send_sem=send_sem.at[k, slot], recv_sem=recv_sem.at[k, slot],
            device_id=to, device_id_type=MESH)

    xp = place(z, 1 - x, c, y)
    yp = place(z, x, c, 1 - y)
    cpart = place(z, x, 1 - c, y)

    def zto(d):
        return place(z + 1 - 2 * d, x, c, y)

    def z_has(d, s):
        return (z - s >= 0) if d == 0 else (z + s <= ZN - 1)

    def z_next(d):
        return (z < ZN - 1) if d == 0 else (z > 0)

    def zo_of(d, s):
        return z - s if d == 0 else z + s

    def z_send(k, base, d, s, xo, yo, first, quarters, src=None):
        cond = jnp.logical_and(z_has(d, s), z_next(d))
        zo = zo_of(d, s)
        dst = part(k, zo, xo, yo, first, quarters)
        cp = link(k, base + d * 3 + s, dst if src is None else src, dst, zto(d))

        @pl.when(cond)
        def _():
            cp.start()

    def z_wait(k, base, d, s, xo, yo, first, quarters):
        zo = zo_of(d, s + 1)
        dst = part(k, zo, xo, yo, first, quarters)
        link(k, base + d * 3 + s, dst, dst, zto(d)).wait_recv()

    def go(k, slot, ref, to, src=None, cond=None):
        cp = link(k, slot, ref if src is None else src, ref, to)
        cp.start()

    def wait(k, slot, ref):
        link(k, slot, ref, ref, xp).wait_recv()

    def begin():
        for k in range(n):
            pltpu.make_async_copy(own[k], part(k, z, x, y), local_sem.at[k]).start()

    def do(k, e):
        kind = e[0]
        if kind == "own":
            for d in (0, 1):
                z_send(k, ZM, d, 0, x, y, 0, 4, src=own[k])
            go(k, XM + z, part(k, z, x, y), xp, src=own[k])
            go(k, YM + z, part(k, z, x, y), yp, src=own[k])
        elif kind == "near":
            wait(k, XM + z, part(k, z, 1 - x, y))
            for d in (0, 1):
                z_send(k, ZX, d, 0, 1 - x, y, 0, 1)
            go(k, YX + z, part(k, z, 1 - x, y, 0, 2), yp)
            wait(k, YM + z, part(k, z, x, 1 - y))
            for d in (0, 1):
                z_send(k, ZY, d, 0, x, 1 - y, 3, 1)
            go(k, XY + z, part(k, z, x, 1 - y, 2, 2), xp)
        elif kind == "chain":
            s = e[1]
            for d in (0, 1):
                @pl.when(z_has(d, s + 1))
                def _():
                    z_wait(k, ZM, d, s, x, y, 0, 4)
                    zo = zo_of(d, s + 1)
                    if s < 2:
                        @pl.when(z_next(d))
                        def _():
                            ref = part(k, zo, x, y)
                            link(k, ZM + d * 3 + s + 1, ref, ref, zto(d)).start()
                    ref = part(k, zo, x, y, 1, 3)
                    link(k, XM + zo, ref, ref, xp).start()
                    ref = part(k, zo, x, y, 0, 3)
                    link(k, YM + zo, ref, ref, yp).start()
        elif kind == "side":
            s = e[1]
            for d in (0, 1):
                @pl.when(z_has(d, s + 1))
                def _():
                    zo = zo_of(d, s + 1)
                    for base, xo, yo, first in ((ZX, 1 - x, y, 0), (ZY, x, 1 - y, 3)):
                        z_wait(k, base, d, s, xo, yo, first, 1)
                        if s < 2:
                            @pl.when(z_next(d))
                            def _():
                                ref = part(k, zo, xo, yo, first, 1)
                                link(k, base + d * 3 + s + 1, ref, ref, zto(d)).start()
        elif kind == "cross":
            s = e[1]
            for d in (0, 1):
                @pl.when(z_has(d, s + 1))
                def _():
                    zo = zo_of(d, s + 1)
                    wait(k, XM + zo, part(k, zo, 1 - x, y, 1, 3))
                    ref = part(k, zo, 1 - x, y, 0, 2)
                    link(k, YX + zo, ref, ref, yp).start()
                    wait(k, YM + zo, part(k, zo, x, 1 - y, 0, 3))
                    ref = part(k, zo, x, 1 - y, 2, 2)
                    link(k, XY + zo, ref, ref, xp).start()
            if s == 0:
                pltpu.make_async_copy(own[k], part(k, z, x, y), local_sem.at[k]).wait()
                ref = full[k].at[:, block(k, x, c, y), :]
                link(k, CP, ref, ref, cpart).start()
            if s == 2:
                ref = full[k].at[:, block(k, 1 - x, c, y), :]
                link(k, CP + 1, ref, ref, cpart).start()
                ref = full[k].at[:, block(k, x, c, 1 - y), :]
                link(k, CP + 2, ref, ref, cpart).start()
        elif kind == "last":
            for zo in range(ZN):
                wait(k, XY + zo, part(k, zo, 1 - x, 1 - y, 2, 2))
                wait(k, YX + zo, part(k, zo, 1 - x, 1 - y, 0, 2))
            ref = full[k].at[:, block(k, 1 - x, c, 1 - y), :]
            link(k, CP + 3, ref, ref, cpart).start()
        elif kind == "ready":
            for j, (xo, yo) in enumerate(((x, y), (1 - x, y), (x, 1 - y), (1 - x, 1 - y))):
                ref = full[k].at[:, block(k, xo, 1 - c, yo), :]
                link(k, CP + j, ref, ref, cpart).wait_recv()

    def finish():
        for k in range(n):
            for j, (xo, yo) in enumerate(((x, y), (1 - x, y), (x, 1 - y), (1 - x, 1 - y))):
                ref = full[k].at[:, block(k, xo, c, yo), :]
                link(k, CP + j, ref, ref, cpart).wait_send()
            for d in (0, 1):
                for s in range(3):
                    @pl.when(jnp.logical_and(z_has(d, s), z_next(d)))
                    def _():
                        zo = zo_of(d, s)
                        for base, xo, yo, first, q in ((ZM, x, y, 0, 4), (ZX, 1 - x, y, 0, 1), (ZY, x, 1 - y, 3, 1)):
                            ref = part(k, zo, xo, yo, first, q)
                            link(k, base + d * 3 + s, ref, ref, zto(d)).wait_send()
            ref = part(k, z, x, y)
            link(k, XM + z, ref, ref, xp).wait_send()
            link(k, YM + z, ref, ref, yp).wait_send()
            for t in range(1, ZN):
                zo = lax.rem(z + t, ZN)
                ref = part(k, zo, x, y, 1, 3)
                link(k, XM + zo, ref, ref, xp).wait_send()
                ref = part(k, zo, x, y, 0, 3)
                link(k, YM + zo, ref, ref, yp).wait_send()
            for zo in range(ZN):
                ref = part(k, zo, 1 - x, y, 0, 2)
                link(k, YX + zo, ref, ref, yp).wait_send()
                ref = part(k, zo, x, 1 - y, 2, 2)
                link(k, XY + zo, ref, ref, xp).wait_send()

    return begin, do, finish


def scatter_events(outs, part_sums, landings, send_sem, recv_sem):
    n = len(outs)
    lxm, lym, lxy, lyx, lzm, lzx, lzy = landings
    z, x, c, y = here()
    xp = place(z, 1 - x, c, y)
    yp = place(z, x, c, 1 - y)

    def rows_of(k):
        return outs[k].shape[0]

    def width(k):
        return outs[k].shape[1]

    def mine(k, zo, xo, yo, first=0, quarters=4):
        h = rows_of(k)
        row = pl.multiple_of(((zo * 2 + xo) * 2 + yo) * h, h)
        return part_sums[k].at[pl.ds(row, h), span(width(k), first, quarters)]

    def link(k, slot, src, dst, to):
        return pltpu.make_async_remote_copy(
            src_ref=src, dst_ref=dst, send_sem=send_sem.at[k, slot], recv_sem=recv_sem.at[k, slot],
            device_id=to, device_id_type=MESH)

    def quarter_slice(k, first, quarters):
        return span(width(k), first, quarters)

    def land_x(k, zo, first, quarters):
        return lxm[k].at[zo, :, quarter_slice(k, first, quarters)]

    def land_y(k, zo, first, quarters):
        return lym[k].at[zo, :, quarter_slice(k, first, quarters)]

    def z_has(d, s):
        return (z - s >= 0) if d == 0 else (z + s <= ZN - 1)

    def z_next(d):
        return (z < ZN - 1) if d == 0 else (z > 0)

    def zo_of(d, s):
        return z - s if d == 0 else z + s

    def z_slot(d, s, zo):
        return ZN if (d == 1 and s == 0) else zo

    def toward(d):
        return place(z - 1 + 2 * d, x, c, y)

    def add_in(k, zo, xo, yo, first, quarters, others):
        ref = mine(k, zo, xo, yo, first, quarters)
        h = rows_of(k)

        @pl.loop(0, h // 16)
        def _(i):
            rows = pl.ds(pl.multiple_of(i * 16, 16), 16)
            total = ref[rows, :].astype(f32)
            for o in others:
                total = total + o[rows, :].astype(f32)
            ref[rows, :] = total.astype(bf16)

    def wait(k, slot, dst):
        link(k, slot, dst, dst, xp).wait_recv()

    def do(k, e):
        kind = e[0]
        if kind == "last":
            for zo in range(ZN):
                link(k, XY + zo, mine(k, zo, 1 - x, 1 - y, 2, 2), lxy[k].at[zo], xp).start()
                link(k, YX + zo, mine(k, zo, 1 - x, 1 - y, 0, 2), lyx[k].at[zo], yp).start()
        elif kind == "cross":
            s = e[1]
            for d in (0, 1):
                @pl.when(z_has(d, s + 1))
                def _():
                    zo = zo_of(d, s + 1)
                    wait(k, YX + zo, lyx[k].at[zo])
                    add_in(k, zo, 1 - x, y, 0, 2, [lyx[k].at[zo]])
                    link(k, XM + zo, mine(k, zo, 1 - x, y, 1, 3), land_x(k, zo, 1, 3), xp).start()
                    wait(k, XY + zo, lxy[k].at[zo])
                    add_in(k, zo, x, 1 - y, 2, 2, [lxy[k].at[zo]])
                    link(k, YM + zo, mine(k, zo, x, 1 - y, 0, 3), land_y(k, zo, 0, 3), yp).start()
        elif kind == "side":
            s = e[1]
            for d in (0, 1):
                @pl.when(z_has(d, s + 1))
                def _():
                    zo = zo_of(d, s + 1)
                    for base, landing, xo, yo, first in ((ZX, lzx, 1 - x, y, 0), (ZY, lzy, x, 1 - y, 3)):
                        if s < 2:
                            @pl.when(z_next(d))
                            def _():
                                got = landing[k].at[z_slot(d, s + 1, zo)]
                                wait(k, base + d * 3 + s + 1, got)
                                add_in(k, zo, xo, yo, first, 1, [got])
                        link(k, base + d * 3 + s, mine(k, zo, xo, yo, first, 1),
                             landing[k].at[z_slot(d, s, zo)], toward(d)).start()
        elif kind == "chain":
            s = e[1]
            for d in (0, 1):
                @pl.when(z_has(d, s + 1))
                def _():
                    zo = zo_of(d, s + 1)
                    wait(k, XM + zo, land_x(k, zo, 1, 3))
                    wait(k, YM + zo, land_y(k, zo, 0, 3))
                    add_in(k, zo, x, y, 0, 1, [land_y(k, zo, 0, 1)])
                    add_in(k, zo, x, y, 1, 2, [land_y(k, zo, 1, 2), land_x(k, zo, 1, 2)])
                    add_in(k, zo, x, y, 3, 1, [land_x(k, zo, 3, 1)])
                    if s < 2:
                        @pl.when(z_next(d))
                        def _():
                            got = lzm[k].at[z_slot(d, s + 1, zo)]
                            wait(k, ZM + d * 3 + s + 1, got)
                            add_in(k, zo, x, y, 0, 4, [got])
                    link(k, ZM + d * 3 + s, mine(k, zo, x, y), lzm[k].at[z_slot(d, s, zo)], toward(d)).start()
        elif kind == "near":
            for slot, own_slot, xo, yo, first, cross_land, side_base, side_land, side_first, to, land in (
                (YX, XM, 1 - x, y, 0, lyx, ZX, lzx, 0, xp, land_x),
                (XY, YM, x, 1 - y, 2, lxy, ZY, lzy, 3, yp, land_y),
            ):
                wait(k, slot + z, cross_land[k].at[z])
                add_in(k, z, xo, yo, first, 2, [cross_land[k].at[z]])
                for d in (0, 1):
                    @pl.when(z_next(d))
                    def _():
                        got = side_land[k].at[z_slot(d, 0, z)]
                        wait(k, side_base + d * 3, got)
                        add_in(k, z, xo, yo, side_first, 1, [got])
                link(k, own_slot + z, mine(k, z, xo, yo), land(k, z, 0, 4), to).start()
        elif kind == "own":
            wait(k, XM + z, land_x(k, z, 0, 4))
            wait(k, YM + z, land_y(k, z, 0, 4))
            h = rows_of(k)
            own = mine(k, z, x, y)
            from_x, from_y = land_x(k, z, 0, 4), land_y(k, z, 0, 4)

            @pl.loop(0, h // 16)
            def _(i):
                rows = pl.ds(pl.multiple_of(i * 16, 16), 16)
                outs[k][rows, :] = own[rows, :].astype(f32) + from_x[rows, :].astype(f32) + from_y[rows, :].astype(f32)

            for d in (0, 1):
                @pl.when(z_next(d))
                def _():
                    got = lzm[k].at[z_slot(d, 0, z)]
                    wait(k, ZM + d * 3, got)

                    @pl.loop(0, h // 16)
                    def _(i):
                        rows = pl.ds(pl.multiple_of(i * 16, 16), 16)
                        outs[k][rows, :] += got[rows, :].astype(f32)

    def finish():
        for k in range(n):
            for zo in range(ZN):
                link(k, XY + zo, mine(k, zo, 1 - x, 1 - y, 2, 2), lxy[k].at[zo], xp).wait_send()
                link(k, YX + zo, mine(k, zo, 1 - x, 1 - y, 0, 2), lyx[k].at[zo], yp).wait_send()
            for t in range(1, ZN):
                zo = lax.rem(z + t, ZN)
                link(k, XM + zo, mine(k, zo, 1 - x, y, 1, 3), land_x(k, zo, 1, 3), xp).wait_send()
                link(k, YM + zo, mine(k, zo, x, 1 - y, 0, 3), land_y(k, zo, 0, 3), yp).wait_send()
            link(k, XM + z, mine(k, z, 1 - x, y), land_x(k, z, 0, 4), xp).wait_send()
            link(k, YM + z, mine(k, z, x, 1 - y), land_y(k, z, 0, 4), yp).wait_send()
            for d in (0, 1):
                for s in range(3):
                    @pl.when(z_has(d, s + 1))
                    def _():
                        zo = zo_of(d, s + 1)
                        to = z_slot(d, s, zo)
                        link(k, ZX + d * 3 + s, mine(k, zo, 1 - x, y, 0, 1), lzx[k].at[to], toward(d)).wait_send()
                        link(k, ZY + d * 3 + s, mine(k, zo, x, 1 - y, 3, 1), lzy[k].at[to], toward(d)).wait_send()
                        link(k, ZM + d * 3 + s, mine(k, zo, x, y), lzm[k].at[to], toward(d)).wait_send()

    return do, finish


HEADS = 16


epsilon = 1e-05


def nn(a, b):
    return jnp.dot(a, b, preferred_element_type=f32)


def nt(a, b):
    return lax.dot_general(a, b, (((1,), (1,)), ((), ())), preferred_element_type=f32)


def tn(a, b):
    return lax.dot_general(a, b, (((0,), (0,)), ((), ())), preferred_element_type=f32)


CH = 1024
SKIP, QKV, OUT, UP, DOWN = range(5)
CHUNKS = (
    [(SKIP, 0), (SKIP, 1), (QKV, 0), (QKV, 1), (QKV, 2), (OUT, 0)] + [(UP, i) for i in range(4)]
    + [(DOWN, i) for i in range(4)] + [(UP, i) for i in range(4)] + [(OUT, 0)] + [(QKV, i) for i in range(3)]
    + [(SKIP, 0), (SKIP, 1)]
)
LEFTS = [(DOWN, 0), (DOWN, 1), (DOWN, 2), (DOWN, 3), (UP, 0), (OUT, 0), (QKV, 0), (SKIP, 0), (SKIP, 1)]
GATHER_PIECES = [(0, 0, 1024), (1, 0, 3072), (2, 0, 1024), (3, 0, 2048), (3, 2048, 2048), (4, 0, 512), (4, 512, 512)]
SCATTER_PIECES = [(4, 0, 1024), (3, 0, 4096), (2, 0, 1024), (1, 0, 3072), (0, 0, 512), (0, 512, 512)]
STAGES = [("own",), ("near",)] + [(e, s) for s in range(3) for e in ("chain", "side")] + [
    ("cross", s) for s in range(3)] + [("last",), ("ready",)]
(PR, MK, TR, F1, F2, F3, AF, F5, F6, F7, F8, FR, B2, B3, B5, B6, A, L1, L2, R, W0, W1, W2, W3, W4,
 G0, G1, G2, G3, G4, G5, G6, E0, E1, E2, E3, E4, E5) = range(38)
GATHER = [G0, G1, G2, G3, G4, G5, G6]
SCATTER = [E0, E1, E2, E3, E4, E5]
PLAN = [
    (G0, 0), (PR, 0), (MK, 0), (TR, 7), (PR, 1), (TR, 8), (G0, 1), (G0, 2),
    (PR, 2), (G0, 3), (G1, 0), (G0, 4), (G0, 5), (PR, 3), (G1, 1), (G1, 2),
    (G0, 6), (G0, 7), (G0, 8), (G0, 9), (PR, 4), (G1, 3), (G2, 0), (G0, 10),
    (G1, 4), (PR, 5), (G1, 5), (G0, 11), (G2, 1), (G2, 2), (G3, 0), (G0, 12),
    (F1, 0), (G1, 6), (F1, 1), (G1, 7), (G1, 8), (G1, 9), (G2, 3), (F2, 0),
    (G2, 4), (F2, 1), (G1, 10), (G3, 1), (F2, 2), (F2, 3), (G3, 2), (G2, 5),
    (TR, 6), (G2, 6), (G3, 3), (G4, 0), (G1, 11), (G3, 4), (G2, 7), (G2, 8),
    (G2, 9), (G3, 5), (G1, 12), (F3, 0), (G2, 10), (F3, 1), (F3, 2), (G3, 6),
    (G4, 1), (G4, 2), (G5, 0), (G3, 7), (G3, 8), (G3, 9), (AF, 0), (G2, 11),
    (G3, 10), (G4, 3), (AF, 1), (G2, 12), (G4, 4), (AF, 2), (G4, 5), (AF, 3),
    (G4, 6), (G5, 1), (G5, 2), (TR, 5), (G4, 7), (G4, 8), (F5, 0), (G3, 11),
    (G5, 3), (G6, 0), (F6, 0), (G4, 9), (G5, 4), (G3, 12), (G4, 10), (G5, 5),
    (F6, 1), (F6, 2), (F6, 3), (TR, 4), (F7, 0), (G5, 6), (TR, 0), (F7, 1),
    (G5, 7), (G5, 8), (G6, 1), (G6, 2), (TR, 1), (G4, 11), (G5, 9), (G6, 3),
    (G5, 10), (G4, 12), (F7, 2), (G6, 4), (G6, 5), (TR, 2), (F7, 3), (G6, 6),
    (TR, 3), (G5, 11), (G6, 7), (G6, 8), (G6, 9), (G6, 10), (W4, 0), (G5, 12),
    (W4, 1), (G6, 11), (E0, 11), (G6, 12), (F8, 0), (F8, 1), (F8, 2), (F8, 3),
    (E0, 10), (E0, 9), (E0, 8), (E0, 7), (FR, 0), (B2, 0), (B2, 1), (B2, 2),
    (E0, 6), (E0, 5), (B2, 3), (W3, 0), (W3, 1), (E1, 11), (L2, 0), (E0, 4),
    (L2, 1), (E0, 3), (L2, 2), (L2, 3), (B3, 0), (A, 0), (E0, 2), (E0, 1),
    (E1, 10), (E1, 9), (E1, 8), (E1, 7), (W2, 0), (E2, 11), (A, 1), (A, 2),
    (E0, 0), (A, 3), (E1, 6), (E1, 5), (B5, 0), (B5, 1), (B5, 2), (W1, 0),
    (W1, 1), (E3, 11), (E1, 4), (L1, 0), (E2, 10), (E2, 9), (E2, 8), (E2, 7),
    (E1, 3), (L1, 1), (L1, 2), (E1, 2), (L1, 3), (E3, 10), (E3, 9), (E2, 6),
    (E2, 5), (E3, 8), (E3, 7), (E1, 1), (R, 0), (W0, 0), (E4, 11), (W0, 1),
    (E5, 11), (R, 1), (E3, 6), (E2, 4), (E2, 3), (E3, 5), (E3, 4), (E2, 2),
    (E2, 1), (E3, 3), (E1, 0), (E4, 10), (E4, 9), (E4, 8), (E4, 7), (E3, 2),
    (E5, 10), (E5, 9), (E5, 8), (E5, 7), (R, 2), (E3, 1), (B6, 0), (E2, 0),
    (E4, 6), (E4, 5), (E5, 6), (E5, 5), (E4, 4), (E4, 3), (R, 3), (B6, 1),
    (E5, 4), (E5, 3), (E4, 2), (E4, 1), (E3, 0), (R, 4), (E5, 2), (E5, 1),
    (E4, 0), (R, 5), (E5, 0),
]


def layer_kernel(*refs):
    n = 5
    tokens, skip, cot, seg, valid, mine_small = refs[:6]
    own = refs[6 : 6 + n]
    small_out = refs[11]
    outs = refs[12:17]
    result, grad_tokens, grad_skip = refs[17:20]
    full = refs[20:25]
    r = refs[25:]
    turned, theirs, gcat, part_sums = r[:n], r[n : 2 * n], r[2 * n : 3 * n], r[3 * n : 4 * n]
    m = len(SCATTER_PIECES)
    landings = [r[4 * n + i * m : 4 * n + (i + 1) * m] for i in range(7)]
    (wbuf, lbuf, hid, gnorm, mid, pbuf, abuf, acc, small, small_land, params, params_wide, params_land,
     log_total, steep, distance,
     ag_send, ag_recv, ag_local, rs_send, rs_recv, pair_send, pair_recv, wsem, lsem, misc_sem,
     small_send, small_recv, params_send, params_recv) = r[4 * n + 7 * m :]
    z, x, c, y = here()
    cpart = place(z, x, 1 - c, y)
    T = cot.shape[0]

    ag_begin, ag_do, ag_finish = gather_events(
        [own[k].at[:, pl.ds(at, w)] for k, at, w in GATHER_PIECES],
        [full[k].at[:, :, pl.ds(at, w)] for k, at, w in GATHER_PIECES], ag_send, ag_recv, ag_local)
    rs_do, rs_finish = scatter_events(
        [outs[k].at[:, pl.ds(at, w)] for k, at, w in SCATTER_PIECES],
        [part_sums[k].at[:, pl.ds(at, w)] for k, at, w in SCATTER_PIECES], landings, rs_send, rs_recv)

    def chunk_copies(i):
        k, j = CHUNKS[i]
        slot, depth = i % 2, full[k].shape[1]
        if k in (SKIP, DOWN):
            blocks = CH // depth
            return [pltpu.make_async_copy(full[k].at[j * blocks + b], wbuf.at[slot, pl.ds(b * depth, depth), :], wsem.at[slot, b])
                    for b in range(blocks)]
        return [pltpu.make_async_copy(full[k].at[b, :, pl.ds(j * CH, CH)], wbuf.at[slot, pl.ds(b * depth, depth), :], wsem.at[slot, b])
                for b in range(ZN)]

    state = {"next": 0, "done": 0, "ready": set()}

    def arrived(i):
        k, j = CHUNKS[i]
        lo, hi = (j * CH, (j + 1) * CH) if k in (QKV, UP) else (0, CH)
        return all(p in state["ready"] for p, (w, at, wide) in enumerate(GATHER_PIECES) if w == k and at < hi and at + wide > lo)

    def pump():
        while state["next"] < min(len(CHUNKS), state["done"] + 2) and arrived(state["next"]):
            for cp in chunk_copies(state["next"]):
                cp.start()
            state["next"] += 1

    def ready(k):
        state["ready"].add(k)
        pump()

    def take(i):
        assert state["done"] == i and state["next"] > i
        for cp in chunk_copies(i):
            cp.wait()

    def release(i):
        state["done"] = i + 1
        pump()

    in_copies = [pltpu.make_async_copy(a, lbuf.at[i], lsem.at[i]) for i, a in enumerate((tokens, skip))]
    cot_copy = pltpu.make_async_copy(cot, gcat[DOWN].at[pl.ds(0, T), :], misc_sem.at[0])
    result_copy = pltpu.make_async_copy(lbuf.at[0], result, misc_sem.at[1])
    out_copies = [pltpu.make_async_copy(lbuf.at[i], o, misc_sem.at[2 + i]) for i, o in enumerate((grad_tokens, grad_skip))]
    ag_begin()
    for cp in in_copies:
        cp.start()
    cot_copy.start()
    greet_all(16, 2)

    def pair(k, j):
        if j == 0:
            src, dst = turned[k].at[1 - c], theirs[k]
        elif k == DOWN:
            src, dst = cot, gcat[k].at[pl.ds(T, T), :]
        elif k == UP:
            cols = pl.ds((j - 1) * CH, CH)
            src, dst = gcat[k].at[pl.ds(0, T), cols], gcat[k].at[pl.ds(T, T), cols]
        else:
            src, dst = gcat[k].at[pl.ds(0, T), :], gcat[k].at[pl.ds(T, T), :]
        return pltpu.make_async_remote_copy(
            src_ref=src, dst_ref=dst, send_sem=pair_send.at[k, j], recv_sem=pair_recv.at[k, j],
            device_id=cpart, device_id_type=MESH)

    def pieces(k):
        return range(5) if k == UP else range(2)

    meet = [cpart, place(z, 1 - x, c, y), place(z, x, c, 1 - y),
            place(z + 1 - 2 * lax.rem(z, 2), x, c, y), place(lax.rem(z + 2, 4), x, c, y)]

    def meeting(ref, land, send, recv, t):
        return pltpu.make_async_remote_copy(
            src_ref=ref, dst_ref=land.at[t], send_sem=send.at[t], recv_sem=recv.at[t],
            device_id=meet[t], device_id_type=MESH)

    def params_step(t):
        if t == 0:
            params[...] = mine_small[...]
        else:
            cp = meeting(params, params_land, params_send, params_recv, t - 1)
            cp.wait_send()
            cp.wait_recv()
            params[...] = (params[...].astype(f32) + params_land[t - 1].astype(f32)).astype(bf16)
        if t < 5:
            meeting(params, params_land, params_send, params_recv, t).start()
        else:
            params_wide[...] = params[...].astype(f32)

    def small_step(t):
        if t:
            cp = meeting(small, small_land, small_send, small_recv, t - 1)
            cp.wait_send()
            cp.wait_recv()
            small[...] += small_land[t - 1]
        if t < 5:
            meeting(small, small_land, small_send, small_recv, t).start()
        else:
            small_out[...] = small[...]

    def make_masks():
        acc[...] = jnp.zeros_like(acc)
        small[...] = jnp.zeros_like(small)
        heads = lax.broadcasted_iota(jnp.int32, steep.shape, 0).astype(f32)
        steep[...] = jnp.exp((heads + 1.0) * -0.34657359027997264)
        seg_row = jnp.broadcast_to(seg[...].astype(f32), (T, T))
        live = jnp.broadcast_to(valid[...].astype(f32), (T, T)).T
        key_at = lax.broadcasted_iota(jnp.int32, (T, T), 0)
        query_at = lax.broadcasted_iota(jnp.int32, (T, T), 1)
        allowed = jnp.logical_and(seg_row.T == seg_row, jnp.logical_or(live == 1.0, key_at == query_at))
        distance[...] = jnp.where(allowed, jnp.abs(key_at - query_at).astype(f32), 1e33)
        pair(DOWN, 1).start()

    def turn(i):
        k, j = LEFTS[i]
        group = 2 * outs[k].shape[0]
        seg = min(group, 128)
        if k == SKIP:
            in_copies[j].wait()
        for t in range(CH // 128):
            cols = slice(t * 128, (t + 1) * 128)
            if k == SKIP:
                block = lbuf[j, :, cols].T
            elif k == DOWN:
                block = part_sums[UP][0:T, j * CH + t * 128 : j * CH + (t + 1) * 128].T
            else:
                block = abuf[:, cols].T
            for s in range(0, 128, seg):
                row = j * CH + t * 128 + s
                core, at = (row // group) % 2, row // (2 * group) * group + row % group
                turned[k][core, at : at + seg, :] = block[s : s + seg, :]
        if i + 1 == len(LEFTS) or LEFTS[i + 1][0] != k:
            pair(k, 0).start()

    def forward_product(left, slot, finish):
        @pl.loop(0, 2)
        def _(j):
            at = pl.multiple_of(j * 512, 512)
            finish(at, nn(left(), wbuf[slot, :, pl.ds(at, 512)]))

    def back_product(left, slot, finish):
        @pl.loop(0, 2)
        def _(j):
            at = pl.multiple_of(j * 512, 512)
            finish(at, nt(left(), wbuf[slot, pl.ds(at, 512), :]))

    def store_in(ref, offset=0):
        def finish(at, value):
            ref[:, pl.ds(pl.multiple_of(at + offset, 512), 512)] = value.astype(ref.dtype)

        return finish

    def add_to(ref):
        def finish(at, value):
            ref[:, pl.ds(at, 512)] += value

        return finish

    def to_hidden(i):
        take(i)

        def first(at, value):
            hid[:, pl.ds(at, 512)] = value + params_wide[0:1, pl.ds(at, 512)]

        forward_product(lambda: lbuf[i], i % 2, add_to(hid) if i else first)
        release(i)

    def norm_forward(source, gain, i):
        @pl.loop(0, 4)
        def _(j):
            rows = pl.ds(pl.multiple_of(i * 64 + j * 16, 16), 16)
            v = source[rows, :]
            center = v - jnp.mean(v, axis=-1, keepdims=True)
            rate = lax.rsqrt(jnp.mean(center * center, axis=-1, keepdims=True) + epsilon)
            abuf[rows, :] = (
                center * rate * params_wide[gain : gain + 1, :] + params_wide[gain + 1 : gain + 2, :]).astype(bf16)

    def to_projected(i):
        take(2 + i)
        forward_product(lambda: abuf[...], i % 2, store_in(pbuf, i * CH))
        release(2 + i)

    def heads_of(p):
        at = pl.multiple_of(p * 128, 128)
        return [pbuf[:, pl.ds(pl.multiple_of(at + j * CH, 128), 128)] for j in range(3)]

    def half_masks():
        low = lax.broadcasted_iota(jnp.int32, (T, 128), 1) < 64
        return low, jnp.logical_not(low)

    def attend(i):
        masks = half_masks()

        @pl.loop(2 * i, 2 * i + 2)
        def _(p):
            q, k, v = heads_of(p)
            res = []
            for e in (0, 1):
                head = pl.ds(2 * p + e, 1)
                scores = nt(k, jnp.where(masks[e], q, jnp.zeros_like(q))) * 0.125 - distance[...] * steep[head, :]
                top = jnp.max(scores, axis=0, keepdims=True)
                raised = jnp.exp(scores - top)
                total = jnp.sum(raised, axis=0, keepdims=True)
                log_total[head, :] = top + jnp.log(total)
                res.append(tn((raised / total).astype(bf16), v))
            abuf[:, pl.ds(pl.multiple_of(p * 128, 128), 128)] = jnp.where(masks[0], res[0], res[1]).astype(bf16)

    def to_middle():
        take(5)

        def finish(at, value):
            mid[:, pl.ds(at, 512)] = hid[:, pl.ds(at, 512)] + value

        forward_product(lambda: abuf[...], 1, finish)
        release(5)

    def to_activated(i):
        take(6 + i)

        def finish(at, value):
            cols = pl.ds(pl.multiple_of(i * CH + at, 512), 512)
            u = value + params_wide[6 + i : 7 + i, pl.ds(at, 512)]
            cdf = 0.5 * (1.0 + lax.erf(u * 0.7071067811865476))
            part_sums[UP][0:T, cols] = (u * cdf).astype(bf16)
            gcat[UP][0:T, cols] = (cdf + u * jnp.exp(-0.5 * u * u) * 0.3989422804014327).astype(bf16)

        forward_product(lambda: abuf[...], i % 2, finish)
        release(6 + i)

    def through_down(i):
        take(10 + i)
        forward_product(
            lambda: part_sums[UP][0:T, i * CH : (i + 1) * CH], i % 2, add_to(gnorm) if i else store_in(gnorm))

        def finish(at, value):
            cols = pl.ds(pl.multiple_of(i * CH + at, 512), 512)
            got = (value * gcat[UP][0:T, cols].astype(f32)).astype(bf16)
            gcat[UP][0:T, cols] = got
            small[6 + i : 7 + i, pl.ds(at, 512)] = jnp.sum(got.astype(f32), axis=0, keepdims=True)

        back_product(lambda: gcat[DOWN][0:T, :], i % 2, finish)
        release(10 + i)
        pair(UP, 1 + i).start()

    def to_result():
        @pl.loop(0, T // 16)
        def _(i):
            rows = pl.ds(pl.multiple_of(i * 16, 16), 16)
            lbuf[0, rows, :] = (mid[rows, :] + (gnorm[rows, :] + params_wide[5:6, :])).astype(bf16)

        result_copy.start()

    def weight_product(k, lo, hi):
        tiles = (hi - lo) // 512
        if lo == 0:
            if k == DOWN:
                cot_copy.wait()
                small[5:6, :] = jnp.sum(gcat[DOWN][0:T, :].astype(f32), axis=0, keepdims=True)
            for j in pieces(k):
                pair(k, j).wait_recv()

        @pl.loop(0, part_sums[k].shape[0] // 256 * tiles)
        def _(i):
            rows = pl.ds(pl.multiple_of(lax.div(i, tiles) * 256, 256), 256)
            cols = pl.ds(pl.multiple_of(lo + lax.rem(i, tiles) * 512, 512), 512)
            both = nn(turned[k][c, rows, :], gcat[k][pl.ds(0, T), cols])
            both += nn(theirs[k][rows, :], gcat[k][pl.ds(T, T), cols])
            part_sums[k][rows, cols] = both.astype(bf16)

    def into_norm(i, base, k):
        take(base + i)
        back_product(lambda: gcat[k][0:T, i * CH : (i + 1) * CH], (base + i) % 2, add_to(gnorm) if i else store_in(gnorm))
        release(base + i)

    def norm_back(source, i, gain, base, emit):
        @pl.loop(0, 4)
        def _(j):
            rows = pl.ds(pl.multiple_of(i * 64 + j * 16, 16), 16)
            v = source[rows, :]
            center = v - jnp.mean(v, axis=-1, keepdims=True)
            rate = lax.rsqrt(jnp.mean(center * center, axis=-1, keepdims=True) + epsilon)
            xhat = center * rate
            g = gnorm[rows, :]
            gx = g * xhat
            acc[base] += gx[0:8] + gx[8:16]
            acc[base + 1] += g[0:8] + g[8:16]
            e = g * params_wide[gain : gain + 1, :]
            emit(rows, rate * (e - jnp.mean(e, axis=-1, keepdims=True) - xhat * jnp.mean(e * xhat, axis=-1, keepdims=True)))

    def second_norm(i):
        def emit(rows, value):
            total = gcat[DOWN][rows, :].astype(f32) + value
            mid[rows, :] = total
            gcat[OUT][rows, :] = total.astype(bf16)

        norm_back(mid, i, 3, 0, emit)
        if i == 3:
            pair(OUT, 1).start()

    def to_attended():
        take(18)
        back_product(lambda: gcat[OUT][0:T, :], 0, store_in(abuf))
        release(18)

    def attend_back(i):
        masks = half_masks()

        @pl.loop(2 * i, 2 * i + 2)
        def _(p):
            at = pl.multiple_of(p * 128, 128)
            q, k, v = heads_of(p)
            g = abuf[:, pl.ds(at, 128)]
            res = []
            for e in (0, 1):
                head = pl.ds(2 * p + e, 1)
                scores = nt(k, jnp.where(masks[e], q, jnp.zeros_like(q))) * 0.125 - distance[...] * steep[head, :]
                probable = jnp.exp(scores - log_total[head, :])
                gp = nt(v, jnp.where(masks[e], g, jnp.zeros_like(g)))
                gv = nn(probable.astype(bf16), g)
                inner = jnp.sum(gp * probable, axis=0, keepdims=True)
                gs = (probable * (gp - inner)).astype(bf16)
                res.append((tn(gs, k) * 0.125, nn(gs, q) * 0.125, gv))
            for j in range(3):
                gcat[QKV][0:T, pl.ds(pl.multiple_of(at + CH * j, 128), 128)] = jnp.where(
                    masks[0], res[0][j], res[1][j]).astype(bf16)

        if i == 3:
            pair(QKV, 1).start()

    def first_norm(i):
        def emit(rows, value):
            total = (mid[rows, :] + value).astype(bf16)
            gcat[SKIP][rows, :] = total
            wide = total.astype(f32)
            acc[4] += wide[0:8] + wide[8:16]

        norm_back(hid, i, 1, 2, emit)
        if i == 3:
            pair(SKIP, 1).start()
            for row, a in ((0, 4), (1, 2), (2, 3), (3, 0), (4, 1)):
                small[row : row + 1, :] = jnp.sum(acc[a], axis=0, keepdims=True)

    def to_inputs(i):
        take(22 + i)
        if i == 0:
            result_copy.wait()
        back_product(lambda: gcat[SKIP][0:T, :], i % 2, store_in(lbuf.at[i]))
        release(22 + i)
        out_copies[i].start()

    steps = {
        PR: params_step, MK: lambda i: make_masks(), TR: turn, F1: to_hidden, F2: lambda i: norm_forward(hid, 1, i),
        F3: to_projected, AF: attend, F5: lambda i: to_middle(), F6: lambda i: norm_forward(mid, 3, i),
        F7: to_activated, F8: through_down, FR: lambda i: to_result(),
        B2: lambda i: into_norm(i, 14, UP), L2: second_norm, B3: lambda i: to_attended(), A: attend_back,
        B5: lambda i: into_norm(i, 19, QKV), L1: first_norm, B6: to_inputs, R: small_step,
        W4: lambda i: weight_product(DOWN, 512 * i, 512 * i + 512),
        W3: lambda i: weight_product(UP, 2048 * i, 2048 * i + 2048), W2: lambda i: weight_product(OUT, 0, 1024),
        W1: lambda i: weight_product(QKV, 1536 * i, 1536 * i + 1536),
        W0: lambda i: weight_product(SKIP, 512 * i, 512 * i + 512),
    }
    for name, at in PLAN:
        if name in GATHER:
            k = GATHER.index(name)
            ag_do(k, STAGES[at])
            if STAGES[at] == ("ready",):
                ready(k)
        elif name in SCATTER:
            rs_do(SCATTER.index(name), STAGES[at])
        else:
            steps[name](at)

    for cp in out_copies:
        cp.wait()
    for k in range(n):
        for j in pieces(k):
            pair(k, j).wait_send()
    ag_finish()
    rs_finish()


def whole_layer(tokens, skip, cot, seg_ids, valid, small, shards):
    T, d = cot.shape
    n = len(shards)
    hw = [s.shape for s in shards]
    dims = [(16 * h, w) for h, w in hw]
    pieces = [(hw[k][0], w) for k, _, w in SCATTER_PIECES]
    ng, ns = len(GATHER_PIECES), len(SCATTER_PIECES)
    sem = pltpu.SemaphoreType.DMA
    V = pltpu.VMEM
    scratch = (
        [V((2, h, T), bf16) for h, _ in dims]
        + [V((h, T), bf16) for h, _ in dims]
        + [V((2 * T, w), bf16) for _, w in dims]
        + [V((h, w), bf16) for h, w in dims]
        + [V((count, h, w // cut), bf16) for count, cut in ((4, 1), (4, 1), (4, 2), (4, 2), (5, 1), (5, 4), (5, 4)) for h, w in pieces]
        + [V((2, CH, CH), bf16), V((2, T, CH), bf16), V((T, d), f32), V((T, d), f32), V((T, d), f32),
           V((T, 3 * d), bf16), V((T, d), bf16), V((5, 8, d), f32), V((16, d), f32), V((5, 16, d), f32),
           V((16, d), bf16), V((16, d), f32), V((5, 16, d), bf16), V((HEADS, T), f32), V((HEADS, T), f32), V((T, T), f32),
           sem((ng, SLOTS)), sem((ng, SLOTS)), sem((ng,)), sem((ns, SLOTS)), sem((ns, SLOTS)), sem((n, 5)), sem((n, 5)),
           sem((2, 4)), sem((2,)), sem((4,)), sem((5,)), sem((5,)), sem((5,)), sem((5,))]
    )
    vm, anywhere = pl.BlockSpec(memory_space=V), pl.BlockSpec(memory_space=pl.ANY)
    outs = ([jax.ShapeDtypeStruct((16, d), f32)] + [jax.ShapeDtypeStruct(s, f32) for s in hw]
            + [jax.ShapeDtypeStruct((T, d), bf16)] * 3 + [jax.ShapeDtypeStruct((4, 8 * h, w), bf16) for h, w in hw])
    return pl.pallas_call(
        layer_kernel, out_shape=outs,
        in_specs=[anywhere] * 3 + [vm] * 8,
        out_specs=[vm] * 6 + [anywhere] * 8,
        scratch_shapes=scratch,
        compiler_params=pltpu.CompilerParams(collective_id=0, has_side_effects=True, vmem_limit_bytes=67043328),
        name="whole_layer",
    )(tokens, skip, cot, seg_ids, valid, small, *shards)


def product(left, right):
    return jnp.dot(left, right, preferred_element_type=jnp.float32)


def outer_product(left, right):
    return lax.dot_general(
        left, right, (((0,), (0,)), ((), ())), preferred_element_type=jnp.float32
    )


def product_back(left, right):
    return lax.dot_general(
        left, right, (((1,), (1,)), ((), ())), preferred_element_type=jnp.float32
    )


def norm_rows(values, gain, shift):
    center = values - jnp.mean(values, axis=-1, keepdims=True)
    spread = jnp.mean(center * center, axis=-1, keepdims=True)
    return center * lax.rsqrt(spread + epsilon) * gain + shift


def gelu_exact(values):
    return 0.5 * values * (1.0 + lax.erf(values * 0.7071067811865476))


def attend_mask(seg_row, valid_row, head_count):
    count_rows = seg_row.shape[0]
    places = jnp.arange(count_rows, dtype=jnp.int32)
    same_utt = seg_row[:, None] == seg_row[None, :]
    diagonal = places[:, None] == places[None, :]
    allowed = same_utt & ((valid_row[None, :] == 1) | diagonal)
    slopes = 2.0 ** (-8.0 * (jnp.arange(head_count, dtype=jnp.float32) + 1.0) / head_count)
    distance = jnp.abs(places[:, None] - places[None, :]).astype(jnp.float32)
    return (allowed, -slopes[:, None, None] * distance[None, :, :])


def split_heads(projected, head_count):
    row_count = projected.shape[0]
    feature_width = projected.shape[1] // 3
    head_size = feature_width // head_count
    queries = projected[:, :feature_width].reshape(row_count, head_count, head_size)
    keys_all = projected[:, feature_width : 2 * feature_width].reshape(
        row_count, head_count, head_size
    )
    values_all = projected[:, 2 * feature_width :].reshape(row_count, head_count, head_size)
    return (queries, keys_all, values_all)


def masked_scores(queries, keys_all, allowed, linear_bias):
    score_scale = queries.shape[2] ** (-0.5)
    raw = (
        jnp.einsum("qhd,khd->hqk", queries, keys_all, preferred_element_type=jnp.float32)
        * score_scale
        + linear_bias
    )
    return jnp.where(allowed[None, :, :], raw, -1e30)


def forward_pass(tokens, skip, weights, allowed, linear_bias, head_count):
    w_skip, b_skip, g_one, beta_one, w_qkv, w_out, g_two, beta_two, w_up, b_up, w_down, b_down = (
        weights
    )
    row_count, feature_width = tokens.shape
    joined = jnp.concatenate([tokens, skip], axis=1)
    hidden = product(joined, w_skip) + b_skip.astype(jnp.float32)
    normed = norm_rows(hidden, g_one.astype(jnp.float32), beta_one.astype(jnp.float32)).astype(
        jnp.bfloat16
    )
    projected = product(normed, w_qkv).astype(jnp.bfloat16)
    queries, keys_all, values_all = split_heads(projected, head_count)
    masked = masked_scores(queries, keys_all, allowed, linear_bias)
    row_top = jnp.max(masked, axis=-1, keepdims=True)
    exponent = jnp.exp(masked - row_top)
    row_total = jnp.sum(exponent, axis=-1, keepdims=True)
    soft_weights = (exponent / row_total).astype(jnp.bfloat16)
    log_total = row_top + jnp.log(row_total)
    weighted = jnp.einsum(
        "hqk,khd->qhd", soft_weights, values_all, preferred_element_type=jnp.float32
    )
    attended = weighted.reshape(row_count, feature_width).astype(jnp.bfloat16)
    middle = hidden + product(attended, w_out)
    normed_two = norm_rows(middle, g_two.astype(jnp.float32), beta_two.astype(jnp.float32)).astype(
        jnp.bfloat16
    )
    hidden_up = product(normed_two, w_up) + b_up.astype(jnp.float32)
    activated = gelu_exact(hidden_up).astype(jnp.bfloat16)
    result = middle + (product(activated, w_down) + b_down.astype(jnp.float32))
    stored = (
        joined,
        hidden,
        normed,
        projected,
        log_total,
        attended,
        middle,
        normed_two,
        hidden_up,
        activated,
    )
    return (stored, result)


def backward_feed(stored, weights, cotangent):
    (
        joined,
        hidden,
        normed,
        projected,
        log_total,
        attended,
        middle,
        normed_two,
        hidden_up,
        activated,
    ) = stored
    w_skip, b_skip, g_one, beta_one, w_qkv, w_out, g_two, beta_two, w_up, b_up, w_down, b_down = (
        weights
    )
    grad_result = cotangent.astype(jnp.float32)
    grad_activated = product_back(cotangent, w_down)
    grad_b_down = jnp.sum(grad_result, axis=0)
    gelu_value, gelu_pull = jax.vjp(gelu_exact, hidden_up)
    grad_up = gelu_pull(grad_activated)[0].astype(jnp.bfloat16)
    grad_b_up = jnp.sum(grad_up.astype(jnp.float32), axis=0)
    grad_normed_two = product_back(grad_up, w_up)
    norm_value, norm_pull = jax.vjp(
        norm_rows, middle, g_two.astype(jnp.float32), beta_two.astype(jnp.float32)
    )
    grad_middle_norm, grad_g_two, grad_beta_two = norm_pull(grad_normed_two)
    grad_middle = grad_result + grad_middle_norm
    feed_terms = (grad_up, grad_b_up, cotangent, grad_b_down, grad_g_two, grad_beta_two)
    return (feed_terms, grad_middle)


def backward_front(stored, weights, grad_middle, allowed, linear_bias, head_count):
    (
        joined,
        hidden,
        normed,
        projected,
        log_total,
        attended,
        middle,
        normed_two,
        hidden_up,
        activated,
    ) = stored
    w_skip, b_skip, g_one, beta_one, w_qkv, w_out, g_two, beta_two, w_up, b_up, w_down, b_down = (
        weights
    )
    row_count, feature_width = hidden.shape
    branch_grad = grad_middle.astype(jnp.bfloat16)
    grad_attended = product_back(branch_grad, w_out).astype(jnp.bfloat16)
    queries, keys_all, values_all = split_heads(projected, head_count)
    score_scale = queries.shape[2] ** (-0.5)
    masked = masked_scores(queries, keys_all, allowed, linear_bias)
    probable = jnp.exp(masked - log_total)
    soft_weights = probable.astype(jnp.bfloat16)
    grad_heads = grad_attended.reshape(row_count, head_count, feature_width // head_count)
    grad_probable = jnp.einsum(
        "qhd,khd->hqk", grad_heads, values_all, preferred_element_type=jnp.float32
    )
    grad_values = jnp.einsum(
        "hqk,qhd->khd", soft_weights, grad_heads, preferred_element_type=jnp.float32
    )
    inner_sum = jnp.sum(grad_probable * probable, axis=-1, keepdims=True)
    grad_scores = (probable * (grad_probable - inner_sum)).astype(jnp.bfloat16)
    grad_queries = (
        jnp.einsum("hqk,khd->qhd", grad_scores, keys_all, preferred_element_type=jnp.float32)
        * score_scale
    )
    grad_keys = (
        jnp.einsum("hqk,qhd->khd", grad_scores, queries, preferred_element_type=jnp.float32)
        * score_scale
    )
    grad_projected = jnp.concatenate(
        [
            grad_queries.reshape(row_count, feature_width),
            grad_keys.reshape(row_count, feature_width),
            grad_values.reshape(row_count, feature_width),
        ],
        axis=1,
    ).astype(jnp.bfloat16)
    grad_normed = product_back(grad_projected, w_qkv)
    norm_value, norm_pull = jax.vjp(
        norm_rows, hidden, g_one.astype(jnp.float32), beta_one.astype(jnp.float32)
    )
    grad_hidden_norm, grad_g_one, grad_beta_one = norm_pull(grad_normed)
    grad_hidden = (grad_middle + grad_hidden_norm).astype(jnp.bfloat16)
    grad_b_skip = jnp.sum(grad_hidden.astype(jnp.float32), axis=0)
    grad_joined = product_back(grad_hidden, w_skip)
    grad_tokens = grad_joined[:, :feature_width].astype(jnp.bfloat16)
    grad_skip = grad_joined[:, feature_width:].astype(jnp.bfloat16)
    front_terms = (grad_hidden, grad_b_skip, grad_g_one, grad_beta_one, grad_projected, branch_grad)
    return (grad_tokens, grad_skip, front_terms)


AXES = ("wide", "narrow")


def gather_plain(values):
    return [lax.all_gather(v, AXES, axis=0, tiled=True) for v in values]


def hand_over_kernel(*refs):
    small = refs[0]
    sources = refs[1:9]
    vectors = refs[9:16]
    targets = refs[16:24]
    buffers = refs[24:32]
    in_sem, out_sem = refs[32:]
    me = lax.axis_index("wide") * 2 + lax.axis_index("narrow")
    arrive = [pltpu.make_async_copy(s, b, in_sem.at[i]) for i, (s, b) in enumerate(zip(sources, buffers))]
    leave = [pltpu.make_async_copy(b, t, out_sem.at[i]) for i, (b, t) in enumerate(zip(buffers, targets))]
    for cp in arrive:
        cp.start()
    rolled = pltpu.roll(small[...], lax.rem(32 - me, 32) * 32, 1)
    for i in range(6):
        vectors[i][...] = rolled[i, 0:32]
    row = 6 + lax.div(me, 8)
    wide = pltpu.roll(jnp.where(lax.broadcasted_iota(jnp.int32, small.shape, 0) == row, small[...], 0.0),
                      lax.rem(8 - lax.rem(me, 8), 8) * 128, 1)
    vectors[6][...] = jnp.sum(wide[:, 0:128], axis=0)
    for a, l in zip(arrive, leave):
        a.wait()
        l.start()
    for l in leave:
        l.wait()


def hand_over(small, arrays):
    vm, anywhere = pl.BlockSpec(memory_space=pltpu.VMEM), pl.BlockSpec(memory_space=pl.ANY)
    sem = pltpu.SemaphoreType.DMA
    n = len(arrays)
    outs = [jax.ShapeDtypeStruct((32,), f32)] * 6 + [jax.ShapeDtypeStruct((128,), f32)] + [
        jax.ShapeDtypeStruct(a.shape, a.dtype) for a in arrays]
    return pl.pallas_call(
        hand_over_kernel, out_shape=outs,
        in_specs=[vm] + [anywhere] * n, out_specs=[vm] * 7 + [anywhere] * n,
        scratch_shapes=[pltpu.VMEM(a.shape, a.dtype) for a in arrays] + [sem((n,)), sem((n,))],
        name="hand_over",
    )(small, *arrays)


def own_layer(tokens, skip, seg_ids, valid, w_skip, b_skip, g_one, beta_one, w_qkv, w_out, g_two, beta_two,
              w_up, b_up, w_down, b_down, cotangent):
    me = lax.axis_index("wide") * 2 + lax.axis_index("narrow")
    narrow = jnp.stack([b_skip, g_one, beta_one, g_two, beta_two, b_down])
    place_of = jnp.arange(1024, dtype=jnp.int32)
    narrow = jnp.where(place_of // 32 == me, jnp.tile(narrow, (1, 32)), jnp.zeros((), bf16))
    wide_at = (jnp.arange(4, dtype=jnp.int32)[:, None] * 8 + place_of[None, :] // 128)
    wide = jnp.where(wide_at == me, jnp.tile(b_up[None, :], (4, 8)), jnp.zeros((), bf16))
    small = jnp.concatenate([narrow, wide, jnp.zeros((6, 1024), bf16)])
    small, *rest = whole_layer(
        tokens, skip, cotangent, seg_ids, valid, small, (w_skip, w_qkv, w_out, w_up, w_down))
    (grad_b_skip, grad_g_one, grad_beta_one, grad_g_two, grad_beta_two, grad_b_down, grad_b_up,
     grad_w_skip, grad_w_qkv, grad_w_out, grad_w_up, grad_w_down, result, grad_tokens, grad_skip) = hand_over(small, rest[:8])
    return (
        result, grad_tokens, grad_skip,
        grad_w_skip, grad_b_skip, grad_g_one, grad_beta_one, grad_w_qkv, grad_w_out,
        grad_g_two, grad_beta_two, grad_w_up, grad_b_up, grad_w_down, grad_b_down,
    )


def plain_layer(tokens, skip, seg_ids, valid, w_skip, b_skip, g_one, beta_one, w_qkv, w_out, g_two, beta_two,
                w_up, b_up, w_down, b_down, cotangent):
    weights = gather_plain(
        (w_skip, b_skip, g_one, beta_one, w_qkv, w_out, g_two, beta_two, w_up, b_up, w_down, b_down))
    allowed, linear_bias = attend_mask(seg_ids[0], valid[0], HEADS)
    stored, result = forward_pass(tokens, skip, weights, allowed, linear_bias, HEADS)
    (joined, hidden, normed, projected, log_total, attended, middle, normed_two, hidden_up, activated) = stored
    feed_terms, grad_middle = backward_feed(stored, weights, cotangent)
    grad_tokens, grad_skip, front_terms = backward_front(
        stored, weights, grad_middle, allowed, linear_bias, HEADS)
    grad_up, grad_b_up, grad_result, grad_b_down, grad_g_two, grad_beta_two = feed_terms
    grad_hidden, grad_b_skip, grad_g_one, grad_beta_one, grad_projected, branch_grad = front_terms
    lefts = (joined, normed, attended, normed_two, activated)
    rights = (grad_hidden, grad_projected, branch_grad, grad_up, grad_result)

    def scatter(v):
        return lax.psum_scatter(v, AXES, scatter_dimension=0, tiled=True)

    big = [scatter(outer_product(a, b)) for a, b in zip(lefts, rights)]
    grad_b_skip, grad_g_one, grad_beta_one, grad_g_two, grad_beta_two, grad_b_up, grad_b_down = [
        scatter(v) for v in
        (grad_b_skip, grad_g_one, grad_beta_one, grad_g_two, grad_beta_two, grad_b_up, grad_b_down)]
    return (
        result.astype(bf16), grad_tokens, grad_skip,
        big[0], grad_b_skip, grad_g_one, grad_beta_one, big[1], big[2],
        grad_g_two, grad_beta_two, big[3], grad_b_up, big[4], grad_b_down,
    )


def solution(mesh):
    return jax.shard_map(
        own_layer if dict(mesh.shape) == {"wide": 16, "narrow": 2} else plain_layer,
        mesh=mesh,
        in_specs=(
            P(("wide", "narrow"), None),
            P(("wide", "narrow"), None),
            P(("wide", "narrow"), None),
            P(("wide", "narrow"), None),
            P(("wide", "narrow"), None),
            P(("wide", "narrow")),
            P(("wide", "narrow")),
            P(("wide", "narrow")),
            P(("wide", "narrow"), None),
            P(("wide", "narrow"), None),
            P(("wide", "narrow")),
            P(("wide", "narrow")),
            P(("wide", "narrow"), None),
            P(("wide", "narrow")),
            P(("wide", "narrow"), None),
            P(("wide", "narrow")),
            P(("wide", "narrow"), None),
        ),
        out_specs=(
            P(("wide", "narrow"), None),
            P(("wide", "narrow"), None),
            P(("wide", "narrow"), None),
            P(("wide", "narrow"), None),
            P(("wide", "narrow")),
            P(("wide", "narrow")),
            P(("wide", "narrow")),
            P(("wide", "narrow"), None),
            P(("wide", "narrow"), None),
            P(("wide", "narrow")),
            P(("wide", "narrow")),
            P(("wide", "narrow"), None),
            P(("wide", "narrow")),
            P(("wide", "narrow"), None),
            P(("wide", "narrow")),
        ),
        check_vma=False,
    )
```

```python
import jax
import jax.numpy as jnp
from jax import lax
from jax.experimental import pallas as pl
from jax.experimental.pallas import tpu as pltpu
from jax.sharding import PartitionSpec as P

f32 = jnp.float32
bf16 = jnp.bfloat16

MESH = pl.DeviceIdType.MESH
ZN = 4
SLOTS = 38
ZM, ZX, ZY, XM, XY, YM, YX, CP = 0, 6, 12, 18, 22, 26, 30, 34


def here():
    w = lax.axis_index("wide")
    y = lax.axis_index("narrow")
    c = lax.rem(w, 2)
    x = lax.rem(lax.div(w, 2), 2)
    z = lax.div(w, 4)
    return z, x, c, y


def place(z, x, c, y):
    return ((z * 2 + x) * 2 + c, y)


def greet_partners():
    barrier = pltpu.get_barrier_semaphore()
    z, x, c, y = here()

    def greet(to):
        pl.semaphore_signal(barrier, inc=1, device_id=to, device_id_type=MESH)

    for to in (place(z, x, 1 - c, y), place(z, 1 - x, c, y), place(z, x, c, 1 - y), place(lax.rem(z + 2, ZN), x, c, y)):
        greet(to)

    @pl.when(z > 0)
    def _():
        greet(place(z - 1, x, c, y))

    @pl.when(z < ZN - 1)
    def _():
        greet(place(z + 1, x, c, y))

    pl.semaphore_wait(barrier, 4 + jnp.where(z > 0, 1, 0) + jnp.where(z < ZN - 1, 1, 0))


def span(width, side, first, quarters):
    cuts = (0, side, width // 2, width - side, width)
    return pl.ds(cuts[first], cuts[first + quarters] - cuts[first])


def gather_events(own, full, sides, send_sem, recv_sem, local_sem):
    n = len(own)
    z, x, c, y = here()

    def block(k, xo, co, yo):
        h = own[k].shape[0]
        return pl.ds(pl.multiple_of(((xo * 2 + co) * 2 + yo) * h, h), h)

    def part(k, zo, xo, yo, first=0, quarters=4):
        return full[k].at[zo, block(k, xo, c, yo), span(own[k].shape[1], sides[k], first, quarters)]

    def link(k, slot, src, dst, to):
        return pltpu.make_async_remote_copy(
            src_ref=src, dst_ref=dst, send_sem=send_sem.at[k, slot], recv_sem=recv_sem.at[k, slot],
            device_id=to, device_id_type=MESH)

    xp = place(z, 1 - x, c, y)
    yp = place(z, x, c, 1 - y)
    cpart = place(z, x, 1 - c, y)

    def zto(d):
        return place(z + 1 - 2 * d, x, c, y)

    def z_has(d, s):
        return (z - s >= 0) if d == 0 else (z + s <= ZN - 1)

    def z_next(d):
        return (z < ZN - 1) if d == 0 else (z > 0)

    def zo_of(d, s):
        return z - s if d == 0 else z + s

    def z_send(k, base, d, s, xo, yo, first, quarters, src=None):
        cond = jnp.logical_and(z_has(d, s), z_next(d))
        zo = zo_of(d, s)
        dst = part(k, zo, xo, yo, first, quarters)
        cp = link(k, base + d * 3 + s, dst if src is None else src, dst, zto(d))

        @pl.when(cond)
        def _():
            cp.start()

    def z_wait(k, base, d, s, xo, yo, first, quarters):
        zo = zo_of(d, s + 1)
        dst = part(k, zo, xo, yo, first, quarters)
        link(k, base + d * 3 + s, dst, dst, zto(d)).wait_recv()

    def go(k, slot, ref, to, src=None, cond=None):
        cp = link(k, slot, ref if src is None else src, ref, to)
        cp.start()

    def wait(k, slot, ref):
        link(k, slot, ref, ref, xp).wait_recv()

    def begin():
        for k in range(n):
            pltpu.make_async_copy(own[k], part(k, z, x, y), local_sem.at[k]).start()

    def do(k, e):
        kind = e[0]
        if kind == "own":
            for d in (0, 1):
                z_send(k, ZM, d, 0, x, y, 0, 4, src=own[k])
            go(k, XM + z, part(k, z, x, y), xp, src=own[k])
            go(k, YM + z, part(k, z, x, y), yp, src=own[k])
        elif kind == "near":
            wait(k, XM + z, part(k, z, 1 - x, y))
            for d in (0, 1):
                z_send(k, ZX, d, 0, 1 - x, y, 0, 1)
            go(k, YX + z, part(k, z, 1 - x, y, 0, 2), yp)
            wait(k, YM + z, part(k, z, x, 1 - y))
            for d in (0, 1):
                z_send(k, ZY, d, 0, x, 1 - y, 3, 1)
            go(k, XY + z, part(k, z, x, 1 - y, 2, 2), xp)
        elif kind == "chain":
            s = e[1]
            for d in (0, 1):
                @pl.when(z_has(d, s + 1))
                def _():
                    z_wait(k, ZM, d, s, x, y, 0, 4)
                    zo = zo_of(d, s + 1)
                    if s < 2:
                        @pl.when(z_next(d))
                        def _():
                            ref = part(k, zo, x, y)
                            link(k, ZM + d * 3 + s + 1, ref, ref, zto(d)).start()
                    ref = part(k, zo, x, y, 1, 3)
                    link(k, XM + zo, ref, ref, xp).start()
                    ref = part(k, zo, x, y, 0, 3)
                    link(k, YM + zo, ref, ref, yp).start()
        elif kind == "side":
            s = e[1]
            for d in (0, 1):
                @pl.when(z_has(d, s + 1))
                def _():
                    zo = zo_of(d, s + 1)
                    for base, xo, yo, first in ((ZX, 1 - x, y, 0), (ZY, x, 1 - y, 3)):
                        z_wait(k, base, d, s, xo, yo, first, 1)
                        if s < 2:
                            @pl.when(z_next(d))
                            def _():
                                ref = part(k, zo, xo, yo, first, 1)
                                link(k, base + d * 3 + s + 1, ref, ref, zto(d)).start()
        elif kind == "cross":
            s = e[1]
            for d in (0, 1):
                @pl.when(z_has(d, s + 1))
                def _():
                    zo = zo_of(d, s + 1)
                    wait(k, XM + zo, part(k, zo, 1 - x, y, 1, 3))
                    ref = part(k, zo, 1 - x, y, 0, 2)
                    link(k, YX + zo, ref, ref, yp).start()
                    wait(k, YM + zo, part(k, zo, x, 1 - y, 0, 3))
                    ref = part(k, zo, x, 1 - y, 2, 2)
                    link(k, XY + zo, ref, ref, xp).start()
            if s == 0:
                pltpu.make_async_copy(own[k], part(k, z, x, y), local_sem.at[k]).wait()
                ref = full[k].at[:, block(k, x, c, y), :]
                link(k, CP, ref, ref, cpart).start()
            if s == 2:
                ref = full[k].at[:, block(k, 1 - x, c, y), :]
                link(k, CP + 1, ref, ref, cpart).start()
                ref = full[k].at[:, block(k, x, c, 1 - y), :]
                link(k, CP + 2, ref, ref, cpart).start()
        elif kind == "last":
            for zo in range(ZN):
                wait(k, XY + zo, part(k, zo, 1 - x, 1 - y, 2, 2))
                wait(k, YX + zo, part(k, zo, 1 - x, 1 - y, 0, 2))
            ref = full[k].at[:, block(k, 1 - x, c, 1 - y), :]
            link(k, CP + 3, ref, ref, cpart).start()
        elif kind == "ready":
            for j, (xo, yo) in enumerate(((x, y), (1 - x, y), (x, 1 - y), (1 - x, 1 - y))):
                ref = full[k].at[:, block(k, xo, 1 - c, yo), :]
                link(k, CP + j, ref, ref, cpart).wait_recv()

    def finish():
        for k in range(n):
            for j, (xo, yo) in enumerate(((x, y), (1 - x, y), (x, 1 - y), (1 - x, 1 - y))):
                ref = full[k].at[:, block(k, xo, c, yo), :]
                link(k, CP + j, ref, ref, cpart).wait_send()
            for d in (0, 1):
                for s in range(3):
                    @pl.when(jnp.logical_and(z_has(d, s), z_next(d)))
                    def _():
                        zo = zo_of(d, s)
                        for base, xo, yo, first, q in ((ZM, x, y, 0, 4), (ZX, 1 - x, y, 0, 1), (ZY, x, 1 - y, 3, 1)):
                            ref = part(k, zo, xo, yo, first, q)
                            link(k, base + d * 3 + s, ref, ref, zto(d)).wait_send()
            ref = part(k, z, x, y)
            link(k, XM + z, ref, ref, xp).wait_send()
            link(k, YM + z, ref, ref, yp).wait_send()
            for t in range(1, ZN):
                zo = lax.rem(z + t, ZN)
                ref = part(k, zo, x, y, 1, 3)
                link(k, XM + zo, ref, ref, xp).wait_send()
                ref = part(k, zo, x, y, 0, 3)
                link(k, YM + zo, ref, ref, yp).wait_send()
            for zo in range(ZN):
                ref = part(k, zo, 1 - x, y, 0, 2)
                link(k, YX + zo, ref, ref, yp).wait_send()
                ref = part(k, zo, x, 1 - y, 2, 2)
                link(k, XY + zo, ref, ref, xp).wait_send()

    return begin, do, finish


def scatter_events(outs, part_sums, sides, landings, send_sem, recv_sem):
    n = len(outs)
    lxm, lym, lxy, lyx, lzm, lzx, lzy = landings
    z, x, c, y = here()
    xp = place(z, 1 - x, c, y)
    yp = place(z, x, c, 1 - y)

    def rows_of(k):
        return outs[k].shape[0]

    def width(k):
        return outs[k].shape[1]

    def mine(k, zo, xo, yo, first=0, quarters=4):
        h = rows_of(k)
        row = pl.multiple_of(((zo * 2 + xo) * 2 + yo) * h, h)
        return part_sums[k].at[pl.ds(row, h), span(width(k), sides[k], first, quarters)]

    def link(k, slot, src, dst, to):
        return pltpu.make_async_remote_copy(
            src_ref=src, dst_ref=dst, send_sem=send_sem.at[k, slot], recv_sem=recv_sem.at[k, slot],
            device_id=to, device_id_type=MESH)

    def quarter_slice(k, first, quarters):
        return span(width(k), sides[k], first, quarters)

    def land_x(k, zo, first, quarters):
        return lxm[k].at[zo, :, quarter_slice(k, first, quarters)]

    def land_y(k, zo, first, quarters):
        return lym[k].at[zo, :, quarter_slice(k, first, quarters)]

    def z_has(d, s):
        return (z - s >= 0) if d == 0 else (z + s <= ZN - 1)

    def z_next(d):
        return (z < ZN - 1) if d == 0 else (z > 0)

    def zo_of(d, s):
        return z - s if d == 0 else z + s

    def z_slot(d, s, zo):
        return ZN if (d == 1 and s == 0) else zo

    def toward(d):
        return place(z - 1 + 2 * d, x, c, y)

    def add_in(k, zo, xo, yo, first, quarters, others):
        ref = mine(k, zo, xo, yo, first, quarters)
        h = rows_of(k)

        @pl.loop(0, h // 16)
        def _(i):
            rows = pl.ds(pl.multiple_of(i * 16, 16), 16)
            total = ref[rows, :].astype(f32)
            for o in others:
                total = total + o[rows, :].astype(f32)
            ref[rows, :] = total.astype(bf16)

    def wait(k, slot, dst):
        link(k, slot, dst, dst, xp).wait_recv()

    def do(k, e):
        kind = e[0]
        if kind == "last":
            for zo in range(ZN):
                link(k, XY + zo, mine(k, zo, 1 - x, 1 - y, 2, 2), lxy[k].at[zo], xp).start()
                link(k, YX + zo, mine(k, zo, 1 - x, 1 - y, 0, 2), lyx[k].at[zo], yp).start()
        elif kind == "cross":
            s = e[1]
            for d in (0, 1):
                @pl.when(z_has(d, s + 1))
                def _():
                    zo = zo_of(d, s + 1)
                    wait(k, YX + zo, lyx[k].at[zo])
                    add_in(k, zo, 1 - x, y, 0, 2, [lyx[k].at[zo]])
                    link(k, XM + zo, mine(k, zo, 1 - x, y, 1, 3), land_x(k, zo, 1, 3), xp).start()
                    wait(k, XY + zo, lxy[k].at[zo])
                    add_in(k, zo, x, 1 - y, 2, 2, [lxy[k].at[zo]])
                    link(k, YM + zo, mine(k, zo, x, 1 - y, 0, 3), land_y(k, zo, 0, 3), yp).start()
        elif kind == "side":
            s = e[1]
            for d in (0, 1):
                @pl.when(z_has(d, s + 1))
                def _():
                    zo = zo_of(d, s + 1)
                    for base, landing, xo, yo, first in ((ZX, lzx, 1 - x, y, 0), (ZY, lzy, x, 1 - y, 3)):
                        if s < 2:
                            @pl.when(z_next(d))
                            def _():
                                got = landing[k].at[z_slot(d, s + 1, zo)]
                                wait(k, base + d * 3 + s + 1, got)
                                add_in(k, zo, xo, yo, first, 1, [got])
                        link(k, base + d * 3 + s, mine(k, zo, xo, yo, first, 1),
                             landing[k].at[z_slot(d, s, zo)], toward(d)).start()
        elif kind == "chain":
            s = e[1]
            for d in (0, 1):
                @pl.when(z_has(d, s + 1))
                def _():
                    zo = zo_of(d, s + 1)
                    wait(k, XM + zo, land_x(k, zo, 1, 3))
                    wait(k, YM + zo, land_y(k, zo, 0, 3))
                    add_in(k, zo, x, y, 0, 1, [land_y(k, zo, 0, 1)])
                    add_in(k, zo, x, y, 1, 2, [land_y(k, zo, 1, 2), land_x(k, zo, 1, 2)])
                    add_in(k, zo, x, y, 3, 1, [land_x(k, zo, 3, 1)])
                    if s < 2:
                        @pl.when(z_next(d))
                        def _():
                            got = lzm[k].at[z_slot(d, s + 1, zo)]
                            wait(k, ZM + d * 3 + s + 1, got)
                            add_in(k, zo, x, y, 0, 4, [got])
                    link(k, ZM + d * 3 + s, mine(k, zo, x, y), lzm[k].at[z_slot(d, s, zo)], toward(d)).start()
        elif kind == "near":
            for slot, own_slot, xo, yo, first, cross_land, side_base, side_land, side_first, to, land in (
                (YX, XM, 1 - x, y, 0, lyx, ZX, lzx, 0, xp, land_x),
                (XY, YM, x, 1 - y, 2, lxy, ZY, lzy, 3, yp, land_y),
            ):
                wait(k, slot + z, cross_land[k].at[z])
                add_in(k, z, xo, yo, first, 2, [cross_land[k].at[z]])
                for d in (0, 1):
                    @pl.when(z_next(d))
                    def _():
                        got = side_land[k].at[z_slot(d, 0, z)]
                        wait(k, side_base + d * 3, got)
                        add_in(k, z, xo, yo, side_first, 1, [got])
                link(k, own_slot + z, mine(k, z, xo, yo), land(k, z, 0, 4), to).start()
        elif kind == "own":
            wait(k, XM + z, land_x(k, z, 0, 4))
            wait(k, YM + z, land_y(k, z, 0, 4))
            h = rows_of(k)
            own = mine(k, z, x, y)
            from_x, from_y = land_x(k, z, 0, 4), land_y(k, z, 0, 4)

            @pl.loop(0, h // 16)
            def _(i):
                rows = pl.ds(pl.multiple_of(i * 16, 16), 16)
                outs[k][rows, :] = own[rows, :].astype(f32) + from_x[rows, :].astype(f32) + from_y[rows, :].astype(f32)

            for d in (0, 1):
                @pl.when(z_next(d))
                def _():
                    got = lzm[k].at[z_slot(d, 0, z)]
                    wait(k, ZM + d * 3, got)

                    @pl.loop(0, h // 16)
                    def _(i):
                        rows = pl.ds(pl.multiple_of(i * 16, 16), 16)
                        outs[k][rows, :] += got[rows, :].astype(f32)

    def finish():
        for k in range(n):
            for zo in range(ZN):
                link(k, XY + zo, mine(k, zo, 1 - x, 1 - y, 2, 2), lxy[k].at[zo], xp).wait_send()
                link(k, YX + zo, mine(k, zo, 1 - x, 1 - y, 0, 2), lyx[k].at[zo], yp).wait_send()
            for t in range(1, ZN):
                zo = lax.rem(z + t, ZN)
                link(k, XM + zo, mine(k, zo, 1 - x, y, 1, 3), land_x(k, zo, 1, 3), xp).wait_send()
                link(k, YM + zo, mine(k, zo, x, 1 - y, 0, 3), land_y(k, zo, 0, 3), yp).wait_send()
            link(k, XM + z, mine(k, z, 1 - x, y), land_x(k, z, 0, 4), xp).wait_send()
            link(k, YM + z, mine(k, z, x, 1 - y), land_y(k, z, 0, 4), yp).wait_send()
            for d in (0, 1):
                for s in range(3):
                    @pl.when(z_has(d, s + 1))
                    def _():
                        zo = zo_of(d, s + 1)
                        to = z_slot(d, s, zo)
                        link(k, ZX + d * 3 + s, mine(k, zo, 1 - x, y, 0, 1), lzx[k].at[to], toward(d)).wait_send()
                        link(k, ZY + d * 3 + s, mine(k, zo, x, 1 - y, 3, 1), lzy[k].at[to], toward(d)).wait_send()
                        link(k, ZM + d * 3 + s, mine(k, zo, x, y), lzm[k].at[to], toward(d)).wait_send()

    return do, finish


HEADS = 16


epsilon = 1e-05


def nn(a, b):
    return jnp.dot(a, b, preferred_element_type=f32)


def nt(a, b):
    return lax.dot_general(a, b, (((1,), (1,)), ((), ())), preferred_element_type=f32)


def tn(a, b):
    return lax.dot_general(a, b, (((0,), (0,)), ((), ())), preferred_element_type=f32)


CH = 1024
SKIP, QKV, OUT, UP, DOWN = range(5)
CHUNKS = (
    [(SKIP, 0), (SKIP, 1), (QKV, 0), (QKV, 1), (QKV, 2), (OUT, 0)] + [(UP, i) for i in range(4)]
    + [(DOWN, i) for i in range(4)] + [(UP, i) for i in range(4)] + [(OUT, 0)] + [(QKV, i) for i in range(3)]
    + [(SKIP, 0), (SKIP, 1)]
)
LEFTS = [(DOWN, 0), (DOWN, 1), (DOWN, 2), (DOWN, 3), (UP, 0), (OUT, 0), (QKV, 0), (SKIP, 0), (SKIP, 1)]
GATHER_PIECES = [(0, 0, 1024, 128), (1, 0, 3072, 640), (2, 0, 1024, 384), (3, 0, 2048, 768), (3, 2048, 2048, 896), (4, 0, 512, 128), (4, 512, 512, 128)]
SCATTER_PIECES = [(4, 0, 1024, 128), (3, 0, 4096, 1024), (2, 0, 1024, 256), (1, 0, 3072, 640), (0, 0, 512, 128), (0, 512, 512, 128)]
STAGES = [("own",), ("near",)] + [(e, s) for s in range(3) for e in ("chain", "side")] + [
    ("cross", s) for s in range(3)] + [("last",), ("ready",)]
(PR, MK, TR, F1, F2, F3, AF, F5, F6, F7, F8, FR, B2, B3, B5, B6, A, L1, L2, R, W0, W1, W2, W3, W4, BF,
 G0, G1, G2, G3, G4, G5, G6, E0, E1, E2, E3, E4, E5) = range(39)
GATHER = [G0, G1, G2, G3, G4, G5, G6]
SCATTER = [E0, E1, E2, E3, E4, E5]
PLAN = [
    (G0, 0), (G1, 0), (PR, 0), (MK, 0), (TR, 7), (PR, 1), (TR, 8), (G0, 1),
    (G0, 2), (G1, 1), (G2, 0), (G1, 2), (G0, 3), (PR, 2), (G0, 4), (G1, 3),
    (G2, 1), (G2, 2), (G1, 4), (G0, 5), (G0, 6), (G1, 5), (PR, 3), (G2, 3),
    (G3, 0), (G2, 4), (G1, 6), (G0, 7), (G0, 8), (G0, 9), (G0, 10), (G1, 7),
    (G1, 8), (G1, 9), (PR, 4), (G2, 5), (G1, 10), (G3, 1), (G4, 0), (G3, 2),
    (G2, 6), (PR, 5), (G0, 11), (G2, 7), (G2, 8), (G2, 9), (G3, 3), (G0, 12),
    (F1, 0), (F1, 1), (G1, 11), (F2, 0), (F2, 1), (G3, 4), (F2, 2), (F2, 3),
    (TR, 6), (G1, 12), (G3, 5), (G4, 1), (G4, 2), (G5, 0), (F3, 0), (G2, 10),
    (G3, 6), (F3, 1), (G3, 7), (G3, 8), (F3, 2), (AF, 0), (G4, 3), (G3, 9),
    (AF, 1), (G2, 11), (G4, 4), (AF, 2), (G2, 12), (G5, 1), (G4, 5), (G5, 2),
    (G3, 10), (AF, 3), (G4, 6), (TR, 5), (F5, 0), (G5, 3), (G6, 0), (G4, 7),
    (G4, 8), (G4, 9), (G3, 11), (F6, 0), (F6, 1), (G4, 10), (F6, 2), (G5, 4),
    (F6, 3), (G5, 5), (G3, 12), (TR, 4), (F7, 0), (G6, 1), (G6, 2), (TR, 0),
    (F7, 1), (G4, 11), (G5, 6), (G5, 7), (G6, 3), (G5, 8), (TR, 1), (G5, 9),
    (G4, 12), (F7, 2), (G6, 4), (G6, 5), (G5, 10), (TR, 2), (F7, 3), (TR, 3),
    (G6, 6), (G5, 11), (G6, 7), (G6, 8), (W4, 0), (G6, 9), (G6, 10), (G5, 12),
    (W4, 1), (E0, 11), (G6, 11), (G6, 12), (F8, 0), (BF, 0), (F8, 1), (BF, 1),
    (F8, 2), (BF, 2), (E0, 10), (E0, 9), (E0, 8), (E0, 7), (F8, 3), (BF, 3),
    (FR, 0), (B2, 0), (B2, 1), (E0, 6), (E0, 5), (B2, 2), (B2, 3), (W3, 0),
    (W3, 1), (E1, 11), (E0, 4), (L2, 0), (E0, 3), (L2, 1), (L2, 2), (L2, 3),
    (B3, 0), (E0, 2), (E0, 1), (A, 0), (E1, 10), (E1, 9), (E1, 8), (E1, 7),
    (W2, 0), (E2, 11), (A, 1), (A, 2), (E0, 0), (A, 3), (E1, 6), (E1, 5),
    (B5, 0), (B5, 1), (B5, 2), (W1, 0), (W1, 1), (E3, 11), (E1, 4), (L1, 0),
    (E2, 10), (E2, 9), (E2, 8), (E2, 7), (E1, 3), (L1, 1), (L1, 2), (L1, 3),
    (E1, 2), (R, 0), (E3, 10), (E3, 9), (E3, 8), (E2, 6), (E2, 5), (E3, 7),
    (E1, 1), (W0, 0), (E4, 11), (W0, 1), (E5, 11), (R, 1), (E3, 6), (E2, 4),
    (E2, 3), (E3, 5), (E3, 4), (E2, 2), (E2, 1), (E3, 3), (E1, 0), (E4, 10),
    (E4, 9), (E4, 8), (E4, 7), (E3, 2), (E5, 10), (E5, 9), (E5, 8), (E5, 7),
    (R, 2), (E3, 1), (B6, 0), (E2, 0), (E4, 6), (E4, 5), (E5, 6), (E5, 5),
    (E4, 4), (R, 3), (E4, 3), (B6, 1), (E5, 4), (E5, 3), (E4, 2), (E3, 0),
    (R, 4), (E4, 1), (E5, 2), (E5, 1), (E4, 0), (R, 5), (E5, 0),
]


def layer_kernel(*refs):
    n = 5
    tokens, skip, cot, seg, valid = refs[:5]
    vectors = refs[5:12]
    own = refs[12 : 12 + n]
    small_out = refs[17]
    targets = refs[18:23]
    result, grad_tokens, grad_skip = refs[23:26]
    full = refs[26:31]
    outs = refs[31 : 31 + n]
    r = refs[31 + n :]
    turned, theirs, gcat, part_sums = r[:n], r[n : 2 * n], r[2 * n : 3 * n], r[3 * n : 4 * n]
    m = len(SCATTER_PIECES)
    landings = [r[4 * n + i * m : 4 * n + (i + 1) * m] for i in range(7)]
    (wbuf, lbuf, hid, gnorm, mid, pbuf, abuf, acc, small, small_land, params, params_wide, params_land,
     log_total, steep, distance,
     ag_send, ag_recv, ag_local, rs_send, rs_recv, pair_send, pair_recv, wsem, lsem, misc_sem,
     small_send, small_recv, params_send, params_recv, out_sem) = r[4 * n + 7 * m :]
    z, x, c, y = here()
    cpart = place(z, x, 1 - c, y)
    T = cot.shape[0]

    ag_begin, ag_do, ag_finish = gather_events(
        [own[k].at[:, pl.ds(at, w)] for k, at, w, _ in GATHER_PIECES],
        [full[k].at[:, :, pl.ds(at, w)] for k, at, w, _ in GATHER_PIECES], [p[3] for p in GATHER_PIECES], ag_send, ag_recv, ag_local)
    rs_do, rs_finish = scatter_events(
        [outs[k].at[:, pl.ds(at, w)] for k, at, w, _ in SCATTER_PIECES],
        [part_sums[k].at[:, pl.ds(at, w)] for k, at, w, _ in SCATTER_PIECES], [p[3] for p in SCATTER_PIECES], landings, rs_send, rs_recv)

    def chunk_copies(i):
        k, j = CHUNKS[i]
        slot, depth = i % 2, full[k].shape[1]
        if k in (SKIP, DOWN):
            blocks = CH // depth
            return [pltpu.make_async_copy(full[k].at[j * blocks + b], wbuf.at[slot, pl.ds(b * depth, depth), :], wsem.at[slot, b])
                    for b in range(blocks)]
        return [pltpu.make_async_copy(full[k].at[b, :, pl.ds(j * CH, CH)], wbuf.at[slot, pl.ds(b * depth, depth), :], wsem.at[slot, b])
                for b in range(ZN)]

    state = {"next": 0, "done": 0, "ready": set()}

    def arrived(i):
        k, j = CHUNKS[i]
        lo, hi = (j * CH, (j + 1) * CH) if k in (QKV, UP) else (0, CH)
        return all(p in state["ready"] for p, (w, at, wide, _) in enumerate(GATHER_PIECES) if w == k and at < hi and at + wide > lo)

    def pump():
        while state["next"] < min(len(CHUNKS), state["done"] + 2) and arrived(state["next"]):
            for cp in chunk_copies(state["next"]):
                cp.start()
            state["next"] += 1

    def ready(k):
        state["ready"].add(k)
        pump()

    def take(i):
        assert state["done"] == i and state["next"] > i
        for cp in chunk_copies(i):
            cp.wait()

    def release(i):
        state["done"] = i + 1
        pump()

    in_copies = [pltpu.make_async_copy(a, lbuf.at[i], lsem.at[i]) for i, a in enumerate((tokens, skip))]
    cot_copy = pltpu.make_async_copy(cot, gcat[DOWN].at[pl.ds(0, T), :], misc_sem.at[0])
    result_copy = pltpu.make_async_copy(lbuf.at[0], result, misc_sem.at[1])
    out_copies = [pltpu.make_async_copy(lbuf.at[i], o, misc_sem.at[2 + i]) for i, o in enumerate((grad_tokens, grad_skip))]
    grad_copies = [pltpu.make_async_copy(outs[k].at[:, pl.ds(at, w)], targets[k].at[:, pl.ds(at, w)], out_sem.at[p])
                   for p, (k, at, w, _) in enumerate(SCATTER_PIECES)]
    ag_begin()
    for cp in in_copies:
        cp.start()
    cot_copy.start()
    greet_partners()

    def pair(k, j):
        if k == DOWN and j != 1:
            rows = pl.ds(CH // 2 * (j - 1 if j else 0), CH // 2)
            src, dst = turned[k].at[1 - c, rows, :], theirs[k].at[rows, :]
        elif j == 0:
            src, dst = turned[k].at[1 - c], theirs[k]
        elif k == DOWN:
            src, dst = cot, gcat[k].at[pl.ds(T, T), :]
        elif k == UP:
            cols = pl.ds((j - 1) * CH, CH)
            src, dst = gcat[k].at[pl.ds(0, T), cols], gcat[k].at[pl.ds(T, T), cols]
        else:
            src, dst = gcat[k].at[pl.ds(0, T), :], gcat[k].at[pl.ds(T, T), :]
        return pltpu.make_async_remote_copy(
            src_ref=src, dst_ref=dst, send_sem=pair_send.at[k, j], recv_sem=pair_recv.at[k, j],
            device_id=cpart, device_id_type=MESH)

    def pieces(k):
        return range(5) if k in (UP, DOWN) else range(2)

    meet = [cpart, place(z, 1 - x, c, y), place(z, x, c, 1 - y),
            place(z + 1 - 2 * lax.rem(z, 2), x, c, y), place(lax.rem(z + 2, 4), x, c, y)]

    def meeting(ref, land, send, recv, t):
        return pltpu.make_async_remote_copy(
            src_ref=ref, dst_ref=land.at[t], send_sem=send.at[t], recv_sem=recv.at[t],
            device_id=meet[t], device_id_type=MESH)

    def params_step(t):
        if t == 0:
            me = lax.axis_index("wide") * 2 + lax.axis_index("narrow")
            params_wide[...] = jnp.zeros_like(params_wide)
            for i in range(6):
                params_wide[i : i + 1, 0:32] = vectors[i][...].astype(f32)
            narrow = pltpu.roll(params_wide[...], me * 32, 1)
            params_wide[...] = jnp.zeros_like(params_wide)
            for i in range(4):
                params_wide[6 + i : 7 + i, 0:128] = vectors[6][...].astype(f32)
            wide = pltpu.roll(params_wide[...], lax.rem(me, 8) * 128, 1)
            row = lax.broadcasted_iota(jnp.int32, wide.shape, 0)
            params[...] = jnp.where(row == 6 + lax.div(me, 8), wide, narrow).astype(bf16)
        else:
            cp = meeting(params, params_land, params_send, params_recv, t - 1)
            cp.wait_send()
            cp.wait_recv()
            params[...] = (params[...].astype(f32) + params_land[t - 1].astype(f32)).astype(bf16)
        if t < 5:
            meeting(params, params_land, params_send, params_recv, t).start()
        else:
            params_wide[...] = params[...].astype(f32)

    def small_step(t):
        if t:
            cp = meeting(small, small_land, small_send, small_recv, t - 1)
            cp.wait_send()
            cp.wait_recv()
            small[...] += small_land[t - 1]
        if t < 5:
            meeting(small, small_land, small_send, small_recv, t).start()
        else:
            small_out[...] = small[...]

    def make_masks():
        acc[...] = jnp.zeros_like(acc)
        small[...] = jnp.zeros_like(small)
        heads = lax.broadcasted_iota(jnp.int32, steep.shape, 0).astype(f32)
        steep[...] = jnp.exp((heads + 1.0) * -0.34657359027997264)
        seg_row = jnp.broadcast_to(seg[...].astype(f32), (T, T))
        live = jnp.broadcast_to(valid[...].astype(f32), (T, T)).T
        key_at = lax.broadcasted_iota(jnp.int32, (T, T), 0)
        query_at = lax.broadcasted_iota(jnp.int32, (T, T), 1)
        allowed = jnp.logical_and(seg_row.T == seg_row, jnp.logical_or(live == 1.0, key_at == query_at))
        distance[...] = jnp.where(allowed, jnp.abs(key_at - query_at).astype(f32), 1e33)
        pair(DOWN, 1).start()

    def turn(i):
        k, j = LEFTS[i]
        group = 2 * outs[k].shape[0]
        seg = min(group, 128)
        if k == SKIP:
            in_copies[j].wait()
        for t in range(CH // 128):
            cols = slice(t * 128, (t + 1) * 128)
            if k == SKIP:
                block = lbuf[j, :, cols].T
            elif k == DOWN:
                block = part_sums[UP][0:T, j * CH + t * 128 : j * CH + (t + 1) * 128].T
            else:
                block = abuf[:, cols].T
            for s in range(0, 128, seg):
                row = j * CH + t * 128 + s
                core, at = (row // group) % 2, row // (2 * group) * group + row % group
                turned[k][core, at : at + seg, :] = block[s : s + seg, :]
        if k == DOWN:
            pair(k, j + 1 if j else 0).start()
        elif i + 1 == len(LEFTS) or LEFTS[i + 1][0] != k:
            pair(k, 0).start()

    def forward_product(left, slot, finish):
        @pl.loop(0, 2)
        def _(j):
            at = pl.multiple_of(j * 512, 512)
            finish(at, nn(left(), wbuf[slot, :, pl.ds(at, 512)]))

    def back_product(left, slot, finish):
        @pl.loop(0, 2)
        def _(j):
            at = pl.multiple_of(j * 512, 512)
            finish(at, nt(left(), wbuf[slot, pl.ds(at, 512), :]))

    def store_in(ref, offset=0):
        def finish(at, value):
            ref[:, pl.ds(pl.multiple_of(at + offset, 512), 512)] = value.astype(ref.dtype)

        return finish

    def add_to(ref):
        def finish(at, value):
            ref[:, pl.ds(at, 512)] += value

        return finish

    def to_hidden(i):
        take(i)

        def first(at, value):
            hid[:, pl.ds(at, 512)] = value + params_wide[0:1, pl.ds(at, 512)]

        forward_product(lambda: lbuf[i], i % 2, add_to(hid) if i else first)
        release(i)

    def norm_forward(source, gain, i):
        @pl.loop(0, 4)
        def _(j):
            rows = pl.ds(pl.multiple_of(i * 64 + j * 16, 16), 16)
            v = source[rows, :]
            center = v - jnp.mean(v, axis=-1, keepdims=True)
            rate = lax.rsqrt(jnp.mean(center * center, axis=-1, keepdims=True) + epsilon)
            abuf[rows, :] = (
                center * rate * params_wide[gain : gain + 1, :] + params_wide[gain + 1 : gain + 2, :]).astype(bf16)

    def to_projected(i):
        take(2 + i)
        forward_product(lambda: abuf[...], i % 2, store_in(pbuf, i * CH))
        release(2 + i)

    def heads_of(p):
        at = pl.multiple_of(p * 128, 128)
        return [pbuf[:, pl.ds(pl.multiple_of(at + j * CH, 128), 128)] for j in range(3)]

    def half_masks():
        low = lax.broadcasted_iota(jnp.int32, (T, 128), 1) < 64
        return low, jnp.logical_not(low)

    def attend(i):
        masks = half_masks()

        @pl.loop(2 * i, 2 * i + 2)
        def _(p):
            q, k, v = heads_of(p)
            res = []
            for e in (0, 1):
                head = pl.ds(2 * p + e, 1)
                scores = nt(k, jnp.where(masks[e], q, jnp.zeros_like(q))) * 0.125 - distance[...] * steep[head, :]
                top = jnp.max(scores, axis=0, keepdims=True)
                raised = jnp.exp(scores - top)
                total = jnp.sum(raised, axis=0, keepdims=True)
                log_total[head, :] = top + jnp.log(total)
                res.append(tn((raised / total).astype(bf16), v))
            abuf[:, pl.ds(pl.multiple_of(p * 128, 128), 128)] = jnp.where(masks[0], res[0], res[1]).astype(bf16)

    def to_middle():
        take(5)

        def finish(at, value):
            mid[:, pl.ds(at, 512)] = hid[:, pl.ds(at, 512)] + value

        forward_product(lambda: abuf[...], 1, finish)
        release(5)

    def to_activated(i):
        take(6 + i)

        def finish(at, value):
            cols = pl.ds(pl.multiple_of(i * CH + at, 512), 512)
            u = value + params_wide[6 + i : 7 + i, pl.ds(at, 512)]
            cdf = 0.5 * (1.0 + lax.erf(u * 0.7071067811865476))
            part_sums[UP][0:T, cols] = (u * cdf).astype(bf16)
            gcat[UP][0:T, cols] = (cdf + u * jnp.exp(-0.5 * u * u) * 0.3989422804014327).astype(bf16)

        forward_product(lambda: abuf[...], i % 2, finish)
        release(6 + i)

    def through_down(i):
        take(10 + i)
        forward_product(
            lambda: part_sums[UP][0:T, i * CH : (i + 1) * CH], i % 2, add_to(gnorm) if i else store_in(gnorm))

    def back_through_down(i):
        def finish(at, value):
            cols = pl.ds(pl.multiple_of(i * CH + at, 512), 512)
            got = (value * gcat[UP][0:T, cols].astype(f32)).astype(bf16)
            gcat[UP][0:T, cols] = got
            small[6 + i : 7 + i, pl.ds(at, 512)] = jnp.sum(got.astype(f32), axis=0, keepdims=True)

        back_product(lambda: gcat[DOWN][0:T, :], i % 2, finish)
        release(10 + i)
        pair(UP, 1 + i).start()

    def to_result():
        @pl.loop(0, T // 16)
        def _(i):
            rows = pl.ds(pl.multiple_of(i * 16, 16), 16)
            lbuf[0, rows, :] = (mid[rows, :] + (gnorm[rows, :] + params_wide[5:6, :])).astype(bf16)

        result_copy.start()

    def weight_product(k, lo, hi):
        tiles = (hi - lo) // 512
        if lo == 0:
            if k == DOWN:
                cot_copy.wait()
                small[5:6, :] = jnp.sum(gcat[DOWN][0:T, :].astype(f32), axis=0, keepdims=True)
            for j in pieces(k):
                pair(k, j).wait_recv()

        @pl.loop(0, part_sums[k].shape[0] // 256 * tiles)
        def _(i):
            rows = pl.ds(pl.multiple_of(lax.div(i, tiles) * 256, 256), 256)
            cols = pl.ds(pl.multiple_of(lo + lax.rem(i, tiles) * 512, 512), 512)
            both = nn(turned[k][c, rows, :], gcat[k][pl.ds(0, T), cols])
            both += nn(theirs[k][rows, :], gcat[k][pl.ds(T, T), cols])
            part_sums[k][rows, cols] = both.astype(bf16)

    def into_norm(i, base, k):
        take(base + i)
        back_product(lambda: gcat[k][0:T, i * CH : (i + 1) * CH], (base + i) % 2, add_to(gnorm) if i else store_in(gnorm))
        release(base + i)

    def norm_back(source, i, gain, base, emit):
        @pl.loop(0, 4)
        def _(j):
            rows = pl.ds(pl.multiple_of(i * 64 + j * 16, 16), 16)
            v = source[rows, :]
            center = v - jnp.mean(v, axis=-1, keepdims=True)
            rate = lax.rsqrt(jnp.mean(center * center, axis=-1, keepdims=True) + epsilon)
            xhat = center * rate
            g = gnorm[rows, :]
            gx = g * xhat
            acc[base] += gx[0:8] + gx[8:16]
            acc[base + 1] += g[0:8] + g[8:16]
            e = g * params_wide[gain : gain + 1, :]
            emit(rows, rate * (e - jnp.mean(e, axis=-1, keepdims=True) - xhat * jnp.mean(e * xhat, axis=-1, keepdims=True)))

    def second_norm(i):
        def emit(rows, value):
            total = gcat[DOWN][rows, :].astype(f32) + value
            mid[rows, :] = total
            gcat[OUT][rows, :] = total.astype(bf16)

        norm_back(mid, i, 3, 0, emit)
        if i == 3:
            pair(OUT, 1).start()

    def to_attended():
        take(18)
        back_product(lambda: gcat[OUT][0:T, :], 0, store_in(abuf))
        release(18)

    def attend_back(i):
        masks = half_masks()

        @pl.loop(2 * i, 2 * i + 2)
        def _(p):
            at = pl.multiple_of(p * 128, 128)
            q, k, v = heads_of(p)
            g = abuf[:, pl.ds(at, 128)]
            res = []
            for e in (0, 1):
                head = pl.ds(2 * p + e, 1)
                scores = nt(k, jnp.where(masks[e], q, jnp.zeros_like(q))) * 0.125 - distance[...] * steep[head, :]
                probable = jnp.exp(scores - log_total[head, :])
                gp = nt(v, jnp.where(masks[e], g, jnp.zeros_like(g)))
                gv = nn(probable.astype(bf16), g)
                inner = jnp.sum(gp * probable, axis=0, keepdims=True)
                gs = (probable * (gp - inner)).astype(bf16)
                res.append((tn(gs, k) * 0.125, nn(gs, q) * 0.125, gv))
            for j in range(3):
                gcat[QKV][0:T, pl.ds(pl.multiple_of(at + CH * j, 128), 128)] = jnp.where(
                    masks[0], res[0][j], res[1][j]).astype(bf16)

        if i == 3:
            pair(QKV, 1).start()

    def first_norm(i):
        def emit(rows, value):
            total = (mid[rows, :] + value).astype(bf16)
            gcat[SKIP][rows, :] = total
            wide = total.astype(f32)
            acc[4] += wide[0:8] + wide[8:16]

        norm_back(hid, i, 1, 2, emit)
        if i == 3:
            pair(SKIP, 1).start()
            for row, a in ((0, 4), (1, 2), (2, 3), (3, 0), (4, 1)):
                small[row : row + 1, :] = jnp.sum(acc[a], axis=0, keepdims=True)

    def to_inputs(i):
        take(22 + i)
        if i == 0:
            result_copy.wait()
        back_product(lambda: gcat[SKIP][0:T, :], i % 2, store_in(lbuf.at[i]))
        release(22 + i)
        out_copies[i].start()

    steps = {
        PR: params_step, MK: lambda i: make_masks(), TR: turn, F1: to_hidden, F2: lambda i: norm_forward(hid, 1, i),
        F3: to_projected, AF: attend, F5: lambda i: to_middle(), F6: lambda i: norm_forward(mid, 3, i),
        F7: to_activated, F8: through_down, BF: back_through_down, FR: lambda i: to_result(),
        B2: lambda i: into_norm(i, 14, UP), L2: second_norm, B3: lambda i: to_attended(), A: attend_back,
        B5: lambda i: into_norm(i, 19, QKV), L1: first_norm, B6: to_inputs, R: small_step,
        W4: lambda i: weight_product(DOWN, 512 * i, 512 * i + 512),
        W3: lambda i: weight_product(UP, 2048 * i, 2048 * i + 2048), W2: lambda i: weight_product(OUT, 0, 1024),
        W1: lambda i: weight_product(QKV, 1536 * i, 1536 * i + 1536),
        W0: lambda i: weight_product(SKIP, 512 * i, 512 * i + 512),
    }
    for name, at in PLAN:
        if name in GATHER:
            k = GATHER.index(name)
            ag_do(k, STAGES[at])
            if STAGES[at] == ("ready",):
                ready(k)
        elif name in SCATTER:
            p = SCATTER.index(name)
            rs_do(p, STAGES[at])
            if STAGES[at] == ("own",):
                grad_copies[p].start()
        else:
            steps[name](at)

    for cp in out_copies + grad_copies:
        cp.wait()
    for k in range(n):
        for j in pieces(k):
            pair(k, j).wait_send()
    ag_finish()
    rs_finish()


def whole_layer(tokens, skip, cot, seg_ids, valid, vectors, shards):
    T, d = cot.shape
    n = len(shards)
    hw = [s.shape for s in shards]
    dims = [(16 * h, w) for h, w in hw]
    pieces = [(hw[k][0], w, side) for k, _, w, side in SCATTER_PIECES]
    ng, ns = len(GATHER_PIECES), len(SCATTER_PIECES)
    sem = pltpu.SemaphoreType.DMA
    V = pltpu.VMEM
    scratch = (
        [V(s, f32) for s in hw]
        + [V((2, h, T), bf16) for h, _ in dims]
        + [V((h, T), bf16) for h, _ in dims]
        + [V((2 * T, w), bf16) for _, w in dims]
        + [V((h, w), bf16) for h, w in dims]
        + [V((4, h, w), bf16) for _ in range(2) for h, w, _ in pieces]
        + [V((4, h, w // 2), bf16) for _ in range(2) for h, w, _ in pieces]
        + [V((5, h, w), bf16) for h, w, _ in pieces]
        + [V((5, h, side), bf16) for _ in range(2) for h, _, side in pieces]
        + [V((2, CH, CH), bf16), V((2, T, CH), bf16), V((T, d), f32), V((T, d), f32), V((T, d), f32),
           V((T, 3 * d), bf16), V((T, d), bf16), V((5, 8, d), f32), V((16, d), f32), V((5, 16, d), f32),
           V((16, d), bf16), V((16, d), f32), V((5, 16, d), bf16), V((HEADS, T), f32), V((HEADS, T), f32), V((T, T), f32),
           sem((ng, SLOTS)), sem((ng, SLOTS)), sem((ng,)), sem((ns, SLOTS)), sem((ns, SLOTS)), sem((n, 5)), sem((n, 5)),
           sem((2, 4)), sem((2,)), sem((4,)), sem((5,)), sem((5,)), sem((5,)), sem((5,)), sem((ns,))]
    )
    vm, anywhere = pl.BlockSpec(memory_space=V), pl.BlockSpec(memory_space=pl.ANY)
    outs = ([jax.ShapeDtypeStruct((16, d), f32)] + [jax.ShapeDtypeStruct(s, f32) for s in hw]
            + [jax.ShapeDtypeStruct((T, d), bf16)] * 3 + [jax.ShapeDtypeStruct((4, 8 * h, w), bf16) for h, w in hw])
    return pl.pallas_call(
        layer_kernel, out_shape=outs,
        in_specs=[anywhere] * 3 + [vm] * 14,
        out_specs=[vm] + [anywhere] * 13,
        scratch_shapes=scratch,
        compiler_params=pltpu.CompilerParams(collective_id=0, has_side_effects=True, vmem_limit_bytes=67043328),
        name="whole_layer",
    )(tokens, skip, cot, seg_ids, valid, *vectors, *shards)


def product(left, right):
    return jnp.dot(left, right, preferred_element_type=jnp.float32)


def outer_product(left, right):
    return lax.dot_general(
        left, right, (((0,), (0,)), ((), ())), preferred_element_type=jnp.float32
    )


def product_back(left, right):
    return lax.dot_general(
        left, right, (((1,), (1,)), ((), ())), preferred_element_type=jnp.float32
    )


def norm_rows(values, gain, shift):
    center = values - jnp.mean(values, axis=-1, keepdims=True)
    spread = jnp.mean(center * center, axis=-1, keepdims=True)
    return center * lax.rsqrt(spread + epsilon) * gain + shift


def gelu_exact(values):
    return 0.5 * values * (1.0 + lax.erf(values * 0.7071067811865476))


def attend_mask(seg_row, valid_row, head_count):
    count_rows = seg_row.shape[0]
    places = jnp.arange(count_rows, dtype=jnp.int32)
    same_utt = seg_row[:, None] == seg_row[None, :]
    diagonal = places[:, None] == places[None, :]
    allowed = same_utt & ((valid_row[None, :] == 1) | diagonal)
    slopes = 2.0 ** (-8.0 * (jnp.arange(head_count, dtype=jnp.float32) + 1.0) / head_count)
    distance = jnp.abs(places[:, None] - places[None, :]).astype(jnp.float32)
    return (allowed, -slopes[:, None, None] * distance[None, :, :])


def split_heads(projected, head_count):
    row_count = projected.shape[0]
    feature_width = projected.shape[1] // 3
    head_size = feature_width // head_count
    queries = projected[:, :feature_width].reshape(row_count, head_count, head_size)
    keys_all = projected[:, feature_width : 2 * feature_width].reshape(
        row_count, head_count, head_size
    )
    values_all = projected[:, 2 * feature_width :].reshape(row_count, head_count, head_size)
    return (queries, keys_all, values_all)


def masked_scores(queries, keys_all, allowed, linear_bias):
    score_scale = queries.shape[2] ** (-0.5)
    raw = (
        jnp.einsum("qhd,khd->hqk", queries, keys_all, preferred_element_type=jnp.float32)
        * score_scale
        + linear_bias
    )
    return jnp.where(allowed[None, :, :], raw, -1e30)


def forward_pass(tokens, skip, weights, allowed, linear_bias, head_count):
    w_skip, b_skip, g_one, beta_one, w_qkv, w_out, g_two, beta_two, w_up, b_up, w_down, b_down = (
        weights
    )
    row_count, feature_width = tokens.shape
    joined = jnp.concatenate([tokens, skip], axis=1)
    hidden = product(joined, w_skip) + b_skip.astype(jnp.float32)
    normed = norm_rows(hidden, g_one.astype(jnp.float32), beta_one.astype(jnp.float32)).astype(
        jnp.bfloat16
    )
    projected = product(normed, w_qkv).astype(jnp.bfloat16)
    queries, keys_all, values_all = split_heads(projected, head_count)
    masked = masked_scores(queries, keys_all, allowed, linear_bias)
    row_top = jnp.max(masked, axis=-1, keepdims=True)
    exponent = jnp.exp(masked - row_top)
    row_total = jnp.sum(exponent, axis=-1, keepdims=True)
    soft_weights = (exponent / row_total).astype(jnp.bfloat16)
    log_total = row_top + jnp.log(row_total)
    weighted = jnp.einsum(
        "hqk,khd->qhd", soft_weights, values_all, preferred_element_type=jnp.float32
    )
    attended = weighted.reshape(row_count, feature_width).astype(jnp.bfloat16)
    middle = hidden + product(attended, w_out)
    normed_two = norm_rows(middle, g_two.astype(jnp.float32), beta_two.astype(jnp.float32)).astype(
        jnp.bfloat16
    )
    hidden_up = product(normed_two, w_up) + b_up.astype(jnp.float32)
    activated = gelu_exact(hidden_up).astype(jnp.bfloat16)
    result = middle + (product(activated, w_down) + b_down.astype(jnp.float32))
    stored = (
        joined,
        hidden,
        normed,
        projected,
        log_total,
        attended,
        middle,
        normed_two,
        hidden_up,
        activated,
    )
    return (stored, result)


def backward_feed(stored, weights, cotangent):
    (
        joined,
        hidden,
        normed,
        projected,
        log_total,
        attended,
        middle,
        normed_two,
        hidden_up,
        activated,
    ) = stored
    w_skip, b_skip, g_one, beta_one, w_qkv, w_out, g_two, beta_two, w_up, b_up, w_down, b_down = (
        weights
    )
    grad_result = cotangent.astype(jnp.float32)
    grad_activated = product_back(cotangent, w_down)
    grad_b_down = jnp.sum(grad_result, axis=0)
    gelu_value, gelu_pull = jax.vjp(gelu_exact, hidden_up)
    grad_up = gelu_pull(grad_activated)[0].astype(jnp.bfloat16)
    grad_b_up = jnp.sum(grad_up.astype(jnp.float32), axis=0)
    grad_normed_two = product_back(grad_up, w_up)
    norm_value, norm_pull = jax.vjp(
        norm_rows, middle, g_two.astype(jnp.float32), beta_two.astype(jnp.float32)
    )
    grad_middle_norm, grad_g_two, grad_beta_two = norm_pull(grad_normed_two)
    grad_middle = grad_result + grad_middle_norm
    feed_terms = (grad_up, grad_b_up, cotangent, grad_b_down, grad_g_two, grad_beta_two)
    return (feed_terms, grad_middle)


def backward_front(stored, weights, grad_middle, allowed, linear_bias, head_count):
    (
        joined,
        hidden,
        normed,
        projected,
        log_total,
        attended,
        middle,
        normed_two,
        hidden_up,
        activated,
    ) = stored
    w_skip, b_skip, g_one, beta_one, w_qkv, w_out, g_two, beta_two, w_up, b_up, w_down, b_down = (
        weights
    )
    row_count, feature_width = hidden.shape
    branch_grad = grad_middle.astype(jnp.bfloat16)
    grad_attended = product_back(branch_grad, w_out).astype(jnp.bfloat16)
    queries, keys_all, values_all = split_heads(projected, head_count)
    score_scale = queries.shape[2] ** (-0.5)
    masked = masked_scores(queries, keys_all, allowed, linear_bias)
    probable = jnp.exp(masked - log_total)
    soft_weights = probable.astype(jnp.bfloat16)
    grad_heads = grad_attended.reshape(row_count, head_count, feature_width // head_count)
    grad_probable = jnp.einsum(
        "qhd,khd->hqk", grad_heads, values_all, preferred_element_type=jnp.float32
    )
    grad_values = jnp.einsum(
        "hqk,qhd->khd", soft_weights, grad_heads, preferred_element_type=jnp.float32
    )
    inner_sum = jnp.sum(grad_probable * probable, axis=-1, keepdims=True)
    grad_scores = (probable * (grad_probable - inner_sum)).astype(jnp.bfloat16)
    grad_queries = (
        jnp.einsum("hqk,khd->qhd", grad_scores, keys_all, preferred_element_type=jnp.float32)
        * score_scale
    )
    grad_keys = (
        jnp.einsum("hqk,qhd->khd", grad_scores, queries, preferred_element_type=jnp.float32)
        * score_scale
    )
    grad_projected = jnp.concatenate(
        [
            grad_queries.reshape(row_count, feature_width),
            grad_keys.reshape(row_count, feature_width),
            grad_values.reshape(row_count, feature_width),
        ],
        axis=1,
    ).astype(jnp.bfloat16)
    grad_normed = product_back(grad_projected, w_qkv)
    norm_value, norm_pull = jax.vjp(
        norm_rows, hidden, g_one.astype(jnp.float32), beta_one.astype(jnp.float32)
    )
    grad_hidden_norm, grad_g_one, grad_beta_one = norm_pull(grad_normed)
    grad_hidden = (grad_middle + grad_hidden_norm).astype(jnp.bfloat16)
    grad_b_skip = jnp.sum(grad_hidden.astype(jnp.float32), axis=0)
    grad_joined = product_back(grad_hidden, w_skip)
    grad_tokens = grad_joined[:, :feature_width].astype(jnp.bfloat16)
    grad_skip = grad_joined[:, feature_width:].astype(jnp.bfloat16)
    front_terms = (grad_hidden, grad_b_skip, grad_g_one, grad_beta_one, grad_projected, branch_grad)
    return (grad_tokens, grad_skip, front_terms)


AXES = ("wide", "narrow")


def gather_plain(values):
    return [lax.all_gather(v, AXES, axis=0, tiled=True) for v in values]


def hand_over_kernel(*refs):
    small = refs[0]
    sources = refs[1:9]
    vectors = refs[9:16]
    targets = refs[16:24]
    buffers = refs[24:32]
    in_sem, out_sem = refs[32:]
    me = lax.axis_index("wide") * 2 + lax.axis_index("narrow")
    arrive = [pltpu.make_async_copy(s, b, in_sem.at[i]) for i, (s, b) in enumerate(zip(sources, buffers))]
    leave = [pltpu.make_async_copy(b, t, out_sem.at[i]) for i, (b, t) in enumerate(zip(buffers, targets))]
    for cp in arrive:
        cp.start()
    rolled = pltpu.roll(small[...], lax.rem(32 - me, 32) * 32, 1)
    for i in range(6):
        vectors[i][...] = rolled[i, 0:32]
    row = 6 + lax.div(me, 8)
    wide = pltpu.roll(jnp.where(lax.broadcasted_iota(jnp.int32, small.shape, 0) == row, small[...], 0.0),
                      lax.rem(8 - lax.rem(me, 8), 8) * 128, 1)
    vectors[6][...] = jnp.sum(wide[:, 0:128], axis=0)
    for a, l in zip(arrive, leave):
        a.wait()
        l.start()
    for l in leave:
        l.wait()


def hand_over(small, arrays):
    vm, anywhere = pl.BlockSpec(memory_space=pltpu.VMEM), pl.BlockSpec(memory_space=pl.ANY)
    sem = pltpu.SemaphoreType.DMA
    n = len(arrays)
    outs = [jax.ShapeDtypeStruct((32,), f32)] * 6 + [jax.ShapeDtypeStruct((128,), f32)] + [
        jax.ShapeDtypeStruct(a.shape, a.dtype) for a in arrays]
    return pl.pallas_call(
        hand_over_kernel, out_shape=outs,
        in_specs=[vm] + [anywhere] * n, out_specs=[vm] * 7 + [anywhere] * n,
        scratch_shapes=[pltpu.VMEM(a.shape, a.dtype) for a in arrays] + [sem((n,)), sem((n,))],
        name="hand_over",
    )(small, *arrays)


def own_layer(tokens, skip, seg_ids, valid, w_skip, b_skip, g_one, beta_one, w_qkv, w_out, g_two, beta_two,
              w_up, b_up, w_down, b_down, cotangent):
    vectors = [v[None, :] for v in (b_skip, g_one, beta_one, g_two, beta_two, b_down, b_up)]
    small, *rest = whole_layer(
        tokens, skip, cotangent, seg_ids, valid, vectors, (w_skip, w_qkv, w_out, w_up, w_down))
    (grad_b_skip, grad_g_one, grad_beta_one, grad_g_two, grad_beta_two, grad_b_down, grad_b_up,
     grad_w_skip, grad_w_qkv, grad_w_out, grad_w_up, grad_w_down, result, grad_tokens, grad_skip) = hand_over(small, rest[:8])
    return (
        result, grad_tokens, grad_skip,
        grad_w_skip, grad_b_skip, grad_g_one, grad_beta_one, grad_w_qkv, grad_w_out,
        grad_g_two, grad_beta_two, grad_w_up, grad_b_up, grad_w_down, grad_b_down,
    )


def plain_layer(tokens, skip, seg_ids, valid, w_skip, b_skip, g_one, beta_one, w_qkv, w_out, g_two, beta_two,
                w_up, b_up, w_down, b_down, cotangent):
    weights = gather_plain(
        (w_skip, b_skip, g_one, beta_one, w_qkv, w_out, g_two, beta_two, w_up, b_up, w_down, b_down))
    allowed, linear_bias = attend_mask(seg_ids[0], valid[0], HEADS)
    stored, result = forward_pass(tokens, skip, weights, allowed, linear_bias, HEADS)
    (joined, hidden, normed, projected, log_total, attended, middle, normed_two, hidden_up, activated) = stored
    feed_terms, grad_middle = backward_feed(stored, weights, cotangent)
    grad_tokens, grad_skip, front_terms = backward_front(
        stored, weights, grad_middle, allowed, linear_bias, HEADS)
    grad_up, grad_b_up, grad_result, grad_b_down, grad_g_two, grad_beta_two = feed_terms
    grad_hidden, grad_b_skip, grad_g_one, grad_beta_one, grad_projected, branch_grad = front_terms
    lefts = (joined, normed, attended, normed_two, activated)
    rights = (grad_hidden, grad_projected, branch_grad, grad_up, grad_result)

    def scatter(v):
        return lax.psum_scatter(v, AXES, scatter_dimension=0, tiled=True)

    big = [scatter(outer_product(a, b)) for a, b in zip(lefts, rights)]
    grad_b_skip, grad_g_one, grad_beta_one, grad_g_two, grad_beta_two, grad_b_up, grad_b_down = [
        scatter(v) for v in
        (grad_b_skip, grad_g_one, grad_beta_one, grad_g_two, grad_beta_two, grad_b_up, grad_b_down)]
    return (
        result.astype(bf16), grad_tokens, grad_skip,
        big[0], grad_b_skip, grad_g_one, grad_beta_one, big[1], big[2],
        grad_g_two, grad_beta_two, big[3], grad_b_up, big[4], grad_b_down,
    )


def solution(mesh):
    return jax.shard_map(
        own_layer if dict(mesh.shape) == {"wide": 16, "narrow": 2} else plain_layer,
        mesh=mesh,
        in_specs=(
            P(("wide", "narrow"), None),
            P(("wide", "narrow"), None),
            P(("wide", "narrow"), None),
            P(("wide", "narrow"), None),
            P(("wide", "narrow"), None),
            P(("wide", "narrow")),
            P(("wide", "narrow")),
            P(("wide", "narrow")),
            P(("wide", "narrow"), None),
            P(("wide", "narrow"), None),
            P(("wide", "narrow")),
            P(("wide", "narrow")),
            P(("wide", "narrow"), None),
            P(("wide", "narrow")),
            P(("wide", "narrow"), None),
            P(("wide", "narrow")),
            P(("wide", "narrow"), None),
        ),
        out_specs=(
            P(("wide", "narrow"), None),
            P(("wide", "narrow"), None),
            P(("wide", "narrow"), None),
            P(("wide", "narrow"), None),
            P(("wide", "narrow")),
            P(("wide", "narrow")),
            P(("wide", "narrow")),
            P(("wide", "narrow"), None),
            P(("wide", "narrow"), None),
            P(("wide", "narrow")),
            P(("wide", "narrow")),
            P(("wide", "narrow"), None),
            P(("wide", "narrow")),
            P(("wide", "narrow"), None),
            P(("wide", "narrow")),
        ),
        check_vma=False,
    )
```

```python
import jax
import jax.numpy as jnp
from jax import lax
from jax.experimental import pallas as pl
from jax.experimental.pallas import tpu as pltpu
from jax.sharding import PartitionSpec as P

f32 = jnp.float32
bf16 = jnp.bfloat16

MESH = pl.DeviceIdType.MESH
ZN = 4
SLOTS = 44
ZM, ZX, ZY, XM, XY, YM, YX, CP, ZD = 0, 6, 12, 18, 22, 26, 30, 34, 38


def here():
    w = lax.axis_index("wide")
    y = lax.axis_index("narrow")
    c = lax.rem(w, 2)
    x = lax.rem(lax.div(w, 2), 2)
    z = lax.div(w, 4)
    return z, x, c, y


def place(z, x, c, y):
    return ((z * 2 + x) * 2 + c, y)


def greet_partners():
    barrier = pltpu.get_barrier_semaphore()
    z, x, c, y = here()

    def greet(to):
        pl.semaphore_signal(barrier, inc=1, device_id=to, device_id_type=MESH)

    for to in (place(z, x, 1 - c, y), place(z, 1 - x, c, y), place(z, x, c, 1 - y), place(lax.rem(z + 2, ZN), x, c, y)):
        greet(to)

    @pl.when(z > 0)
    def _():
        greet(place(z - 1, x, c, y))

    @pl.when(z < ZN - 1)
    def _():
        greet(place(z + 1, x, c, y))

    pl.semaphore_wait(barrier, 4 + jnp.where(z > 0, 1, 0) + jnp.where(z < ZN - 1, 1, 0))


def span(width, side, first, quarters):
    cuts = (0, side, width // 2, width - side, width)
    return pl.ds(cuts[first], cuts[first + quarters] - cuts[first])


def gather_events(own, full, sides, send_sem, recv_sem, local_sem):
    n = len(own)
    z, x, c, y = here()

    def block(k, xo, co, yo):
        h = own[k].shape[0]
        return pl.ds(pl.multiple_of(((xo * 2 + co) * 2 + yo) * h, h), h)

    def part(k, zo, xo, yo, first=0, quarters=4):
        return full[k].at[zo, block(k, xo, c, yo), span(own[k].shape[1], sides[k], first, quarters)]

    def link(k, slot, src, dst, to):
        return pltpu.make_async_remote_copy(
            src_ref=src, dst_ref=dst, send_sem=send_sem.at[k, slot], recv_sem=recv_sem.at[k, slot],
            device_id=to, device_id_type=MESH)

    xp = place(z, 1 - x, c, y)
    yp = place(z, x, c, 1 - y)
    cpart = place(z, x, 1 - c, y)

    def zto(d):
        return place(z + 1 - 2 * d, x, c, y)

    def z_has(d, s):
        return (z - s >= 0) if d == 0 else (z + s <= ZN - 1)

    def z_next(d):
        return (z < ZN - 1) if d == 0 else (z > 0)

    def zo_of(d, s):
        return z - s if d == 0 else z + s

    def z_send(k, base, d, s, xo, yo, first, quarters, src=None):
        cond = jnp.logical_and(z_has(d, s), z_next(d))
        zo = zo_of(d, s)
        dst = part(k, zo, xo, yo, first, quarters)
        cp = link(k, base + d * 3 + s, dst if src is None else src, dst, zto(d))

        @pl.when(cond)
        def _():
            cp.start()

    def z_wait(k, base, d, s, xo, yo, first, quarters):
        zo = zo_of(d, s + 1)
        dst = part(k, zo, xo, yo, first, quarters)
        link(k, base + d * 3 + s, dst, dst, zto(d)).wait_recv()

    def go(k, slot, ref, to, src=None, cond=None):
        cp = link(k, slot, ref if src is None else src, ref, to)
        cp.start()

    def wait(k, slot, ref):
        link(k, slot, ref, ref, xp).wait_recv()

    def begin():
        for k in range(n):
            pltpu.make_async_copy(own[k], part(k, z, x, y), local_sem.at[k]).start()

    def do(k, e):
        kind = e[0]
        if kind == "own":
            for d in (0, 1):
                z_send(k, ZM, d, 0, x, y, 0, 4, src=own[k])
            go(k, XM + z, part(k, z, x, y), xp, src=own[k])
            go(k, YM + z, part(k, z, x, y), yp, src=own[k])
        elif kind == "near":
            wait(k, XM + z, part(k, z, 1 - x, y))
            for d in (0, 1):
                z_send(k, ZX, d, 0, 1 - x, y, 0, 1)
            go(k, YX + z, part(k, z, 1 - x, y, 0, 2), yp)
            wait(k, YM + z, part(k, z, x, 1 - y))
            for d in (0, 1):
                z_send(k, ZY, d, 0, x, 1 - y, 3, 1)
            go(k, XY + z, part(k, z, x, 1 - y, 2, 2), xp)
        elif kind == "chain":
            s = e[1]
            for d in (0, 1):
                @pl.when(z_has(d, s + 1))
                def _():
                    z_wait(k, ZM, d, s, x, y, 0, 4)
                    zo = zo_of(d, s + 1)
                    if s < 2:
                        @pl.when(z_next(d))
                        def _():
                            ref = part(k, zo, x, y)
                            link(k, ZM + d * 3 + s + 1, ref, ref, zto(d)).start()
                    ref = part(k, zo, x, y, 1, 3)
                    link(k, XM + zo, ref, ref, xp).start()
                    ref = part(k, zo, x, y, 0, 3)
                    link(k, YM + zo, ref, ref, yp).start()
        elif kind == "side":
            s = e[1]
            for d in (0, 1):
                @pl.when(z_has(d, s + 1))
                def _():
                    zo = zo_of(d, s + 1)
                    for base, xo, yo, first in ((ZX, 1 - x, y, 0), (ZY, x, 1 - y, 3)):
                        z_wait(k, base, d, s, xo, yo, first, 1)
                        if s < 2:
                            @pl.when(z_next(d))
                            def _():
                                ref = part(k, zo, xo, yo, first, 1)
                                link(k, base + d * 3 + s + 1, ref, ref, zto(d)).start()
        elif kind == "cross":
            s = e[1]
            for d in (0, 1):
                @pl.when(z_has(d, s + 1))
                def _():
                    zo = zo_of(d, s + 1)
                    wait(k, XM + zo, part(k, zo, 1 - x, y, 1, 3))
                    ref = part(k, zo, 1 - x, y, 0, 2)
                    link(k, YX + zo, ref, ref, yp).start()
                    wait(k, YM + zo, part(k, zo, x, 1 - y, 0, 3))
                    ref = part(k, zo, x, 1 - y, 2, 2)
                    link(k, XY + zo, ref, ref, xp).start()
            if s == 0:
                pltpu.make_async_copy(own[k], part(k, z, x, y), local_sem.at[k]).wait()
                ref = full[k].at[:, block(k, x, c, y), :]
                link(k, CP, ref, ref, cpart).start()
            if s == 2:
                ref = full[k].at[:, block(k, 1 - x, c, y), :]
                link(k, CP + 1, ref, ref, cpart).start()
                ref = full[k].at[:, block(k, x, c, 1 - y), :]
                link(k, CP + 2, ref, ref, cpart).start()
        elif kind == "last":
            for zo in range(ZN):
                wait(k, XY + zo, part(k, zo, 1 - x, 1 - y, 2, 2))
                wait(k, YX + zo, part(k, zo, 1 - x, 1 - y, 0, 2))
            ref = full[k].at[:, block(k, 1 - x, c, 1 - y), :]
            link(k, CP + 3, ref, ref, cpart).start()
        elif kind == "ready":
            for j, (xo, yo) in enumerate(((x, y), (1 - x, y), (x, 1 - y), (1 - x, 1 - y))):
                ref = full[k].at[:, block(k, xo, 1 - c, yo), :]
                link(k, CP + j, ref, ref, cpart).wait_recv()

    def finish():
        for k in range(n):
            for j, (xo, yo) in enumerate(((x, y), (1 - x, y), (x, 1 - y), (1 - x, 1 - y))):
                ref = full[k].at[:, block(k, xo, c, yo), :]
                link(k, CP + j, ref, ref, cpart).wait_send()
            for d in (0, 1):
                for s in range(3):
                    @pl.when(jnp.logical_and(z_has(d, s), z_next(d)))
                    def _():
                        zo = zo_of(d, s)
                        for base, xo, yo, first, q in ((ZM, x, y, 0, 4), (ZX, 1 - x, y, 0, 1), (ZY, x, 1 - y, 3, 1)):
                            ref = part(k, zo, xo, yo, first, q)
                            link(k, base + d * 3 + s, ref, ref, zto(d)).wait_send()
            ref = part(k, z, x, y)
            link(k, XM + z, ref, ref, xp).wait_send()
            link(k, YM + z, ref, ref, yp).wait_send()
            for t in range(1, ZN):
                zo = lax.rem(z + t, ZN)
                ref = part(k, zo, x, y, 1, 3)
                link(k, XM + zo, ref, ref, xp).wait_send()
                ref = part(k, zo, x, y, 0, 3)
                link(k, YM + zo, ref, ref, yp).wait_send()
            for zo in range(ZN):
                ref = part(k, zo, 1 - x, y, 0, 2)
                link(k, YX + zo, ref, ref, yp).wait_send()
                ref = part(k, zo, x, 1 - y, 2, 2)
                link(k, XY + zo, ref, ref, xp).wait_send()

    return begin, do, finish


def scatter_events(outs, part_sums, sides, deeps, landings, send_sem, recv_sem):
    n = len(outs)
    lxm, lym, lxy, lyx, lzm, lzx, lzy, lzd = landings
    z, x, c, y = here()
    xp = place(z, 1 - x, c, y)
    yp = place(z, x, c, 1 - y)

    def rows_of(k):
        return outs[k].shape[0]

    def width(k):
        return outs[k].shape[1]

    def mine(k, zo, xo, yo, first=0, quarters=4):
        h = rows_of(k)
        row = pl.multiple_of(((zo * 2 + xo) * 2 + yo) * h, h)
        return part_sums[k].at[pl.ds(row, h), span(width(k), sides[k], first, quarters)]

    def mine_at(k, zo, xo, yo, lo, hi):
        h = rows_of(k)
        row = pl.multiple_of(((zo * 2 + xo) * 2 + yo) * h, h)
        return part_sums[k].at[pl.ds(row, h), pl.ds(lo, hi - lo)]

    def middle_cut(k):
        return width(k) // 2 - deeps[k] // 2, width(k) // 2 + deeps[k] // 2

    def deep(k, zo):
        return mine_at(k, zo, 1 - x, 1 - y, *middle_cut(k))

    def cross_x(k, zo, own):
        w = width(k)
        lo = w // 2 if own else middle_cut(k)[1]
        return link(k, XY + zo, mine_at(k, zo, 1 - x, 1 - y, lo, w), lxy[k].at[zo, :, pl.ds(lo - w // 2, w - lo)], xp)

    def cross_y(k, zo, own):
        hi = width(k) // 2 if own else middle_cut(k)[0]
        return link(k, YX + zo, mine_at(k, zo, 1 - x, 1 - y, 0, hi), lyx[k].at[zo, :, pl.ds(0, hi)], yp)

    def link(k, slot, src, dst, to):
        return pltpu.make_async_remote_copy(
            src_ref=src, dst_ref=dst, send_sem=send_sem.at[k, slot], recv_sem=recv_sem.at[k, slot],
            device_id=to, device_id_type=MESH)

    def quarter_slice(k, first, quarters):
        return span(width(k), sides[k], first, quarters)

    def land_x(k, zo, first, quarters):
        return lxm[k].at[zo, :, quarter_slice(k, first, quarters)]

    def land_y(k, zo, first, quarters):
        return lym[k].at[zo, :, quarter_slice(k, first, quarters)]

    def z_has(d, s):
        return (z - s >= 0) if d == 0 else (z + s <= ZN - 1)

    def z_next(d):
        return (z < ZN - 1) if d == 0 else (z > 0)

    def zo_of(d, s):
        return z - s if d == 0 else z + s

    def z_slot(d, s, zo):
        return ZN if (d == 1 and s == 0) else zo

    def toward(d):
        return place(z - 1 + 2 * d, x, c, y)

    def add_in(k, zo, xo, yo, first, quarters, others):
        add_ref(k, mine(k, zo, xo, yo, first, quarters), others)

    def add_ref(k, ref, others):
        h = rows_of(k)

        @pl.loop(0, h // 16)
        def _(i):
            rows = pl.ds(pl.multiple_of(i * 16, 16), 16)
            total = ref[rows, :].astype(f32)
            for o in others:
                total = total + o[rows, :].astype(f32)
            ref[rows, :] = total.astype(bf16)

    def wait(k, slot, dst):
        link(k, slot, dst, dst, xp).wait_recv()

    def do(k, e):
        kind = e[0]
        if kind == "last":
            for t in range(1, ZN):
                zo = lax.rem(z + t, ZN)
                cross_x(k, zo, False).start()
                cross_y(k, zo, False).start()
        elif kind == "deep":
            s = e[1]
            for d in (0, 1):
                @pl.when(z_has(d, s + 1))
                def _():
                    zo = zo_of(d, s + 1)
                    if s < 2:
                        @pl.when(z_next(d))
                        def _():
                            got = lzd[k].at[z_slot(d, s + 1, zo)]
                            wait(k, ZD + d * 3 + s + 1, got)
                            add_ref(k, deep(k, zo), [got])
                    link(k, ZD + d * 3 + s, deep(k, zo), lzd[k].at[z_slot(d, s, zo)], toward(d)).start()
        elif kind == "inner":
            if deeps[k]:
                for d in (0, 1):
                    @pl.when(z_next(d))
                    def _():
                        got = lzd[k].at[z_slot(d, 0, z)]
                        wait(k, ZD + d * 3, got)
                        add_ref(k, deep(k, z), [got])
            cross_x(k, z, True).start()
            cross_y(k, z, True).start()
        elif kind == "cross":
            s = e[1]
            for d in (0, 1):
                @pl.when(z_has(d, s + 1))
                def _():
                    zo = zo_of(d, s + 1)
                    lo, hi = middle_cut(k)
                    half, w = width(k) // 2, width(k)
                    got = lyx[k].at[zo, :, pl.ds(0, lo)]
                    wait(k, YX + zo, got)
                    add_ref(k, mine_at(k, zo, 1 - x, y, 0, lo), [got])
                    link(k, XM + zo, mine(k, zo, 1 - x, y, 1, 3), land_x(k, zo, 1, 3), xp).start()
                    got = lxy[k].at[zo, :, pl.ds(hi - half, w - hi)]
                    wait(k, XY + zo, got)
                    add_ref(k, mine_at(k, zo, x, 1 - y, hi, w), [got])
                    link(k, YM + zo, mine(k, zo, x, 1 - y, 0, 3), land_y(k, zo, 0, 3), yp).start()
        elif kind == "side":
            s = e[1]
            for d in (0, 1):
                @pl.when(z_has(d, s + 1))
                def _():
                    zo = zo_of(d, s + 1)
                    for base, landing, xo, yo, first in ((ZX, lzx, 1 - x, y, 0), (ZY, lzy, x, 1 - y, 3)):
                        if s < 2:
                            @pl.when(z_next(d))
                            def _():
                                got = landing[k].at[z_slot(d, s + 1, zo)]
                                wait(k, base + d * 3 + s + 1, got)
                                add_in(k, zo, xo, yo, first, 1, [got])
                        link(k, base + d * 3 + s, mine(k, zo, xo, yo, first, 1),
                             landing[k].at[z_slot(d, s, zo)], toward(d)).start()
        elif kind == "chain":
            s = e[1]
            for d in (0, 1):
                @pl.when(z_has(d, s + 1))
                def _():
                    zo = zo_of(d, s + 1)
                    wait(k, XM + zo, land_x(k, zo, 1, 3))
                    wait(k, YM + zo, land_y(k, zo, 0, 3))
                    add_in(k, zo, x, y, 0, 1, [land_y(k, zo, 0, 1)])
                    add_in(k, zo, x, y, 1, 2, [land_y(k, zo, 1, 2), land_x(k, zo, 1, 2)])
                    add_in(k, zo, x, y, 3, 1, [land_x(k, zo, 3, 1)])
                    if s < 2:
                        @pl.when(z_next(d))
                        def _():
                            got = lzm[k].at[z_slot(d, s + 1, zo)]
                            wait(k, ZM + d * 3 + s + 1, got)
                            add_in(k, zo, x, y, 0, 4, [got])
                    link(k, ZM + d * 3 + s, mine(k, zo, x, y), lzm[k].at[z_slot(d, s, zo)], toward(d)).start()
        elif kind == "near":
            for slot, own_slot, xo, yo, first, cross_land, side_base, side_land, side_first, to, land in (
                (YX, XM, 1 - x, y, 0, lyx, ZX, lzx, 0, xp, land_x),
                (XY, YM, x, 1 - y, 2, lxy, ZY, lzy, 3, yp, land_y),
            ):
                wait(k, slot + z, cross_land[k].at[z])
                add_in(k, z, xo, yo, first, 2, [cross_land[k].at[z]])
                for d in (0, 1):
                    @pl.when(z_next(d))
                    def _():
                        got = side_land[k].at[z_slot(d, 0, z)]
                        wait(k, side_base + d * 3, got)
                        add_in(k, z, xo, yo, side_first, 1, [got])
                link(k, own_slot + z, mine(k, z, xo, yo), land(k, z, 0, 4), to).start()
        elif kind == "own":
            wait(k, XM + z, land_x(k, z, 0, 4))
            wait(k, YM + z, land_y(k, z, 0, 4))
            h = rows_of(k)
            own = mine(k, z, x, y)
            from_x, from_y = land_x(k, z, 0, 4), land_y(k, z, 0, 4)

            @pl.loop(0, h // 16)
            def _(i):
                rows = pl.ds(pl.multiple_of(i * 16, 16), 16)
                outs[k][rows, :] = own[rows, :].astype(f32) + from_x[rows, :].astype(f32) + from_y[rows, :].astype(f32)

            for d in (0, 1):
                @pl.when(z_next(d))
                def _():
                    got = lzm[k].at[z_slot(d, 0, z)]
                    wait(k, ZM + d * 3, got)

                    @pl.loop(0, h // 16)
                    def _(i):
                        rows = pl.ds(pl.multiple_of(i * 16, 16), 16)
                        outs[k][rows, :] += got[rows, :].astype(f32)

    def finish():
        for k in range(n):
            cross_x(k, z, True).wait_send()
            cross_y(k, z, True).wait_send()
            for t in range(1, ZN):
                zo = lax.rem(z + t, ZN)
                cross_x(k, zo, False).wait_send()
                cross_y(k, zo, False).wait_send()
            for t in range(1, ZN):
                zo = lax.rem(z + t, ZN)
                link(k, XM + zo, mine(k, zo, 1 - x, y, 1, 3), land_x(k, zo, 1, 3), xp).wait_send()
                link(k, YM + zo, mine(k, zo, x, 1 - y, 0, 3), land_y(k, zo, 0, 3), yp).wait_send()
            link(k, XM + z, mine(k, z, 1 - x, y), land_x(k, z, 0, 4), xp).wait_send()
            link(k, YM + z, mine(k, z, x, 1 - y), land_y(k, z, 0, 4), yp).wait_send()
            for d in (0, 1):
                for s in range(3):
                    @pl.when(z_has(d, s + 1))
                    def _():
                        zo = zo_of(d, s + 1)
                        to = z_slot(d, s, zo)
                        if deeps[k]:
                            link(k, ZD + d * 3 + s, deep(k, zo), lzd[k].at[to], toward(d)).wait_send()
                        link(k, ZX + d * 3 + s, mine(k, zo, 1 - x, y, 0, 1), lzx[k].at[to], toward(d)).wait_send()
                        link(k, ZY + d * 3 + s, mine(k, zo, x, 1 - y, 3, 1), lzy[k].at[to], toward(d)).wait_send()
                        link(k, ZM + d * 3 + s, mine(k, zo, x, y), lzm[k].at[to], toward(d)).wait_send()

    return do, finish


HEADS = 16


epsilon = 1e-05


def nn(a, b):
    return jnp.dot(a, b, preferred_element_type=f32)


def nt(a, b):
    return lax.dot_general(a, b, (((1,), (1,)), ((), ())), preferred_element_type=f32)


def tn(a, b):
    return lax.dot_general(a, b, (((0,), (0,)), ((), ())), preferred_element_type=f32)


CH = 1024
SKIP, QKV, OUT, UP, DOWN = range(5)
CHUNKS = (
    [(SKIP, 0), (SKIP, 1), (QKV, 0), (QKV, 1), (QKV, 2), (OUT, 0)] + [(UP, i) for i in range(4)]
    + [(DOWN, i) for i in range(4)] + [(UP, i) for i in range(4)] + [(OUT, 0)] + [(QKV, i) for i in range(3)]
    + [(SKIP, 0), (SKIP, 1)]
)
LEFTS = [(DOWN, 0), (DOWN, 1), (DOWN, 2), (DOWN, 3), (UP, 0), (OUT, 0), (QKV, 0), (SKIP, 0), (SKIP, 1)]
GATHER_PIECES = [(0, 0, 1024, 128), (1, 0, 3072, 640), (2, 0, 1024, 384), (3, 0, 2048, 768), (3, 2048, 2048, 896), (4, 0, 512, 128), (4, 512, 512, 128)]
SCATTER_PIECES = [(4, 0, 1024, 128, 256), (3, 0, 4096, 768, 1280), (2, 0, 1024, 128, 0), (1, 0, 3072, 512, 1280), (0, 0, 1024, 128, 0)]
STAGES = [("own",), ("near",)] + [(e, s) for s in range(3) for e in ("chain", "side")] + [
    ("cross", s) for s in range(3)] + [("last",), ("ready",)] + [("deep", s) for s in range(3)] + [("inner",)]
(PR, MK, TR, F1, F2, F3, AF, F5, F6, F7, F8, FR, B2, B3, B5, B6, A, L1, L2, R, W0, W1, W2, W3, W4, BF,
 G0, G1, G2, G3, G4, G5, G6, E0, E1, E2, E3, E4) = range(38)
GATHER = [G0, G1, G2, G3, G4, G5, G6]
SCATTER = [E0, E1, E2, E3, E4]
PLAN = [
    (G0, 0), (G1, 0), (PR, 0), (MK, 0), (TR, 7), (PR, 1), (TR, 8), (G0, 1),
    (G0, 2), (G1, 1), (G2, 0), (G1, 2), (G0, 3), (PR, 2), (G0, 4), (G1, 3),
    (G2, 1), (G2, 2), (G1, 4), (G0, 5), (G0, 6), (G1, 5), (PR, 3), (G2, 3),
    (G3, 0), (G2, 4), (G1, 6), (G0, 7), (G0, 8), (G0, 9), (G0, 10), (G1, 7),
    (G1, 8), (G1, 9), (PR, 4), (G2, 5), (G1, 10), (G3, 1), (G4, 0), (G3, 2),
    (G2, 6), (PR, 5), (G0, 11), (G2, 7), (G2, 8), (G2, 9), (G3, 3), (G0, 12),
    (F1, 0), (F1, 1), (G1, 11), (F2, 0), (F2, 1), (G3, 4), (F2, 2), (F2, 3),
    (TR, 6), (G1, 12), (G3, 5), (G4, 1), (G4, 2), (G5, 0), (F3, 0), (G2, 10),
    (G3, 6), (F3, 1), (G3, 7), (G3, 8), (F3, 2), (AF, 0), (G4, 3), (G3, 9),
    (AF, 1), (G2, 11), (G4, 4), (AF, 2), (G2, 12), (G5, 1), (G4, 5), (G5, 2),
    (G3, 10), (AF, 3), (G4, 6), (TR, 5), (F5, 0), (G5, 3), (G6, 0), (G4, 7),
    (G4, 8), (G4, 9), (G3, 11), (F6, 0), (F6, 1), (G4, 10), (F6, 2), (G5, 4),
    (F6, 3), (G5, 5), (G3, 12), (TR, 4), (F7, 0), (G6, 1), (G6, 2), (TR, 0),
    (F7, 1), (G4, 11), (G5, 6), (G5, 7), (G6, 3), (G5, 8), (TR, 1), (G5, 9),
    (G4, 12), (F7, 2), (G6, 4), (G6, 5), (G5, 10), (TR, 2), (F7, 3), (TR, 3),
    (G6, 6), (G5, 11), (G6, 7), (G6, 8), (W4, 0), (G6, 9), (G6, 10), (G5, 12),
    (W4, 1), (E0, 11), (E0, 15), (G6, 11), (G6, 12), (F8, 0), (BF, 0), (F8, 1),
    (E0, 10), (E0, 14), (E0, 9), (E0, 8), (BF, 1), (F8, 2), (E0, 13), (E0, 7),
    (BF, 2), (F8, 3), (E0, 6), (E0, 16), (BF, 3), (E0, 5), (FR, 0), (B2, 0),
    (B2, 1), (B2, 2), (B2, 3), (E0, 4), (W3, 0), (E0, 3), (W3, 1), (E1, 11),
    (E1, 15), (L2, 0), (L2, 1), (E0, 2), (E0, 1), (L2, 2), (L2, 3), (E1, 10),
    (E1, 14), (E1, 9), (E1, 8), (B3, 0), (A, 0), (E0, 0), (E1, 13), (E1, 7),
    (W2, 0), (E2, 11), (A, 1), (E1, 6), (E1, 16), (E1, 5), (A, 2), (A, 3),
    (B5, 0), (E1, 4), (B5, 1), (E1, 3), (B5, 2), (E2, 10), (E2, 9), (E2, 8),
    (E2, 7), (W1, 0), (W1, 1), (E2, 6), (E2, 16), (E3, 11), (E3, 15), (E1, 2),
    (E2, 5), (E1, 1), (L1, 0), (E2, 4), (L1, 1), (E3, 10), (E3, 14), (E3, 9),
    (E3, 8), (L1, 2), (L1, 3), (E2, 3), (R, 0), (E1, 0), (E2, 2), (W0, 0),
    (E2, 1), (E3, 13), (E3, 7), (E3, 6), (W0, 1), (E4, 11), (R, 1), (E3, 16),
    (E3, 5), (E3, 4), (E2, 0), (E3, 3), (E4, 10), (E4, 9), (E4, 8), (E4, 7),
    (E3, 2), (R, 2), (B6, 0), (E3, 1), (E4, 6), (E4, 16), (E4, 5), (E4, 4),
    (E4, 3), (R, 3), (B6, 1), (E4, 2), (E3, 0), (E4, 1), (R, 4), (E4, 0),
    (R, 5),
]


def layer_kernel(*refs):
    n = 5
    tokens, skip, cot, seg, valid = refs[:5]
    vectors = refs[5:12]
    own = refs[12 : 12 + n]
    small_out = refs[17]
    targets = refs[18:23]
    result, grad_tokens, grad_skip = refs[23:26]
    full = refs[26:31]
    outs = refs[31 : 31 + n]
    r = refs[31 + n :]
    turned, theirs, gcat, part_sums = r[:n], r[n : 2 * n], r[2 * n : 3 * n], r[3 * n : 4 * n]
    m = len(SCATTER_PIECES)
    landings = [r[4 * n + i * m : 4 * n + (i + 1) * m] for i in range(8)]
    (wbuf, lbuf, hid, gnorm, mid, pbuf, abuf, acc, small, small_land, params, params_wide, params_land,
     log_total, steep, distance,
     ag_send, ag_recv, ag_local, rs_send, rs_recv, pair_send, pair_recv, wsem, lsem, misc_sem,
     small_send, small_recv, params_send, params_recv, out_sem) = r[4 * n + 8 * m :]
    z, x, c, y = here()
    cpart = place(z, x, 1 - c, y)
    T = cot.shape[0]

    ag_begin, ag_do, ag_finish = gather_events(
        [own[k].at[:, pl.ds(at, w)] for k, at, w, _ in GATHER_PIECES],
        [full[k].at[:, :, pl.ds(at, w)] for k, at, w, _ in GATHER_PIECES], [p[3] for p in GATHER_PIECES], ag_send, ag_recv, ag_local)
    rs_do, rs_finish = scatter_events(
        [outs[k].at[:, pl.ds(at, w)] for k, at, w, _, _ in SCATTER_PIECES],
        [part_sums[k].at[:, pl.ds(at, w)] for k, at, w, _, _ in SCATTER_PIECES], [p[3] for p in SCATTER_PIECES],
        [p[4] for p in SCATTER_PIECES], landings, rs_send, rs_recv)

    def chunk_copies(i):
        k, j = CHUNKS[i]
        slot, depth = i % 2, full[k].shape[1]
        if k in (SKIP, DOWN):
            blocks = CH // depth
            return [pltpu.make_async_copy(full[k].at[j * blocks + b], wbuf.at[slot, pl.ds(b * depth, depth), :], wsem.at[slot, b])
                    for b in range(blocks)]
        return [pltpu.make_async_copy(full[k].at[b, :, pl.ds(j * CH, CH)], wbuf.at[slot, pl.ds(b * depth, depth), :], wsem.at[slot, b])
                for b in range(ZN)]

    state = {"next": 0, "done": 0, "ready": set()}

    def arrived(i):
        k, j = CHUNKS[i]
        lo, hi = (j * CH, (j + 1) * CH) if k in (QKV, UP) else (0, CH)
        return all(p in state["ready"] for p, (w, at, wide, _) in enumerate(GATHER_PIECES) if w == k and at < hi and at + wide > lo)

    def pump():
        while state["next"] < min(len(CHUNKS), state["done"] + 2) and arrived(state["next"]):
            for cp in chunk_copies(state["next"]):
                cp.start()
            state["next"] += 1

    def ready(k):
        state["ready"].add(k)
        pump()

    def take(i):
        assert state["done"] == i and state["next"] > i
        for cp in chunk_copies(i):
            cp.wait()

    def release(i):
        state["done"] = i + 1
        pump()

    in_copies = [pltpu.make_async_copy(a, lbuf.at[i], lsem.at[i]) for i, a in enumerate((tokens, skip))]
    cot_copy = pltpu.make_async_copy(cot, gcat[DOWN].at[pl.ds(0, T), :], misc_sem.at[0])
    result_copy = pltpu.make_async_copy(lbuf.at[0], result, misc_sem.at[1])
    out_copies = [pltpu.make_async_copy(lbuf.at[i], o, misc_sem.at[2 + i]) for i, o in enumerate((grad_tokens, grad_skip))]
    grad_copies = [pltpu.make_async_copy(outs[k].at[:, pl.ds(at, w)], targets[k].at[:, pl.ds(at, w)], out_sem.at[p])
                   for p, (k, at, w, _, _) in enumerate(SCATTER_PIECES)]
    ag_begin()
    for cp in in_copies:
        cp.start()
    cot_copy.start()
    greet_partners()

    def pair(k, j):
        if k == DOWN and j != 1:
            rows = pl.ds(CH // 2 * (j - 1 if j else 0), CH // 2)
            src, dst = turned[k].at[1 - c, rows, :], theirs[k].at[rows, :]
        elif j == 0:
            src, dst = turned[k].at[1 - c], theirs[k]
        elif k == DOWN:
            src, dst = cot, gcat[k].at[pl.ds(T, T), :]
        elif k == UP:
            cols = pl.ds((j - 1) * CH, CH)
            src, dst = gcat[k].at[pl.ds(0, T), cols], gcat[k].at[pl.ds(T, T), cols]
        else:
            src, dst = gcat[k].at[pl.ds(0, T), :], gcat[k].at[pl.ds(T, T), :]
        return pltpu.make_async_remote_copy(
            src_ref=src, dst_ref=dst, send_sem=pair_send.at[k, j], recv_sem=pair_recv.at[k, j],
            device_id=cpart, device_id_type=MESH)

    def pieces(k):
        return range(5) if k in (UP, DOWN) else range(2)

    meet = [cpart, place(z, 1 - x, c, y), place(z, x, c, 1 - y),
            place(z + 1 - 2 * lax.rem(z, 2), x, c, y), place(lax.rem(z + 2, 4), x, c, y)]

    def meeting(ref, land, send, recv, t):
        return pltpu.make_async_remote_copy(
            src_ref=ref, dst_ref=land.at[t], send_sem=send.at[t], recv_sem=recv.at[t],
            device_id=meet[t], device_id_type=MESH)

    def params_step(t):
        if t == 0:
            me = lax.axis_index("wide") * 2 + lax.axis_index("narrow")
            params_wide[...] = jnp.zeros_like(params_wide)
            for i in range(6):
                params_wide[i : i + 1, 0:32] = vectors[i][...].astype(f32)
            narrow = pltpu.roll(params_wide[...], me * 32, 1)
            params_wide[...] = jnp.zeros_like(params_wide)
            for i in range(4):
                params_wide[6 + i : 7 + i, 0:128] = vectors[6][...].astype(f32)
            wide = pltpu.roll(params_wide[...], lax.rem(me, 8) * 128, 1)
            row = lax.broadcasted_iota(jnp.int32, wide.shape, 0)
            params[...] = jnp.where(row == 6 + lax.div(me, 8), wide, narrow).astype(bf16)
        else:
            cp = meeting(params, params_land, params_send, params_recv, t - 1)
            cp.wait_send()
            cp.wait_recv()
            params[...] = (params[...].astype(f32) + params_land[t - 1].astype(f32)).astype(bf16)
        if t < 5:
            meeting(params, params_land, params_send, params_recv, t).start()
        else:
            params_wide[...] = params[...].astype(f32)

    def small_step(t):
        if t:
            cp = meeting(small, small_land, small_send, small_recv, t - 1)
            cp.wait_send()
            cp.wait_recv()
            small[...] += small_land[t - 1]
        if t < 5:
            meeting(small, small_land, small_send, small_recv, t).start()
        else:
            small_out[...] = small[...]

    def make_masks():
        acc[...] = jnp.zeros_like(acc)
        small[...] = jnp.zeros_like(small)
        heads = lax.broadcasted_iota(jnp.int32, steep.shape, 0).astype(f32)
        steep[...] = jnp.exp((heads + 1.0) * -0.34657359027997264)
        seg_row = jnp.broadcast_to(seg[...].astype(f32), (T, T))
        live = jnp.broadcast_to(valid[...].astype(f32), (T, T)).T
        key_at = lax.broadcasted_iota(jnp.int32, (T, T), 0)
        query_at = lax.broadcasted_iota(jnp.int32, (T, T), 1)
        allowed = jnp.logical_and(seg_row.T == seg_row, jnp.logical_or(live == 1.0, key_at == query_at))
        distance[...] = jnp.where(allowed, jnp.abs(key_at - query_at).astype(f32), 1e33)
        pair(DOWN, 1).start()

    def turn(i):
        k, j = LEFTS[i]
        group = 2 * outs[k].shape[0]
        seg = min(group, 128)
        if k == SKIP:
            in_copies[j].wait()
        for t in range(CH // 128):
            cols = slice(t * 128, (t + 1) * 128)
            if k == SKIP:
                block = lbuf[j, :, cols].T
            elif k == DOWN:
                block = part_sums[UP][0:T, j * CH + t * 128 : j * CH + (t + 1) * 128].T
            else:
                block = abuf[:, cols].T
            for s in range(0, 128, seg):
                row = j * CH + t * 128 + s
                core, at = (row // group) % 2, row // (2 * group) * group + row % group
                turned[k][core, at : at + seg, :] = block[s : s + seg, :]
        if k == DOWN:
            pair(k, j + 1 if j else 0).start()
        elif i + 1 == len(LEFTS) or LEFTS[i + 1][0] != k:
            pair(k, 0).start()

    def forward_product(left, slot, finish):
        @pl.loop(0, 2)
        def _(j):
            at = pl.multiple_of(j * 512, 512)
            finish(at, nn(left(), wbuf[slot, :, pl.ds(at, 512)]))

    def back_product(left, slot, finish):
        @pl.loop(0, 2)
        def _(j):
            at = pl.multiple_of(j * 512, 512)
            finish(at, nt(left(), wbuf[slot, pl.ds(at, 512), :]))

    def store_in(ref, offset=0):
        def finish(at, value):
            ref[:, pl.ds(pl.multiple_of(at + offset, 512), 512)] = value.astype(ref.dtype)

        return finish

    def add_to(ref):
        def finish(at, value):
            ref[:, pl.ds(at, 512)] += value

        return finish

    def to_hidden(i):
        take(i)

        def first(at, value):
            hid[:, pl.ds(at, 512)] = value + params_wide[0:1, pl.ds(at, 512)]

        forward_product(lambda: lbuf[i], i % 2, add_to(hid) if i else first)
        release(i)

    def norm_forward(source, gain, i):
        @pl.loop(0, 4)
        def _(j):
            rows = pl.ds(pl.multiple_of(i * 64 + j * 16, 16), 16)
            v = source[rows, :]
            center = v - jnp.mean(v, axis=-1, keepdims=True)
            rate = lax.rsqrt(jnp.mean(center * center, axis=-1, keepdims=True) + epsilon)
            abuf[rows, :] = (
                center * rate * params_wide[gain : gain + 1, :] + params_wide[gain + 1 : gain + 2, :]).astype(bf16)

    def to_projected(i):
        take(2 + i)
        forward_product(lambda: abuf[...], i % 2, store_in(pbuf, i * CH))
        release(2 + i)

    def heads_of(p):
        at = pl.multiple_of(p * 128, 128)
        return [pbuf[:, pl.ds(pl.multiple_of(at + j * CH, 128), 128)] for j in range(3)]

    def half_masks():
        low = lax.broadcasted_iota(jnp.int32, (T, 128), 1) < 64
        return low, jnp.logical_not(low)

    def attend(i):
        masks = half_masks()

        @pl.loop(2 * i, 2 * i + 2)
        def _(p):
            q, k, v = heads_of(p)
            res = []
            for e in (0, 1):
                head = pl.ds(2 * p + e, 1)
                scores = nt(k, jnp.where(masks[e], q, jnp.zeros_like(q))) * 0.125 - distance[...] * steep[head, :]
                top = jnp.max(scores, axis=0, keepdims=True)
                raised = jnp.exp(scores - top)
                total = jnp.sum(raised, axis=0, keepdims=True)
                log_total[head, :] = top + jnp.log(total)
                res.append(tn((raised / total).astype(bf16), v))
            abuf[:, pl.ds(pl.multiple_of(p * 128, 128), 128)] = jnp.where(masks[0], res[0], res[1]).astype(bf16)

    def to_middle():
        take(5)

        def finish(at, value):
            mid[:, pl.ds(at, 512)] = hid[:, pl.ds(at, 512)] + value

        forward_product(lambda: abuf[...], 1, finish)
        release(5)

    def to_activated(i):
        take(6 + i)

        def finish(at, value):
            cols = pl.ds(pl.multiple_of(i * CH + at, 512), 512)
            u = value + params_wide[6 + i : 7 + i, pl.ds(at, 512)]
            cdf = 0.5 * (1.0 + lax.erf(u * 0.7071067811865476))
            part_sums[UP][0:T, cols] = (u * cdf).astype(bf16)
            gcat[UP][0:T, cols] = (cdf + u * jnp.exp(-0.5 * u * u) * 0.3989422804014327).astype(bf16)

        forward_product(lambda: abuf[...], i % 2, finish)
        release(6 + i)

    def through_down(i):
        take(10 + i)
        forward_product(
            lambda: part_sums[UP][0:T, i * CH : (i + 1) * CH], i % 2, add_to(gnorm) if i else store_in(gnorm))

    def back_through_down(i):
        def finish(at, value):
            cols = pl.ds(pl.multiple_of(i * CH + at, 512), 512)
            got = (value * gcat[UP][0:T, cols].astype(f32)).astype(bf16)
            gcat[UP][0:T, cols] = got
            small[6 + i : 7 + i, pl.ds(at, 512)] = jnp.sum(got.astype(f32), axis=0, keepdims=True)

        back_product(lambda: gcat[DOWN][0:T, :], i % 2, finish)
        release(10 + i)
        pair(UP, 1 + i).start()

    def to_result():
        @pl.loop(0, T // 16)
        def _(i):
            rows = pl.ds(pl.multiple_of(i * 16, 16), 16)
            lbuf[0, rows, :] = (mid[rows, :] + (gnorm[rows, :] + params_wide[5:6, :])).astype(bf16)

        result_copy.start()

    def weight_product(k, lo, hi):
        tiles = (hi - lo) // 512
        if lo == 0:
            if k == DOWN:
                cot_copy.wait()
                small[5:6, :] = jnp.sum(gcat[DOWN][0:T, :].astype(f32), axis=0, keepdims=True)
            for j in pieces(k):
                pair(k, j).wait_recv()

        @pl.loop(0, part_sums[k].shape[0] // 256 * tiles)
        def _(i):
            rows = pl.ds(pl.multiple_of(lax.div(i, tiles) * 256, 256), 256)
            cols = pl.ds(pl.multiple_of(lo + lax.rem(i, tiles) * 512, 512), 512)
            both = nn(turned[k][c, rows, :], gcat[k][pl.ds(0, T), cols])
            both += nn(theirs[k][rows, :], gcat[k][pl.ds(T, T), cols])
            part_sums[k][rows, cols] = both.astype(bf16)

    def into_norm(i, base, k):
        take(base + i)
        back_product(lambda: gcat[k][0:T, i * CH : (i + 1) * CH], (base + i) % 2, add_to(gnorm) if i else store_in(gnorm))
        release(base + i)

    def norm_back(source, i, gain, base, emit):
        @pl.loop(0, 4)
        def _(j):
            rows = pl.ds(pl.multiple_of(i * 64 + j * 16, 16), 16)
            v = source[rows, :]
            center = v - jnp.mean(v, axis=-1, keepdims=True)
            rate = lax.rsqrt(jnp.mean(center * center, axis=-1, keepdims=True) + epsilon)
            xhat = center * rate
            g = gnorm[rows, :]
            gx = g * xhat
            acc[base] += gx[0:8] + gx[8:16]
            acc[base + 1] += g[0:8] + g[8:16]
            e = g * params_wide[gain : gain + 1, :]
            emit(rows, rate * (e - jnp.mean(e, axis=-1, keepdims=True) - xhat * jnp.mean(e * xhat, axis=-1, keepdims=True)))

    def second_norm(i):
        def emit(rows, value):
            total = gcat[DOWN][rows, :].astype(f32) + value
            mid[rows, :] = total
            gcat[OUT][rows, :] = total.astype(bf16)

        norm_back(mid, i, 3, 0, emit)
        if i == 3:
            pair(OUT, 1).start()

    def to_attended():
        take(18)
        back_product(lambda: gcat[OUT][0:T, :], 0, store_in(abuf))
        release(18)

    def attend_back(i):
        masks = half_masks()

        @pl.loop(2 * i, 2 * i + 2)
        def _(p):
            at = pl.multiple_of(p * 128, 128)
            q, k, v = heads_of(p)
            g = abuf[:, pl.ds(at, 128)]
            res = []
            for e in (0, 1):
                head = pl.ds(2 * p + e, 1)
                scores = nt(k, jnp.where(masks[e], q, jnp.zeros_like(q))) * 0.125 - distance[...] * steep[head, :]
                probable = jnp.exp(scores - log_total[head, :])
                gp = nt(v, jnp.where(masks[e], g, jnp.zeros_like(g)))
                gv = nn(probable.astype(bf16), g)
                inner = jnp.sum(gp * probable, axis=0, keepdims=True)
                gs = (probable * (gp - inner)).astype(bf16)
                res.append((tn(gs, k) * 0.125, nn(gs, q) * 0.125, gv))
            for j in range(3):
                gcat[QKV][0:T, pl.ds(pl.multiple_of(at + CH * j, 128), 128)] = jnp.where(
                    masks[0], res[0][j], res[1][j]).astype(bf16)

        if i == 3:
            pair(QKV, 1).start()

    def first_norm(i):
        def emit(rows, value):
            total = (mid[rows, :] + value).astype(bf16)
            gcat[SKIP][rows, :] = total
            wide = total.astype(f32)
            acc[4] += wide[0:8] + wide[8:16]

        norm_back(hid, i, 1, 2, emit)
        if i == 3:
            pair(SKIP, 1).start()
            for row, a in ((0, 4), (1, 2), (2, 3), (3, 0), (4, 1)):
                small[row : row + 1, :] = jnp.sum(acc[a], axis=0, keepdims=True)

    def to_inputs(i):
        take(22 + i)
        if i == 0:
            result_copy.wait()
        back_product(lambda: gcat[SKIP][0:T, :], i % 2, store_in(lbuf.at[i]))
        release(22 + i)
        out_copies[i].start()

    steps = {
        PR: params_step, MK: lambda i: make_masks(), TR: turn, F1: to_hidden, F2: lambda i: norm_forward(hid, 1, i),
        F3: to_projected, AF: attend, F5: lambda i: to_middle(), F6: lambda i: norm_forward(mid, 3, i),
        F7: to_activated, F8: through_down, BF: back_through_down, FR: lambda i: to_result(),
        B2: lambda i: into_norm(i, 14, UP), L2: second_norm, B3: lambda i: to_attended(), A: attend_back,
        B5: lambda i: into_norm(i, 19, QKV), L1: first_norm, B6: to_inputs, R: small_step,
        W4: lambda i: weight_product(DOWN, 512 * i, 512 * i + 512),
        W3: lambda i: weight_product(UP, 2048 * i, 2048 * i + 2048), W2: lambda i: weight_product(OUT, 0, 1024),
        W1: lambda i: weight_product(QKV, 1536 * i, 1536 * i + 1536),
        W0: lambda i: weight_product(SKIP, 512 * i, 512 * i + 512),
    }
    for name, at in PLAN:
        if name in GATHER:
            k = GATHER.index(name)
            ag_do(k, STAGES[at])
            if STAGES[at] == ("ready",):
                ready(k)
        elif name in SCATTER:
            p = SCATTER.index(name)
            rs_do(p, STAGES[at])
            if STAGES[at] == ("own",):
                grad_copies[p].start()
        else:
            steps[name](at)

    for cp in out_copies + grad_copies:
        cp.wait()
    for k in range(n):
        for j in pieces(k):
            pair(k, j).wait_send()
    ag_finish()
    rs_finish()


def whole_layer(tokens, skip, cot, seg_ids, valid, vectors, shards):
    T, d = cot.shape
    n = len(shards)
    hw = [s.shape for s in shards]
    dims = [(16 * h, w) for h, w in hw]
    pieces = [(hw[k][0], w, side, deep) for k, _, w, side, deep in SCATTER_PIECES]
    ng, ns = len(GATHER_PIECES), len(SCATTER_PIECES)
    sem = pltpu.SemaphoreType.DMA
    V = pltpu.VMEM
    scratch = (
        [V(s, f32) for s in hw]
        + [V((2, h, T), bf16) for h, _ in dims]
        + [V((h, T), bf16) for h, _ in dims]
        + [V((2 * T, w), bf16) for _, w in dims]
        + [V((h, w), bf16) for h, w in dims]
        + [V((4, h, w), bf16) for _ in range(2) for h, w, _, _ in pieces]
        + [V((4, h, w // 2), bf16) for _ in range(2) for h, w, _, _ in pieces]
        + [V((5, h, w), bf16) for h, w, _, _ in pieces]
        + [V((5, h, side), bf16) for _ in range(2) for h, _, side, _ in pieces]
        + [V((5, h, max(deep, 128)), bf16) for h, _, _, deep in pieces]
        + [V((2, CH, CH), bf16), V((2, T, CH), bf16), V((T, d), f32), V((T, d), f32), V((T, d), f32),
           V((T, 3 * d), bf16), V((T, d), bf16), V((5, 8, d), f32), V((16, d), f32), V((5, 16, d), f32),
           V((16, d), bf16), V((16, d), f32), V((5, 16, d), bf16), V((HEADS, T), f32), V((HEADS, T), f32), V((T, T), f32),
           sem((ng, SLOTS)), sem((ng, SLOTS)), sem((ng,)), sem((ns, SLOTS)), sem((ns, SLOTS)), sem((n, 5)), sem((n, 5)),
           sem((2, 4)), sem((2,)), sem((4,)), sem((5,)), sem((5,)), sem((5,)), sem((5,)), sem((ns,))]
    )
    vm, anywhere = pl.BlockSpec(memory_space=V), pl.BlockSpec(memory_space=pl.ANY)
    outs = ([jax.ShapeDtypeStruct((16, d), f32)] + [jax.ShapeDtypeStruct(s, f32) for s in hw]
            + [jax.ShapeDtypeStruct((T, d), bf16)] * 3 + [jax.ShapeDtypeStruct((4, 8 * h, w), bf16) for h, w in hw])
    return pl.pallas_call(
        layer_kernel, out_shape=outs,
        in_specs=[anywhere] * 3 + [vm] * 14,
        out_specs=[vm] + [anywhere] * 13,
        scratch_shapes=scratch,
        compiler_params=pltpu.CompilerParams(collective_id=0, has_side_effects=True, vmem_limit_bytes=67043328),
        name="whole_layer",
    )(tokens, skip, cot, seg_ids, valid, *vectors, *shards)


def product(left, right):
    return jnp.dot(left, right, preferred_element_type=jnp.float32)


def outer_product(left, right):
    return lax.dot_general(
        left, right, (((0,), (0,)), ((), ())), preferred_element_type=jnp.float32
    )


def product_back(left, right):
    return lax.dot_general(
        left, right, (((1,), (1,)), ((), ())), preferred_element_type=jnp.float32
    )


def norm_rows(values, gain, shift):
    center = values - jnp.mean(values, axis=-1, keepdims=True)
    spread = jnp.mean(center * center, axis=-1, keepdims=True)
    return center * lax.rsqrt(spread + epsilon) * gain + shift


def gelu_exact(values):
    return 0.5 * values * (1.0 + lax.erf(values * 0.7071067811865476))


def attend_mask(seg_row, valid_row, head_count):
    count_rows = seg_row.shape[0]
    places = jnp.arange(count_rows, dtype=jnp.int32)
    same_utt = seg_row[:, None] == seg_row[None, :]
    diagonal = places[:, None] == places[None, :]
    allowed = same_utt & ((valid_row[None, :] == 1) | diagonal)
    slopes = 2.0 ** (-8.0 * (jnp.arange(head_count, dtype=jnp.float32) + 1.0) / head_count)
    distance = jnp.abs(places[:, None] - places[None, :]).astype(jnp.float32)
    return (allowed, -slopes[:, None, None] * distance[None, :, :])


def split_heads(projected, head_count):
    row_count = projected.shape[0]
    feature_width = projected.shape[1] // 3
    head_size = feature_width // head_count
    queries = projected[:, :feature_width].reshape(row_count, head_count, head_size)
    keys_all = projected[:, feature_width : 2 * feature_width].reshape(
        row_count, head_count, head_size
    )
    values_all = projected[:, 2 * feature_width :].reshape(row_count, head_count, head_size)
    return (queries, keys_all, values_all)


def masked_scores(queries, keys_all, allowed, linear_bias):
    score_scale = queries.shape[2] ** (-0.5)
    raw = (
        jnp.einsum("qhd,khd->hqk", queries, keys_all, preferred_element_type=jnp.float32)
        * score_scale
        + linear_bias
    )
    return jnp.where(allowed[None, :, :], raw, -1e30)


def forward_pass(tokens, skip, weights, allowed, linear_bias, head_count):
    w_skip, b_skip, g_one, beta_one, w_qkv, w_out, g_two, beta_two, w_up, b_up, w_down, b_down = (
        weights
    )
    row_count, feature_width = tokens.shape
    joined = jnp.concatenate([tokens, skip], axis=1)
    hidden = product(joined, w_skip) + b_skip.astype(jnp.float32)
    normed = norm_rows(hidden, g_one.astype(jnp.float32), beta_one.astype(jnp.float32)).astype(
        jnp.bfloat16
    )
    projected = product(normed, w_qkv).astype(jnp.bfloat16)
    queries, keys_all, values_all = split_heads(projected, head_count)
    masked = masked_scores(queries, keys_all, allowed, linear_bias)
    row_top = jnp.max(masked, axis=-1, keepdims=True)
    exponent = jnp.exp(masked - row_top)
    row_total = jnp.sum(exponent, axis=-1, keepdims=True)
    soft_weights = (exponent / row_total).astype(jnp.bfloat16)
    log_total = row_top + jnp.log(row_total)
    weighted = jnp.einsum(
        "hqk,khd->qhd", soft_weights, values_all, preferred_element_type=jnp.float32
    )
    attended = weighted.reshape(row_count, feature_width).astype(jnp.bfloat16)
    middle = hidden + product(attended, w_out)
    normed_two = norm_rows(middle, g_two.astype(jnp.float32), beta_two.astype(jnp.float32)).astype(
        jnp.bfloat16
    )
    hidden_up = product(normed_two, w_up) + b_up.astype(jnp.float32)
    activated = gelu_exact(hidden_up).astype(jnp.bfloat16)
    result = middle + (product(activated, w_down) + b_down.astype(jnp.float32))
    stored = (
        joined,
        hidden,
        normed,
        projected,
        log_total,
        attended,
        middle,
        normed_two,
        hidden_up,
        activated,
    )
    return (stored, result)


def backward_feed(stored, weights, cotangent):
    (
        joined,
        hidden,
        normed,
        projected,
        log_total,
        attended,
        middle,
        normed_two,
        hidden_up,
        activated,
    ) = stored
    w_skip, b_skip, g_one, beta_one, w_qkv, w_out, g_two, beta_two, w_up, b_up, w_down, b_down = (
        weights
    )
    grad_result = cotangent.astype(jnp.float32)
    grad_activated = product_back(cotangent, w_down)
    grad_b_down = jnp.sum(grad_result, axis=0)
    gelu_value, gelu_pull = jax.vjp(gelu_exact, hidden_up)
    grad_up = gelu_pull(grad_activated)[0].astype(jnp.bfloat16)
    grad_b_up = jnp.sum(grad_up.astype(jnp.float32), axis=0)
    grad_normed_two = product_back(grad_up, w_up)
    norm_value, norm_pull = jax.vjp(
        norm_rows, middle, g_two.astype(jnp.float32), beta_two.astype(jnp.float32)
    )
    grad_middle_norm, grad_g_two, grad_beta_two = norm_pull(grad_normed_two)
    grad_middle = grad_result + grad_middle_norm
    feed_terms = (grad_up, grad_b_up, cotangent, grad_b_down, grad_g_two, grad_beta_two)
    return (feed_terms, grad_middle)


def backward_front(stored, weights, grad_middle, allowed, linear_bias, head_count):
    (
        joined,
        hidden,
        normed,
        projected,
        log_total,
        attended,
        middle,
        normed_two,
        hidden_up,
        activated,
    ) = stored
    w_skip, b_skip, g_one, beta_one, w_qkv, w_out, g_two, beta_two, w_up, b_up, w_down, b_down = (
        weights
    )
    row_count, feature_width = hidden.shape
    branch_grad = grad_middle.astype(jnp.bfloat16)
    grad_attended = product_back(branch_grad, w_out).astype(jnp.bfloat16)
    queries, keys_all, values_all = split_heads(projected, head_count)
    score_scale = queries.shape[2] ** (-0.5)
    masked = masked_scores(queries, keys_all, allowed, linear_bias)
    probable = jnp.exp(masked - log_total)
    soft_weights = probable.astype(jnp.bfloat16)
    grad_heads = grad_attended.reshape(row_count, head_count, feature_width // head_count)
    grad_probable = jnp.einsum(
        "qhd,khd->hqk", grad_heads, values_all, preferred_element_type=jnp.float32
    )
    grad_values = jnp.einsum(
        "hqk,qhd->khd", soft_weights, grad_heads, preferred_element_type=jnp.float32
    )
    inner_sum = jnp.sum(grad_probable * probable, axis=-1, keepdims=True)
    grad_scores = (probable * (grad_probable - inner_sum)).astype(jnp.bfloat16)
    grad_queries = (
        jnp.einsum("hqk,khd->qhd", grad_scores, keys_all, preferred_element_type=jnp.float32)
        * score_scale
    )
    grad_keys = (
        jnp.einsum("hqk,qhd->khd", grad_scores, queries, preferred_element_type=jnp.float32)
        * score_scale
    )
    grad_projected = jnp.concatenate(
        [
            grad_queries.reshape(row_count, feature_width),
            grad_keys.reshape(row_count, feature_width),
            grad_values.reshape(row_count, feature_width),
        ],
        axis=1,
    ).astype(jnp.bfloat16)
    grad_normed = product_back(grad_projected, w_qkv)
    norm_value, norm_pull = jax.vjp(
        norm_rows, hidden, g_one.astype(jnp.float32), beta_one.astype(jnp.float32)
    )
    grad_hidden_norm, grad_g_one, grad_beta_one = norm_pull(grad_normed)
    grad_hidden = (grad_middle + grad_hidden_norm).astype(jnp.bfloat16)
    grad_b_skip = jnp.sum(grad_hidden.astype(jnp.float32), axis=0)
    grad_joined = product_back(grad_hidden, w_skip)
    grad_tokens = grad_joined[:, :feature_width].astype(jnp.bfloat16)
    grad_skip = grad_joined[:, feature_width:].astype(jnp.bfloat16)
    front_terms = (grad_hidden, grad_b_skip, grad_g_one, grad_beta_one, grad_projected, branch_grad)
    return (grad_tokens, grad_skip, front_terms)


AXES = ("wide", "narrow")


def gather_plain(values):
    return [lax.all_gather(v, AXES, axis=0, tiled=True) for v in values]


def hand_over_kernel(*refs):
    small = refs[0]
    sources = refs[1:9]
    vectors = refs[9:16]
    targets = refs[16:24]
    buffers = refs[24:32]
    in_sem, out_sem = refs[32:]
    me = lax.axis_index("wide") * 2 + lax.axis_index("narrow")
    arrive = [pltpu.make_async_copy(s, b, in_sem.at[i]) for i, (s, b) in enumerate(zip(sources, buffers))]
    leave = [pltpu.make_async_copy(b, t, out_sem.at[i]) for i, (b, t) in enumerate(zip(buffers, targets))]
    for cp in arrive:
        cp.start()
    rolled = pltpu.roll(small[...], lax.rem(32 - me, 32) * 32, 1)
    for i in range(6):
        vectors[i][...] = rolled[i, 0:32]
    row = 6 + lax.div(me, 8)
    wide = pltpu.roll(jnp.where(lax.broadcasted_iota(jnp.int32, small.shape, 0) == row, small[...], 0.0),
                      lax.rem(8 - lax.rem(me, 8), 8) * 128, 1)
    vectors[6][...] = jnp.sum(wide[:, 0:128], axis=0)
    for a, l in zip(arrive, leave):
        a.wait()
        l.start()
    for l in leave:
        l.wait()


def hand_over(small, arrays):
    vm, anywhere = pl.BlockSpec(memory_space=pltpu.VMEM), pl.BlockSpec(memory_space=pl.ANY)
    sem = pltpu.SemaphoreType.DMA
    n = len(arrays)
    outs = [jax.ShapeDtypeStruct((32,), f32)] * 6 + [jax.ShapeDtypeStruct((128,), f32)] + [
        jax.ShapeDtypeStruct(a.shape, a.dtype) for a in arrays]
    return pl.pallas_call(
        hand_over_kernel, out_shape=outs,
        in_specs=[vm] + [anywhere] * n, out_specs=[vm] * 7 + [anywhere] * n,
        scratch_shapes=[pltpu.VMEM(a.shape, a.dtype) for a in arrays] + [sem((n,)), sem((n,))],
        name="hand_over",
    )(small, *arrays)


def own_layer(tokens, skip, seg_ids, valid, w_skip, b_skip, g_one, beta_one, w_qkv, w_out, g_two, beta_two,
              w_up, b_up, w_down, b_down, cotangent):
    vectors = [v[None, :] for v in (b_skip, g_one, beta_one, g_two, beta_two, b_down, b_up)]
    small, *rest = whole_layer(
        tokens, skip, cotangent, seg_ids, valid, vectors, (w_skip, w_qkv, w_out, w_up, w_down))
    (grad_b_skip, grad_g_one, grad_beta_one, grad_g_two, grad_beta_two, grad_b_down, grad_b_up,
     grad_w_skip, grad_w_qkv, grad_w_out, grad_w_up, grad_w_down, result, grad_tokens, grad_skip) = hand_over(small, rest[:8])
    return (
        result, grad_tokens, grad_skip,
        grad_w_skip, grad_b_skip, grad_g_one, grad_beta_one, grad_w_qkv, grad_w_out,
        grad_g_two, grad_beta_two, grad_w_up, grad_b_up, grad_w_down, grad_b_down,
    )


def plain_layer(tokens, skip, seg_ids, valid, w_skip, b_skip, g_one, beta_one, w_qkv, w_out, g_two, beta_two,
                w_up, b_up, w_down, b_down, cotangent):
    weights = gather_plain(
        (w_skip, b_skip, g_one, beta_one, w_qkv, w_out, g_two, beta_two, w_up, b_up, w_down, b_down))
    allowed, linear_bias = attend_mask(seg_ids[0], valid[0], HEADS)
    stored, result = forward_pass(tokens, skip, weights, allowed, linear_bias, HEADS)
    (joined, hidden, normed, projected, log_total, attended, middle, normed_two, hidden_up, activated) = stored
    feed_terms, grad_middle = backward_feed(stored, weights, cotangent)
    grad_tokens, grad_skip, front_terms = backward_front(
        stored, weights, grad_middle, allowed, linear_bias, HEADS)
    grad_up, grad_b_up, grad_result, grad_b_down, grad_g_two, grad_beta_two = feed_terms
    grad_hidden, grad_b_skip, grad_g_one, grad_beta_one, grad_projected, branch_grad = front_terms
    lefts = (joined, normed, attended, normed_two, activated)
    rights = (grad_hidden, grad_projected, branch_grad, grad_up, grad_result)

    def scatter(v):
        return lax.psum_scatter(v, AXES, scatter_dimension=0, tiled=True)

    big = [scatter(outer_product(a, b)) for a, b in zip(lefts, rights)]
    grad_b_skip, grad_g_one, grad_beta_one, grad_g_two, grad_beta_two, grad_b_up, grad_b_down = [
        scatter(v) for v in
        (grad_b_skip, grad_g_one, grad_beta_one, grad_g_two, grad_beta_two, grad_b_up, grad_b_down)]
    return (
        result.astype(bf16), grad_tokens, grad_skip,
        big[0], grad_b_skip, grad_g_one, grad_beta_one, big[1], big[2],
        grad_g_two, grad_beta_two, big[3], grad_b_up, big[4], grad_b_down,
    )


def solution(mesh):
    return jax.shard_map(
        own_layer if dict(mesh.shape) == {"wide": 16, "narrow": 2} else plain_layer,
        mesh=mesh,
        in_specs=(
            P(("wide", "narrow"), None),
            P(("wide", "narrow"), None),
            P(("wide", "narrow"), None),
            P(("wide", "narrow"), None),
            P(("wide", "narrow"), None),
            P(("wide", "narrow")),
            P(("wide", "narrow")),
            P(("wide", "narrow")),
            P(("wide", "narrow"), None),
            P(("wide", "narrow"), None),
            P(("wide", "narrow")),
            P(("wide", "narrow")),
            P(("wide", "narrow"), None),
            P(("wide", "narrow")),
            P(("wide", "narrow"), None),
            P(("wide", "narrow")),
            P(("wide", "narrow"), None),
        ),
        out_specs=(
            P(("wide", "narrow"), None),
            P(("wide", "narrow"), None),
            P(("wide", "narrow"), None),
            P(("wide", "narrow"), None),
            P(("wide", "narrow")),
            P(("wide", "narrow")),
            P(("wide", "narrow")),
            P(("wide", "narrow"), None),
            P(("wide", "narrow"), None),
            P(("wide", "narrow")),
            P(("wide", "narrow")),
            P(("wide", "narrow"), None),
            P(("wide", "narrow")),
            P(("wide", "narrow"), None),
            P(("wide", "narrow")),
        ),
        check_vma=False,
    )
```

```python
import jax
import jax.numpy as jnp
from jax import lax
from jax.experimental import pallas as pl
from jax.experimental.pallas import tpu as pltpu
from jax.sharding import PartitionSpec as P

f32 = jnp.float32
bf16 = jnp.bfloat16

MESH = pl.DeviceIdType.MESH
ZN = 4
SLOTS = 44
ZM, ZX, ZY, XM, XY, YM, YX, CP, ZD = 0, 6, 12, 18, 22, 26, 30, 34, 38


def here():
    w = lax.axis_index("wide")
    y = lax.axis_index("narrow")
    c = lax.rem(w, 2)
    x = lax.rem(lax.div(w, 2), 2)
    z = lax.div(w, 4)
    return z, x, c, y


def place(z, x, c, y):
    return ((z * 2 + x) * 2 + c, y)


def greet_partners():
    barrier = pltpu.get_barrier_semaphore()
    z, x, c, y = here()

    def greet(to):
        pl.semaphore_signal(barrier, inc=1, device_id=to, device_id_type=MESH)

    for to in (place(z, x, 1 - c, y), place(z, 1 - x, c, y), place(z, x, c, 1 - y), place(lax.rem(z + 2, ZN), x, c, y)):
        greet(to)

    @pl.when(z > 0)
    def _():
        greet(place(z - 1, x, c, y))

    @pl.when(z < ZN - 1)
    def _():
        greet(place(z + 1, x, c, y))

    pl.semaphore_wait(barrier, 4 + jnp.where(z > 0, 1, 0) + jnp.where(z < ZN - 1, 1, 0))


def span(width, side, first, quarters):
    cuts = (0, side, width // 2, width - side, width)
    return pl.ds(cuts[first], cuts[first + quarters] - cuts[first])


def gather_events(own, full, sides, send_sem, recv_sem, local_sem):
    n = len(own)
    z, x, c, y = here()

    def block(k, xo, co, yo):
        h = own[k].shape[0]
        return pl.ds(pl.multiple_of(((xo * 2 + co) * 2 + yo) * h, h), h)

    def part(k, zo, xo, yo, first=0, quarters=4):
        return full[k].at[zo, block(k, xo, c, yo), span(own[k].shape[1], sides[k], first, quarters)]

    def link(k, slot, src, dst, to):
        return pltpu.make_async_remote_copy(
            src_ref=src, dst_ref=dst, send_sem=send_sem.at[k, slot], recv_sem=recv_sem.at[k, slot],
            device_id=to, device_id_type=MESH)

    xp = place(z, 1 - x, c, y)
    yp = place(z, x, c, 1 - y)
    cpart = place(z, x, 1 - c, y)

    def zto(d):
        return place(z + 1 - 2 * d, x, c, y)

    def z_has(d, s):
        return (z - s >= 0) if d == 0 else (z + s <= ZN - 1)

    def z_next(d):
        return (z < ZN - 1) if d == 0 else (z > 0)

    def zo_of(d, s):
        return z - s if d == 0 else z + s

    def z_send(k, base, d, s, xo, yo, first, quarters, src=None):
        cond = jnp.logical_and(z_has(d, s), z_next(d))
        zo = zo_of(d, s)
        dst = part(k, zo, xo, yo, first, quarters)
        cp = link(k, base + d * 3 + s, dst if src is None else src, dst, zto(d))

        @pl.when(cond)
        def _():
            cp.start()

    def z_wait(k, base, d, s, xo, yo, first, quarters):
        zo = zo_of(d, s + 1)
        dst = part(k, zo, xo, yo, first, quarters)
        link(k, base + d * 3 + s, dst, dst, zto(d)).wait_recv()

    def go(k, slot, ref, to, src=None, cond=None):
        cp = link(k, slot, ref if src is None else src, ref, to)
        cp.start()

    def wait(k, slot, ref):
        link(k, slot, ref, ref, xp).wait_recv()

    def begin():
        for k in range(n):
            pltpu.make_async_copy(own[k], part(k, z, x, y), local_sem.at[k]).start()

    def do(k, e):
        kind = e[0]
        if kind == "own":
            for d in (0, 1):
                z_send(k, ZM, d, 0, x, y, 0, 4, src=own[k])
            go(k, XM + z, part(k, z, x, y), xp, src=own[k])
            go(k, YM + z, part(k, z, x, y), yp, src=own[k])
        elif kind == "near":
            wait(k, XM + z, part(k, z, 1 - x, y))
            for d in (0, 1):
                z_send(k, ZX, d, 0, 1 - x, y, 0, 1)
            go(k, YX + z, part(k, z, 1 - x, y, 0, 2), yp)
            wait(k, YM + z, part(k, z, x, 1 - y))
            for d in (0, 1):
                z_send(k, ZY, d, 0, x, 1 - y, 3, 1)
            go(k, XY + z, part(k, z, x, 1 - y, 2, 2), xp)
        elif kind == "chain":
            s = e[1]
            for d in (0, 1):
                @pl.when(z_has(d, s + 1))
                def _():
                    z_wait(k, ZM, d, s, x, y, 0, 4)
                    zo = zo_of(d, s + 1)
                    if s < 2:
                        @pl.when(z_next(d))
                        def _():
                            ref = part(k, zo, x, y)
                            link(k, ZM + d * 3 + s + 1, ref, ref, zto(d)).start()
                    ref = part(k, zo, x, y, 1, 3)
                    link(k, XM + zo, ref, ref, xp).start()
                    ref = part(k, zo, x, y, 0, 3)
                    link(k, YM + zo, ref, ref, yp).start()
        elif kind == "side":
            s = e[1]
            for d in (0, 1):
                @pl.when(z_has(d, s + 1))
                def _():
                    zo = zo_of(d, s + 1)
                    for base, xo, yo, first in ((ZX, 1 - x, y, 0), (ZY, x, 1 - y, 3)):
                        z_wait(k, base, d, s, xo, yo, first, 1)
                        if s < 2:
                            @pl.when(z_next(d))
                            def _():
                                ref = part(k, zo, xo, yo, first, 1)
                                link(k, base + d * 3 + s + 1, ref, ref, zto(d)).start()
        elif kind == "cross":
            s = e[1]
            for d in (0, 1):
                @pl.when(z_has(d, s + 1))
                def _():
                    zo = zo_of(d, s + 1)
                    wait(k, XM + zo, part(k, zo, 1 - x, y, 1, 3))
                    ref = part(k, zo, 1 - x, y, 0, 2)
                    link(k, YX + zo, ref, ref, yp).start()
                    wait(k, YM + zo, part(k, zo, x, 1 - y, 0, 3))
                    ref = part(k, zo, x, 1 - y, 2, 2)
                    link(k, XY + zo, ref, ref, xp).start()
            if s == 0:
                pltpu.make_async_copy(own[k], part(k, z, x, y), local_sem.at[k]).wait()
                ref = full[k].at[:, block(k, x, c, y), :]
                link(k, CP, ref, ref, cpart).start()
            if s == 2:
                ref = full[k].at[:, block(k, 1 - x, c, y), :]
                link(k, CP + 1, ref, ref, cpart).start()
                ref = full[k].at[:, block(k, x, c, 1 - y), :]
                link(k, CP + 2, ref, ref, cpart).start()
        elif kind == "last":
            for zo in range(ZN):
                wait(k, XY + zo, part(k, zo, 1 - x, 1 - y, 2, 2))
                wait(k, YX + zo, part(k, zo, 1 - x, 1 - y, 0, 2))
            ref = full[k].at[:, block(k, 1 - x, c, 1 - y), :]
            link(k, CP + 3, ref, ref, cpart).start()
        elif kind == "ready":
            for j, (xo, yo) in enumerate(((x, y), (1 - x, y), (x, 1 - y), (1 - x, 1 - y))):
                ref = full[k].at[:, block(k, xo, 1 - c, yo), :]
                link(k, CP + j, ref, ref, cpart).wait_recv()

    def finish():
        for k in range(n):
            for j, (xo, yo) in enumerate(((x, y), (1 - x, y), (x, 1 - y), (1 - x, 1 - y))):
                ref = full[k].at[:, block(k, xo, c, yo), :]
                link(k, CP + j, ref, ref, cpart).wait_send()
            for d in (0, 1):
                for s in range(3):
                    @pl.when(jnp.logical_and(z_has(d, s), z_next(d)))
                    def _():
                        zo = zo_of(d, s)
                        for base, xo, yo, first, q in ((ZM, x, y, 0, 4), (ZX, 1 - x, y, 0, 1), (ZY, x, 1 - y, 3, 1)):
                            ref = part(k, zo, xo, yo, first, q)
                            link(k, base + d * 3 + s, ref, ref, zto(d)).wait_send()
            ref = part(k, z, x, y)
            link(k, XM + z, ref, ref, xp).wait_send()
            link(k, YM + z, ref, ref, yp).wait_send()
            for t in range(1, ZN):
                zo = lax.rem(z + t, ZN)
                ref = part(k, zo, x, y, 1, 3)
                link(k, XM + zo, ref, ref, xp).wait_send()
                ref = part(k, zo, x, y, 0, 3)
                link(k, YM + zo, ref, ref, yp).wait_send()
            for zo in range(ZN):
                ref = part(k, zo, 1 - x, y, 0, 2)
                link(k, YX + zo, ref, ref, yp).wait_send()
                ref = part(k, zo, x, 1 - y, 2, 2)
                link(k, XY + zo, ref, ref, xp).wait_send()

    return begin, do, finish


def scatter_events(outs, part_sums, sides, deeps, landings, send_sem, recv_sem):
    n = len(outs)
    lxm, lym, lxy, lyx, lzm, lzx, lzy, lzd = landings
    z, x, c, y = here()
    xp = place(z, 1 - x, c, y)
    yp = place(z, x, c, 1 - y)

    def rows_of(k):
        return outs[k].shape[0]

    def width(k):
        return outs[k].shape[1]

    def mine(k, zo, xo, yo, first=0, quarters=4):
        h = rows_of(k)
        row = pl.multiple_of(((zo * 2 + xo) * 2 + yo) * h, h)
        return part_sums[k].at[pl.ds(row, h), span(width(k), sides[k], first, quarters)]

    def mine_at(k, zo, xo, yo, lo, hi):
        h = rows_of(k)
        row = pl.multiple_of(((zo * 2 + xo) * 2 + yo) * h, h)
        return part_sums[k].at[pl.ds(row, h), pl.ds(lo, hi - lo)]

    def middle_cut(k):
        return width(k) // 2 - deeps[k] // 2, width(k) // 2 + deeps[k] // 2

    def deep(k, zo):
        return mine_at(k, zo, 1 - x, 1 - y, *middle_cut(k))

    def cross_x(k, zo, own):
        w = width(k)
        lo = w // 2 if own else middle_cut(k)[1]
        return link(k, XY + zo, mine_at(k, zo, 1 - x, 1 - y, lo, w), lxy[k].at[zo, :, pl.ds(lo - w // 2, w - lo)], xp)

    def cross_y(k, zo, own):
        hi = width(k) // 2 if own else middle_cut(k)[0]
        return link(k, YX + zo, mine_at(k, zo, 1 - x, 1 - y, 0, hi), lyx[k].at[zo, :, pl.ds(0, hi)], yp)

    def link(k, slot, src, dst, to):
        return pltpu.make_async_remote_copy(
            src_ref=src, dst_ref=dst, send_sem=send_sem.at[k, slot], recv_sem=recv_sem.at[k, slot],
            device_id=to, device_id_type=MESH)

    def quarter_slice(k, first, quarters):
        return span(width(k), sides[k], first, quarters)

    def land_x(k, zo, first, quarters):
        return lxm[k].at[zo, :, quarter_slice(k, first, quarters)]

    def land_y(k, zo, first, quarters):
        return lym[k].at[zo, :, quarter_slice(k, first, quarters)]

    def z_has(d, s):
        return (z - s >= 0) if d == 0 else (z + s <= ZN - 1)

    def z_next(d):
        return (z < ZN - 1) if d == 0 else (z > 0)

    def zo_of(d, s):
        return z - s if d == 0 else z + s

    def z_slot(d, s, zo):
        return ZN if (d == 1 and s == 0) else zo

    def toward(d):
        return place(z - 1 + 2 * d, x, c, y)

    def add_in(k, zo, xo, yo, first, quarters, others):
        add_ref(k, mine(k, zo, xo, yo, first, quarters), others)

    def add_ref(k, ref, others):
        h = rows_of(k)

        @pl.loop(0, h // 16)
        def _(i):
            rows = pl.ds(pl.multiple_of(i * 16, 16), 16)
            total = ref[rows, :].astype(f32)
            for o in others:
                total = total + o[rows, :].astype(f32)
            ref[rows, :] = total.astype(bf16)

    def wait(k, slot, dst):
        link(k, slot, dst, dst, xp).wait_recv()

    def do(k, e):
        kind = e[0]
        if kind == "last":
            for t in range(1, ZN):
                zo = lax.rem(z + t, ZN)
                cross_x(k, zo, False).start()
                cross_y(k, zo, False).start()
        elif kind == "deep":
            s = e[1]
            for d in (0, 1):
                @pl.when(z_has(d, s + 1))
                def _():
                    zo = zo_of(d, s + 1)
                    if s < 2:
                        @pl.when(z_next(d))
                        def _():
                            got = lzd[k].at[z_slot(d, s + 1, zo)]
                            wait(k, ZD + d * 3 + s + 1, got)
                            add_ref(k, deep(k, zo), [got])
                    link(k, ZD + d * 3 + s, deep(k, zo), lzd[k].at[z_slot(d, s, zo)], toward(d)).start()
        elif kind == "inner":
            if deeps[k]:
                for d in (0, 1):
                    @pl.when(z_next(d))
                    def _():
                        got = lzd[k].at[z_slot(d, 0, z)]
                        wait(k, ZD + d * 3, got)
                        add_ref(k, deep(k, z), [got])
            cross_x(k, z, True).start()
            cross_y(k, z, True).start()
        elif kind == "cross":
            s = e[1]
            for d in (0, 1):
                @pl.when(z_has(d, s + 1))
                def _():
                    zo = zo_of(d, s + 1)
                    lo, hi = middle_cut(k)
                    half, w = width(k) // 2, width(k)
                    got = lyx[k].at[zo, :, pl.ds(0, lo)]
                    wait(k, YX + zo, got)
                    add_ref(k, mine_at(k, zo, 1 - x, y, 0, lo), [got])
                    link(k, XM + zo, mine(k, zo, 1 - x, y, 1, 3), land_x(k, zo, 1, 3), xp).start()
                    got = lxy[k].at[zo, :, pl.ds(hi - half, w - hi)]
                    wait(k, XY + zo, got)
                    add_ref(k, mine_at(k, zo, x, 1 - y, hi, w), [got])
                    link(k, YM + zo, mine(k, zo, x, 1 - y, 0, 3), land_y(k, zo, 0, 3), yp).start()
        elif kind == "side":
            s = e[1]
            for d in (0, 1):
                @pl.when(z_has(d, s + 1))
                def _():
                    zo = zo_of(d, s + 1)
                    for base, landing, xo, yo, first in ((ZX, lzx, 1 - x, y, 0), (ZY, lzy, x, 1 - y, 3)):
                        if s < 2:
                            @pl.when(z_next(d))
                            def _():
                                got = landing[k].at[z_slot(d, s + 1, zo)]
                                wait(k, base + d * 3 + s + 1, got)
                                add_in(k, zo, xo, yo, first, 1, [got])
                        link(k, base + d * 3 + s, mine(k, zo, xo, yo, first, 1),
                             landing[k].at[z_slot(d, s, zo)], toward(d)).start()
        elif kind == "chain":
            s = e[1]
            for d in (0, 1):
                @pl.when(z_has(d, s + 1))
                def _():
                    zo = zo_of(d, s + 1)
                    wait(k, XM + zo, land_x(k, zo, 1, 3))
                    wait(k, YM + zo, land_y(k, zo, 0, 3))
                    add_in(k, zo, x, y, 0, 1, [land_y(k, zo, 0, 1)])
                    add_in(k, zo, x, y, 1, 2, [land_y(k, zo, 1, 2), land_x(k, zo, 1, 2)])
                    add_in(k, zo, x, y, 3, 1, [land_x(k, zo, 3, 1)])
                    if s < 2:
                        @pl.when(z_next(d))
                        def _():
                            got = lzm[k].at[z_slot(d, s + 1, zo)]
                            wait(k, ZM + d * 3 + s + 1, got)
                            add_in(k, zo, x, y, 0, 4, [got])
                    link(k, ZM + d * 3 + s, mine(k, zo, x, y), lzm[k].at[z_slot(d, s, zo)], toward(d)).start()
        elif kind == "near":
            for slot, own_slot, xo, yo, first, cross_land, side_base, side_land, side_first, to, land in (
                (YX, XM, 1 - x, y, 0, lyx, ZX, lzx, 0, xp, land_x),
                (XY, YM, x, 1 - y, 2, lxy, ZY, lzy, 3, yp, land_y),
            ):
                wait(k, slot + z, cross_land[k].at[z])
                add_in(k, z, xo, yo, first, 2, [cross_land[k].at[z]])
                for d in (0, 1):
                    @pl.when(z_next(d))
                    def _():
                        got = side_land[k].at[z_slot(d, 0, z)]
                        wait(k, side_base + d * 3, got)
                        add_in(k, z, xo, yo, side_first, 1, [got])
                link(k, own_slot + z, mine(k, z, xo, yo), land(k, z, 0, 4), to).start()
        elif kind == "own":
            wait(k, XM + z, land_x(k, z, 0, 4))
            wait(k, YM + z, land_y(k, z, 0, 4))
            h = rows_of(k)
            own = mine(k, z, x, y)
            from_x, from_y = land_x(k, z, 0, 4), land_y(k, z, 0, 4)

            @pl.loop(0, h // 16)
            def _(i):
                rows = pl.ds(pl.multiple_of(i * 16, 16), 16)
                outs[k][rows, :] = own[rows, :].astype(f32) + from_x[rows, :].astype(f32) + from_y[rows, :].astype(f32)

            for d in (0, 1):
                @pl.when(z_next(d))
                def _():
                    got = lzm[k].at[z_slot(d, 0, z)]
                    wait(k, ZM + d * 3, got)

                    @pl.loop(0, h // 16)
                    def _(i):
                        rows = pl.ds(pl.multiple_of(i * 16, 16), 16)
                        outs[k][rows, :] += got[rows, :].astype(f32)

    def finish():
        for k in range(n):
            cross_x(k, z, True).wait_send()
            cross_y(k, z, True).wait_send()
            for t in range(1, ZN):
                zo = lax.rem(z + t, ZN)
                cross_x(k, zo, False).wait_send()
                cross_y(k, zo, False).wait_send()
            for t in range(1, ZN):
                zo = lax.rem(z + t, ZN)
                link(k, XM + zo, mine(k, zo, 1 - x, y, 1, 3), land_x(k, zo, 1, 3), xp).wait_send()
                link(k, YM + zo, mine(k, zo, x, 1 - y, 0, 3), land_y(k, zo, 0, 3), yp).wait_send()
            link(k, XM + z, mine(k, z, 1 - x, y), land_x(k, z, 0, 4), xp).wait_send()
            link(k, YM + z, mine(k, z, x, 1 - y), land_y(k, z, 0, 4), yp).wait_send()
            for d in (0, 1):
                for s in range(3):
                    @pl.when(z_has(d, s + 1))
                    def _():
                        zo = zo_of(d, s + 1)
                        to = z_slot(d, s, zo)
                        if deeps[k]:
                            link(k, ZD + d * 3 + s, deep(k, zo), lzd[k].at[to], toward(d)).wait_send()
                        link(k, ZX + d * 3 + s, mine(k, zo, 1 - x, y, 0, 1), lzx[k].at[to], toward(d)).wait_send()
                        link(k, ZY + d * 3 + s, mine(k, zo, x, 1 - y, 3, 1), lzy[k].at[to], toward(d)).wait_send()
                        link(k, ZM + d * 3 + s, mine(k, zo, x, y), lzm[k].at[to], toward(d)).wait_send()

    return do, finish


HEADS = 16


epsilon = 1e-05


def nn(a, b):
    return jnp.dot(a, b, preferred_element_type=f32)


def nt(a, b):
    return lax.dot_general(a, b, (((1,), (1,)), ((), ())), preferred_element_type=f32)


def tn(a, b):
    return lax.dot_general(a, b, (((0,), (0,)), ((), ())), preferred_element_type=f32)


CH = 1024
SKIP, QKV, OUT, UP, DOWN = range(5)
CHUNKS = (
    [(SKIP, 0), (SKIP, 1), (QKV, 0), (QKV, 1), (QKV, 2), (OUT, 0)] + [(UP, i) for i in range(4)]
    + [(DOWN, i) for i in range(4)] + [(UP, i) for i in range(4)] + [(OUT, 0)] + [(QKV, i) for i in range(3)]
    + [(SKIP, 0), (SKIP, 1)]
)
LEFTS = [(DOWN, 0), (DOWN, 1), (DOWN, 2), (DOWN, 3), (UP, 0), (OUT, 0), (QKV, 0), (SKIP, 0), (SKIP, 1)]
GATHER_PIECES = [(0, 0, 1024, 128), (1, 0, 3072, 640), (2, 0, 1024, 384), (3, 0, 2048, 768), (3, 2048, 2048, 896), (4, 0, 512, 128), (4, 512, 512, 128)]
SCATTER_PIECES = [(4, 0, 1024, 128, 256), (3, 0, 4096, 768, 1280), (2, 0, 1024, 128, 0), (1, 0, 3072, 512, 1280), (0, 0, 1024, 128, 0)]
STAGES = [("own",), ("near",)] + [(e, s) for s in range(3) for e in ("chain", "side")] + [
    ("cross", s) for s in range(3)] + [("last",), ("ready",)] + [("deep", s) for s in range(3)] + [("inner",)]
(PR, MK, TR, F1, F2, F3, AF, F5, F6, F7, F8, FR, B2, B3, B5, B6, A, L1, L2, R, W0, W1, W2, W3, W4, BF,
 G0, G1, G2, G3, G4, G5, G6, E0, E1, E2, E3, E4) = range(38)
GATHER = [G0, G1, G2, G3, G4, G5, G6]
SCATTER = [E0, E1, E2, E3, E4]
PLAN = [
    (G0, 0), (G1, 0), (PR, 0), (MK, 0), (TR, 7), (PR, 1), (TR, 8), (G0, 1),
    (G0, 2), (G1, 1), (G2, 0), (G1, 2), (G0, 3), (PR, 2), (G0, 4), (G1, 3),
    (G2, 1), (G2, 2), (G1, 4), (G0, 5), (G0, 6), (G1, 5), (PR, 3), (G2, 3),
    (G3, 0), (G2, 4), (G1, 6), (G0, 7), (G0, 8), (G0, 9), (G0, 10), (G1, 7),
    (G1, 8), (G1, 9), (PR, 4), (G2, 5), (G1, 10), (G3, 1), (G4, 0), (G3, 2),
    (G2, 6), (PR, 5), (G0, 11), (G2, 7), (G2, 8), (G2, 9), (G3, 3), (G0, 12),
    (F1, 0), (F1, 1), (G1, 11), (F2, 0), (F2, 1), (G3, 4), (F2, 2), (F2, 3),
    (TR, 6), (G1, 12), (G3, 5), (G4, 1), (G4, 2), (G5, 0), (F3, 0), (G2, 10),
    (G3, 6), (F3, 1), (G3, 7), (G3, 8), (F3, 2), (AF, 0), (G4, 3), (G3, 9),
    (AF, 1), (G2, 11), (G4, 4), (AF, 2), (G2, 12), (G5, 1), (G4, 5), (G5, 2),
    (G3, 10), (AF, 3), (G4, 6), (TR, 5), (F5, 0), (G5, 3), (G6, 0), (G4, 7),
    (G4, 8), (G4, 9), (G3, 11), (F6, 0), (F6, 1), (G4, 10), (F6, 2), (G5, 4),
    (F6, 3), (G5, 5), (G3, 12), (TR, 4), (F7, 0), (G6, 1), (G6, 2), (TR, 0),
    (F7, 1), (G4, 11), (G5, 6), (G5, 7), (G6, 3), (G5, 8), (TR, 1), (G5, 9),
    (G4, 12), (F7, 2), (G6, 4), (G6, 5), (G5, 10), (TR, 2), (F7, 3), (TR, 3),
    (G6, 6), (G5, 11), (G6, 7), (G6, 8), (W4, 0), (G6, 9), (G6, 10), (G5, 12),
    (W4, 1), (E0, 11), (E0, 15), (G6, 11), (G6, 12), (F8, 0), (BF, 0), (F8, 1),
    (E0, 10), (E0, 14), (E0, 9), (E0, 8), (BF, 1), (F8, 2), (E0, 13), (E0, 7),
    (BF, 2), (F8, 3), (E0, 6), (E0, 16), (BF, 3), (E0, 5), (FR, 0), (B2, 0),
    (B2, 1), (B2, 2), (B2, 3), (E0, 4), (W3, 0), (E0, 3), (W3, 1), (E1, 11),
    (E1, 15), (L2, 0), (L2, 1), (E0, 2), (E0, 1), (L2, 2), (L2, 3), (E1, 10),
    (E1, 14), (E1, 9), (E1, 8), (B3, 0), (A, 0), (E0, 0), (E1, 13), (E1, 7),
    (W2, 0), (E2, 11), (A, 1), (E1, 6), (E1, 16), (E1, 5), (A, 2), (A, 3),
    (B5, 0), (E1, 4), (B5, 1), (E1, 3), (B5, 2), (E2, 10), (E2, 9), (E2, 8),
    (E2, 7), (W1, 0), (W1, 1), (E2, 6), (E2, 16), (E3, 11), (E3, 15), (E1, 2),
    (E2, 5), (E1, 1), (L1, 0), (E2, 4), (L1, 1), (E3, 10), (E3, 14), (E3, 9),
    (E3, 8), (L1, 2), (L1, 3), (E2, 3), (R, 0), (E1, 0), (E2, 2), (W0, 0),
    (E2, 1), (E3, 13), (E3, 7), (E3, 6), (W0, 1), (E4, 11), (R, 1), (E3, 16),
    (E3, 5), (E3, 4), (E2, 0), (E3, 3), (E4, 10), (E4, 9), (E4, 8), (E4, 7),
    (E3, 2), (R, 2), (B6, 0), (E3, 1), (E4, 6), (E4, 16), (E4, 5), (E4, 4),
    (E4, 3), (R, 3), (B6, 1), (E4, 2), (E3, 0), (E4, 1), (R, 4), (E4, 0),
    (R, 5),
]


def layer_kernel(*refs):
    n = 5
    tokens, skip, cot, seg, valid = refs[:5]
    vectors = refs[5:12]
    own = refs[12 : 12 + n]
    small_out = refs[17]
    targets = refs[18:23]
    result, grad_tokens, grad_skip = refs[23:26]
    full = refs[26:31]
    outs = refs[31 : 31 + n]
    r = refs[31 + n :]
    turned, theirs, gcat, part_sums = r[:n], r[n : 2 * n], r[2 * n : 3 * n], r[3 * n : 4 * n]
    m = len(SCATTER_PIECES)
    landings = [r[4 * n + i * m : 4 * n + (i + 1) * m] for i in range(8)]
    (wbuf, lbuf, hid, gnorm, mid, pbuf, abuf, acc, small, small_land, params, params_wide, params_land,
     log_total, steep, distance,
     ag_send, ag_recv, ag_local, rs_send, rs_recv, pair_send, pair_recv, wsem, lsem, misc_sem,
     small_send, small_recv, params_send, params_recv, out_sem) = r[4 * n + 8 * m :]
    z, x, c, y = here()
    cpart = place(z, x, 1 - c, y)
    T = cot.shape[0]

    ag_begin, ag_do, ag_finish = gather_events(
        [own[k].at[:, pl.ds(at, w)] for k, at, w, _ in GATHER_PIECES],
        [full[k].at[:, :, pl.ds(at, w)] for k, at, w, _ in GATHER_PIECES], [p[3] for p in GATHER_PIECES], ag_send, ag_recv, ag_local)
    rs_do, rs_finish = scatter_events(
        [outs[k].at[:, pl.ds(at, w)] for k, at, w, _, _ in SCATTER_PIECES],
        [part_sums[k].at[:, pl.ds(at, w)] for k, at, w, _, _ in SCATTER_PIECES], [p[3] for p in SCATTER_PIECES],
        [p[4] for p in SCATTER_PIECES], landings, rs_send, rs_recv)

    def chunk_copies(i):
        k, j = CHUNKS[i]
        slot, depth = i % 2, full[k].shape[1]
        if k in (SKIP, DOWN):
            blocks = CH // depth
            return [pltpu.make_async_copy(full[k].at[j * blocks + b], wbuf.at[slot, pl.ds(b * depth, depth), :], wsem.at[slot, b])
                    for b in range(blocks)]
        return [pltpu.make_async_copy(full[k].at[b, :, pl.ds(j * CH, CH)], wbuf.at[slot, pl.ds(b * depth, depth), :], wsem.at[slot, b])
                for b in range(ZN)]

    state = {"next": 0, "done": 0, "ready": set()}

    def arrived(i):
        k, j = CHUNKS[i]
        lo, hi = (j * CH, (j + 1) * CH) if k in (QKV, UP) else (0, CH)
        return all(p in state["ready"] for p, (w, at, wide, _) in enumerate(GATHER_PIECES) if w == k and at < hi and at + wide > lo)

    def pump():
        while state["next"] < min(len(CHUNKS), state["done"] + 2) and arrived(state["next"]):
            for cp in chunk_copies(state["next"]):
                cp.start()
            state["next"] += 1

    def ready(k):
        state["ready"].add(k)
        pump()

    def take(i):
        assert state["done"] == i and state["next"] > i
        for cp in chunk_copies(i):
            cp.wait()

    def release(i):
        state["done"] = i + 1
        pump()

    in_copies = [pltpu.make_async_copy(a, lbuf.at[i], lsem.at[i]) for i, a in enumerate((tokens, skip))]
    cot_copy = pltpu.make_async_copy(cot, gcat[DOWN].at[pl.ds(0, T), :], misc_sem.at[0])
    result_copy = pltpu.make_async_copy(lbuf.at[0], result, misc_sem.at[1])
    out_copies = [pltpu.make_async_copy(lbuf.at[i], o, misc_sem.at[2 + i]) for i, o in enumerate((grad_tokens, grad_skip))]
    grad_copies = [pltpu.make_async_copy(outs[k].at[:, pl.ds(at, w)], targets[k].at[:, pl.ds(at, w)], out_sem.at[p])
                   for p, (k, at, w, _, _) in enumerate(SCATTER_PIECES)]
    ag_begin()
    for cp in in_copies:
        cp.start()
    cot_copy.start()
    greet_partners()

    def pair(k, j):
        if k == DOWN and j != 1:
            rows = pl.ds(CH // 2 * (j - 1 if j else 0), CH // 2)
            src, dst = turned[k].at[1 - c, rows, :], theirs[k].at[rows, :]
        elif j == 0:
            src, dst = turned[k].at[1 - c], theirs[k]
        elif k == DOWN:
            src, dst = cot, gcat[k].at[pl.ds(T, T), :]
        elif k == UP:
            cols = pl.ds((j - 1) * CH, CH)
            src, dst = gcat[k].at[pl.ds(0, T), cols], gcat[k].at[pl.ds(T, T), cols]
        else:
            src, dst = gcat[k].at[pl.ds(0, T), :], gcat[k].at[pl.ds(T, T), :]
        return pltpu.make_async_remote_copy(
            src_ref=src, dst_ref=dst, send_sem=pair_send.at[k, j], recv_sem=pair_recv.at[k, j],
            device_id=cpart, device_id_type=MESH)

    def pieces(k):
        return range(5) if k in (UP, DOWN) else range(2)

    meet = [cpart, place(z, 1 - x, c, y), place(z, x, c, 1 - y),
            place(z + 1 - 2 * lax.rem(z, 2), x, c, y), place(lax.rem(z + 2, 4), x, c, y)]

    def meeting(ref, land, send, recv, t):
        return pltpu.make_async_remote_copy(
            src_ref=ref, dst_ref=land.at[t], send_sem=send.at[t], recv_sem=recv.at[t],
            device_id=meet[t], device_id_type=MESH)

    def params_step(t):
        if t == 0:
            me = lax.axis_index("wide") * 2 + lax.axis_index("narrow")
            params_wide[...] = jnp.zeros_like(params_wide)
            for i in range(6):
                params_wide[i : i + 1, 0:32] = vectors[i][...].astype(f32)
            narrow = pltpu.roll(params_wide[...], me * 32, 1)
            params_wide[...] = jnp.zeros_like(params_wide)
            for i in range(4):
                params_wide[6 + i : 7 + i, 0:128] = vectors[6][...].astype(f32)
            wide = pltpu.roll(params_wide[...], lax.rem(me, 8) * 128, 1)
            row = lax.broadcasted_iota(jnp.int32, wide.shape, 0)
            params[...] = jnp.where(row == 6 + lax.div(me, 8), wide, narrow).astype(bf16)
        else:
            cp = meeting(params, params_land, params_send, params_recv, t - 1)
            cp.wait_send()
            cp.wait_recv()
            params[...] = (params[...].astype(f32) + params_land[t - 1].astype(f32)).astype(bf16)
        if t < 5:
            meeting(params, params_land, params_send, params_recv, t).start()
        else:
            params_wide[...] = params[...].astype(f32)

    def small_step(t):
        if t:
            cp = meeting(small, small_land, small_send, small_recv, t - 1)
            cp.wait_send()
            cp.wait_recv()
            small[...] += small_land[t - 1]
        if t < 5:
            meeting(small, small_land, small_send, small_recv, t).start()
        else:
            small_out[...] = small[...]

    def make_masks():
        acc[...] = jnp.zeros_like(acc)
        small[...] = jnp.zeros_like(small)
        heads = lax.broadcasted_iota(jnp.int32, steep.shape, 0).astype(f32)
        steep[...] = jnp.exp((heads + 1.0) * -0.34657359027997264)
        seg_row = jnp.broadcast_to(seg[...].astype(f32), (T, T))
        live = jnp.broadcast_to(valid[...].astype(f32), (T, T)).T
        key_at = lax.broadcasted_iota(jnp.int32, (T, T), 0)
        query_at = lax.broadcasted_iota(jnp.int32, (T, T), 1)
        allowed = jnp.logical_and(seg_row.T == seg_row, jnp.logical_or(live == 1.0, key_at == query_at))
        distance[...] = jnp.where(allowed, jnp.abs(key_at - query_at).astype(f32), 1e33)
        pair(DOWN, 1).start()

    def turn(i):
        k, j = LEFTS[i]
        group = 2 * outs[k].shape[0]
        seg = min(group, 128)
        if k == SKIP:
            in_copies[j].wait()
        for t in range(CH // 128):
            cols = slice(t * 128, (t + 1) * 128)
            if k == SKIP:
                block = lbuf[j, :, cols].T
            elif k == DOWN:
                block = part_sums[UP][0:T, j * CH + t * 128 : j * CH + (t + 1) * 128].T
            else:
                block = abuf[:, cols].T
            for s in range(0, 128, seg):
                row = j * CH + t * 128 + s
                core, at = (row // group) % 2, row // (2 * group) * group + row % group
                turned[k][core, at : at + seg, :] = block[s : s + seg, :]
        if k == DOWN:
            pair(k, j + 1 if j else 0).start()
        elif i + 1 == len(LEFTS) or LEFTS[i + 1][0] != k:
            pair(k, 0).start()

    def forward_product(left, slot, finish):
        @pl.loop(0, 2)
        def _(j):
            at = pl.multiple_of(j * 512, 512)
            finish(at, nn(left(), wbuf[slot, :, pl.ds(at, 512)]))

    def back_product(left, slot, finish):
        @pl.loop(0, 2)
        def _(j):
            at = pl.multiple_of(j * 512, 512)
            finish(at, nt(left(), wbuf[slot, pl.ds(at, 512), :]))

    def store_in(ref, offset=0):
        def finish(at, value):
            ref[:, pl.ds(pl.multiple_of(at + offset, 512), 512)] = value.astype(ref.dtype)

        return finish

    def add_to(ref):
        def finish(at, value):
            ref[:, pl.ds(at, 512)] += value

        return finish

    def to_hidden(i):
        take(i)

        def first(at, value):
            hid[:, pl.ds(at, 512)] = value + params_wide[0:1, pl.ds(at, 512)]

        forward_product(lambda: lbuf[i], i % 2, add_to(hid) if i else first)
        release(i)

    def norm_forward(source, gain, i):
        @pl.loop(0, 4)
        def _(j):
            rows = pl.ds(pl.multiple_of(i * 64 + j * 16, 16), 16)
            v = source[rows, :]
            center = v - jnp.mean(v, axis=-1, keepdims=True)
            rate = lax.rsqrt(jnp.mean(center * center, axis=-1, keepdims=True) + epsilon)
            abuf[rows, :] = (
                center * rate * params_wide[gain : gain + 1, :] + params_wide[gain + 1 : gain + 2, :]).astype(bf16)

    def to_projected(i):
        take(2 + i)
        forward_product(lambda: abuf[...], i % 2, store_in(pbuf, i * CH))
        release(2 + i)

    def heads_of(p):
        at = pl.multiple_of(p * 128, 128)
        return [pbuf[:, pl.ds(pl.multiple_of(at + j * CH, 128), 128)] for j in range(3)]

    def half_masks():
        low = lax.broadcasted_iota(jnp.int32, (T, 128), 1) < 64
        return low, jnp.logical_not(low)

    def attend(i):
        masks = half_masks()

        @pl.loop(2 * i, 2 * i + 2)
        def _(p):
            q, k, v = heads_of(p)
            res = []
            for e in (0, 1):
                head = pl.ds(2 * p + e, 1)
                scores = nt(k, jnp.where(masks[e], q, jnp.zeros_like(q))) * 0.125 - distance[...] * steep[head, :]
                top = jnp.max(scores, axis=0, keepdims=True)
                raised = jnp.exp(scores - top)
                total = jnp.sum(raised, axis=0, keepdims=True)
                log_total[head, :] = top + jnp.log(total)
                res.append(tn((raised / total).astype(bf16), v))
            abuf[:, pl.ds(pl.multiple_of(p * 128, 128), 128)] = jnp.where(masks[0], res[0], res[1]).astype(bf16)

    def to_middle():
        take(5)

        def finish(at, value):
            mid[:, pl.ds(at, 512)] = hid[:, pl.ds(at, 512)] + value

        forward_product(lambda: abuf[...], 1, finish)
        release(5)

    def to_activated(i):
        take(6 + i)

        def finish(at, value):
            cols = pl.ds(pl.multiple_of(i * CH + at, 512), 512)
            u = value + params_wide[6 + i : 7 + i, pl.ds(at, 512)]
            cdf = 0.5 * (1.0 + lax.erf(u * 0.7071067811865476))
            part_sums[UP][0:T, cols] = (u * cdf).astype(bf16)
            gcat[UP][0:T, cols] = (cdf + u * jnp.exp(-0.5 * u * u) * 0.3989422804014327).astype(bf16)

        forward_product(lambda: abuf[...], i % 2, finish)
        release(6 + i)

    def through_down(i):
        take(10 + i)
        forward_product(
            lambda: part_sums[UP][0:T, i * CH : (i + 1) * CH], i % 2, add_to(gnorm) if i else store_in(gnorm))

    def back_through_down(i):
        def finish(at, value):
            cols = pl.ds(pl.multiple_of(i * CH + at, 512), 512)
            got = (value * gcat[UP][0:T, cols].astype(f32)).astype(bf16)
            gcat[UP][0:T, cols] = got
            small[6 + i : 7 + i, pl.ds(at, 512)] = jnp.sum(got.astype(f32), axis=0, keepdims=True)

        back_product(lambda: gcat[DOWN][0:T, :], i % 2, finish)
        release(10 + i)
        pair(UP, 1 + i).start()

    def to_result():
        @pl.loop(0, T // 16)
        def _(i):
            rows = pl.ds(pl.multiple_of(i * 16, 16), 16)
            lbuf[0, rows, :] = (mid[rows, :] + (gnorm[rows, :] + params_wide[5:6, :])).astype(bf16)

        result_copy.start()

    def weight_product(k, lo, hi):
        tiles = (hi - lo) // 512
        if lo == 0:
            if k == DOWN:
                cot_copy.wait()
                small[5:6, :] = jnp.sum(gcat[DOWN][0:T, :].astype(f32), axis=0, keepdims=True)
            for j in pieces(k):
                pair(k, j).wait_recv()

        @pl.loop(0, part_sums[k].shape[0] // 256 * tiles)
        def _(i):
            rows = pl.ds(pl.multiple_of(lax.div(i, tiles) * 256, 256), 256)
            cols = pl.ds(pl.multiple_of(lo + lax.rem(i, tiles) * 512, 512), 512)
            both = nn(turned[k][c, rows, :], gcat[k][pl.ds(0, T), cols])
            both += nn(theirs[k][rows, :], gcat[k][pl.ds(T, T), cols])
            part_sums[k][rows, cols] = both.astype(bf16)

    def into_norm(i, base, k):
        take(base + i)
        back_product(lambda: gcat[k][0:T, i * CH : (i + 1) * CH], (base + i) % 2, add_to(gnorm) if i else store_in(gnorm))
        release(base + i)

    def norm_back(source, i, gain, base, emit):
        @pl.loop(0, 4)
        def _(j):
            rows = pl.ds(pl.multiple_of(i * 64 + j * 16, 16), 16)
            v = source[rows, :]
            center = v - jnp.mean(v, axis=-1, keepdims=True)
            rate = lax.rsqrt(jnp.mean(center * center, axis=-1, keepdims=True) + epsilon)
            xhat = center * rate
            g = gnorm[rows, :]
            gx = g * xhat
            acc[base] += gx[0:8] + gx[8:16]
            acc[base + 1] += g[0:8] + g[8:16]
            e = g * params_wide[gain : gain + 1, :]
            emit(rows, rate * (e - jnp.mean(e, axis=-1, keepdims=True) - xhat * jnp.mean(e * xhat, axis=-1, keepdims=True)))

    def second_norm(i):
        def emit(rows, value):
            total = gcat[DOWN][rows, :].astype(f32) + value
            mid[rows, :] = total
            gcat[OUT][rows, :] = total.astype(bf16)

        norm_back(mid, i, 3, 0, emit)
        if i == 3:
            pair(OUT, 1).start()

    def to_attended():
        take(18)
        back_product(lambda: gcat[OUT][0:T, :], 0, store_in(abuf))
        release(18)

    def attend_back(i):
        masks = half_masks()

        @pl.loop(2 * i, 2 * i + 2)
        def _(p):
            at = pl.multiple_of(p * 128, 128)
            q, k, v = heads_of(p)
            g = abuf[:, pl.ds(at, 128)]
            res = []
            for e in (0, 1):
                head = pl.ds(2 * p + e, 1)
                scores = nt(k, jnp.where(masks[e], q, jnp.zeros_like(q))) * 0.125 - distance[...] * steep[head, :]
                probable = jnp.exp(scores - log_total[head, :])
                gp = nt(v, jnp.where(masks[e], g, jnp.zeros_like(g)))
                gv = nn(probable.astype(bf16), g)
                inner = jnp.sum(gp * probable, axis=0, keepdims=True)
                gs = (probable * (gp - inner)).astype(bf16)
                res.append((tn(gs, k) * 0.125, nn(gs, q) * 0.125, gv))
            for j in range(3):
                gcat[QKV][0:T, pl.ds(pl.multiple_of(at + CH * j, 128), 128)] = jnp.where(
                    masks[0], res[0][j], res[1][j]).astype(bf16)

        if i == 3:
            pair(QKV, 1).start()

    def first_norm(i):
        def emit(rows, value):
            total = (mid[rows, :] + value).astype(bf16)
            gcat[SKIP][rows, :] = total
            wide = total.astype(f32)
            acc[4] += wide[0:8] + wide[8:16]

        norm_back(hid, i, 1, 2, emit)
        if i == 3:
            pair(SKIP, 1).start()
            for row, a in ((0, 4), (1, 2), (2, 3), (3, 0), (4, 1)):
                small[row : row + 1, :] = jnp.sum(acc[a], axis=0, keepdims=True)

    def to_inputs(i):
        take(22 + i)
        if i == 0:
            result_copy.wait()
        back_product(lambda: gcat[SKIP][0:T, :], i % 2, store_in(lbuf.at[i]))
        release(22 + i)
        out_copies[i].start()

    steps = {
        PR: params_step, MK: lambda i: make_masks(), TR: turn, F1: to_hidden, F2: lambda i: norm_forward(hid, 1, i),
        F3: to_projected, AF: attend, F5: lambda i: to_middle(), F6: lambda i: norm_forward(mid, 3, i),
        F7: to_activated, F8: through_down, BF: back_through_down, FR: lambda i: to_result(),
        B2: lambda i: into_norm(i, 14, UP), L2: second_norm, B3: lambda i: to_attended(), A: attend_back,
        B5: lambda i: into_norm(i, 19, QKV), L1: first_norm, B6: to_inputs, R: small_step,
        W4: lambda i: weight_product(DOWN, 512 * i, 512 * i + 512),
        W3: lambda i: weight_product(UP, 2048 * i, 2048 * i + 2048), W2: lambda i: weight_product(OUT, 0, 1024),
        W1: lambda i: weight_product(QKV, 1536 * i, 1536 * i + 1536),
        W0: lambda i: weight_product(SKIP, 512 * i, 512 * i + 512),
    }
    for name, at in PLAN:
        if name in GATHER:
            k = GATHER.index(name)
            ag_do(k, STAGES[at])
            if STAGES[at] == ("ready",):
                ready(k)
        elif name in SCATTER:
            p = SCATTER.index(name)
            rs_do(p, STAGES[at])
            if STAGES[at] == ("own",):
                grad_copies[p].start()
        else:
            steps[name](at)

    for cp in out_copies + grad_copies:
        cp.wait()
    for k in range(n):
        for j in pieces(k):
            pair(k, j).wait_send()
    ag_finish()
    rs_finish()


def whole_layer(tokens, skip, cot, seg_ids, valid, vectors, shards):
    T, d = cot.shape
    n = len(shards)
    hw = [s.shape for s in shards]
    dims = [(16 * h, w) for h, w in hw]
    pieces = [(hw[k][0], w, side, deep) for k, _, w, side, deep in SCATTER_PIECES]
    ng, ns = len(GATHER_PIECES), len(SCATTER_PIECES)
    sem = pltpu.SemaphoreType.DMA
    V = pltpu.VMEM
    scratch = (
        [V(s, f32) for s in hw]
        + [V((2, h, T), bf16) for h, _ in dims]
        + [V((h, T), bf16) for h, _ in dims]
        + [V((2 * T, w), bf16) for _, w in dims]
        + [V((h, w), bf16) for h, w in dims]
        + [V((4, h, w), bf16) for _ in range(2) for h, w, _, _ in pieces]
        + [V((4, h, w // 2), bf16) for _ in range(2) for h, w, _, _ in pieces]
        + [V((5, h, w), bf16) for h, w, _, _ in pieces]
        + [V((5, h, side), bf16) for _ in range(2) for h, _, side, _ in pieces]
        + [V((5, h, max(deep, 128)), bf16) for h, _, _, deep in pieces]
        + [V((2, CH, CH), bf16), V((2, T, CH), bf16), V((T, d), f32), V((T, d), f32), V((T, d), f32),
           V((T, 3 * d), bf16), V((T, d), bf16), V((5, 8, d), f32), V((16, d), f32), V((5, 16, d), f32),
           V((16, d), bf16), V((16, d), f32), V((5, 16, d), bf16), V((HEADS, T), f32), V((HEADS, T), f32), V((T, T), f32),
           sem((ng, SLOTS)), sem((ng, SLOTS)), sem((ng,)), sem((ns, SLOTS)), sem((ns, SLOTS)), sem((n, 5)), sem((n, 5)),
           sem((2, 4)), sem((2,)), sem((4,)), sem((5,)), sem((5,)), sem((5,)), sem((5,)), sem((ns,))]
    )
    vm, anywhere = pl.BlockSpec(memory_space=V), pl.BlockSpec(memory_space=pl.ANY)
    outs = ([jax.ShapeDtypeStruct((16, d), f32)] + [jax.ShapeDtypeStruct(s, f32) for s in hw]
            + [jax.ShapeDtypeStruct((T, d), bf16)] * 3 + [jax.ShapeDtypeStruct((4, 8 * h, w), bf16) for h, w in hw])
    return pl.pallas_call(
        layer_kernel, out_shape=outs,
        in_specs=[anywhere] * 3 + [vm] * 14,
        out_specs=[vm] + [anywhere] * 13,
        scratch_shapes=scratch,
        compiler_params=pltpu.CompilerParams(collective_id=0, has_side_effects=True, vmem_limit_bytes=67043328),
        name="whole_layer",
    )(tokens, skip, cot, seg_ids, valid, *vectors, *shards)


def product(left, right):
    return jnp.dot(left, right, preferred_element_type=jnp.float32)


def outer_product(left, right):
    return lax.dot_general(
        left, right, (((0,), (0,)), ((), ())), preferred_element_type=jnp.float32
    )


def product_back(left, right):
    return lax.dot_general(
        left, right, (((1,), (1,)), ((), ())), preferred_element_type=jnp.float32
    )


def norm_rows(values, gain, shift):
    center = values - jnp.mean(values, axis=-1, keepdims=True)
    spread = jnp.mean(center * center, axis=-1, keepdims=True)
    return center * lax.rsqrt(spread + epsilon) * gain + shift


def gelu_exact(values):
    return 0.5 * values * (1.0 + lax.erf(values * 0.7071067811865476))


def attend_mask(seg_row, valid_row, head_count):
    count_rows = seg_row.shape[0]
    places = jnp.arange(count_rows, dtype=jnp.int32)
    same_utt = seg_row[:, None] == seg_row[None, :]
    diagonal = places[:, None] == places[None, :]
    allowed = same_utt & ((valid_row[None, :] == 1) | diagonal)
    slopes = 2.0 ** (-8.0 * (jnp.arange(head_count, dtype=jnp.float32) + 1.0) / head_count)
    distance = jnp.abs(places[:, None] - places[None, :]).astype(jnp.float32)
    return (allowed, -slopes[:, None, None] * distance[None, :, :])


def split_heads(projected, head_count):
    row_count = projected.shape[0]
    feature_width = projected.shape[1] // 3
    head_size = feature_width // head_count
    queries = projected[:, :feature_width].reshape(row_count, head_count, head_size)
    keys_all = projected[:, feature_width : 2 * feature_width].reshape(
        row_count, head_count, head_size
    )
    values_all = projected[:, 2 * feature_width :].reshape(row_count, head_count, head_size)
    return (queries, keys_all, values_all)


def masked_scores(queries, keys_all, allowed, linear_bias):
    score_scale = queries.shape[2] ** (-0.5)
    raw = (
        jnp.einsum("qhd,khd->hqk", queries, keys_all, preferred_element_type=jnp.float32)
        * score_scale
        + linear_bias
    )
    return jnp.where(allowed[None, :, :], raw, -1e30)


def forward_pass(tokens, skip, weights, allowed, linear_bias, head_count):
    w_skip, b_skip, g_one, beta_one, w_qkv, w_out, g_two, beta_two, w_up, b_up, w_down, b_down = (
        weights
    )
    row_count, feature_width = tokens.shape
    joined = jnp.concatenate([tokens, skip], axis=1)
    hidden = product(joined, w_skip) + b_skip.astype(jnp.float32)
    normed = norm_rows(hidden, g_one.astype(jnp.float32), beta_one.astype(jnp.float32)).astype(
        jnp.bfloat16
    )
    projected = product(normed, w_qkv).astype(jnp.bfloat16)
    queries, keys_all, values_all = split_heads(projected, head_count)
    masked = masked_scores(queries, keys_all, allowed, linear_bias)
    row_top = jnp.max(masked, axis=-1, keepdims=True)
    exponent = jnp.exp(masked - row_top)
    row_total = jnp.sum(exponent, axis=-1, keepdims=True)
    soft_weights = (exponent / row_total).astype(jnp.bfloat16)
    log_total = row_top + jnp.log(row_total)
    weighted = jnp.einsum(
        "hqk,khd->qhd", soft_weights, values_all, preferred_element_type=jnp.float32
    )
    attended = weighted.reshape(row_count, feature_width).astype(jnp.bfloat16)
    middle = hidden + product(attended, w_out)
    normed_two = norm_rows(middle, g_two.astype(jnp.float32), beta_two.astype(jnp.float32)).astype(
        jnp.bfloat16
    )
    hidden_up = product(normed_two, w_up) + b_up.astype(jnp.float32)
    activated = gelu_exact(hidden_up).astype(jnp.bfloat16)
    result = middle + (product(activated, w_down) + b_down.astype(jnp.float32))
    stored = (
        joined,
        hidden,
        normed,
        projected,
        log_total,
        attended,
        middle,
        normed_two,
        hidden_up,
        activated,
    )
    return (stored, result)


def backward_feed(stored, weights, cotangent):
    (
        joined,
        hidden,
        normed,
        projected,
        log_total,
        attended,
        middle,
        normed_two,
        hidden_up,
        activated,
    ) = stored
    w_skip, b_skip, g_one, beta_one, w_qkv, w_out, g_two, beta_two, w_up, b_up, w_down, b_down = (
        weights
    )
    grad_result = cotangent.astype(jnp.float32)
    grad_activated = product_back(cotangent, w_down)
    grad_b_down = jnp.sum(grad_result, axis=0)
    gelu_value, gelu_pull = jax.vjp(gelu_exact, hidden_up)
    grad_up = gelu_pull(grad_activated)[0].astype(jnp.bfloat16)
    grad_b_up = jnp.sum(grad_up.astype(jnp.float32), axis=0)
    grad_normed_two = product_back(grad_up, w_up)
    norm_value, norm_pull = jax.vjp(
        norm_rows, middle, g_two.astype(jnp.float32), beta_two.astype(jnp.float32)
    )
    grad_middle_norm, grad_g_two, grad_beta_two = norm_pull(grad_normed_two)
    grad_middle = grad_result + grad_middle_norm
    feed_terms = (grad_up, grad_b_up, cotangent, grad_b_down, grad_g_two, grad_beta_two)
    return (feed_terms, grad_middle)


def backward_front(stored, weights, grad_middle, allowed, linear_bias, head_count):
    (
        joined,
        hidden,
        normed,
        projected,
        log_total,
        attended,
        middle,
        normed_two,
        hidden_up,
        activated,
    ) = stored
    w_skip, b_skip, g_one, beta_one, w_qkv, w_out, g_two, beta_two, w_up, b_up, w_down, b_down = (
        weights
    )
    row_count, feature_width = hidden.shape
    branch_grad = grad_middle.astype(jnp.bfloat16)
    grad_attended = product_back(branch_grad, w_out).astype(jnp.bfloat16)
    queries, keys_all, values_all = split_heads(projected, head_count)
    score_scale = queries.shape[2] ** (-0.5)
    masked = masked_scores(queries, keys_all, allowed, linear_bias)
    probable = jnp.exp(masked - log_total)
    soft_weights = probable.astype(jnp.bfloat16)
    grad_heads = grad_attended.reshape(row_count, head_count, feature_width // head_count)
    grad_probable = jnp.einsum(
        "qhd,khd->hqk", grad_heads, values_all, preferred_element_type=jnp.float32
    )
    grad_values = jnp.einsum(
        "hqk,qhd->khd", soft_weights, grad_heads, preferred_element_type=jnp.float32
    )
    inner_sum = jnp.sum(grad_probable * probable, axis=-1, keepdims=True)
    grad_scores = (probable * (grad_probable - inner_sum)).astype(jnp.bfloat16)
    grad_queries = (
        jnp.einsum("hqk,khd->qhd", grad_scores, keys_all, preferred_element_type=jnp.float32)
        * score_scale
    )
    grad_keys = (
        jnp.einsum("hqk,qhd->khd", grad_scores, queries, preferred_element_type=jnp.float32)
        * score_scale
    )
    grad_projected = jnp.concatenate(
        [
            grad_queries.reshape(row_count, feature_width),
            grad_keys.reshape(row_count, feature_width),
            grad_values.reshape(row_count, feature_width),
        ],
        axis=1,
    ).astype(jnp.bfloat16)
    grad_normed = product_back(grad_projected, w_qkv)
    norm_value, norm_pull = jax.vjp(
        norm_rows, hidden, g_one.astype(jnp.float32), beta_one.astype(jnp.float32)
    )
    grad_hidden_norm, grad_g_one, grad_beta_one = norm_pull(grad_normed)
    grad_hidden = (grad_middle + grad_hidden_norm).astype(jnp.bfloat16)
    grad_b_skip = jnp.sum(grad_hidden.astype(jnp.float32), axis=0)
    grad_joined = product_back(grad_hidden, w_skip)
    grad_tokens = grad_joined[:, :feature_width].astype(jnp.bfloat16)
    grad_skip = grad_joined[:, feature_width:].astype(jnp.bfloat16)
    front_terms = (grad_hidden, grad_b_skip, grad_g_one, grad_beta_one, grad_projected, branch_grad)
    return (grad_tokens, grad_skip, front_terms)


AXES = ("wide", "narrow")


def gather_plain(values):
    return [lax.all_gather(v, AXES, axis=0, tiled=True) for v in values]


def hand_over_kernel(*refs):
    table = refs[0]
    sources = refs[1:9]
    vectors = refs[9:16]
    targets = refs[16:24]
    buffers = refs[24:32]
    small, in_sem, out_sem = refs[32:]
    me = lax.axis_index("wide") * 2 + lax.axis_index("narrow")
    arrive = [pltpu.make_async_copy(s, b, in_sem.at[i]) for i, (s, b) in enumerate(zip(sources, buffers))]
    leave = [pltpu.make_async_copy(b, t, out_sem.at[i]) for i, (b, t) in enumerate(zip(buffers, targets))]
    load = pltpu.make_async_copy(table, small, in_sem.at[len(sources)])
    load.start()
    for cp in arrive:
        cp.start()
    load.wait()
    rolled = pltpu.roll(small[...], lax.rem(32 - me, 32) * 32, 1)
    for i in range(6):
        vectors[i][...] = rolled[i, 0:32]
    row = 6 + lax.div(me, 8)
    wide = pltpu.roll(jnp.where(lax.broadcasted_iota(jnp.int32, small.shape, 0) == row, small[...], 0.0),
                      lax.rem(8 - lax.rem(me, 8), 8) * 128, 1)
    vectors[6][...] = jnp.sum(wide[:, 0:128], axis=0)
    for a, l in zip(arrive, leave):
        a.wait()
        l.start()
    for l in leave:
        l.wait()


def hand_over(small, arrays):
    vm, anywhere = pl.BlockSpec(memory_space=pltpu.VMEM), pl.BlockSpec(memory_space=pl.ANY)
    sem = pltpu.SemaphoreType.DMA
    n = len(arrays)
    outs = [jax.ShapeDtypeStruct((32,), f32)] * 6 + [jax.ShapeDtypeStruct((128,), f32)] + [
        jax.ShapeDtypeStruct(a.shape, a.dtype) for a in arrays]
    return pl.pallas_call(
        hand_over_kernel, out_shape=outs,
        in_specs=[anywhere] * (n + 1), out_specs=[vm] * 7 + [anywhere] * n,
        scratch_shapes=[pltpu.VMEM(a.shape, a.dtype) for a in arrays] + [pltpu.VMEM(small.shape, f32), sem((n + 1,)), sem((n,))],
        name="hand_over",
    )(small, *arrays)


def own_layer(tokens, skip, seg_ids, valid, w_skip, b_skip, g_one, beta_one, w_qkv, w_out, g_two, beta_two,
              w_up, b_up, w_down, b_down, cotangent):
    vectors = [v[None, :] for v in (b_skip, g_one, beta_one, g_two, beta_two, b_down, b_up)]
    small, *rest = whole_layer(
        tokens, skip, cotangent, seg_ids, valid, vectors, (w_skip, w_qkv, w_out, w_up, w_down))
    (grad_b_skip, grad_g_one, grad_beta_one, grad_g_two, grad_beta_two, grad_b_down, grad_b_up,
     grad_w_skip, grad_w_qkv, grad_w_out, grad_w_up, grad_w_down, result, grad_tokens, grad_skip) = hand_over(small, rest[:8])
    return (
        result, grad_tokens, grad_skip,
        grad_w_skip, grad_b_skip, grad_g_one, grad_beta_one, grad_w_qkv, grad_w_out,
        grad_g_two, grad_beta_two, grad_w_up, grad_b_up, grad_w_down, grad_b_down,
    )


def plain_layer(tokens, skip, seg_ids, valid, w_skip, b_skip, g_one, beta_one, w_qkv, w_out, g_two, beta_two,
                w_up, b_up, w_down, b_down, cotangent):
    weights = gather_plain(
        (w_skip, b_skip, g_one, beta_one, w_qkv, w_out, g_two, beta_two, w_up, b_up, w_down, b_down))
    allowed, linear_bias = attend_mask(seg_ids[0], valid[0], HEADS)
    stored, result = forward_pass(tokens, skip, weights, allowed, linear_bias, HEADS)
    (joined, hidden, normed, projected, log_total, attended, middle, normed_two, hidden_up, activated) = stored
    feed_terms, grad_middle = backward_feed(stored, weights, cotangent)
    grad_tokens, grad_skip, front_terms = backward_front(
        stored, weights, grad_middle, allowed, linear_bias, HEADS)
    grad_up, grad_b_up, grad_result, grad_b_down, grad_g_two, grad_beta_two = feed_terms
    grad_hidden, grad_b_skip, grad_g_one, grad_beta_one, grad_projected, branch_grad = front_terms
    lefts = (joined, normed, attended, normed_two, activated)
    rights = (grad_hidden, grad_projected, branch_grad, grad_up, grad_result)

    def scatter(v):
        return lax.psum_scatter(v, AXES, scatter_dimension=0, tiled=True)

    big = [scatter(outer_product(a, b)) for a, b in zip(lefts, rights)]
    grad_b_skip, grad_g_one, grad_beta_one, grad_g_two, grad_beta_two, grad_b_up, grad_b_down = [
        scatter(v) for v in
        (grad_b_skip, grad_g_one, grad_beta_one, grad_g_two, grad_beta_two, grad_b_up, grad_b_down)]
    return (
        result.astype(bf16), grad_tokens, grad_skip,
        big[0], grad_b_skip, grad_g_one, grad_beta_one, big[1], big[2],
        grad_g_two, grad_beta_two, big[3], grad_b_up, big[4], grad_b_down,
    )


def solution(mesh):
    return jax.shard_map(
        own_layer if dict(mesh.shape) == {"wide": 16, "narrow": 2} else plain_layer,
        mesh=mesh,
        in_specs=(
            P(("wide", "narrow"), None),
            P(("wide", "narrow"), None),
            P(("wide", "narrow"), None),
            P(("wide", "narrow"), None),
            P(("wide", "narrow"), None),
            P(("wide", "narrow")),
            P(("wide", "narrow")),
            P(("wide", "narrow")),
            P(("wide", "narrow"), None),
            P(("wide", "narrow"), None),
            P(("wide", "narrow")),
            P(("wide", "narrow")),
            P(("wide", "narrow"), None),
            P(("wide", "narrow")),
            P(("wide", "narrow"), None),
            P(("wide", "narrow")),
            P(("wide", "narrow"), None),
        ),
        out_specs=(
            P(("wide", "narrow"), None),
            P(("wide", "narrow"), None),
            P(("wide", "narrow"), None),
            P(("wide", "narrow"), None),
            P(("wide", "narrow")),
            P(("wide", "narrow")),
            P(("wide", "narrow")),
            P(("wide", "narrow"), None),
            P(("wide", "narrow"), None),
            P(("wide", "narrow")),
            P(("wide", "narrow")),
            P(("wide", "narrow"), None),
            P(("wide", "narrow")),
            P(("wide", "narrow"), None),
            P(("wide", "narrow")),
        ),
        check_vma=False,
    )
```
